32 devices in a mesh: seq: 4 (over y, x), wt: 8 (over z, core).
Axes of the slice: x: 2, y: 2, z: 4, core: 2. Of those that a mesh axis runs over, the one named last changes fastest.
Arguments:
- inputs: bfloat16 [8, 512, 2048], P('wt', 'seq'), may hold values from -6 to 6
- segment_ids: int32 [8, 512], P('wt'), may hold values from 0 to 2, never falling along the last dimension, each value on 1 to 256 neighbouring positions
- valid_lengths: int32 [8], replicated, may hold values from 256 to 512, as said below
- teacher: bfloat16 [8, 512, 2048], P('wt', 'seq')
- w_qkv: bfloat16 [2048, 2560], P(('seq', 'wt')), may hold values from -0.125 to 0.125
- conv_weight: bfloat16 [3, 2048], P(None, 'seq'), may hold values from -3 to 3
- w_out: bfloat16 [2048, 2048], P(('seq', 'wt')), may hold values from -2 to 2
- norm_gain: bfloat16 [2048], P(('seq', 'wt')), may hold values from 0.5 to 1.5
- w_gate_up: bfloat16 [2, 2048, 5632], P(None, 'seq', 'wt'), may hold values from -0.125 to 0.125
- w_down: bfloat16 [5632, 2048], P('wt', 'seq'), may hold values from -0.078125 to 0.078125
- mlp_gain: bfloat16 [2048], P(('seq', 'wt')), may hold values from 0.5 to 1.5
Outputs:
- outputs: bfloat16 [8, 512, 2048], P('wt', 'seq')
- inputs_grad: float32 [8, 512, 2048], P('wt', 'seq')
- mean_loss: float32 [], replicated
- grad_w_qkv: float32 [2048, 2560], P(('seq', 'wt'))
- grad_conv: float32 [3, 2048], P(None, ('seq', 'wt'))
- grad_w_out: float32 [2048, 2048], P(('seq', 'wt'))
- grad_norm_gain: float32 [2048], P(('seq', 'wt'))
- grad_w_gate_up: float32 [2, 2048, 5632], P(None, 'seq', 'wt')
- grad_w_down: float32 [5632, 2048], P('wt', 'seq')
- grad_mlp_gain: float32 [2048], P(('seq', 'wt'))
The draws below stay inside these ranges and needn't reach their ends.
Inputs may be any that keep to these rules, and one draw needn't show every extreme that they name: `segment_ids`: in each sequence the document numbers start at 0, never fall and take every value up to 2; a document holds at most 256 tokens, and some document exactly that many. `valid_lengths`: some sequence counts in full, another in its first half.
All inputs are finite; a program needn't handle non-finite values.
Results may differ from the reference program's by a relative error of at most 0.011.
Values may be sent and summed in bfloat16 or wider, within the bound.
A program may use at most 192 MiB of HBM per device.

```python
import math
from functools import partial
import jax
import jax.numpy as jnp
import numpy as np
from jax import lax

D = 2048
H = 16
FEAT = 16
FF = 5632
KCONV = 3
DV = 128
QKV = 2560
SEQS = 8
LEN = 512
DOCS = 3


def draw_valid_lengths(key, part):
    key_lengths = jax.random.fold_in(key, 11)
    key_pick = jax.random.fold_in(key, 23)
    lengths = jax.random.randint(key_lengths, (SEQS,), LEN // 2, LEN + 1)
    chosen = jax.random.randint(key_pick, (), 0, SEQS)
    places = jnp.arange(SEQS)
    lengths = jnp.where(places == chosen, LEN, lengths)
    lengths = jnp.where(places == (chosen + 1) % SEQS, LEN // 2, lengths)
    return lengths.astype(jnp.int32)


def draw_teacher(key, part):
    position = (jnp.arange(SEQS)[:, None] * LEN + jnp.arange(LEN)[None, :]).astype(jnp.float32) / (SEQS * LEN)
    samples = jax.random.normal(key, (SEQS, LEN, D), jnp.float32)
    row_scale = 1.0 + 2.0 * position
    return (samples * row_scale[:, :, None]).astype(jnp.bfloat16)


def level_of(key, shape, cuts, smallest, largest):
    loudness, own = 1.0, jax.random.fold_in(key, 6)
    for dim, parts in cuts:
        draws = jnp.exp(jax.random.uniform(jax.random.fold_in(own, dim), (parts,), jnp.float32, smallest / len(cuts), largest / len(cuts)))
        loudness = loudness * jnp.repeat(draws, shape[dim] // parts).reshape([-1 if axis == dim else 1 for axis in range(len(shape))])
    return loudness


def length_profile(count, total, limit, skew):
    weights = [(1 << 20) // math.isqrt(rank ** skew) + 1 for rank in range(2, count + 1)]
    rest, given = total - limit - (count - 1), [1] * (count - 1)
    while rest > 0:
        free = [i for i in range(count - 1) if given[i] < limit]
        whole, budget = sum([weights[i] for i in free]), rest
        for i in free:
            more = min(limit - given[i], max(1, budget * weights[i] // whole), rest)
            given[i] = given[i] + more
            rest = rest - more
    return np.array([limit] + given)


def ragged(key, amount, total, bound, slope):
    if amount == 2:
        one = jax.random.randint(key, (), max(1, total - bound), min(bound, total - 1) + 1)
        return jnp.stack([one, total - one])
    tallies = jnp.asarray(length_profile(amount, total, bound, slope), jnp.int32)
    couples = (amount - 1) // 2
    donor, receiver = tallies[1:1 + 2 * couples:2], tallies[2:2 + 2 * couples:2]
    room = jnp.minimum(donor - 1, bound - receiver)
    moved = jax.random.randint(jax.random.fold_in(key, 1), (couples,), 0, 1 << 20) % (room + 1)
    tallies = tallies.at[1:1 + 2 * couples:2].set(donor - moved).at[2:2 + 2 * couples:2].set(receiver + moved)
    return tallies[jax.random.permutation(jax.random.fold_in(key, 2), amount)]


def noise(key, shape, spread, most, shards=(), kind=jnp.bfloat16):
    level = level_of(key, shape, shards, -0.22, 0.18) if shards else 1.0
    entries = jax.random.normal(key, shape, jnp.float32) * spread * level
    return jnp.minimum(jnp.maximum(entries, -most), most).astype(kind)


def setup_inputs(seed: int = 0) -> dict:
    key_list = jax.random.split(jax.random.key(seed), 12)
    inputs = noise(key_list[0], (SEQS, LEN, D), 1.0, 6.0, ((0, 8), (1, 4)))
    segment_ids = jax.vmap(lambda own: jnp.searchsorted(jnp.cumsum(ragged(own, DOCS, LEN, LEN // 2, 1)), jnp.arange(LEN), side="right"))(jax.random.split(key_list[1], SEQS)).reshape((SEQS, LEN)).astype(jnp.int32)
    valid_lengths = draw_valid_lengths(jax.random.fold_in(key_list[11], 71), 0)
    teacher = draw_teacher(jax.random.fold_in(key_list[11], 71), 0)
    w_qkv = noise(key_list[4], (D, QKV), D ** -0.5, 0.125, ((0, 32),))
    conv_weight = noise(key_list[5], (KCONV, D), 0.6, 3.0, ((1, 4),))
    w_out = noise(key_list[6], (D, D), 8 ** -0.5, 2.0, ((0, 32),))
    norm_gain = jnp.clip(1.0 + 0.1 * jax.random.normal(key_list[7], (D,), jnp.float32), 0.5, 1.5).astype(jnp.bfloat16)
    w_gate_up = noise(key_list[8], (2, D, FF), D ** -0.5, 0.125, ((1, 4), (2, 8)))
    w_down = noise(key_list[9], (FF, D), FF ** -0.5, 0.078125, ((0, 8), (1, 4)))
    mlp_gain = jnp.clip(1.0 + 0.1 * jax.random.normal(key_list[10], (D,), jnp.float32), 0.5, 1.5).astype(jnp.bfloat16)
    return {"inputs": inputs, "segment_ids": segment_ids, "valid_lengths": valid_lengths, "teacher": teacher, "w_qkv": w_qkv, "conv_weight": conv_weight, "w_out": w_out, "norm_gain": norm_gain, "w_gate_up": w_gate_up, "w_down": w_down, "mlp_gain": mlp_gain}


epsilon = 1e-05
highest = lax.Precision.HIGHEST

@jax.custom_vjp
def low(v):
    return lax.optimization_barrier(v.astype(jnp.bfloat16)).astype(jnp.float32)

@jax.custom_vjp
def low_back(v):
    return v

def low_keep(v):
    return (low(v), None)

def low_pass(kept, grad):
    return (grad,)

def back_keep(v):
    return (v, None)

def back_low(kept, grad):
    return (low(grad),)
low.defvjp(low_keep, low_pass)
low_back.defvjp(back_keep, back_low)

def matmul(former, latter):
    return jnp.dot(former, latter, precision=highest, preferred_element_type=jnp.float32)

def rms_norm(values, gain_vector):
    inverse_root = lax.rsqrt(lax.optimization_barrier(jnp.mean(values * values, axis=-1, keepdims=True)) + epsilon)
    return values * inverse_root * gain_vector

def short_conv(values, segment, conv_weight):
    summed = conv_weight[0] * values
    for tap_index in range(1, KCONV):
        shifted = jnp.concatenate([jnp.zeros((tap_index, values.shape[1]), jnp.float32), values[:-tap_index]], axis=0)
        earlier = jnp.concatenate([jnp.full((tap_index,), -1, jnp.int32), segment[:-tap_index]], axis=0)
        summed = summed + conv_weight[tap_index] * shifted * (earlier == segment).astype(jnp.float32)[:, None]
    return summed

def head_mix(queries, key_rows, values, segment):
    length = segment.shape[0]
    places = jnp.arange(length, dtype=jnp.int32)
    allowed = (segment[:, None] == segment[None, :]) & (places[:, None] >= places[None, :])
    scores = low_back(matmul(queries, key_rows.T)) * 0.25
    kernel = jnp.where(allowed, 1.0 + scores + 0.5 * scores * scores, 0.0)
    denominator = lax.optimization_barrier(jnp.sum(kernel, axis=1, keepdims=True))
    numerator = low_back(matmul(low(kernel), values))
    return numerator / denominator

def whole_layer(inputs, w_qkv, conv_weight, w_out, norm_gain, w_gate_up, w_down, mlp_gain, segment, teacher, keep_mask):
    length = inputs.shape[0]
    hidden = low(rms_norm(inputs, norm_gain))
    projected = low(low_back(matmul(hidden, w_qkv))).reshape(length, H, 2 * FEAT + DV)
    queries = projected[:, :, :FEAT].transpose(1, 0, 2)
    key_rows = projected[:, :, FEAT:2 * FEAT].transpose(1, 0, 2)
    raw_values = projected[:, :, 2 * FEAT:].reshape(length, D)
    mixed_values = low(short_conv(raw_values, segment, conv_weight)).reshape(length, H, DV).transpose(1, 0, 2)
    mixing = jax.checkpoint(partial(head_mix, segment=segment))
    heads_out = lax.map(lambda operands: mixing(operands[0], operands[1], operands[2]), (queries, key_rows, mixed_values))
    mixer = low(low_back(heads_out.transpose(1, 0, 2).reshape(length, D)))
    attended = inputs + low_back(matmul(mixer, w_out))
    normed = low(rms_norm(attended, mlp_gain))
    gate = low_back(matmul(normed, w_gate_up[0]))
    up = low_back(matmul(normed, w_gate_up[1]))
    active = low(jax.nn.silu(gate) * up)
    outputs = attended + low_back(matmul(active, w_down))
    residual_error = (outputs - teacher) * keep_mask[:, None]
    return (outputs, 0.5 * jnp.sum(residual_error * residual_error))

def reference(inputs, segment_ids, valid_lengths, teacher, w_qkv, conv_weight, w_out, norm_gain, w_gate_up, w_down, mlp_gain):
    params = tuple((weight.astype(jnp.float32) for weight in (w_qkv, conv_weight, w_out, norm_gain, w_gate_up, w_down, mlp_gain)))
    places = jnp.arange(LEN, dtype=jnp.int32)

    def one_sequence(totals, pieces):
        seq_rows, segment, seq_valid, target = pieces
        keep_mask = (places < seq_valid).astype(jnp.float32)

        def forward(start_rows, *weights):
            return whole_layer(start_rows, *weights, segment, target.astype(jnp.float32), keep_mask)
        (outputs, energy), pullback = jax.vjp(forward, seq_rows.astype(jnp.float32), *params)
        gradients = pullback((jnp.zeros_like(outputs), jnp.ones_like(energy)))
        totals = tuple((running_total + gradient for running_total, gradient in zip(totals, gradients[1:])))
        return (totals, (outputs.astype(jnp.bfloat16), gradients[0], energy))
    starting = tuple((jnp.zeros_like(parameter) for parameter in params))
    totals, (outputs, inputs_grad, energies) = lax.scan(one_sequence, starting, (inputs, segment_ids, valid_lengths, teacher))
    mean_loss = 2.0 * jnp.sum(energies) / (jnp.sum(valid_lengths).astype(jnp.float32) * D)
    return (outputs, inputs_grad, mean_loss, totals[0], totals[1], totals[2], totals[3], totals[4], totals[5], totals[6])
```

```python
import jax
import jax.numpy as jnp
from jax import lax
from jax.experimental import pallas as pl
from jax.experimental.pallas import tpu as pltpu
from jax.sharding import PartitionSpec as P

H = 16
FEAT = 16
KCONV = 3
DV = 128


epsilon = 1e-05
block_limit = 512


def rms_norm(values, gain_vector):
    inverse_root = lax.rsqrt(jnp.mean(values * values, axis=-1, keepdims=True) + epsilon)
    return values * inverse_root * gain_vector


def contract_last(former, latter):
    return lax.dot_general(
        former, latter, (((1,), (1,)), ((), ())), preferred_element_type=jnp.float32
    )


def contract_first(former, latter):
    return lax.dot_general(
        former, latter, (((0,), (0,)), ((), ())), preferred_element_type=jnp.float32
    )


def shift_down(values, amount, filler):
    padding = jnp.full((amount,) + values.shape[1:], filler, values.dtype)
    return jnp.concatenate([padding, values[:-amount]], axis=0)


def shift_up(values, amount):
    padding = jnp.zeros((amount,) + values.shape[1:], values.dtype)
    return jnp.concatenate([values[amount:], padding], axis=0)


def gated_unit(gate_in, up_in):
    return jax.nn.silu(gate_in) * up_in


def block_kernel(query_block, key_block, query_segments, key_segments, query_start, key_start):
    row_width = query_segments.shape[0]
    scaled_dots = (
        jnp.einsum("hfq,hfk->hqk", query_block, key_block, preferred_element_type=jnp.float32)
        * 0.25
    )
    query_places = query_start + jnp.arange(row_width, dtype=jnp.int32)
    key_places = key_start + jnp.arange(row_width, dtype=jnp.int32)
    allowed = (query_segments[:, None] == key_segments[None, :]) & (
        query_places[:, None] >= key_places[None, :]
    )
    kernel = jnp.where(allowed[None], 1.0 + scaled_dots + 0.5 * scaled_dots * scaled_dots, 0.0)
    return (scaled_dots, allowed, kernel)


def attend_forward(queries, key_rows, values, segments, block_rows):
    head_count, length, value_width = values.shape
    block_count = length // block_rows

    def query_step(query_index, running):
        outputs, denominators = running
        query_start = query_index * block_rows
        query_block = lax.dynamic_slice_in_dim(queries, query_start, block_rows, 2)
        query_segments = lax.dynamic_slice_in_dim(segments, query_start, block_rows, 0)

        def key_step(inner_index, inner_running):
            numerator, denominator = inner_running
            key_start = inner_index * block_rows
            key_block = lax.dynamic_slice_in_dim(key_rows, key_start, block_rows, 2)
            value_block = lax.dynamic_slice_in_dim(values, key_start, block_rows, 1)
            key_segments = lax.dynamic_slice_in_dim(segments, key_start, block_rows, 0)
            scaled_dots, allowed, kernel = block_kernel(
                query_block, key_block, query_segments, key_segments, query_start, key_start
            )
            numerator = numerator + jnp.einsum(
                "hqk,hkd->hqd",
                kernel.astype(jnp.bfloat16),
                value_block,
                preferred_element_type=jnp.float32,
            )
            denominator = denominator + jnp.sum(kernel, axis=2)
            return (numerator, denominator)

        starting = (
            jnp.zeros((head_count, block_rows, value_width), jnp.float32),
            jnp.zeros((head_count, block_rows), jnp.float32),
        )
        numerator, denominator = lax.fori_loop(0, query_index + 1, key_step, starting)
        outputs = lax.dynamic_update_slice_in_dim(
            outputs, numerator / denominator[:, :, None], query_start, 1
        )
        denominators = lax.dynamic_update_slice_in_dim(denominators, denominator, query_start, 1)
        return (outputs, denominators)

    initial = (
        jnp.zeros((head_count, length, value_width), jnp.float32),
        jnp.zeros((head_count, length), jnp.float32),
    )
    return lax.fori_loop(0, block_count, query_step, initial)


def attend_backward(
    queries, key_rows, values, segments, outputs, denominators, incoming, block_rows
):
    head_count, length, value_width = values.shape
    feature_width = queries.shape[1]
    block_count = length // block_rows

    def query_step(query_index, running):
        query_grads, key_grads, value_grads = running
        query_start = query_index * block_rows
        query_block = lax.dynamic_slice_in_dim(queries, query_start, block_rows, 2)
        query_segments = lax.dynamic_slice_in_dim(segments, query_start, block_rows, 0)
        incoming_block = lax.dynamic_slice_in_dim(incoming, query_start, block_rows, 1)
        output_block = lax.dynamic_slice_in_dim(outputs, query_start, block_rows, 1)
        denominator = lax.dynamic_slice_in_dim(denominators, query_start, block_rows, 1)
        numerator_grad = (incoming_block / denominator[:, :, None]).astype(jnp.bfloat16)
        denominator_grad = -jnp.sum(incoming_block * output_block, axis=2) / denominator

        def key_step(inner_index, inner_running):
            query_total, key_grads, value_grads = inner_running
            key_start = inner_index * block_rows
            key_block = lax.dynamic_slice_in_dim(key_rows, key_start, block_rows, 2)
            value_block = lax.dynamic_slice_in_dim(values, key_start, block_rows, 1)
            key_segments = lax.dynamic_slice_in_dim(segments, key_start, block_rows, 0)
            scaled_dots, allowed, kernel = block_kernel(
                query_block, key_block, query_segments, key_segments, query_start, key_start
            )
            weights_low = kernel.astype(jnp.bfloat16)
            weight_grad = jnp.einsum(
                "hqd,hkd->hqk", numerator_grad, value_block, preferred_element_type=jnp.float32
            )
            kernel_grad = jnp.where(allowed[None], weight_grad + denominator_grad[:, :, None], 0.0)
            dots_grad = (0.25 * kernel_grad * (1.0 + scaled_dots)).astype(jnp.bfloat16)
            query_total = query_total + jnp.einsum(
                "hqk,hfk->hfq", dots_grad, key_block, preferred_element_type=jnp.float32
            )
            key_part = jnp.einsum(
                "hqk,hfq->hfk", dots_grad, query_block, preferred_element_type=jnp.float32
            )
            value_part = jnp.einsum(
                "hqk,hqd->hkd", weights_low, numerator_grad, preferred_element_type=jnp.float32
            )
            key_grads = lax.dynamic_update_slice_in_dim(
                key_grads,
                lax.dynamic_slice_in_dim(key_grads, key_start, block_rows, 2) + key_part,
                key_start,
                2,
            )
            value_grads = lax.dynamic_update_slice_in_dim(
                value_grads,
                lax.dynamic_slice_in_dim(value_grads, key_start, block_rows, 1) + value_part,
                key_start,
                1,
            )
            return (query_total, key_grads, value_grads)

        starting = jnp.zeros((head_count, feature_width, block_rows), jnp.float32)
        query_total, key_grads, value_grads = lax.fori_loop(
            0, query_index + 1, key_step, (starting, key_grads, value_grads)
        )
        query_grads = lax.dynamic_update_slice_in_dim(query_grads, query_total, query_start, 2)
        return (query_grads, key_grads, value_grads)

    initial = (
        jnp.zeros((head_count, feature_width, length), jnp.float32),
        jnp.zeros((head_count, feature_width, length), jnp.float32),
        jnp.zeros((head_count, length, value_width), jnp.float32),
    )
    return lax.fori_loop(0, block_count, query_step, initial)


MESH = pl.DeviceIdType.MESH
VMEM = pl.BlockSpec(memory_space=pltpu.VMEM)


class Place:
    def __init__(self, seq, wt):
        self.seq, self.wt = seq, wt
        self.ys, self.zs = seq // 2, wt // 2
        self.s, self.w = lax.axis_index("seq"), lax.axis_index("wt")
        self.y, self.x = lax.div(self.s, 2), lax.rem(self.s, 2)
        self.z, self.c = lax.div(self.w, 2), lax.rem(self.w, 2)

    def across(self):
        return (self.y * 2 + 1 - self.x, self.w)

    def beside(self, step):
        return lax.rem(self.y + step, self.ys)

    def column(self, y):
        return (y * 2 + self.x, self.w)

    def partner(self):
        return (self.s, self.z * 2 + 1 - self.c)

    def level(self, z):
        return (self.s, z * 2 + self.c)

    def meet(self, square, line):
        barrier = pltpu.get_barrier_semaphore()
        count = 0
        if square:
            for step in range(1, self.seq):
                device = (lax.rem(self.s + step, self.seq), self.w)
                pl.semaphore_signal(barrier, inc=1, device_id=device, device_id_type=MESH)
                count += 1
        if line:
            for step in range(1, self.wt):
                device = (self.s, lax.rem(self.w + step, self.wt))
                pl.semaphore_signal(barrier, inc=1, device_id=device, device_id_type=MESH)
                count += 1
        pl.semaphore_wait(barrier, count)


def send(source, target, leaving, arriving, device):
    return pltpu.make_async_remote_copy(
        src_ref=source,
        dst_ref=target,
        send_sem=leaving,
        recv_sem=arriving,
        device_id=device,
        device_id_type=MESH,
    )


def add_into(target, sources):
    if len(target.shape) == 3:
        for index in range(target.shape[0]):
            add_into(target.at[index], [source.at[index] for source in sources])
        return
    rows = target.shape[0]
    tile = next(t for t in (64, 32, 16, 8, rows) if rows % t == 0)

    def step(index, carry):
        window = pl.ds(pl.multiple_of(index * tile, tile), tile)
        total = sources[0][window, :].astype(jnp.float32)
        for source in sources[1:]:
            total = total + source[window, :].astype(jnp.float32)
        target[window, :] = total.astype(target.dtype)
        return carry

    lax.fori_loop(0, rows // tile, step, 0)


class SquareGather:
    @staticmethod
    def semaphores(seq):
        return [
            pltpu.SemaphoreType.DMA((2 + seq // 2,)),
            pltpu.SemaphoreType.DMA((seq // 2, 3)),
            pltpu.SemaphoreType.DMA((seq, 2)),
        ]

    def __init__(self, at, view, own, sems):
        self.at, self.view, self.own = at, view, own
        self.over_x, self.over_y, self.got = sems
        self.sent = []

    def go(self, source, s, half, leaving, device):
        copy = send(source, self.view(s, half), leaving, self.got.at[s, half], device)
        copy.start()
        self.sent.append(copy)

    def wait(self, s, half):
        slot = self.view(s, half)
        send(slot, slot, self.over_x.at[0], self.got.at[s, half], self.at.across()).wait_recv()

    def start(self):
        at = self.at
        for half in range(2):
            self.go(self.own(half), at.s, half, self.over_x.at[half], at.across())
            for step in range(1, at.ys):
                target = at.column(at.beside(step))
                self.go(self.own(1 - half), at.s, 1 - half, self.over_y.at[step, half], target)

    def relay(self):
        at = self.at
        other = at.y * 2 + 1 - at.x
        self.wait(other, 0)
        for step in range(1, at.ys):
            self.go(self.view(other, 0), other, 0, self.over_y.at[step, 2], at.column(at.beside(step)))
        for step in range(1, at.ys):
            s = at.beside(step) * 2 + at.x
            self.wait(s, 1)
            self.go(self.view(s, 1), s, 1, self.over_x.at[1 + step], at.across())

    def finish(self):
        at = self.at
        self.wait(at.y * 2 + 1 - at.x, 1)
        for step in range(1, at.ys):
            y = at.beside(step)
            self.wait(y * 2 + at.x, 0)
            self.wait(y * 2 + 1 - at.x, 0)
            self.wait(y * 2 + 1 - at.x, 1)
        for copy in self.sent:
            copy.wait_send()


class SquareSum:
    @staticmethod
    def scratch(seq, half_shape):
        ys = seq // 2
        return [
            pltpu.VMEM((ys,) + half_shape, jnp.bfloat16),
            pltpu.VMEM((ys, 2) + half_shape, jnp.bfloat16),
            pltpu.VMEM((ys,) + half_shape, jnp.bfloat16),
            pltpu.VMEM(half_shape, jnp.bfloat16),
            pltpu.VMEM((ys,) + half_shape, jnp.bfloat16),
            pltpu.VMEM(half_shape, jnp.bfloat16),
            pltpu.SemaphoreType.DMA((ys, 2, 2)),
            pltpu.SemaphoreType.DMA((ys, 3, 2)),
        ]

    def __init__(self, at, part, scratch):
        self.at, self.part = at, part
        self.from_x, self.from_y, self.last_y, self.last_x, self.sum_y, self.sum_x, self.xs, self.yss = scratch
        self.sent = []

    def go(self, source, target, leaving, arriving, device):
        copy = send(source, target, leaving, arriving, device)
        copy.start()
        self.sent.append(copy)

    def wait(self, slot, leaving, arriving):
        send(slot, slot, leaving, arriving, self.at.across()).wait_recv()

    def start(self):
        at = self.at
        for y in range(at.ys):
            self.go(
                self.part(y * 2 + 1 - at.x, 0),
                self.from_x.at[y],
                self.xs.at[y, 0, 0],
                self.xs.at[y, 0, 1],
                at.across(),
            )
        for step in range(1, at.ys):
            y = at.beside(step)
            for x in range(2):
                self.go(
                    self.part(y * 2 + x, 1),
                    self.from_y.at[at.y, x],
                    self.yss.at[step, x, 0],
                    self.yss.at[at.y, x, 1],
                    at.column(y),
                )

    def relay(self):
        at = self.at
        for step in range(1, at.ys):
            y = at.beside(step)
            self.wait(self.from_x.at[y], self.xs.at[y, 0, 0], self.xs.at[y, 0, 1])
            add_into(self.sum_y.at[y], [self.part(y * 2 + at.x, 0), self.from_x.at[y]])
            self.go(
                self.sum_y.at[y],
                self.last_y.at[at.y],
                self.yss.at[step, 2, 0],
                self.yss.at[at.y, 2, 1],
                at.column(y),
            )
        terms = []
        for step in range(1, at.ys):
            y = at.beside(step)
            for x in range(2):
                self.wait(self.from_y.at[y, x], self.yss.at[step, x, 0], self.yss.at[y, x, 1])
            terms.append(self.from_y.at[y, 1 - at.x])
        add_into(self.sum_x, [self.part(at.y * 2 + 1 - at.x, 1)] + terms)
        self.go(self.sum_x, self.last_x, self.xs.at[0, 1, 0], self.xs.at[0, 1, 1], at.across())

    def finish(self, total):
        at = self.at
        self.wait(self.from_x.at[at.y], self.xs.at[0, 0, 0], self.xs.at[at.y, 0, 1])
        terms = [self.part(at.s, 0), self.from_x.at[at.y]]
        for step in range(1, at.ys):
            y = at.beside(step)
            self.wait(self.last_y.at[y], self.yss.at[step, 2, 0], self.yss.at[y, 2, 1])
            terms.append(self.last_y.at[y])
        add_into(total(0), terms)
        self.wait(self.last_x, self.xs.at[0, 1, 0], self.xs.at[0, 1, 1])
        terms = [self.part(at.s, 1), self.last_x]
        for step in range(1, at.ys):
            terms.append(self.from_y.at[at.beside(step), at.x])
        add_into(total(1), terms)
        for copy in self.sent:
            copy.wait_send()


class LineGather:
    @staticmethod
    def semaphores(wt):
        return [pltpu.SemaphoreType.DMA((5, wt // 2))]

    def __init__(self, at, view, sems):
        self.at, self.view, self.sems = at, view, sems[0]

    def up(self, z, source=None):
        slot = self.view(z * 2 + self.at.c)
        source = slot if source is None else source
        return send(source, slot, self.sems.at[0, z], self.sems.at[3, z], self.at.level(self.at.z + 1))

    def down(self, z, source=None):
        slot = self.view(z * 2 + self.at.c)
        source = slot if source is None else source
        return send(source, slot, self.sems.at[1, z], self.sems.at[3, z], self.at.level(self.at.z - 1))

    def over(self, z, source=None):
        slot = self.view(z * 2 + self.at.c)
        source = slot if source is None else source
        return send(source, slot, self.sems.at[2, z], self.sems.at[4, z], self.at.partner())

    def start(self, source=None):
        at = self.at

        @pl.when(at.z + 1 < at.zs)
        def _():
            self.up(at.z, source).start()

        @pl.when(at.z > 0)
        def _():
            self.down(at.z, source).start()

        self.over(at.z, source).start()

    def step(self, index):
        at = self.at
        below, above = at.z - 1 - index, at.z + 1 + index

        @pl.when(below >= 0)
        def _():
            self.up(below).wait_recv()

            @pl.when(at.z + 1 < at.zs)
            def _():
                self.up(below).start()

            self.over(below).start()

        @pl.when(above < at.zs)
        def _():
            self.down(above).wait_recv()

            @pl.when(at.z > 0)
            def _():
                self.down(above).start()

            self.over(above).start()

    def finish(self):
        at = self.at
        for z in range(at.zs):
            slot = self.view(z * 2 + 1 - at.c)
            send(slot, slot, self.sems.at[2, z], self.sems.at[4, z], at.partner()).wait_recv()
        for z in range(at.zs):

            @pl.when((at.z >= z) & (at.z + 1 < at.zs))
            def _():
                self.up(z).wait_send()

            @pl.when((at.z <= z) & (at.z > 0))
            def _():
                self.down(z).wait_send()

            self.over(z).wait_send()


class LineSum:
    @staticmethod
    def scratch(wt, shape):
        zs = wt // 2
        return [
            pltpu.VMEM((zs,) + shape, jnp.bfloat16),
            pltpu.VMEM((zs,) + shape, jnp.bfloat16),
            pltpu.VMEM((zs,) + shape, jnp.bfloat16),
            pltpu.VMEM((zs,) + shape, jnp.bfloat16),
            pltpu.SemaphoreType.DMA((6, zs)),
        ]

    def __init__(self, at, part, scratch):
        self.at, self.part = at, part
        self.pair, self.held, self.below, self.above, self.sems = scratch

    def over(self, z):
        return send(
            self.part(z * 2 + 1 - self.at.c),
            self.pair.at[z],
            self.sems.at[0, z],
            self.sems.at[1, z],
            self.at.partner(),
        )

    def up(self, z):
        return send(
            self.held.at[z], self.below.at[z], self.sems.at[2, z], self.sems.at[3, z], self.at.level(self.at.z + 1)
        )

    def down(self, z):
        return send(
            self.held.at[z], self.above.at[z], self.sems.at[4, z], self.sems.at[5, z], self.at.level(self.at.z - 1)
        )

    def start(self):
        zs = self.at.zs
        for index in range(zs // 2):
            self.over(zs - 1 - index).start()
            self.over(index).start()

    def paired(self, z):
        self.over(z).wait_recv()
        return [self.part(z * 2 + self.at.c), self.pair.at[z]]

    def step(self, index):
        at = self.at
        high, low = at.zs - 1 - index, index

        @pl.when(at.z < high)
        def _():
            terms = self.paired(high)

            @pl.when(at.z == 0)
            def _():
                add_into(self.held.at[high], terms)

            @pl.when(at.z > 0)
            def _():
                self.up(high).wait_recv()
                add_into(self.held.at[high], terms + [self.below.at[high]])

            self.up(high).start()

        @pl.when(at.z > low)
        def _():
            terms = self.paired(low)

            @pl.when(at.z == at.zs - 1)
            def _():
                add_into(self.held.at[low], terms)

            @pl.when(at.z < at.zs - 1)
            def _():
                self.down(low).wait_recv()
                add_into(self.held.at[low], terms + [self.above.at[low]])

            self.down(low).start()

    def finish(self, total):
        at = self.at
        terms = self.paired(at.z)

        @pl.when(at.z == 0)
        def _():
            self.down(0).wait_recv()
            add_into(total, terms + [self.above.at[0]])

        @pl.when(at.z == at.zs - 1)
        def _():
            self.up(at.zs - 1).wait_recv()
            add_into(total, terms + [self.below.at[at.zs - 1]])

        @pl.when((at.z > 0) & (at.z < at.zs - 1))
        def _():
            self.up(at.z).wait_recv()
            self.down(at.z).wait_recv()
            add_into(total, terms + [self.below.at[at.z], self.above.at[at.z]])

        for z in range(at.zs):

            @pl.when(at.z < z)
            def _():
                self.up(z).wait_send()

            @pl.when(at.z > z)
            def _():
                self.down(z).wait_send()

            self.over(z).wait_send()


def remote_call(kernel, name, number, outs, scratch, *operands):
    return pl.pallas_call(
        kernel,
        name=name,
        out_shape=outs,
        in_specs=[VMEM] * len(operands),
        out_specs=jax.tree.map(lambda _: VMEM, outs),
        scratch_shapes=scratch,
        compiler_params=pltpu.CompilerParams(
            collective_id=number, has_side_effects=True, vmem_limit_bytes=60 * 1024 * 1024
        ),
    )(*operands)


def gather_start(tokens, qkv_rows, out_rows, gains):
    seq, wt = lax.axis_size("seq"), lax.axis_size("wt")
    count, width = tokens.shape
    parts, rows, columns = qkv_rows.shape

    def kernel(x_ref, qkv_ref, out_ref, gain_ref, xs, qkvs, outs, gains_out, *scratch):
        at = Place(seq, wt)
        x_sems, scratch = scratch[:3], scratch[3:]
        line_sems, scratch = [scratch[index : index + 1] for index in range(3)], scratch[3:]
        swap_q, swap_g, local = scratch
        at.meet(True, True)
        half = count // 2
        gather_x = SquareGather(
            at,
            lambda s, h: xs.at[pl.ds(pl.multiple_of(s * count + h * half, half), half)],
            lambda h: x_ref.at[pl.ds(h * half, half)],
            x_sems,
        )
        gather_q = LineGather(at, lambda w: qkvs.at[:, w], line_sems[0])
        gather_g = LineGather(at, lambda w: gains_out.at[:, w], line_sems[1])
        gather_o = LineGather(at, lambda w: outs.at[w], line_sems[2])
        swaps = []
        for step in range(1, seq):
            to = lax.rem(at.s + step, seq)
            swaps.append(
                send(gain_ref, gains_out.at[at.s, at.w], swap_g.at[step, 0], swap_g.at[at.s, 1], (to, at.w))
            )
            swaps.append(
                send(qkv_ref.at[to], qkvs.at[at.s, at.w], swap_q.at[step, 0], swap_q.at[at.s, 1], (to, at.w))
            )
        for copy in swaps:
            copy.start()
        gather_x.start()
        own = [
            pltpu.make_async_copy(qkv_ref.at[at.s], qkvs.at[at.s, at.w], local.at[0]),
            pltpu.make_async_copy(gain_ref, gains_out.at[at.s, at.w], local.at[1]),
            pltpu.make_async_copy(out_ref, outs.at[at.w], local.at[2]),
            pltpu.make_async_copy(x_ref, xs.at[pl.ds(pl.multiple_of(at.s * count, count), count)], local.at[3]),
        ]
        for copy in own:
            copy.start()
        for copy in own:
            copy.wait()
        for step in range(1, seq):
            s = lax.rem(at.s + step, seq)
            slot = gains_out.at[s, at.w]
            send(slot, slot, swap_g.at[step, 0], swap_g.at[s, 1], at.across()).wait_recv()
            slot = qkvs.at[s, at.w]
            send(slot, slot, swap_q.at[step, 0], swap_q.at[s, 1], at.across()).wait_recv()
        gather_g.start()
        gather_q.start()
        gather_o.start()
        gather_x.relay()
        for index in range(at.zs - 1):
            gather_g.step(index)
            gather_q.step(index)
            gather_o.step(index)
        gather_x.finish()
        gather_g.finish()
        gather_q.finish()
        gather_o.finish()
        for copy in swaps:
            copy.wait_send()

    return remote_call(
        kernel,
        "gather_start",
        0,
        [
            jax.ShapeDtypeStruct((seq * count, width), tokens.dtype),
            jax.ShapeDtypeStruct((seq, wt, rows, columns), qkv_rows.dtype),
            jax.ShapeDtypeStruct((wt,) + out_rows.shape, out_rows.dtype),
            jax.ShapeDtypeStruct((seq, wt) + gains.shape, gains.dtype),
        ],
        SquareGather.semaphores(seq)
        + LineGather.semaphores(wt) * 3
        + [
            pltpu.SemaphoreType.DMA((seq, 2)),
            pltpu.SemaphoreType.DMA((seq, 2)),
            pltpu.SemaphoreType.DMA((4,)),
        ],
        tokens,
        qkv_rows,
        out_rows,
        gains,
    )


def square_sum(parts, name, number):
    seq, wt = lax.axis_size("seq"), lax.axis_size("wt")
    half_shape = parts.shape[2:]

    def kernel(parts_ref, total_ref, *scratch):
        at = Place(seq, wt)
        at.meet(True, False)
        work = SquareSum(at, lambda s, h: parts_ref.at[s, h], scratch)
        work.start()
        work.relay()
        work.finish(lambda h: total_ref.at[h])

    return remote_call(
        kernel,
        name,
        number,
        jax.ShapeDtypeStruct((2,) + half_shape, jnp.float32),
        SquareSum.scratch(seq, half_shape),
        parts,
    )


def square_gather(shard, name, number):
    seq, wt = lax.axis_size("seq"), lax.axis_size("wt")
    count, width = shard.shape
    half = count // 2

    def kernel(shard_ref, all_ref, *scratch):
        at = Place(seq, wt)
        at.meet(True, False)
        work = SquareGather(
            at,
            lambda s, h: all_ref.at[pl.ds(pl.multiple_of(s * count + h * half, half), half)],
            lambda h: shard_ref.at[pl.ds(h * half, half)],
            scratch[:3],
        )
        work.start()
        own = pltpu.make_async_copy(
            shard_ref, all_ref.at[pl.ds(pl.multiple_of(at.s * count, count), count)], scratch[3].at[0]
        )
        own.start()
        own.wait()
        work.relay()
        work.finish()

    return remote_call(
        kernel,
        name,
        number,
        jax.ShapeDtypeStruct((seq * count, width), shard.dtype),
        SquareGather.semaphores(seq) + [pltpu.SemaphoreType.DMA((1,))],
        shard,
    )


def line_gather(shard, name, number):
    seq, wt = lax.axis_size("seq"), lax.axis_size("wt")
    count, width = shard.shape

    def kernel(shard_ref, all_ref, *scratch):
        at = Place(seq, wt)
        at.meet(False, True)
        work = LineGather(
            at, lambda w: all_ref.at[pl.ds(pl.multiple_of(w * count, count), count)], scratch[:1]
        )
        work.start(shard_ref)
        own = pltpu.make_async_copy(
            shard_ref, all_ref.at[pl.ds(pl.multiple_of(at.w * count, count), count)], scratch[1].at[0]
        )
        own.start()
        own.wait()
        for index in range(at.zs - 1):
            work.step(index)
        work.finish()

    return remote_call(
        kernel,
        name,
        number,
        jax.ShapeDtypeStruct((wt * count, width), shard.dtype),
        LineGather.semaphores(wt) + [pltpu.SemaphoreType.DMA((1,))],
        shard,
    )


def line_sum(parts, name, number):
    seq, wt = lax.axis_size("seq"), lax.axis_size("wt")
    rows, width = parts.shape
    count = rows // wt

    def kernel(parts_ref, total_ref, *scratch):
        at = Place(seq, wt)
        at.meet(False, True)
        work = LineSum(at, lambda w: parts_ref.at[pl.ds(pl.multiple_of(w * count, count), count)], scratch)
        work.start()
        for index in range(at.zs - 1):
            work.step(index)
        work.finish(total_ref)

    return remote_call(
        kernel,
        name,
        number,
        jax.ShapeDtypeStruct((count, width), jnp.float32),
        LineSum.scratch(wt, (count, width)),
        parts,
    )


def final_sums(hidden_parts, gate_up_parts, down_parts, qkv_parts, out_parts):
    seq, wt = lax.axis_size("seq"), lax.axis_size("wt")
    hidden_half = hidden_parts.shape[2:]
    gate_up_half = gate_up_parts.shape[2:]
    down_rows, down_all = down_parts.shape[1:]
    down_columns = down_all // seq
    down_half = (down_rows, down_columns)
    qkv_shape = (seq,) + qkv_parts.shape[2:]

    def kernel(hidden_ref, gate_up_ref, down_ref, qkv_ref, out_ref, h_total, gu_total, d_total, q_total, o_total, *scratch):
        at = Place(seq, wt)
        at.meet(True, True)
        square, scratch = [scratch[8 * index : 8 * index + 8] for index in range(3)], scratch[24:]
        line, scratch = [scratch[5 * index : 5 * index + 5] for index in range(2)], scratch[10:]
        q_sum, swap = scratch
        hidden = SquareSum(at, lambda s, h: hidden_ref.at[s, h], square[0])
        gate_up = SquareSum(at, lambda s, h: gate_up_ref.at[h, s], square[1])
        down = SquareSum(
            at,
            lambda s, h: down_ref.at[h, :, pl.ds(pl.multiple_of(s * down_columns, down_columns), down_columns)],
            square[2],
        )
        qkv = LineSum(at, lambda w: qkv_ref.at[:, w], line[0])
        out = LineSum(at, lambda w: out_ref.at[w], line[1])
        qkv.start()
        out.start()
        hidden.start()
        gate_up.start()
        down.start()
        hidden.relay()
        for index in range(at.zs - 1):
            qkv.step(index)
            out.step(index)
        qkv.finish(q_sum)
        out.finish(o_total)
        swaps = []
        for step in range(1, seq):
            to = lax.rem(at.s + step, seq)
            copy = send(q_sum.at[to], q_total.at[at.s], swap.at[step, 0], swap.at[at.s, 1], (to, at.w))
            copy.start()
            swaps.append(copy)
        add_into(q_total.at[at.s], [q_sum.at[at.s]])
        gate_up.relay()
        down.relay()
        hidden.finish(lambda h: h_total.at[h])
        gate_up.finish(lambda h: gu_total.at[h])
        down.finish(lambda h: d_total.at[h])
        for step in range(1, seq):
            s = lax.rem(at.s + step, seq)
            slot = q_total.at[s]
            send(slot, slot, swap.at[step, 0], swap.at[s, 1], at.across()).wait_recv()
        for copy in swaps:
            copy.wait_send()

    return remote_call(
        kernel,
        "final_sums",
        7,
        [
            jax.ShapeDtypeStruct((2,) + hidden_half, jnp.float32),
            jax.ShapeDtypeStruct((2,) + gate_up_half, jnp.float32),
            jax.ShapeDtypeStruct((2,) + down_half, jnp.float32),
            jax.ShapeDtypeStruct(qkv_shape, jnp.float32),
            jax.ShapeDtypeStruct(out_parts.shape[1:], jnp.float32),
        ],
        SquareSum.scratch(seq, hidden_half)
        + SquareSum.scratch(seq, gate_up_half)
        + SquareSum.scratch(seq, down_half)
        + LineSum.scratch(wt, qkv_shape)
        + LineSum.scratch(wt, out_parts.shape[1:])
        + [pltpu.VMEM(qkv_shape, jnp.float32), pltpu.SemaphoreType.DMA((seq, 2))],
        hidden_parts,
        gate_up_parts,
        down_parts,
        qkv_parts,
        out_parts,
    )


def small_sums(spread, lined):
    seq, wt = lax.axis_size("seq"), lax.axis_size("wt")
    tile = spread.shape[2:]

    def kernel(spread_ref, lined_ref, total_ref, first, middle, last, first_sems, last_sems):
        at = Place(seq, wt)
        at.meet(True, True)
        copies = []
        for step in range(1, seq):
            to = lax.rem(at.s + step, seq)
            copy = send(spread_ref.at[to], first.at[at.s], first_sems.at[step, 0], first_sems.at[at.s, 1], (to, at.w))
            copy.start()
            copies.append(copy)
        terms = [spread_ref.at[at.s]]
        for step in range(1, seq):
            s = lax.rem(at.s + step, seq)
            slot = first.at[s]
            send(slot, slot, first_sems.at[step, 0], first_sems.at[s, 1], at.across()).wait_recv()
            terms.append(slot)
        add_into(middle, terms + [lined_ref])
        for step in range(1, wt):
            to = lax.rem(at.w + step, wt)
            copy = send(middle.at[to], last.at[at.w], last_sems.at[step, 0], last_sems.at[at.w, 1], (at.s, to))
            copy.start()
            copies.append(copy)
        terms = [middle.at[at.w]]
        for step in range(1, wt):
            w = lax.rem(at.w + step, wt)
            slot = last.at[w]
            send(slot, slot, last_sems.at[step, 0], last_sems.at[w, 1], at.partner()).wait_recv()
            terms.append(slot)
        add_into(total_ref, terms)
        for copy in copies:
            copy.wait_send()

    return remote_call(
        kernel,
        "small_sums",
        8,
        jax.ShapeDtypeStruct(tile, jnp.float32),
        [
            pltpu.VMEM((seq, wt) + tile, jnp.float32),
            pltpu.VMEM((wt,) + tile, jnp.float32),
            pltpu.VMEM((wt,) + tile, jnp.float32),
            pltpu.SemaphoreType.DMA((seq, 2)),
            pltpu.SemaphoreType.DMA((wt, 2)),
        ],
        spread,
        lined,
    )


def rows_of_tile(values, row):
    pad = [(0, 0)] * (values.ndim - 1)
    return jnp.pad(values[..., None, :], pad + [(row, 7 - row), (0, 128 - values.shape[-1])])

def body(
    inputs,
    segment_ids,
    valid_lengths,
    teacher,
    w_qkv,
    conv_weight,
    w_out,
    norm_gain,
    w_gate_up,
    w_down,
    mlp_gain,
):
    seq_parts, wt_parts = lax.axis_size("seq"), lax.axis_size("wt")
    tok_count = inputs.shape[1]
    model_width = inputs.shape[2]
    length = tok_count * seq_parts
    block_rows = min(block_limit, length)
    head_count = H // seq_parts
    head_width = 2 * FEAT + DV
    qkv_width = head_count * head_width
    rows_low = inputs[0]
    rows_in = rows_low.astype(jnp.float32)
    gain_lanes = norm_gain.shape[0]
    gains = rows_of_tile(norm_gain.astype(jnp.float32), 0) + rows_of_tile(mlp_gain.astype(jnp.float32), 1)
    qkv_rows = w_qkv.reshape(w_qkv.shape[0], seq_parts, qkv_width).transpose(1, 0, 2)
    tokens_all, qkv_columns, out_rows, gains_all = gather_start(rows_low, qkv_rows, w_out, gains)
    qkv_columns = qkv_columns.reshape(model_width, qkv_width)
    out_rows = out_rows.reshape(head_count * DV, model_width)
    gain_first = gains_all[:, :, 0, :gain_lanes].reshape(model_width)
    gain_second = gains_all[:, :, 1, :gain_lanes].reshape(model_width)
    gate_up_part, down_part = (
        lax.all_gather(w_gate_up, "seq", axis=1, tiled=True),
        lax.all_gather(w_down, "seq", axis=1, tiled=True),
    )
    hidden_low = rms_norm(tokens_all.astype(jnp.float32), gain_first).astype(jnp.bfloat16)
    projected = jnp.dot(hidden_low, qkv_columns, preferred_element_type=jnp.float32).astype(
        jnp.bfloat16
    )
    grouped = projected.reshape(length, head_count, head_width)
    head_queries = grouped[:, :, :FEAT].transpose(1, 2, 0)
    head_keys = grouped[:, :, FEAT : 2 * FEAT].transpose(1, 2, 0)
    raw_values = grouped[:, :, 2 * FEAT :].astype(jnp.float32)
    segments = segment_ids[0]
    conv_taps = conv_weight.astype(jnp.float32).reshape(KCONV, head_count, DV)
    tap_masks = [jnp.ones((length,), jnp.float32)]
    mixed_values = conv_taps[0] * raw_values
    for tap_index in range(1, KCONV):
        earlier = shift_down(segments, tap_index, -1)
        tap_masks.append((earlier == segments).astype(jnp.float32))
        mixed_values = (
            mixed_values
            + conv_taps[tap_index]
            * shift_down(raw_values, tap_index, 0.0)
            * tap_masks[tap_index][:, None, None]
        )
    conv_low = mixed_values.astype(jnp.bfloat16).transpose(1, 0, 2)
    head_outputs, denominators = attend_forward(
        head_queries, head_keys, conv_low, segments, block_rows
    )
    mixer_low = head_outputs.transpose(1, 0, 2).reshape(length, head_count * DV).astype(jnp.bfloat16)
    mixed_parts = jnp.dot(mixer_low, out_rows, preferred_element_type=jnp.float32).astype(jnp.bfloat16)
    attended = rows_in + square_sum(
        mixed_parts.reshape(seq_parts, 2, tok_count // 2, model_width), "mixed_sum", 1
    ).reshape(tok_count, model_width)
    normed_value, second_pull = jax.vjp(rms_norm, attended, gain_second)
    normed_low = normed_value.astype(jnp.bfloat16)
    normed_all = line_gather(normed_low, "normed_gather", 2)
    gate_all = jnp.dot(normed_all, gate_up_part[0], preferred_element_type=jnp.float32)
    up_all = jnp.dot(normed_all, gate_up_part[1], preferred_element_type=jnp.float32)
    active_value, gate_pull = jax.vjp(gated_unit, gate_all, up_all)
    active_all = active_value.astype(jnp.bfloat16)
    branch_out = line_sum(
        jnp.dot(active_all, down_part, preferred_element_type=jnp.float32).astype(jnp.bfloat16),
        "branch_sum",
        3,
    )
    outputs = attended + branch_out
    sequence_length = lax.dynamic_index_in_dim(
        valid_lengths, lax.axis_index("wt"), 0, keepdims=False
    )
    positions = lax.axis_index("seq") * tok_count + jnp.arange(tok_count, dtype=jnp.int32)
    keep_mask = (positions < sequence_length).astype(jnp.float32)
    residual_error = (outputs - teacher[0].astype(jnp.float32)) * keep_mask[:, None]
    energy = 0.5 * jnp.sum(residual_error * residual_error)
    branch_grad = residual_error.astype(jnp.bfloat16)
    error_all = line_gather(branch_grad, "error_gather", 4)
    active_grad = contract_last(error_all, down_part)
    down_term = contract_first(active_all, error_all)
    gate_grad, up_grad = gate_pull(active_grad)
    gate_up_grad = jnp.stack([gate_grad, up_grad]).astype(jnp.bfloat16)
    gate_up_term = jnp.einsum(
        "tc,gtf->gcf", normed_all, gate_up_grad, preferred_element_type=jnp.float32
    )
    normed_grad = line_sum(
        jnp.einsum(
            "gtf,gcf->tc", gate_up_grad, gate_up_part, preferred_element_type=jnp.float32
        ).astype(jnp.bfloat16),
        "normed_back_sum",
        5,
    )
    attended_back, gain_two_term = second_pull(normed_grad)
    attended_grad = residual_error + attended_back
    mixer_branch = square_gather(attended_grad.astype(jnp.bfloat16), "mix_back_gather", 6)
    out_term = contract_first(mixer_low, mixer_branch)
    mixer_grad = contract_last(mixer_branch, out_rows).astype(jnp.bfloat16)
    head_incoming = (
        mixer_grad.reshape(length, head_count, DV).transpose(1, 0, 2).astype(jnp.float32)
    )
    query_grads, key_grads, value_grads = attend_backward(
        head_queries,
        head_keys,
        conv_low,
        segments,
        head_outputs,
        denominators,
        head_incoming,
        block_rows,
    )
    mixed_grad = value_grads.transpose(1, 0, 2)
    conv_terms = [jnp.sum(mixed_grad * raw_values, axis=0)]
    raw_grad = conv_taps[0] * mixed_grad
    for tap_index in range(1, KCONV):
        masked = mixed_grad * tap_masks[tap_index][:, None, None]
        conv_terms.append(jnp.sum(masked * shift_down(raw_values, tap_index, 0.0), axis=0))
        raw_grad = raw_grad + conv_taps[tap_index] * shift_up(masked, tap_index)
    projected_grad = jnp.concatenate(
        [query_grads.transpose(2, 0, 1), key_grads.transpose(2, 0, 1), raw_grad], axis=2
    ).astype(jnp.bfloat16)
    returned = projected_grad.reshape(length, qkv_width)
    qkv_term = contract_first(hidden_low, returned).astype(jnp.bfloat16)
    hidden_parts = contract_last(returned, qkv_columns).astype(jnp.bfloat16)
    hidden_units = gate_up_part.shape[2]
    hidden_grad, gate_up_total, down_total, qkv_total, out_total = final_sums(
        hidden_parts.reshape(seq_parts, 2, tok_count // 2, model_width),
        gate_up_term.astype(jnp.bfloat16).reshape(2, seq_parts, model_width // seq_parts, hidden_units),
        down_term.astype(jnp.bfloat16).reshape(2, hidden_units // 2, model_width),
        qkv_term.reshape(seq_parts, wt_parts, w_qkv.shape[0], qkv_width),
        out_term.astype(jnp.bfloat16).reshape(wt_parts, w_out.shape[0], model_width),
    )
    _, first_pull = jax.vjp(rms_norm, rows_in, gain_first)
    inputs_back, gain_one_term = first_pull(hidden_grad.reshape(tok_count, model_width))
    inputs_grad = attended_grad + inputs_back
    grad_w_qkv = qkv_total.transpose(1, 0, 2).reshape(w_qkv.shape)
    grad_w_gate_up = gate_up_total
    grad_w_down = down_total.reshape(w_down.shape)
    grad_w_out = out_total
    spread = (
        rows_of_tile(gain_one_term.reshape(seq_parts, wt_parts, gain_lanes), 0)
        + rows_of_tile(gain_two_term.reshape(seq_parts, wt_parts, gain_lanes), 1)
        + rows_of_tile(jnp.broadcast_to(energy, (seq_parts, wt_parts, 1)), 2)
    )
    conv_block = jnp.stack(conv_terms).reshape(KCONV, wt_parts, gain_lanes)
    lined = sum(rows_of_tile(conv_block[tap], 3 + tap) for tap in range(KCONV))
    totals = small_sums(spread, lined)
    grad_norm_gain, grad_mlp_gain = totals[0, :gain_lanes], totals[1, :gain_lanes]
    grad_conv = totals[3 : 3 + KCONV, :gain_lanes]
    valid_total = jnp.sum(valid_lengths).astype(jnp.float32)
    mean_loss = 2.0 * totals[2, 0] / (valid_total * model_width)
    return (
        outputs.astype(jnp.bfloat16)[None],
        inputs_grad[None],
        mean_loss,
        grad_w_qkv,
        grad_conv,
        grad_w_out,
        grad_norm_gain,
        grad_w_gate_up,
        grad_w_down,
        grad_mlp_gain,
    )


def solution(mesh):
    in_specs = (
        P("wt", "seq", None),
        P("wt", None),
        P(),
        P("wt", "seq", None),
        P(("seq", "wt"), None),
        P(None, "seq"),
        P(("seq", "wt"), None),
        P(("seq", "wt")),
        P(None, "seq", "wt"),
        P("wt", "seq"),
        P(("seq", "wt")),
    )
    out_specs = (
        P("wt", "seq", None),
        P("wt", "seq", None),
        P(),
        P(("seq", "wt"), None),
        P(None, ("seq", "wt")),
        P(("seq", "wt"), None),
        P(("seq", "wt")),
        P(None, "seq", "wt"),
        P("wt", "seq"),
        P(("seq", "wt")),
    )
    return jax.shard_map(body, mesh=mesh, in_specs=in_specs, out_specs=out_specs, check_vma=False)
```

```python
import jax
import jax.numpy as jnp
from jax import lax
from jax.experimental import pallas as pl
from jax.experimental.pallas import tpu as pltpu
from jax.sharding import PartitionSpec as P

H = 16
FEAT = 16
KCONV = 3
DV = 128


epsilon = 1e-05
block_limit = 512


def rms_norm(values, gain_vector):
    inverse_root = lax.rsqrt(jnp.mean(values * values, axis=-1, keepdims=True) + epsilon)
    return values * inverse_root * gain_vector


def contract_last(former, latter):
    return lax.dot_general(
        former, latter, (((1,), (1,)), ((), ())), preferred_element_type=jnp.float32
    )


def contract_first(former, latter):
    return lax.dot_general(
        former, latter, (((0,), (0,)), ((), ())), preferred_element_type=jnp.float32
    )


def shift_down(values, amount, filler):
    padding = jnp.full((amount,) + values.shape[1:], filler, values.dtype)
    return jnp.concatenate([padding, values[:-amount]], axis=0)


def shift_up(values, amount):
    padding = jnp.zeros((amount,) + values.shape[1:], values.dtype)
    return jnp.concatenate([values[amount:], padding], axis=0)


def gated_unit(gate_in, up_in):
    return jax.nn.silu(gate_in) * up_in


def block_kernel(query_block, key_block, query_segments, key_segments, query_start, key_start):
    row_width = query_segments.shape[0]
    scaled_dots = (
        jnp.einsum("hfq,hfk->hqk", query_block, key_block, preferred_element_type=jnp.float32)
        * 0.25
    )
    query_places = query_start + jnp.arange(row_width, dtype=jnp.int32)
    key_places = key_start + jnp.arange(row_width, dtype=jnp.int32)
    allowed = (query_segments[:, None] == key_segments[None, :]) & (
        query_places[:, None] >= key_places[None, :]
    )
    kernel = jnp.where(allowed[None], 1.0 + scaled_dots + 0.5 * scaled_dots * scaled_dots, 0.0)
    return (scaled_dots, allowed, kernel)


def attend_forward(queries, key_rows, values, segments, block_rows):
    head_count, length, value_width = values.shape
    block_count = length // block_rows

    def query_step(query_index, running):
        outputs, denominators = running
        query_start = query_index * block_rows
        query_block = lax.dynamic_slice_in_dim(queries, query_start, block_rows, 2)
        query_segments = lax.dynamic_slice_in_dim(segments, query_start, block_rows, 0)

        def key_step(inner_index, inner_running):
            numerator, denominator = inner_running
            key_start = inner_index * block_rows
            key_block = lax.dynamic_slice_in_dim(key_rows, key_start, block_rows, 2)
            value_block = lax.dynamic_slice_in_dim(values, key_start, block_rows, 1)
            key_segments = lax.dynamic_slice_in_dim(segments, key_start, block_rows, 0)
            scaled_dots, allowed, kernel = block_kernel(
                query_block, key_block, query_segments, key_segments, query_start, key_start
            )
            numerator = numerator + jnp.einsum(
                "hqk,hkd->hqd",
                kernel.astype(jnp.bfloat16),
                value_block,
                preferred_element_type=jnp.float32,
            )
            denominator = denominator + jnp.sum(kernel, axis=2)
            return (numerator, denominator)

        starting = (
            jnp.zeros((head_count, block_rows, value_width), jnp.float32),
            jnp.zeros((head_count, block_rows), jnp.float32),
        )
        numerator, denominator = lax.fori_loop(0, query_index + 1, key_step, starting)
        outputs = lax.dynamic_update_slice_in_dim(
            outputs, numerator / denominator[:, :, None], query_start, 1
        )
        denominators = lax.dynamic_update_slice_in_dim(denominators, denominator, query_start, 1)
        return (outputs, denominators)

    initial = (
        jnp.zeros((head_count, length, value_width), jnp.float32),
        jnp.zeros((head_count, length), jnp.float32),
    )
    return lax.fori_loop(0, block_count, query_step, initial)


def attend_backward(
    queries, key_rows, values, segments, outputs, denominators, incoming, block_rows
):
    head_count, length, value_width = values.shape
    feature_width = queries.shape[1]
    block_count = length // block_rows

    def query_step(query_index, running):
        query_grads, key_grads, value_grads = running
        query_start = query_index * block_rows
        query_block = lax.dynamic_slice_in_dim(queries, query_start, block_rows, 2)
        query_segments = lax.dynamic_slice_in_dim(segments, query_start, block_rows, 0)
        incoming_block = lax.dynamic_slice_in_dim(incoming, query_start, block_rows, 1)
        output_block = lax.dynamic_slice_in_dim(outputs, query_start, block_rows, 1)
        denominator = lax.dynamic_slice_in_dim(denominators, query_start, block_rows, 1)
        numerator_grad = (incoming_block / denominator[:, :, None]).astype(jnp.bfloat16)
        denominator_grad = -jnp.sum(incoming_block * output_block, axis=2) / denominator

        def key_step(inner_index, inner_running):
            query_total, key_grads, value_grads = inner_running
            key_start = inner_index * block_rows
            key_block = lax.dynamic_slice_in_dim(key_rows, key_start, block_rows, 2)
            value_block = lax.dynamic_slice_in_dim(values, key_start, block_rows, 1)
            key_segments = lax.dynamic_slice_in_dim(segments, key_start, block_rows, 0)
            scaled_dots, allowed, kernel = block_kernel(
                query_block, key_block, query_segments, key_segments, query_start, key_start
            )
            weights_low = kernel.astype(jnp.bfloat16)
            weight_grad = jnp.einsum(
                "hqd,hkd->hqk", numerator_grad, value_block, preferred_element_type=jnp.float32
            )
            kernel_grad = jnp.where(allowed[None], weight_grad + denominator_grad[:, :, None], 0.0)
            dots_grad = (0.25 * kernel_grad * (1.0 + scaled_dots)).astype(jnp.bfloat16)
            query_total = query_total + jnp.einsum(
                "hqk,hfk->hfq", dots_grad, key_block, preferred_element_type=jnp.float32
            )
            key_part = jnp.einsum(
                "hqk,hfq->hfk", dots_grad, query_block, preferred_element_type=jnp.float32
            )
            value_part = jnp.einsum(
                "hqk,hqd->hkd", weights_low, numerator_grad, preferred_element_type=jnp.float32
            )
            key_grads = lax.dynamic_update_slice_in_dim(
                key_grads,
                lax.dynamic_slice_in_dim(key_grads, key_start, block_rows, 2) + key_part,
                key_start,
                2,
            )
            value_grads = lax.dynamic_update_slice_in_dim(
                value_grads,
                lax.dynamic_slice_in_dim(value_grads, key_start, block_rows, 1) + value_part,
                key_start,
                1,
            )
            return (query_total, key_grads, value_grads)

        starting = jnp.zeros((head_count, feature_width, block_rows), jnp.float32)
        query_total, key_grads, value_grads = lax.fori_loop(
            0, query_index + 1, key_step, (starting, key_grads, value_grads)
        )
        query_grads = lax.dynamic_update_slice_in_dim(query_grads, query_total, query_start, 2)
        return (query_grads, key_grads, value_grads)

    initial = (
        jnp.zeros((head_count, feature_width, length), jnp.float32),
        jnp.zeros((head_count, feature_width, length), jnp.float32),
        jnp.zeros((head_count, length, value_width), jnp.float32),
    )
    return lax.fori_loop(0, block_count, query_step, initial)


MESH = pl.DeviceIdType.MESH
VMEM = pl.BlockSpec(memory_space=pltpu.VMEM)


class Place:
    def __init__(self, seq, wt):
        self.seq, self.wt = seq, wt
        self.ys, self.zs = seq // 2, wt // 2
        self.s, self.w = lax.axis_index("seq"), lax.axis_index("wt")
        self.y, self.x = lax.div(self.s, 2), lax.rem(self.s, 2)
        self.z, self.c = lax.div(self.w, 2), lax.rem(self.w, 2)

    def across(self):
        return (self.y * 2 + 1 - self.x, self.w)

    def beside(self, step):
        return lax.rem(self.y + step, self.ys)

    def column(self, y):
        return (y * 2 + self.x, self.w)

    def partner(self):
        return (self.s, self.z * 2 + 1 - self.c)

    def level(self, z):
        return (self.s, z * 2 + self.c)

    def meet(self, square, line):
        barrier = pltpu.get_barrier_semaphore()
        count = 0
        if square:
            for step in range(1, self.seq):
                device = (lax.rem(self.s + step, self.seq), self.w)
                pl.semaphore_signal(barrier, inc=1, device_id=device, device_id_type=MESH)
                count += 1
        if line:
            for step in range(1, self.wt):
                device = (self.s, lax.rem(self.w + step, self.wt))
                pl.semaphore_signal(barrier, inc=1, device_id=device, device_id_type=MESH)
                count += 1
        pl.semaphore_wait(barrier, count)


def send(source, target, leaving, arriving, device):
    return pltpu.make_async_remote_copy(
        src_ref=source,
        dst_ref=target,
        send_sem=leaving,
        recv_sem=arriving,
        device_id=device,
        device_id_type=MESH,
    )


def add_into(target, sources):
    if len(target.shape) == 3:
        for index in range(target.shape[0]):
            add_into(target.at[index], [source.at[index] for source in sources])
        return
    rows = target.shape[0]
    tile = next(t for t in (64, 32, 16, 8, rows) if rows % t == 0)

    def step(index, carry):
        window = pl.ds(pl.multiple_of(index * tile, tile), tile)
        total = sources[0][window, :].astype(jnp.float32)
        for source in sources[1:]:
            total = total + source[window, :].astype(jnp.float32)
        target[window, :] = total.astype(target.dtype)
        return carry

    lax.fori_loop(0, rows // tile, step, 0)


class SquareGather:
    @staticmethod
    def semaphores(seq):
        return [
            pltpu.SemaphoreType.DMA((2 + seq // 2,)),
            pltpu.SemaphoreType.DMA((seq // 2, 3)),
            pltpu.SemaphoreType.DMA((seq, 2)),
        ]

    def __init__(self, at, view, own, sems):
        self.at, self.view, self.own = at, view, own
        self.over_x, self.over_y, self.got = sems
        self.sent = []

    def go(self, source, s, half, leaving, device):
        copy = send(source, self.view(s, half), leaving, self.got.at[s, half], device)
        copy.start()
        self.sent.append(copy)

    def wait(self, s, half):
        slot = self.view(s, half)
        send(slot, slot, self.over_x.at[0], self.got.at[s, half], self.at.across()).wait_recv()

    def start(self):
        at = self.at
        for half in range(2):
            self.go(self.own(half), at.s, half, self.over_x.at[half], at.across())
            for step in range(1, at.ys):
                target = at.column(at.beside(step))
                self.go(self.own(1 - half), at.s, 1 - half, self.over_y.at[step, half], target)

    def relay(self):
        at = self.at
        other = at.y * 2 + 1 - at.x
        self.wait(other, 0)
        for step in range(1, at.ys):
            self.go(self.view(other, 0), other, 0, self.over_y.at[step, 2], at.column(at.beside(step)))
        for step in range(1, at.ys):
            s = at.beside(step) * 2 + at.x
            self.wait(s, 1)
            self.go(self.view(s, 1), s, 1, self.over_x.at[1 + step], at.across())

    def finish(self):
        at = self.at
        self.wait(at.y * 2 + 1 - at.x, 1)
        for step in range(1, at.ys):
            y = at.beside(step)
            self.wait(y * 2 + at.x, 0)
            self.wait(y * 2 + 1 - at.x, 0)
            self.wait(y * 2 + 1 - at.x, 1)
        for copy in self.sent:
            copy.wait_send()


class SquareSum:
    @staticmethod
    def scratch(seq, half_shape):
        ys = seq // 2
        return [
            pltpu.VMEM((ys,) + half_shape, jnp.bfloat16),
            pltpu.VMEM((ys, 2) + half_shape, jnp.bfloat16),
            pltpu.VMEM((ys,) + half_shape, jnp.bfloat16),
            pltpu.VMEM(half_shape, jnp.bfloat16),
            pltpu.VMEM((ys,) + half_shape, jnp.bfloat16),
            pltpu.VMEM(half_shape, jnp.bfloat16),
            pltpu.SemaphoreType.DMA((ys, 2, 2)),
            pltpu.SemaphoreType.DMA((ys, 3, 2)),
        ]

    def __init__(self, at, part, scratch):
        self.at, self.part = at, part
        self.from_x, self.from_y, self.last_y, self.last_x, self.sum_y, self.sum_x, self.xs, self.yss = scratch
        self.sent = []

    def go(self, source, target, leaving, arriving, device):
        copy = send(source, target, leaving, arriving, device)
        copy.start()
        self.sent.append(copy)

    def wait(self, slot, leaving, arriving):
        send(slot, slot, leaving, arriving, self.at.across()).wait_recv()

    def start(self):
        at = self.at
        for y in range(at.ys):
            self.go(
                self.part(y * 2 + 1 - at.x, 0),
                self.from_x.at[y],
                self.xs.at[y, 0, 0],
                self.xs.at[y, 0, 1],
                at.across(),
            )
        for step in range(1, at.ys):
            y = at.beside(step)
            for x in range(2):
                self.go(
                    self.part(y * 2 + x, 1),
                    self.from_y.at[at.y, x],
                    self.yss.at[step, x, 0],
                    self.yss.at[at.y, x, 1],
                    at.column(y),
                )

    def relay(self):
        at = self.at
        for step in range(1, at.ys):
            y = at.beside(step)
            self.wait(self.from_x.at[y], self.xs.at[y, 0, 0], self.xs.at[y, 0, 1])
            add_into(self.sum_y.at[y], [self.part(y * 2 + at.x, 0), self.from_x.at[y]])
            self.go(
                self.sum_y.at[y],
                self.last_y.at[at.y],
                self.yss.at[step, 2, 0],
                self.yss.at[at.y, 2, 1],
                at.column(y),
            )
        terms = []
        for step in range(1, at.ys):
            y = at.beside(step)
            for x in range(2):
                self.wait(self.from_y.at[y, x], self.yss.at[step, x, 0], self.yss.at[y, x, 1])
            terms.append(self.from_y.at[y, 1 - at.x])
        add_into(self.sum_x, [self.part(at.y * 2 + 1 - at.x, 1)] + terms)
        self.go(self.sum_x, self.last_x, self.xs.at[0, 1, 0], self.xs.at[0, 1, 1], at.across())

    def finish(self, total):
        at = self.at
        self.wait(self.from_x.at[at.y], self.xs.at[0, 0, 0], self.xs.at[at.y, 0, 1])
        terms = [self.part(at.s, 0), self.from_x.at[at.y]]
        for step in range(1, at.ys):
            y = at.beside(step)
            self.wait(self.last_y.at[y], self.yss.at[step, 2, 0], self.yss.at[y, 2, 1])
            terms.append(self.last_y.at[y])
        add_into(total(0), terms)
        self.wait(self.last_x, self.xs.at[0, 1, 0], self.xs.at[0, 1, 1])
        terms = [self.part(at.s, 1), self.last_x]
        for step in range(1, at.ys):
            terms.append(self.from_y.at[at.beside(step), at.x])
        add_into(total(1), terms)
        for copy in self.sent:
            copy.wait_send()


class LineGather:
    @staticmethod
    def semaphores(wt):
        return [pltpu.SemaphoreType.DMA((5, wt // 2))]

    def __init__(self, at, view, sems):
        self.at, self.view, self.sems = at, view, sems[0]

    def up(self, z, source=None):
        slot = self.view(z * 2 + self.at.c)
        source = slot if source is None else source
        return send(source, slot, self.sems.at[0, z], self.sems.at[3, z], self.at.level(self.at.z + 1))

    def down(self, z, source=None):
        slot = self.view(z * 2 + self.at.c)
        source = slot if source is None else source
        return send(source, slot, self.sems.at[1, z], self.sems.at[3, z], self.at.level(self.at.z - 1))

    def over(self, z, source=None):
        slot = self.view(z * 2 + self.at.c)
        source = slot if source is None else source
        return send(source, slot, self.sems.at[2, z], self.sems.at[4, z], self.at.partner())

    def start(self, source=None):
        at = self.at

        @pl.when(at.z + 1 < at.zs)
        def _():
            self.up(at.z, source).start()

        @pl.when(at.z > 0)
        def _():
            self.down(at.z, source).start()

        self.over(at.z, source).start()

    def step(self, index):
        at = self.at
        below, above = at.z - 1 - index, at.z + 1 + index

        @pl.when(below >= 0)
        def _():
            self.up(below).wait_recv()

            @pl.when(at.z + 1 < at.zs)
            def _():
                self.up(below).start()

            self.over(below).start()

        @pl.when(above < at.zs)
        def _():
            self.down(above).wait_recv()

            @pl.when(at.z > 0)
            def _():
                self.down(above).start()

            self.over(above).start()

    def wait_over(self, z):
        slot = self.view(z * 2 + 1 - self.at.c)
        send(slot, slot, self.sems.at[2, z], self.sems.at[4, z], self.at.partner()).wait_recv()

    def finish(self):
        for z in range(self.at.zs):
            self.wait_over(z)
        self.sent()

    def sent(self):
        at = self.at
        for z in range(at.zs):

            @pl.when((at.z >= z) & (at.z + 1 < at.zs))
            def _():
                self.up(z).wait_send()

            @pl.when((at.z <= z) & (at.z > 0))
            def _():
                self.down(z).wait_send()

            self.over(z).wait_send()


class LineSum:
    @staticmethod
    def scratch(wt, shape):
        zs = wt // 2
        return [
            pltpu.VMEM((zs,) + shape, jnp.bfloat16),
            pltpu.VMEM((zs,) + shape, jnp.bfloat16),
            pltpu.VMEM((zs,) + shape, jnp.bfloat16),
            pltpu.VMEM((zs,) + shape, jnp.bfloat16),
            pltpu.SemaphoreType.DMA((6, zs)),
        ]

    def __init__(self, at, part, scratch):
        self.at, self.part = at, part
        self.pair, self.held, self.below, self.above, self.sems = scratch

    def over(self, z):
        return send(
            self.part(z * 2 + 1 - self.at.c),
            self.pair.at[z],
            self.sems.at[0, z],
            self.sems.at[1, z],
            self.at.partner(),
        )

    def up(self, z):
        return send(
            self.held.at[z], self.below.at[z], self.sems.at[2, z], self.sems.at[3, z], self.at.level(self.at.z + 1)
        )

    def down(self, z):
        return send(
            self.held.at[z], self.above.at[z], self.sems.at[4, z], self.sems.at[5, z], self.at.level(self.at.z - 1)
        )

    def start(self):
        zs = self.at.zs
        for index in range(zs // 2):
            self.over(zs - 1 - index).start()
            self.over(index).start()

    def paired(self, z):
        self.over(z).wait_recv()
        return [self.part(z * 2 + self.at.c), self.pair.at[z]]

    def step(self, index):
        at = self.at
        high, low = at.zs - 1 - index, index

        @pl.when(at.z < high)
        def _():
            terms = self.paired(high)

            @pl.when(at.z == 0)
            def _():
                add_into(self.held.at[high], terms)

            @pl.when(at.z > 0)
            def _():
                self.up(high).wait_recv()
                add_into(self.held.at[high], terms + [self.below.at[high]])

            self.up(high).start()

        @pl.when(at.z > low)
        def _():
            terms = self.paired(low)

            @pl.when(at.z == at.zs - 1)
            def _():
                add_into(self.held.at[low], terms)

            @pl.when(at.z < at.zs - 1)
            def _():
                self.down(low).wait_recv()
                add_into(self.held.at[low], terms + [self.above.at[low]])

            self.down(low).start()

    def finish(self, total):
        at = self.at
        terms = self.paired(at.z)

        @pl.when(at.z == 0)
        def _():
            self.down(0).wait_recv()
            add_into(total, terms + [self.above.at[0]])

        @pl.when(at.z == at.zs - 1)
        def _():
            self.up(at.zs - 1).wait_recv()
            add_into(total, terms + [self.below.at[at.zs - 1]])

        @pl.when((at.z > 0) & (at.z < at.zs - 1))
        def _():
            self.up(at.z).wait_recv()
            self.down(at.z).wait_recv()
            add_into(total, terms + [self.below.at[at.z], self.above.at[at.z]])

        for z in range(at.zs):

            @pl.when(at.z < z)
            def _():
                self.up(z).wait_send()

            @pl.when(at.z > z)
            def _():
                self.down(z).wait_send()

            self.over(z).wait_send()


def remote_call(kernel, name, number, outs, scratch, *operands, in_specs=None, out_specs=None):
    return pl.pallas_call(
        kernel,
        name=name,
        out_shape=outs,
        in_specs=[VMEM] * len(operands) if in_specs is None else in_specs,
        out_specs=jax.tree.map(lambda _: VMEM, outs) if out_specs is None else out_specs,
        scratch_shapes=scratch,
        compiler_params=pltpu.CompilerParams(
            collective_id=number, has_side_effects=True, vmem_limit_bytes=60 * 1024 * 1024
        ),
    )(*operands)


def gather_start(tokens, qkv_rows, out_rows, gains):
    seq, wt = lax.axis_size("seq"), lax.axis_size("wt")
    count, width = tokens.shape
    parts, rows, columns = qkv_rows.shape

    def kernel(x_ref, qkv_ref, out_ref, gain_ref, xs, qkvs, outs, gains_out, *scratch):
        at = Place(seq, wt)
        x_sems, scratch = scratch[:3], scratch[3:]
        line_sems, scratch = [scratch[index : index + 1] for index in range(3)], scratch[3:]
        swap_q, swap_g, local = scratch
        at.meet(True, True)
        half = count // 2
        gather_x = SquareGather(
            at,
            lambda s, h: xs.at[pl.ds(pl.multiple_of(s * count + h * half, half), half)],
            lambda h: x_ref.at[pl.ds(h * half, half)],
            x_sems,
        )
        gather_q = LineGather(at, lambda w: qkvs.at[:, w], line_sems[0])
        gather_g = LineGather(at, lambda w: gains_out.at[:, w], line_sems[1])
        gather_o = LineGather(at, lambda w: outs.at[w], line_sems[2])
        swaps = []
        for step in range(1, seq):
            to = lax.rem(at.s + step, seq)
            swaps.append(
                send(gain_ref, gains_out.at[at.s, at.w], swap_g.at[step, 0], swap_g.at[at.s, 1], (to, at.w))
            )
            swaps.append(
                send(qkv_ref.at[to], qkvs.at[at.s, at.w], swap_q.at[step, 0], swap_q.at[at.s, 1], (to, at.w))
            )
        for copy in swaps:
            copy.start()
        gather_x.start()
        own = [
            pltpu.make_async_copy(qkv_ref.at[at.s], qkvs.at[at.s, at.w], local.at[0]),
            pltpu.make_async_copy(gain_ref, gains_out.at[at.s, at.w], local.at[1]),
            pltpu.make_async_copy(out_ref, outs.at[at.w], local.at[2]),
            pltpu.make_async_copy(x_ref, xs.at[pl.ds(pl.multiple_of(at.s * count, count), count)], local.at[3]),
        ]
        for copy in own:
            copy.start()
        for copy in own:
            copy.wait()
        for step in range(1, seq):
            s = lax.rem(at.s + step, seq)
            slot = gains_out.at[s, at.w]
            send(slot, slot, swap_g.at[step, 0], swap_g.at[s, 1], at.across()).wait_recv()
            slot = qkvs.at[s, at.w]
            send(slot, slot, swap_q.at[step, 0], swap_q.at[s, 1], at.across()).wait_recv()
        gather_g.start()
        gather_q.start()
        gather_o.start()
        gather_x.relay()
        for index in range(at.zs - 1):
            gather_g.step(index)
            gather_q.step(index)
            gather_o.step(index)
        gather_x.finish()
        gather_g.finish()
        gather_q.finish()
        gather_o.finish()
        for copy in swaps:
            copy.wait_send()

    return remote_call(
        kernel,
        "gather_start",
        0,
        [
            jax.ShapeDtypeStruct((seq * count, width), tokens.dtype),
            jax.ShapeDtypeStruct((seq, wt, rows, columns), qkv_rows.dtype),
            jax.ShapeDtypeStruct((wt,) + out_rows.shape, out_rows.dtype),
            jax.ShapeDtypeStruct((seq, wt) + gains.shape, gains.dtype),
        ],
        SquareGather.semaphores(seq)
        + LineGather.semaphores(wt) * 3
        + [
            pltpu.SemaphoreType.DMA((seq, 2)),
            pltpu.SemaphoreType.DMA((seq, 2)),
            pltpu.SemaphoreType.DMA((4,)),
        ],
        tokens,
        qkv_rows,
        out_rows,
        gains,
    )


def square_sum(parts, name, number):
    seq, wt = lax.axis_size("seq"), lax.axis_size("wt")
    half_shape = parts.shape[2:]

    def kernel(parts_ref, total_ref, *scratch):
        at = Place(seq, wt)
        at.meet(True, False)
        work = SquareSum(at, lambda s, h: parts_ref.at[s, h], scratch)
        work.start()
        work.relay()
        work.finish(lambda h: total_ref.at[h])

    return remote_call(
        kernel,
        name,
        number,
        jax.ShapeDtypeStruct((2,) + half_shape, jnp.float32),
        SquareSum.scratch(seq, half_shape),
        parts,
    )


def square_gather(shard, name, number):
    seq, wt = lax.axis_size("seq"), lax.axis_size("wt")
    count, width = shard.shape
    half = count // 2

    def kernel(shard_ref, all_ref, *scratch):
        at = Place(seq, wt)
        at.meet(True, False)
        work = SquareGather(
            at,
            lambda s, h: all_ref.at[pl.ds(pl.multiple_of(s * count + h * half, half), half)],
            lambda h: shard_ref.at[pl.ds(h * half, half)],
            scratch[:3],
        )
        work.start()
        own = pltpu.make_async_copy(
            shard_ref, all_ref.at[pl.ds(pl.multiple_of(at.s * count, count), count)], scratch[3].at[0]
        )
        own.start()
        own.wait()
        work.relay()
        work.finish()

    return remote_call(
        kernel,
        name,
        number,
        jax.ShapeDtypeStruct((seq * count, width), shard.dtype),
        SquareGather.semaphores(seq) + [pltpu.SemaphoreType.DMA((1,))],
        shard,
    )


class LinePieces:
    @staticmethod
    def scratch(wt, shape, pieces):
        zs = wt // 2
        return [pltpu.VMEM((zs,) + shape, jnp.bfloat16)] * 4 + [pltpu.SemaphoreType.DMA((6, zs, pieces))]

    def __init__(self, at, part, scratch):
        self.at, self.part = at, part
        self.pair, self.held, self.below, self.above, self.sems = scratch
        self.pieces = self.sems.shape[2]
        self.width = self.pair.shape[2] // self.pieces

    def cut(self, ref, piece):
        return ref.at[:, pl.ds(pl.multiple_of(piece * self.width, self.width), self.width)]

    def over(self, z, piece):
        return send(
            self.cut(self.part(z * 2 + 1 - self.at.c), piece),
            self.cut(self.pair.at[z], piece),
            self.sems.at[0, z, piece],
            self.sems.at[1, z, piece],
            self.at.partner(),
        )

    def up(self, z, piece):
        return send(
            self.cut(self.held.at[z], piece),
            self.cut(self.below.at[z], piece),
            self.sems.at[2, z, piece],
            self.sems.at[3, z, piece],
            self.at.level(self.at.z + 1),
        )

    def down(self, z, piece):
        return send(
            self.cut(self.held.at[z], piece),
            self.cut(self.above.at[z], piece),
            self.sems.at[4, z, piece],
            self.sems.at[5, z, piece],
            self.at.level(self.at.z - 1),
        )

    def terms(self, z, piece):
        self.over(z, piece).wait_recv()
        return [self.cut(self.part(z * 2 + self.at.c), piece), self.cut(self.pair.at[z], piece)]

    def ends(self, z, piece):
        at = self.at

        @pl.when((at.z == 0) & (z > 0))
        def _():
            add_into(self.cut(self.held.at[z], piece), self.terms(z, piece))
            self.up(z, piece).start()

        @pl.when((at.z == at.zs - 1) & (z < at.zs - 1))
        def _():
            add_into(self.cut(self.held.at[z], piece), self.terms(z, piece))
            self.down(z, piece).start()

    def pass_on(self):
        at = self.at
        for index in range(1, at.zs):
            high, low = index, at.zs - 1 - index

            def step(piece, carry):
                @pl.when((at.z < high) & (at.z > 0))
                def _():
                    terms = self.terms(high, piece)
                    self.up(high, piece).wait_recv()
                    add_into(
                        self.cut(self.held.at[high], piece), terms + [self.cut(self.below.at[high], piece)]
                    )
                    self.up(high, piece).start()

                @pl.when((at.z > low) & (at.z < at.zs - 1))
                def _():
                    terms = self.terms(low, piece)
                    self.down(low, piece).wait_recv()
                    add_into(
                        self.cut(self.held.at[low], piece), terms + [self.cut(self.above.at[low], piece)]
                    )
                    self.down(low, piece).start()

                return carry

            lax.fori_loop(0, self.pieces, step, 0)

    def finish(self, total):
        at = self.at

        def step(piece, carry):
            terms = self.terms(at.z, piece)
            below, above = self.cut(self.below.at[at.z], piece), self.cut(self.above.at[at.z], piece)

            @pl.when(at.z == 0)
            def _():
                self.down(at.z, piece).wait_recv()
                add_into(self.cut(total, piece), terms + [above])

            @pl.when(at.z == at.zs - 1)
            def _():
                self.up(at.z, piece).wait_recv()
                add_into(self.cut(total, piece), terms + [below])

            @pl.when((at.z > 0) & (at.z < at.zs - 1))
            def _():
                self.up(at.z, piece).wait_recv()
                self.down(at.z, piece).wait_recv()
                add_into(self.cut(total, piece), terms + [below, above])

            for z in range(at.zs):

                @pl.when(at.z < z)
                def _():
                    self.up(z, piece).wait_send()

                @pl.when(at.z > z)
                def _():
                    self.down(z, piece).wait_send()

                self.over(z, piece).wait_send()
            return carry

        lax.fori_loop(0, self.pieces, step, 0)


def exchange(at, shard, everyone, gather_sems, local, sums, first, second, total, ready, wait_for_ready):
    count = shard.shape[0]
    gather = LineGather(
        at, lambda w: everyone.at[pl.ds(pl.multiple_of(w * count, count), count)], gather_sems
    )
    gather.start(shard)
    own = pltpu.make_async_copy(
        shard, everyone.at[pl.ds(pl.multiple_of(at.w * count, count), count)], local
    )
    own.start()
    own.wait()
    ready[0]()
    last = 2 * (at.zs - 1)
    late = 3 if wait_for_ready else 0

    def turn(index, carry):
        fresh = index <= last
        place = jnp.where(fresh, index, jnp.where(index == last + 3, 0, index - last))
        far, side = lax.div(place + 1, 2), lax.rem(place, 2)
        z = at.z + jnp.where(side == 1, -far, far)
        valid = (z >= 0) & (z < at.zs)

        @pl.when(fresh & (side == 1))
        def _():
            gather.step(far - 1)

        @pl.when(fresh & valid)
        def _():
            gather.wait_over(z)
            first(z)

        if wait_for_ready:

            @pl.when(index == late)
            def _():
                ready[1]()

        @pl.when(valid & (index >= late))
        def _():
            def step(piece, inner):
                second(z, piece)
                sums.over(z, piece).start()

                @pl.when(piece > 0)
                def _():
                    sums.ends(z, piece - 1)

                return inner

            lax.fori_loop(0, sums.pieces, step, 0)
            sums.ends(z, sums.pieces - 1)

        return carry

    lax.fori_loop(0, last + 1 + late, turn, 0)
    sums.pass_on()
    sums.finish(total)
    gather.sent()


PIECES = 4
ANY = pl.BlockSpec(memory_space=pl.ANY)


def feed_forward(normed, gate_up, down_shard):
    seq, wt = lax.axis_size("seq"), lax.axis_size("wt")
    count, width = normed.shape
    units = gate_up.shape[2]
    columns = down_shard.shape[1]
    tokens = wt * count
    zs = wt // 2
    half = units // 2

    def kernel(normed_ref, gate_up_ref, shard_ref, total_ref, normed_out, gate_out, up_out, active_out, down_out, *scratch):
        at = Place(seq, wt)
        everyone, gates, downs, gate_all, up_all, active_all, parts = scratch[:7]
        gather_sems, sum_scratch, square_sems, local, outgoing = (
            scratch[7:8],
            scratch[8:13],
            scratch[13:16],
            scratch[16],
            scratch[17],
        )
        load = pltpu.make_async_copy(gate_up_ref, gates, local.at[0])
        load.start()
        at.meet(True, True)
        weights = SquareGather(
            at,
            lambda s, h: downs.at[
                pl.ds(h * half, half), pl.ds(pl.multiple_of(s * columns, columns), columns)
            ],
            lambda h: shard_ref.at[pl.ds(h * half, half)],
            square_sems,
        )
        sums = LinePieces(
            at, lambda w: parts.at[pl.ds(pl.multiple_of(w * count, count), count)], sum_scratch
        )
        down_store = pltpu.make_async_copy(downs, down_out, local.at[2])

        def ready_first():
            weights.start()
            own = pltpu.make_async_copy(
                shard_ref, downs.at[:, pl.ds(pl.multiple_of(at.s * columns, columns), columns)], local.at[3]
            )
            own.start()
            own.wait()
            load.wait()

        def ready_later():
            weights.relay()
            weights.finish()
            down_store.start()

        def rows(z):
            return pl.ds(pl.multiple_of(z * 2 * count, 2 * count), 2 * count)

        def stores(z):
            return [
                pltpu.make_async_copy(source.at[rows(z)], target.at[rows(z)], outgoing.at[index, z])
                for index, (source, target) in enumerate(
                    ((everyone, normed_out), (gate_all, gate_out), (up_all, up_out), (active_all, active_out))
                )
            ]

        def first(z):
            here = everyone[rows(z), :]
            gate = jnp.dot(here, gates[0], preferred_element_type=jnp.float32)
            up = jnp.dot(here, gates[1], preferred_element_type=jnp.float32)
            gate_all[rows(z), :] = gate
            up_all[rows(z), :] = up
            active_all[rows(z), :] = gated_unit(gate, up).astype(jnp.bfloat16)
            for copy in stores(z):
                copy.start()

        def second(z, piece):
            window = pl.ds(pl.multiple_of(piece * sums.width, sums.width), sums.width)
            parts[rows(z), window] = jnp.dot(
                active_all[rows(z), :], downs[:, window], preferred_element_type=jnp.float32
            ).astype(jnp.bfloat16)

        exchange(
            at,
            normed_ref,
            everyone,
            gather_sems,
            local.at[1],
            sums,
            first,
            second,
            total_ref,
            (ready_first, ready_later),
            True,
        )
        down_store.wait()
        for z in range(zs):
            for copy in stores(z):
                copy.wait()

    return remote_call(
        kernel,
        "feed_forward",
        2,
        [
            jax.ShapeDtypeStruct((count, width), jnp.float32),
            jax.ShapeDtypeStruct((tokens, width), jnp.bfloat16),
            jax.ShapeDtypeStruct((tokens, units), jnp.float32),
            jax.ShapeDtypeStruct((tokens, units), jnp.float32),
            jax.ShapeDtypeStruct((tokens, units), jnp.bfloat16),
            jax.ShapeDtypeStruct((units, width), jnp.bfloat16),
        ],
        [
            pltpu.VMEM((tokens, width), jnp.bfloat16),
            pltpu.VMEM(gate_up.shape, jnp.bfloat16),
            pltpu.VMEM((units, width), jnp.bfloat16),
            pltpu.VMEM((tokens, units), jnp.float32),
            pltpu.VMEM((tokens, units), jnp.float32),
            pltpu.VMEM((tokens, units), jnp.bfloat16),
            pltpu.VMEM((tokens, width), jnp.bfloat16),
        ]
        + LineGather.semaphores(wt)
        + LinePieces.scratch(wt, (count, width), PIECES)
        + SquareGather.semaphores(seq)
        + [pltpu.SemaphoreType.DMA((4,)), pltpu.SemaphoreType.DMA((4, zs))],
        normed,
        gate_up,
        down_shard,
        in_specs=[VMEM, ANY, VMEM],
        out_specs=[VMEM] + [ANY] * 5,
    )


def feed_back(error, gate_up, down, gate, up):
    seq, wt = lax.axis_size("seq"), lax.axis_size("wt")
    count, width = error.shape
    units = gate_up.shape[2]
    tokens = wt * count
    zs = wt // 2

    def kernel(error_ref, gate_up_ref, down_ref, gate_ref, up_ref, total_ref, error_out, back_out, *scratch):
        at = Place(seq, wt)
        everyone, gates, downs, gate_all, up_all, back_all, parts = scratch[:7]
        gather_sems, sum_scratch, local, outgoing = scratch[7:8], scratch[8:13], scratch[13], scratch[14]
        loads = [
            pltpu.make_async_copy(source, target, local.at[index])
            for index, (source, target) in enumerate(
                ((down_ref, downs), (gate_ref, gate_all), (up_ref, up_all), (gate_up_ref, gates))
            )
        ]
        for load in loads:
            load.start()
        at.meet(False, True)
        sums = LinePieces(
            at, lambda w: parts.at[pl.ds(pl.multiple_of(w * count, count), count)], sum_scratch
        )

        def ready_first():
            for load in loads:
                load.wait()

        def rows(z):
            return pl.ds(pl.multiple_of(z * 2 * count, 2 * count), 2 * count)

        def stores(z):
            return [
                pltpu.make_async_copy(everyone.at[rows(z)], error_out.at[rows(z)], outgoing.at[0, z]),
                pltpu.make_async_copy(back_all.at[:, rows(z)], back_out.at[:, rows(z)], outgoing.at[1, z]),
            ]

        def first(z):
            active_back = contract_last(everyone[rows(z), :], downs[...])
            gate_here, up_here = gate_all[rows(z), :], up_all[rows(z), :]
            share = jax.nn.sigmoid(gate_here)
            back_all[0, rows(z), :] = (
                active_back * up_here * share * (1.0 + gate_here * (1.0 - share))
            ).astype(jnp.bfloat16)
            back_all[1, rows(z), :] = (active_back * gate_here * share).astype(jnp.bfloat16)
            for copy in stores(z):
                copy.start()

        def second(z, piece):
            window = pl.ds(pl.multiple_of(piece * sums.width, sums.width), sums.width)
            parts[rows(z), window] = (
                contract_last(back_all[0, rows(z), :], gates[0, window, :])
                + contract_last(back_all[1, rows(z), :], gates[1, window, :])
            ).astype(jnp.bfloat16)

        exchange(
            at,
            error_ref,
            everyone,
            gather_sems,
            local.at[4],
            sums,
            first,
            second,
            total_ref,
            (ready_first,),
            False,
        )
        for z in range(zs):
            for copy in stores(z):
                copy.wait()

    return remote_call(
        kernel,
        "feed_back",
        3,
        [
            jax.ShapeDtypeStruct((count, width), jnp.float32),
            jax.ShapeDtypeStruct((tokens, width), jnp.bfloat16),
            jax.ShapeDtypeStruct((2, tokens, units), jnp.bfloat16),
        ],
        [
            pltpu.VMEM((tokens, width), jnp.bfloat16),
            pltpu.VMEM(gate_up.shape, jnp.bfloat16),
            pltpu.VMEM((units, width), jnp.bfloat16),
            pltpu.VMEM((tokens, units), jnp.float32),
            pltpu.VMEM((tokens, units), jnp.float32),
            pltpu.VMEM((2, tokens, units), jnp.bfloat16),
            pltpu.VMEM((tokens, width), jnp.bfloat16),
        ]
        + LineGather.semaphores(wt)
        + LinePieces.scratch(wt, (count, width), PIECES)
        + [pltpu.SemaphoreType.DMA((5,)), pltpu.SemaphoreType.DMA((2, zs))],
        error,
        gate_up,
        down,
        gate,
        up,
        in_specs=[VMEM, ANY, ANY, ANY, ANY],
        out_specs=[VMEM, ANY, ANY],
    )


def final_sums(hidden_parts, gate_up_parts, down_parts, qkv_parts, out_parts):
    seq, wt = lax.axis_size("seq"), lax.axis_size("wt")
    hidden_half = hidden_parts.shape[2:]
    gate_up_half = gate_up_parts.shape[2:]
    down_rows, down_all = down_parts.shape[1:]
    down_columns = down_all // seq
    down_half = (down_rows, down_columns)
    qkv_shape = (seq,) + qkv_parts.shape[2:]

    def kernel(hidden_ref, gate_up_ref, down_ref, qkv_ref, out_ref, h_total, gu_total, d_total, q_total, o_total, *scratch):
        at = Place(seq, wt)
        at.meet(True, True)
        square, scratch = [scratch[8 * index : 8 * index + 8] for index in range(3)], scratch[24:]
        line, scratch = [scratch[5 * index : 5 * index + 5] for index in range(2)], scratch[10:]
        q_sum, swap = scratch
        hidden = SquareSum(at, lambda s, h: hidden_ref.at[s, h], square[0])
        gate_up = SquareSum(at, lambda s, h: gate_up_ref.at[h, s], square[1])
        down = SquareSum(
            at,
            lambda s, h: down_ref.at[h, :, pl.ds(pl.multiple_of(s * down_columns, down_columns), down_columns)],
            square[2],
        )
        qkv = LineSum(at, lambda w: qkv_ref.at[:, w], line[0])
        out = LineSum(at, lambda w: out_ref.at[w], line[1])
        qkv.start()
        out.start()
        hidden.start()
        gate_up.start()
        down.start()
        hidden.relay()
        for index in range(at.zs - 1):
            qkv.step(index)
            out.step(index)
        qkv.finish(q_sum)
        out.finish(o_total)
        swaps = []
        for step in range(1, seq):
            to = lax.rem(at.s + step, seq)
            copy = send(q_sum.at[to], q_total.at[at.s], swap.at[step, 0], swap.at[at.s, 1], (to, at.w))
            copy.start()
            swaps.append(copy)
        add_into(q_total.at[at.s], [q_sum.at[at.s]])
        gate_up.relay()
        down.relay()
        hidden.finish(lambda h: h_total.at[h])
        gate_up.finish(lambda h: gu_total.at[h])
        down.finish(lambda h: d_total.at[h])
        for step in range(1, seq):
            s = lax.rem(at.s + step, seq)
            slot = q_total.at[s]
            send(slot, slot, swap.at[step, 0], swap.at[s, 1], at.across()).wait_recv()
        for copy in swaps:
            copy.wait_send()

    return remote_call(
        kernel,
        "final_sums",
        7,
        [
            jax.ShapeDtypeStruct((2,) + hidden_half, jnp.float32),
            jax.ShapeDtypeStruct((2,) + gate_up_half, jnp.float32),
            jax.ShapeDtypeStruct((2,) + down_half, jnp.float32),
            jax.ShapeDtypeStruct(qkv_shape, jnp.float32),
            jax.ShapeDtypeStruct(out_parts.shape[1:], jnp.float32),
        ],
        SquareSum.scratch(seq, hidden_half)
        + SquareSum.scratch(seq, gate_up_half)
        + SquareSum.scratch(seq, down_half)
        + LineSum.scratch(wt, qkv_shape)
        + LineSum.scratch(wt, out_parts.shape[1:])
        + [pltpu.VMEM(qkv_shape, jnp.float32), pltpu.SemaphoreType.DMA((seq, 2))],
        hidden_parts,
        gate_up_parts,
        down_parts,
        qkv_parts,
        out_parts,
    )


def small_sums(spread, lined):
    seq, wt = lax.axis_size("seq"), lax.axis_size("wt")
    tile = spread.shape[2:]

    def kernel(spread_ref, lined_ref, total_ref, first, middle, last, first_sems, last_sems):
        at = Place(seq, wt)
        at.meet(True, True)
        copies = []
        for step in range(1, seq):
            to = lax.rem(at.s + step, seq)
            copy = send(spread_ref.at[to], first.at[at.s], first_sems.at[step, 0], first_sems.at[at.s, 1], (to, at.w))
            copy.start()
            copies.append(copy)
        terms = [spread_ref.at[at.s]]
        for step in range(1, seq):
            s = lax.rem(at.s + step, seq)
            slot = first.at[s]
            send(slot, slot, first_sems.at[step, 0], first_sems.at[s, 1], at.across()).wait_recv()
            terms.append(slot)
        add_into(middle, terms + [lined_ref])
        for step in range(1, wt):
            to = lax.rem(at.w + step, wt)
            copy = send(middle.at[to], last.at[at.w], last_sems.at[step, 0], last_sems.at[at.w, 1], (at.s, to))
            copy.start()
            copies.append(copy)
        terms = [middle.at[at.w]]
        for step in range(1, wt):
            w = lax.rem(at.w + step, wt)
            slot = last.at[w]
            send(slot, slot, last_sems.at[step, 0], last_sems.at[w, 1], at.partner()).wait_recv()
            terms.append(slot)
        add_into(total_ref, terms)
        for copy in copies:
            copy.wait_send()

    return remote_call(
        kernel,
        "small_sums",
        8,
        jax.ShapeDtypeStruct(tile, jnp.float32),
        [
            pltpu.VMEM((seq, wt) + tile, jnp.float32),
            pltpu.VMEM((wt,) + tile, jnp.float32),
            pltpu.VMEM((wt,) + tile, jnp.float32),
            pltpu.SemaphoreType.DMA((seq, 2)),
            pltpu.SemaphoreType.DMA((wt, 2)),
        ],
        spread,
        lined,
    )


def rows_of_tile(values, row):
    pad = [(0, 0)] * (values.ndim - 1)
    return jnp.pad(values[..., None, :], pad + [(row, 7 - row), (0, 128 - values.shape[-1])])

def body(
    inputs,
    segment_ids,
    valid_lengths,
    teacher,
    w_qkv,
    conv_weight,
    w_out,
    norm_gain,
    w_gate_up,
    w_down,
    mlp_gain,
):
    seq_parts, wt_parts = lax.axis_size("seq"), lax.axis_size("wt")
    tok_count = inputs.shape[1]
    model_width = inputs.shape[2]
    length = tok_count * seq_parts
    block_rows = min(block_limit, length)
    head_count = H // seq_parts
    head_width = 2 * FEAT + DV
    qkv_width = head_count * head_width
    rows_low = inputs[0]
    rows_in = rows_low.astype(jnp.float32)
    gain_lanes = norm_gain.shape[0]
    gains = rows_of_tile(norm_gain.astype(jnp.float32), 0) + rows_of_tile(mlp_gain.astype(jnp.float32), 1)
    qkv_rows = w_qkv.reshape(w_qkv.shape[0], seq_parts, qkv_width).transpose(1, 0, 2)
    tokens_all, qkv_columns, out_rows, gains_all = gather_start(rows_low, qkv_rows, w_out, gains)
    qkv_columns = qkv_columns.reshape(model_width, qkv_width)
    out_rows = out_rows.reshape(head_count * DV, model_width)
    gain_first = gains_all[:, :, 0, :gain_lanes].reshape(model_width)
    gain_second = gains_all[:, :, 1, :gain_lanes].reshape(model_width)
    gate_up_part = lax.all_gather(w_gate_up, "seq", axis=1, tiled=True)
    hidden_low = rms_norm(tokens_all.astype(jnp.float32), gain_first).astype(jnp.bfloat16)
    projected = jnp.dot(hidden_low, qkv_columns, preferred_element_type=jnp.float32).astype(
        jnp.bfloat16
    )
    grouped = projected.reshape(length, head_count, head_width)
    head_queries = grouped[:, :, :FEAT].transpose(1, 2, 0)
    head_keys = grouped[:, :, FEAT : 2 * FEAT].transpose(1, 2, 0)
    raw_values = grouped[:, :, 2 * FEAT :].astype(jnp.float32)
    segments = segment_ids[0]
    conv_taps = conv_weight.astype(jnp.float32).reshape(KCONV, head_count, DV)
    tap_masks = [jnp.ones((length,), jnp.float32)]
    mixed_values = conv_taps[0] * raw_values
    for tap_index in range(1, KCONV):
        earlier = shift_down(segments, tap_index, -1)
        tap_masks.append((earlier == segments).astype(jnp.float32))
        mixed_values = (
            mixed_values
            + conv_taps[tap_index]
            * shift_down(raw_values, tap_index, 0.0)
            * tap_masks[tap_index][:, None, None]
        )
    conv_low = mixed_values.astype(jnp.bfloat16).transpose(1, 0, 2)
    head_outputs, denominators = attend_forward(
        head_queries, head_keys, conv_low, segments, block_rows
    )
    mixer_low = head_outputs.transpose(1, 0, 2).reshape(length, head_count * DV).astype(jnp.bfloat16)
    mixed_parts = jnp.dot(mixer_low, out_rows, preferred_element_type=jnp.float32).astype(jnp.bfloat16)
    attended = rows_in + square_sum(
        mixed_parts.reshape(seq_parts, 2, tok_count // 2, model_width), "mixed_sum", 1
    ).reshape(tok_count, model_width)
    normed_value, second_pull = jax.vjp(rms_norm, attended, gain_second)
    normed_low = normed_value.astype(jnp.bfloat16)
    branch_out, normed_all, gate_all, up_all, active_all, down_part = feed_forward(
        normed_low, gate_up_part, w_down
    )
    outputs = attended + branch_out
    sequence_length = lax.dynamic_index_in_dim(
        valid_lengths, lax.axis_index("wt"), 0, keepdims=False
    )
    positions = lax.axis_index("seq") * tok_count + jnp.arange(tok_count, dtype=jnp.int32)
    keep_mask = (positions < sequence_length).astype(jnp.float32)
    residual_error = (outputs - teacher[0].astype(jnp.float32)) * keep_mask[:, None]
    energy = 0.5 * jnp.sum(residual_error * residual_error)
    branch_grad = residual_error.astype(jnp.bfloat16)
    normed_grad, error_all, gate_up_grad = feed_back(branch_grad, gate_up_part, down_part, gate_all, up_all)
    down_term = contract_first(active_all, error_all)
    gate_up_term = jnp.einsum(
        "tc,gtf->gcf", normed_all, gate_up_grad, preferred_element_type=jnp.float32
    )
    attended_back, gain_two_term = second_pull(normed_grad)
    attended_grad = residual_error + attended_back
    mixer_branch = square_gather(attended_grad.astype(jnp.bfloat16), "mix_back_gather", 6)
    out_term = contract_first(mixer_low, mixer_branch)
    mixer_grad = contract_last(mixer_branch, out_rows).astype(jnp.bfloat16)
    head_incoming = (
        mixer_grad.reshape(length, head_count, DV).transpose(1, 0, 2).astype(jnp.float32)
    )
    query_grads, key_grads, value_grads = attend_backward(
        head_queries,
        head_keys,
        conv_low,
        segments,
        head_outputs,
        denominators,
        head_incoming,
        block_rows,
    )
    mixed_grad = value_grads.transpose(1, 0, 2)
    conv_terms = [jnp.sum(mixed_grad * raw_values, axis=0)]
    raw_grad = conv_taps[0] * mixed_grad
    for tap_index in range(1, KCONV):
        masked = mixed_grad * tap_masks[tap_index][:, None, None]
        conv_terms.append(jnp.sum(masked * shift_down(raw_values, tap_index, 0.0), axis=0))
        raw_grad = raw_grad + conv_taps[tap_index] * shift_up(masked, tap_index)
    projected_grad = jnp.concatenate(
        [query_grads.transpose(2, 0, 1), key_grads.transpose(2, 0, 1), raw_grad], axis=2
    ).astype(jnp.bfloat16)
    returned = projected_grad.reshape(length, qkv_width)
    qkv_term = contract_first(hidden_low, returned).astype(jnp.bfloat16)
    hidden_parts = contract_last(returned, qkv_columns).astype(jnp.bfloat16)
    hidden_units = gate_up_part.shape[2]
    hidden_grad, gate_up_total, down_total, qkv_total, out_total = final_sums(
        hidden_parts.reshape(seq_parts, 2, tok_count // 2, model_width),
        gate_up_term.astype(jnp.bfloat16).reshape(2, seq_parts, model_width // seq_parts, hidden_units),
        down_term.astype(jnp.bfloat16).reshape(2, hidden_units // 2, model_width),
        qkv_term.reshape(seq_parts, wt_parts, w_qkv.shape[0], qkv_width),
        out_term.astype(jnp.bfloat16).reshape(wt_parts, w_out.shape[0], model_width),
    )
    _, first_pull = jax.vjp(rms_norm, rows_in, gain_first)
    inputs_back, gain_one_term = first_pull(hidden_grad.reshape(tok_count, model_width))
    inputs_grad = attended_grad + inputs_back
    grad_w_qkv = qkv_total.transpose(1, 0, 2).reshape(w_qkv.shape)
    grad_w_gate_up = gate_up_total
    grad_w_down = down_total.reshape(w_down.shape)
    grad_w_out = out_total
    spread = (
        rows_of_tile(gain_one_term.reshape(seq_parts, wt_parts, gain_lanes), 0)
        + rows_of_tile(gain_two_term.reshape(seq_parts, wt_parts, gain_lanes), 1)
        + rows_of_tile(jnp.broadcast_to(energy, (seq_parts, wt_parts, 1)), 2)
    )
    conv_block = jnp.stack(conv_terms).reshape(KCONV, wt_parts, gain_lanes)
    lined = sum(rows_of_tile(conv_block[tap], 3 + tap) for tap in range(KCONV))
    totals = small_sums(spread, lined)
    grad_norm_gain, grad_mlp_gain = totals[0, :gain_lanes], totals[1, :gain_lanes]
    grad_conv = totals[3 : 3 + KCONV, :gain_lanes]
    valid_total = jnp.sum(valid_lengths).astype(jnp.float32)
    mean_loss = 2.0 * totals[2, 0] / (valid_total * model_width)
    return (
        outputs.astype(jnp.bfloat16)[None],
        inputs_grad[None],
        mean_loss,
        grad_w_qkv,
        grad_conv,
        grad_w_out,
        grad_norm_gain,
        grad_w_gate_up,
        grad_w_down,
        grad_mlp_gain,
    )


def solution(mesh):
    in_specs = (
        P("wt", "seq", None),
        P("wt", None),
        P(),
        P("wt", "seq", None),
        P(("seq", "wt"), None),
        P(None, "seq"),
        P(("seq", "wt"), None),
        P(("seq", "wt")),
        P(None, "seq", "wt"),
        P("wt", "seq"),
        P(("seq", "wt")),
    )
    out_specs = (
        P("wt", "seq", None),
        P("wt", "seq", None),
        P(),
        P(("seq", "wt"), None),
        P(None, ("seq", "wt")),
        P(("seq", "wt"), None),
        P(("seq", "wt")),
        P(None, "seq", "wt"),
        P("wt", "seq"),
        P(("seq", "wt")),
    )
    return jax.shard_map(body, mesh=mesh, in_specs=in_specs, out_specs=out_specs, check_vma=False)
```

```python
import jax
import jax.numpy as jnp
from jax import lax
from jax.experimental import pallas as pl
from jax.experimental.pallas import tpu as pltpu
from jax.sharding import PartitionSpec as P

H = 16
FEAT = 16
KCONV = 3
DV = 128


epsilon = 1e-05
block_limit = 512


def rms_norm(values, gain_vector):
    inverse_root = lax.rsqrt(jnp.mean(values * values, axis=-1, keepdims=True) + epsilon)
    return values * inverse_root * gain_vector


def contract_last(former, latter):
    return lax.dot_general(
        former, latter, (((1,), (1,)), ((), ())), preferred_element_type=jnp.float32
    )


def contract_first(former, latter):
    return lax.dot_general(
        former, latter, (((0,), (0,)), ((), ())), preferred_element_type=jnp.float32
    )


def shift_down(values, amount, filler):
    padding = jnp.full((amount,) + values.shape[1:], filler, values.dtype)
    return jnp.concatenate([padding, values[:-amount]], axis=0)


def gated_unit(gate_in, up_in):
    return jax.nn.silu(gate_in) * up_in


def block_kernel(query_block, key_block, query_segments, key_segments, query_start, key_start):
    row_width = query_segments.shape[0]
    scaled_dots = (
        jnp.einsum("hfq,hfk->hqk", query_block, key_block, preferred_element_type=jnp.float32)
        * 0.25
    )
    query_places = query_start + jnp.arange(row_width, dtype=jnp.int32)
    key_places = key_start + jnp.arange(row_width, dtype=jnp.int32)
    allowed = (query_segments[:, None] == key_segments[None, :]) & (
        query_places[:, None] >= key_places[None, :]
    )
    kernel = jnp.where(allowed[None], 1.0 + scaled_dots + 0.5 * scaled_dots * scaled_dots, 0.0)
    return (scaled_dots, allowed, kernel)


def attend_forward(queries, key_rows, values, segments, block_rows):
    head_count, length, value_width = values.shape
    block_count = length // block_rows

    def query_step(query_index, running):
        outputs, denominators = running
        query_start = query_index * block_rows
        query_block = lax.dynamic_slice_in_dim(queries, query_start, block_rows, 2)
        query_segments = lax.dynamic_slice_in_dim(segments, query_start, block_rows, 0)

        def key_step(inner_index, inner_running):
            numerator, denominator = inner_running
            key_start = inner_index * block_rows
            key_block = lax.dynamic_slice_in_dim(key_rows, key_start, block_rows, 2)
            value_block = lax.dynamic_slice_in_dim(values, key_start, block_rows, 1)
            key_segments = lax.dynamic_slice_in_dim(segments, key_start, block_rows, 0)
            scaled_dots, allowed, kernel = block_kernel(
                query_block, key_block, query_segments, key_segments, query_start, key_start
            )
            numerator = numerator + jnp.einsum(
                "hqk,hkd->hqd",
                kernel.astype(jnp.bfloat16),
                value_block,
                preferred_element_type=jnp.float32,
            )
            denominator = denominator + jnp.sum(kernel, axis=2)
            return (numerator, denominator)

        starting = (
            jnp.zeros((head_count, block_rows, value_width), jnp.float32),
            jnp.zeros((head_count, block_rows), jnp.float32),
        )
        numerator, denominator = lax.fori_loop(0, query_index + 1, key_step, starting)
        outputs = lax.dynamic_update_slice_in_dim(
            outputs, numerator / denominator[:, :, None], query_start, 1
        )
        denominators = lax.dynamic_update_slice_in_dim(denominators, denominator, query_start, 1)
        return (outputs, denominators)

    initial = (
        jnp.zeros((head_count, length, value_width), jnp.float32),
        jnp.zeros((head_count, length), jnp.float32),
    )
    return lax.fori_loop(0, block_count, query_step, initial)


MESH = pl.DeviceIdType.MESH
VMEM = pl.BlockSpec(memory_space=pltpu.VMEM)
ANY = pl.BlockSpec(memory_space=pl.ANY)
VMEM_LIMIT = 63 * 1024 * 1024


class Place:
    def __init__(self, seq, wt):
        self.seq, self.wt = seq, wt
        self.ys, self.zs = seq // 2, wt // 2
        self.s, self.w = lax.axis_index("seq"), lax.axis_index("wt")
        self.y, self.x = lax.div(self.s, 2), lax.rem(self.s, 2)
        self.z, self.c = lax.div(self.w, 2), lax.rem(self.w, 2)

    def across(self):
        return (self.y * 2 + 1 - self.x, self.w)

    def beside(self, step):
        return lax.rem(self.y + step, self.ys)

    def column(self, y):
        return (y * 2 + self.x, self.w)

    def partner(self):
        return (self.s, self.z * 2 + 1 - self.c)

    def level(self, z):
        return (self.s, z * 2 + self.c)

    def meet(self, square, line):
        barrier = pltpu.get_barrier_semaphore()
        count = 0
        if square:
            for step in range(1, self.seq):
                device = (lax.rem(self.s + step, self.seq), self.w)
                pl.semaphore_signal(barrier, inc=1, device_id=device, device_id_type=MESH)
                count += 1
        if line:
            for step in range(1, self.wt):
                device = (self.s, lax.rem(self.w + step, self.wt))
                pl.semaphore_signal(barrier, inc=1, device_id=device, device_id_type=MESH)
                count += 1
        pl.semaphore_wait(barrier, count)


def send(source, target, leaving, arriving, device):
    return pltpu.make_async_remote_copy(
        src_ref=source,
        dst_ref=target,
        send_sem=leaving,
        recv_sem=arriving,
        device_id=device,
        device_id_type=MESH,
    )


def add_into(target, sources):
    if len(target.shape) == 3:
        for index in range(target.shape[0]):
            add_into(target.at[index], [source.at[index] for source in sources])
        return
    rows = target.shape[0]
    tile = next(t for t in (64, 32, 16, 8, rows) if rows % t == 0)

    def step(index, carry):
        window = pl.ds(pl.multiple_of(index * tile, tile), tile)
        total = sources[0][window, :].astype(jnp.float32)
        for source in sources[1:]:
            total = total + source[window, :].astype(jnp.float32)
        target[window, :] = total.astype(target.dtype)
        return carry

    lax.fori_loop(0, rows // tile, step, 0)


class SquareGather:
    @staticmethod
    def semaphores(seq):
        return [
            pltpu.SemaphoreType.DMA((2 + seq // 2,)),
            pltpu.SemaphoreType.DMA((seq // 2, 3)),
            pltpu.SemaphoreType.DMA((seq, 2)),
        ]

    def __init__(self, at, view, own, sems):
        self.at, self.view, self.own = at, view, own
        self.over_x, self.over_y, self.got = sems
        self.sent = []

    def go(self, source, s, half, leaving, device):
        copy = send(source, self.view(s, half), leaving, self.got.at[s, half], device)
        copy.start()
        self.sent.append(copy)

    def wait(self, s, half):
        slot = self.view(s, half)
        send(slot, slot, self.over_x.at[0], self.got.at[s, half], self.at.across()).wait_recv()

    def start(self):
        at = self.at
        for half in range(2):
            self.go(self.own(half), at.s, half, self.over_x.at[half], at.across())
            for step in range(1, at.ys):
                target = at.column(at.beside(step))
                self.go(self.own(1 - half), at.s, 1 - half, self.over_y.at[step, half], target)

    def relay(self):
        at = self.at
        other = at.y * 2 + 1 - at.x
        self.wait(other, 0)
        for step in range(1, at.ys):
            self.go(self.view(other, 0), other, 0, self.over_y.at[step, 2], at.column(at.beside(step)))
        for step in range(1, at.ys):
            s = at.beside(step) * 2 + at.x
            self.wait(s, 1)
            self.go(self.view(s, 1), s, 1, self.over_x.at[1 + step], at.across())

    def finish(self):
        at = self.at
        self.wait(at.y * 2 + 1 - at.x, 1)
        for step in range(1, at.ys):
            y = at.beside(step)
            self.wait(y * 2 + at.x, 0)
            self.wait(y * 2 + 1 - at.x, 0)
            self.wait(y * 2 + 1 - at.x, 1)
        for copy in self.sent:
            copy.wait_send()


class SquareSum:
    @staticmethod
    def scratch(seq, half_shape):
        ys = seq // 2
        return [
            pltpu.VMEM((ys,) + half_shape, jnp.bfloat16),
            pltpu.VMEM((ys, 2) + half_shape, jnp.bfloat16),
            pltpu.VMEM((ys,) + half_shape, jnp.bfloat16),
            pltpu.VMEM(half_shape, jnp.bfloat16),
            pltpu.VMEM((ys,) + half_shape, jnp.bfloat16),
            pltpu.VMEM(half_shape, jnp.bfloat16),
            pltpu.SemaphoreType.DMA((ys, 2, 2)),
            pltpu.SemaphoreType.DMA((ys, 3, 2)),
        ]

    def __init__(self, at, part, scratch):
        self.at, self.part = at, part
        self.from_x, self.from_y, self.last_y, self.last_x, self.sum_y, self.sum_x, self.xs, self.yss = scratch
        self.sent = []

    def go(self, source, target, leaving, arriving, device):
        copy = send(source, target, leaving, arriving, device)
        copy.start()
        self.sent.append(copy)

    def wait(self, slot, leaving, arriving):
        send(slot, slot, leaving, arriving, self.at.across()).wait_recv()

    def start(self):
        at = self.at
        for y in range(at.ys):
            self.go(
                self.part(y * 2 + 1 - at.x, 0),
                self.from_x.at[y],
                self.xs.at[y, 0, 0],
                self.xs.at[y, 0, 1],
                at.across(),
            )
        for step in range(1, at.ys):
            y = at.beside(step)
            for x in range(2):
                self.go(
                    self.part(y * 2 + x, 1),
                    self.from_y.at[at.y, x],
                    self.yss.at[step, x, 0],
                    self.yss.at[at.y, x, 1],
                    at.column(y),
                )

    def relay(self):
        at = self.at
        for step in range(1, at.ys):
            y = at.beside(step)
            self.wait(self.from_x.at[y], self.xs.at[y, 0, 0], self.xs.at[y, 0, 1])
            add_into(self.sum_y.at[y], [self.part(y * 2 + at.x, 0), self.from_x.at[y]])
            self.go(
                self.sum_y.at[y],
                self.last_y.at[at.y],
                self.yss.at[step, 2, 0],
                self.yss.at[at.y, 2, 1],
                at.column(y),
            )
        terms = []
        for step in range(1, at.ys):
            y = at.beside(step)
            for x in range(2):
                self.wait(self.from_y.at[y, x], self.yss.at[step, x, 0], self.yss.at[y, x, 1])
            terms.append(self.from_y.at[y, 1 - at.x])
        add_into(self.sum_x, [self.part(at.y * 2 + 1 - at.x, 1)] + terms)
        self.go(self.sum_x, self.last_x, self.xs.at[0, 1, 0], self.xs.at[0, 1, 1], at.across())

    def finish(self, total):
        at = self.at
        self.wait(self.from_x.at[at.y], self.xs.at[0, 0, 0], self.xs.at[at.y, 0, 1])
        terms = [self.part(at.s, 0), self.from_x.at[at.y]]
        for step in range(1, at.ys):
            y = at.beside(step)
            self.wait(self.last_y.at[y], self.yss.at[step, 2, 0], self.yss.at[y, 2, 1])
            terms.append(self.last_y.at[y])
        add_into(total(0), terms)
        self.wait(self.last_x, self.xs.at[0, 1, 0], self.xs.at[0, 1, 1])
        terms = [self.part(at.s, 1), self.last_x]
        for step in range(1, at.ys):
            terms.append(self.from_y.at[at.beside(step), at.x])
        add_into(total(1), terms)
        for copy in self.sent:
            copy.wait_send()


class LineGather:
    @staticmethod
    def semaphores(wt):
        return [pltpu.SemaphoreType.DMA((5, wt // 2))]

    def __init__(self, at, view, sems):
        self.at, self.view, self.sems = at, view, sems[0]

    def up(self, z, source=None):
        slot = self.view(z * 2 + self.at.c)
        source = slot if source is None else source
        return send(source, slot, self.sems.at[0, z], self.sems.at[3, z], self.at.level(self.at.z + 1))

    def down(self, z, source=None):
        slot = self.view(z * 2 + self.at.c)
        source = slot if source is None else source
        return send(source, slot, self.sems.at[1, z], self.sems.at[3, z], self.at.level(self.at.z - 1))

    def over(self, z, source=None):
        slot = self.view(z * 2 + self.at.c)
        source = slot if source is None else source
        return send(source, slot, self.sems.at[2, z], self.sems.at[4, z], self.at.partner())

    def start(self, source=None):
        at = self.at

        @pl.when(at.z + 1 < at.zs)
        def _():
            self.up(at.z, source).start()

        @pl.when(at.z > 0)
        def _():
            self.down(at.z, source).start()

        self.over(at.z, source).start()

    def step(self, index):
        at = self.at
        below, above = at.z - 1 - index, at.z + 1 + index

        @pl.when(below >= 0)
        def _():
            self.up(below).wait_recv()

            @pl.when(at.z + 1 < at.zs)
            def _():
                self.up(below).start()

            self.over(below).start()

        @pl.when(above < at.zs)
        def _():
            self.down(above).wait_recv()

            @pl.when(at.z > 0)
            def _():
                self.down(above).start()

            self.over(above).start()

    def wait_over(self, z):
        slot = self.view(z * 2 + 1 - self.at.c)
        send(slot, slot, self.sems.at[2, z], self.sems.at[4, z], self.at.partner()).wait_recv()

    def finish(self):
        for z in range(self.at.zs):
            self.wait_over(z)
        self.sent()

    def sent(self):
        at = self.at
        for z in range(at.zs):

            @pl.when((at.z >= z) & (at.z + 1 < at.zs))
            def _():
                self.up(z).wait_send()

            @pl.when((at.z <= z) & (at.z > 0))
            def _():
                self.down(z).wait_send()

            self.over(z).wait_send()


class LineSum:
    @staticmethod
    def scratch(wt, shape):
        zs = wt // 2
        return [
            pltpu.VMEM((zs,) + shape, jnp.bfloat16),
            pltpu.VMEM((zs,) + shape, jnp.bfloat16),
            pltpu.VMEM((zs,) + shape, jnp.bfloat16),
            pltpu.VMEM((zs,) + shape, jnp.bfloat16),
            pltpu.SemaphoreType.DMA((6, zs)),
        ]

    def __init__(self, at, part, scratch):
        self.at, self.part = at, part
        self.pair, self.held, self.below, self.above, self.sems = scratch

    def over(self, z):
        return send(
            self.part(z * 2 + 1 - self.at.c),
            self.pair.at[z],
            self.sems.at[0, z],
            self.sems.at[1, z],
            self.at.partner(),
        )

    def up(self, z):
        return send(
            self.held.at[z], self.below.at[z], self.sems.at[2, z], self.sems.at[3, z], self.at.level(self.at.z + 1)
        )

    def down(self, z):
        return send(
            self.held.at[z], self.above.at[z], self.sems.at[4, z], self.sems.at[5, z], self.at.level(self.at.z - 1)
        )

    def start(self):
        zs = self.at.zs
        for index in range(zs // 2):
            self.over(zs - 1 - index).start()
            self.over(index).start()

    def paired(self, z):
        self.over(z).wait_recv()
        return [self.part(z * 2 + self.at.c), self.pair.at[z]]

    def step(self, index):
        at = self.at
        high, low = at.zs - 1 - index, index

        @pl.when(at.z < high)
        def _():
            terms = self.paired(high)

            @pl.when(at.z == 0)
            def _():
                add_into(self.held.at[high], terms)

            @pl.when(at.z > 0)
            def _():
                self.up(high).wait_recv()
                add_into(self.held.at[high], terms + [self.below.at[high]])

            self.up(high).start()

        @pl.when(at.z > low)
        def _():
            terms = self.paired(low)

            @pl.when(at.z == at.zs - 1)
            def _():
                add_into(self.held.at[low], terms)

            @pl.when(at.z < at.zs - 1)
            def _():
                self.down(low).wait_recv()
                add_into(self.held.at[low], terms + [self.above.at[low]])

            self.down(low).start()

    def finish(self, total):
        at = self.at
        terms = self.paired(at.z)

        @pl.when(at.z == 0)
        def _():
            self.down(0).wait_recv()
            add_into(total, terms + [self.above.at[0]])

        @pl.when(at.z == at.zs - 1)
        def _():
            self.up(at.zs - 1).wait_recv()
            add_into(total, terms + [self.below.at[at.zs - 1]])

        @pl.when((at.z > 0) & (at.z < at.zs - 1))
        def _():
            self.up(at.z).wait_recv()
            self.down(at.z).wait_recv()
            add_into(total, terms + [self.below.at[at.z], self.above.at[at.z]])

        for z in range(at.zs):

            @pl.when(at.z < z)
            def _():
                self.up(z).wait_send()

            @pl.when(at.z > z)
            def _():
                self.down(z).wait_send()

            self.over(z).wait_send()


def remote_call(kernel, name, number, outs, scratch, *operands, in_specs=None, out_specs=None):
    return pl.pallas_call(
        kernel,
        name=name,
        out_shape=outs,
        in_specs=[VMEM] * len(operands) if in_specs is None else in_specs,
        out_specs=jax.tree.map(lambda _: VMEM, outs) if out_specs is None else out_specs,
        scratch_shapes=scratch,
        compiler_params=pltpu.CompilerParams(
            collective_id=number, has_side_effects=True, vmem_limit_bytes=VMEM_LIMIT
        ),
    )(*operands)


def gather_start(tokens, qkv_rows, out_rows, gains):
    seq, wt = lax.axis_size("seq"), lax.axis_size("wt")
    count, width = tokens.shape
    parts, rows, columns = qkv_rows.shape

    def kernel(x_ref, qkv_ref, out_ref, gain_ref, xs, qkvs, outs, gains_out, *scratch):
        at = Place(seq, wt)
        x_sems, scratch = scratch[:3], scratch[3:]
        line_sems, scratch = [scratch[index : index + 1] for index in range(3)], scratch[3:]
        swap_q, swap_g, local = scratch
        at.meet(True, True)
        half = count // 2
        gather_x = SquareGather(
            at,
            lambda s, h: xs.at[pl.ds(pl.multiple_of(s * count + h * half, half), half)],
            lambda h: x_ref.at[pl.ds(h * half, half)],
            x_sems,
        )
        gather_q = LineGather(at, lambda w: qkvs.at[:, w], line_sems[0])
        gather_g = LineGather(at, lambda w: gains_out.at[:, w], line_sems[1])
        gather_o = LineGather(at, lambda w: outs.at[w], line_sems[2])
        swaps = []
        for step in range(1, seq):
            to = lax.rem(at.s + step, seq)
            swaps.append(
                send(gain_ref, gains_out.at[at.s, at.w], swap_g.at[step, 0], swap_g.at[at.s, 1], (to, at.w))
            )
            swaps.append(
                send(qkv_ref.at[to], qkvs.at[at.s, at.w], swap_q.at[step, 0], swap_q.at[at.s, 1], (to, at.w))
            )
        for copy in swaps:
            copy.start()
        gather_x.start()
        own = [
            pltpu.make_async_copy(qkv_ref.at[at.s], qkvs.at[at.s, at.w], local.at[0]),
            pltpu.make_async_copy(gain_ref, gains_out.at[at.s, at.w], local.at[1]),
            pltpu.make_async_copy(out_ref, outs.at[at.w], local.at[2]),
            pltpu.make_async_copy(x_ref, xs.at[pl.ds(pl.multiple_of(at.s * count, count), count)], local.at[3]),
        ]
        for copy in own:
            copy.start()
        for copy in own:
            copy.wait()
        for step in range(1, seq):
            s = lax.rem(at.s + step, seq)
            slot = gains_out.at[s, at.w]
            send(slot, slot, swap_g.at[step, 0], swap_g.at[s, 1], at.across()).wait_recv()
            slot = qkvs.at[s, at.w]
            send(slot, slot, swap_q.at[step, 0], swap_q.at[s, 1], at.across()).wait_recv()
        gather_g.start()
        gather_q.start()
        gather_o.start()
        gather_x.relay()
        for index in range(at.zs - 1):
            gather_g.step(index)
            gather_q.step(index)
            gather_o.step(index)
        gather_x.finish()
        gather_g.finish()
        gather_q.finish()
        gather_o.finish()
        for copy in swaps:
            copy.wait_send()

    return remote_call(
        kernel,
        "gather_start",
        0,
        [
            jax.ShapeDtypeStruct((seq * count, width), tokens.dtype),
            jax.ShapeDtypeStruct((seq, wt, rows, columns), qkv_rows.dtype),
            jax.ShapeDtypeStruct((wt,) + out_rows.shape, out_rows.dtype),
            jax.ShapeDtypeStruct((seq, wt) + gains.shape, gains.dtype),
        ],
        SquareGather.semaphores(seq)
        + LineGather.semaphores(wt) * 3
        + [
            pltpu.SemaphoreType.DMA((seq, 2)),
            pltpu.SemaphoreType.DMA((seq, 2)),
            pltpu.SemaphoreType.DMA((4,)),
        ],
        tokens,
        qkv_rows,
        out_rows,
        gains,
    )


def square_sum(parts, name, number):
    seq, wt = lax.axis_size("seq"), lax.axis_size("wt")
    half_shape = parts.shape[2:]

    def kernel(parts_ref, total_ref, *scratch):
        at = Place(seq, wt)
        at.meet(True, False)
        work = SquareSum(at, lambda s, h: parts_ref.at[s, h], scratch)
        work.start()
        work.relay()
        work.finish(lambda h: total_ref.at[h])

    return remote_call(
        kernel,
        name,
        number,
        jax.ShapeDtypeStruct((2,) + half_shape, jnp.float32),
        SquareSum.scratch(seq, half_shape),
        parts,
    )


class LinePieces:
    @staticmethod
    def scratch(wt, shape, pieces):
        zs = wt // 2
        return [pltpu.VMEM((zs,) + shape, jnp.bfloat16)] * 3 + [pltpu.SemaphoreType.DMA((6, zs, pieces))]

    def __init__(self, at, part, scratch):
        self.at, self.part = at, part
        self.pair, self.below, self.above, self.sems = scratch
        self.pieces = self.sems.shape[2]
        self.width = self.pair.shape[2] // self.pieces

    def cut(self, ref, piece):
        return ref.at[:, pl.ds(pl.multiple_of(piece * self.width, self.width), self.width)]

    def own(self, z, piece):
        return self.cut(self.part(z * 2 + self.at.c), piece)

    def over(self, z, piece):
        return send(
            self.cut(self.part(z * 2 + 1 - self.at.c), piece),
            self.cut(self.pair.at[z], piece),
            self.sems.at[0, z, piece],
            self.sems.at[1, z, piece],
            self.at.partner(),
        )

    def up(self, z, piece):
        return send(
            self.own(z, piece),
            self.cut(self.below.at[z], piece),
            self.sems.at[2, z, piece],
            self.sems.at[3, z, piece],
            self.at.level(self.at.z + 1),
        )

    def down(self, z, piece):
        return send(
            self.own(z, piece),
            self.cut(self.above.at[z], piece),
            self.sems.at[4, z, piece],
            self.sems.at[5, z, piece],
            self.at.level(self.at.z - 1),
        )

    def terms(self, z, piece):
        self.over(z, piece).wait_recv()
        return [self.own(z, piece), self.cut(self.pair.at[z], piece)]

    def ends(self, z, piece):
        at = self.at

        @pl.when((at.z == 0) & (z > 0))
        def _():
            add_into(self.own(z, piece), self.terms(z, piece))
            self.up(z, piece).start()

        @pl.when((at.z == at.zs - 1) & (z < at.zs - 1))
        def _():
            add_into(self.own(z, piece), self.terms(z, piece))
            self.down(z, piece).start()

    def pass_on(self, fill=None):
        at = self.at
        upper = at.z * 2 >= at.zs
        for index in range(1, at.zs):
            high, low = index, at.zs - 1 - index

            def lower(piece, when):
                @pl.when((at.z > low) & (at.z < at.zs - 1) & when)
                def _():
                    terms = self.terms(low, piece)
                    self.down(low, piece).wait_recv()
                    add_into(self.own(low, piece), terms + [self.cut(self.above.at[low], piece)])
                    self.down(low, piece).start()

            def step(piece, carry):
                lower(piece, upper)

                @pl.when((at.z < high) & (at.z > 0))
                def _():
                    terms = self.terms(high, piece)
                    self.up(high, piece).wait_recv()
                    add_into(self.own(high, piece), terms + [self.cut(self.below.at[high], piece)])
                    self.up(high, piece).start()

                lower(piece, jnp.logical_not(upper))
                if fill is not None and index == at.zs - 1:
                    fill(piece)
                return carry

            lax.fori_loop(0, self.pieces, step, 0)

    def finish(self, total, fill=None):
        at = self.at

        def step(piece, carry):
            if fill is not None:
                fill(self.pieces + piece)
            terms = self.terms(at.z, piece)
            below, above = self.cut(self.below.at[at.z], piece), self.cut(self.above.at[at.z], piece)

            @pl.when(at.z == 0)
            def _():
                self.down(at.z, piece).wait_recv()
                add_into(self.cut(total, piece), terms + [above])

            @pl.when(at.z == at.zs - 1)
            def _():
                self.up(at.z, piece).wait_recv()
                add_into(self.cut(total, piece), terms + [below])

            @pl.when((at.z > 0) & (at.z < at.zs - 1))
            def _():
                self.up(at.z, piece).wait_recv()
                self.down(at.z, piece).wait_recv()
                add_into(self.cut(total, piece), terms + [below, above])

            for z in range(at.zs):

                @pl.when(at.z < z)
                def _():
                    self.up(z, piece).wait_send()

                @pl.when(at.z > z)
                def _():
                    self.down(z, piece).wait_send()

                self.over(z, piece).wait_send()
            return carry

        lax.fori_loop(0, self.pieces, step, 0)


class SquareTerms:
    @staticmethod
    def semaphores(seq):
        return [pltpu.SemaphoreType.DMA((seq // 2, 2)), pltpu.SemaphoreType.DMA((seq // 2, 2, 2))]

    @staticmethod
    def scratch(seq, half_shape):
        ys = seq // 2
        return [
            pltpu.VMEM((ys,) + half_shape, jnp.bfloat16),
            pltpu.VMEM((ys,) + half_shape, jnp.bfloat16),
            pltpu.VMEM(half_shape, jnp.bfloat16),
            pltpu.VMEM(half_shape, jnp.bfloat16),
            pltpu.SemaphoreType.DMA((ys + 1, 2)),
        ]

    def __init__(self, at, terms, from_x, from_y, sems=None, scratch=None):
        self.at, self.terms, self.from_x, self.from_y = at, terms, from_x, from_y
        if sems is not None:
            self.xs, self.ys = sems
        if scratch is not None:
            self.sum_y, self.last_y, self.sum_x, self.last_x, self.last = scratch

    def first_x(self, y):
        at = self.at
        return send(
            self.terms(y * 2 + 1 - at.x, 0), self.from_x.at[y], self.xs.at[y, 0], self.xs.at[y, 1], at.across()
        )

    def first_y(self, step, x):
        at = self.at
        y = at.beside(step)
        return send(
            self.terms(y * 2 + x, 1),
            self.from_y.at[at.y, x],
            self.ys.at[step, x, 0],
            self.ys.at[at.y, x, 1],
            at.column(y),
        )

    def first_start(self):
        for y in range(self.at.ys):
            self.first_x(y).start()
        for step in range(1, self.at.ys):
            for x in range(2):
                self.first_y(step, x).start()

    def first_wait(self):
        at = self.at
        for y in range(at.ys):
            self.first_x(y).wait()
        for step in range(1, at.ys):
            y = at.beside(step)
            for x in range(2):
                self.first_y(step, x).wait_send()
                slot = self.from_y.at[y, x]
                send(slot, slot, self.ys.at[step, x, 0], self.ys.at[y, x, 1], at.across()).wait_recv()

    def second_sends(self):
        at = self.at
        copies = []
        for step in range(1, at.ys):
            y = at.beside(step)
            copies.append(
                send(self.sum_y.at[y], self.last_y.at[at.y], self.last.at[step, 0], self.last.at[at.y, 1], at.column(y))
            )
        copies.append(
            send(self.sum_x, self.last_x, self.last.at[at.ys, 0], self.last.at[at.ys, 1], at.across())
        )
        return copies

    def second_start(self, fetch, rooms):
        at = self.at
        for step in range(1, at.ys):
            y = at.beside(step)
            fetch([(self.terms(y * 2 + at.x, 0), rooms[0]), (self.from_x.at[y], rooms[1])])
            add_into(self.sum_y.at[y], [rooms[0], rooms[1]])
        fetch([(self.terms(at.y * 2 + 1 - at.x, 1), self.sum_x)])
        for step in range(1, at.ys):
            y = at.beside(step)
            fetch([(self.from_y.at[y, 1 - at.x], rooms[0])])
            add_into(self.sum_x, [self.sum_x, rooms[0]])

    def second_go(self):
        for copy in self.second_sends():
            copy.start()

    def finish(self, fetch, rooms, total):
        at = self.at
        fetch([(self.terms(at.s, 0), rooms[0]), (self.from_x.at[at.y], rooms[1])])
        terms = [rooms[0], rooms[1]]
        for step in range(1, at.ys):
            y = at.beside(step)
            slot = self.last_y.at[y]
            send(slot, slot, self.last.at[step, 0], self.last.at[y, 1], at.across()).wait_recv()
            terms.append(slot)
        add_into(total(0), terms)
        fetch([(self.terms(at.s, 1), rooms[0])])
        self.second_sends()[-1].wait_recv()
        add_into(total(1), [rooms[0], self.last_x])
        for step in range(1, at.ys):
            fetch([(self.from_y.at[at.beside(step), at.x], rooms[0])])
            add_into(total(1), [total(1), rooms[0]])
        for copy in self.second_sends():
            copy.wait_send()


def norm_back(rows, load, store, gain, terms):
    def step(index, carry):
        window = pl.ds(pl.multiple_of(index * 16, 16), 16)
        values, incoming, base = load(window)
        root = lax.rsqrt(jnp.mean(values * values, axis=-1, keepdims=True) + epsilon)
        scaled = incoming * gain
        share = jnp.mean(values * scaled, axis=-1, keepdims=True)
        store(window, base + root * scaled - values * (root * root * root * share))
        term = incoming * values * root
        terms[...] += term[:8] + term[8:]
        return carry

    lax.fori_loop(0, rows // 16, step, 0)


def exchange(
    at, shard, everyone, gather_sems, local, sums, first, second, total, ready, wait_for_ready, fill=None
):
    count = shard.shape[0]
    gather = LineGather(
        at, lambda w: everyone.at[pl.ds(pl.multiple_of(w * count, count), count)], gather_sems
    )
    gather.start(shard)
    own = pltpu.make_async_copy(
        shard, everyone.at[pl.ds(pl.multiple_of(at.w * count, count), count)], local
    )
    own.start()
    own.wait()
    ready[0]()
    last = 2 * (at.zs - 1)
    late = 3 if wait_for_ready else 0

    def turn(index, carry):
        fresh = index <= last
        place = jnp.where(fresh, index, jnp.where(index == last + 3, 0, index - last))
        far, side = lax.div(place + 1, 2), lax.rem(place, 2)
        z = at.z + jnp.where(side == 1, -far, far)
        valid = (z >= 0) & (z < at.zs)

        @pl.when(fresh & (side == 1))
        def _():
            gather.step(far - 1)

        @pl.when(fresh & valid)
        def _():
            gather.wait_over(z)
            first(z)

        if wait_for_ready:

            @pl.when(index == late)
            def _():
                ready[1]()

        @pl.when(valid & (index >= late))
        def _():
            def step(piece, inner):
                second(z, piece)
                sums.over(z, piece).start()

                @pl.when(piece > 0)
                def _():
                    sums.ends(z, piece - 1)

                return inner

            lax.fori_loop(0, sums.pieces, step, 0)
            sums.ends(z, sums.pieces - 1)

        return carry

    lax.fori_loop(0, last + 1 + late, turn, 0)
    sums.pass_on(fill)
    sums.finish(total, fill)
    gather.sent()


PIECES = 4


def feed_forward(normed, gate_up, down_shard):
    seq, wt = lax.axis_size("seq"), lax.axis_size("wt")
    count, width = normed.shape
    units = gate_up.shape[2]
    columns = down_shard.shape[1]
    tokens = wt * count
    zs = wt // 2
    half = units // 2

    def kernel(normed_ref, gate_up_ref, shard_ref, total_ref, normed_out, gate_out, up_out, active_out, down_out, *scratch):
        at = Place(seq, wt)
        everyone, gates, downs, gate_all, up_all, active_all, parts = scratch[:7]
        gather_sems, sum_scratch, square_sems, local, outgoing = (
            scratch[7:8],
            scratch[8:12],
            scratch[12:15],
            scratch[15],
            scratch[16],
        )
        load = pltpu.make_async_copy(gate_up_ref, gates, local.at[0])
        load.start()
        at.meet(True, True)
        weights = SquareGather(
            at,
            lambda s, h: downs.at[
                pl.ds(h * half, half), pl.ds(pl.multiple_of(s * columns, columns), columns)
            ],
            lambda h: shard_ref.at[pl.ds(h * half, half)],
            square_sems,
        )
        sums = LinePieces(
            at, lambda w: parts.at[pl.ds(pl.multiple_of(w * count, count), count)], sum_scratch
        )
        down_store = pltpu.make_async_copy(downs, down_out, local.at[2])

        def ready_first():
            weights.start()
            own = pltpu.make_async_copy(
                shard_ref, downs.at[:, pl.ds(pl.multiple_of(at.s * columns, columns), columns)], local.at[3]
            )
            own.start()
            own.wait()
            load.wait()

        def ready_later():
            weights.relay()
            weights.finish()
            down_store.start()

        def rows(z):
            return pl.ds(pl.multiple_of(z * 2 * count, 2 * count), 2 * count)

        def stores(z):
            return [
                pltpu.make_async_copy(source.at[rows(z)], target.at[rows(z)], outgoing.at[index, z])
                for index, (source, target) in enumerate(
                    ((everyone, normed_out), (gate_all, gate_out), (up_all, up_out), (active_all, active_out))
                )
            ]

        def first(z):
            here = everyone[rows(z), :]
            gate = jnp.dot(here, gates[0], preferred_element_type=jnp.float32)
            up = jnp.dot(here, gates[1], preferred_element_type=jnp.float32)
            gate_all[rows(z), :] = gate
            up_all[rows(z), :] = up
            active_all[rows(z), :] = gated_unit(gate, up).astype(jnp.bfloat16)
            for copy in stores(z):
                copy.start()

        def second(z, piece):
            window = pl.ds(pl.multiple_of(piece * sums.width, sums.width), sums.width)
            parts[rows(z), window] = jnp.dot(
                active_all[rows(z), :], downs[:, window], preferred_element_type=jnp.float32
            ).astype(jnp.bfloat16)

        exchange(
            at,
            normed_ref,
            everyone,
            gather_sems,
            local.at[1],
            sums,
            first,
            second,
            total_ref,
            (ready_first, ready_later),
            True,
        )
        down_store.wait()
        for z in range(zs):
            for copy in stores(z):
                copy.wait()

    return remote_call(
        kernel,
        "feed_forward",
        2,
        [
            jax.ShapeDtypeStruct((count, width), jnp.float32),
            jax.ShapeDtypeStruct((tokens, width), jnp.bfloat16),
            jax.ShapeDtypeStruct((tokens, units), jnp.float32),
            jax.ShapeDtypeStruct((tokens, units), jnp.float32),
            jax.ShapeDtypeStruct((tokens, units), jnp.bfloat16),
            jax.ShapeDtypeStruct((units, width), jnp.bfloat16),
        ],
        [
            pltpu.VMEM((tokens, width), jnp.bfloat16),
            pltpu.VMEM(gate_up.shape, jnp.bfloat16),
            pltpu.VMEM((units, width), jnp.bfloat16),
            pltpu.VMEM((tokens, units), jnp.float32),
            pltpu.VMEM((tokens, units), jnp.float32),
            pltpu.VMEM((tokens, units), jnp.bfloat16),
            pltpu.VMEM((tokens, width), jnp.bfloat16),
        ]
        + LineGather.semaphores(wt)
        + LinePieces.scratch(wt, (count, width), PIECES)
        + SquareGather.semaphores(seq)
        + [pltpu.SemaphoreType.DMA((4,)), pltpu.SemaphoreType.DMA((4, zs))],
        normed,
        gate_up,
        down_shard,
        in_specs=[VMEM, ANY, VMEM],
        out_specs=[VMEM] + [ANY] * 5,
    )


def feed_back(error, attended, gain, gate_up, down, gate, up, active, normed):
    seq, wt = lax.axis_size("seq"), lax.axis_size("wt")
    count, width = error.shape
    units = gate_up.shape[2]
    tokens = wt * count
    zs, ys = wt // 2, seq // 2
    block = width // seq
    gate_half, down_half = (block // 2, units), (units // 2, block)

    def kernel(*refs):
        (error_ref, attended_ref, gain_ref, gate_up_ref, down_ref, gate_ref, up_ref, active_ref, normed_ref), refs = (
            refs[:9],
            refs[9:],
        )
        (grad_ref, mix_ref, gain_terms), refs = refs[:3], refs[3:]
        (gate_out, up_out, down_out, gate_x, gate_y, down_x, down_y), refs = refs[:7], refs[7:]
        (low, everyone, gates, downs, gate_all, up_all, back_all, parts, actives, columns), refs = refs[:10], refs[10:]
        (gate_terms, up_terms, down_terms, total), refs = refs[:4], refs[4:]
        gather_sems, sum_scratch, gate_sems, down_sems, (local, outgoing) = (
            refs[:1],
            refs[1:5],
            refs[5:7],
            refs[7:9],
            refs[9:],
        )
        at = Place(seq, wt)
        loads = [
            pltpu.make_async_copy(source, target, local.at[index])
            for index, (source, target) in enumerate(
                (
                    (down_ref, downs),
                    (gate_ref, gate_all),
                    (up_ref, up_all),
                    (gate_up_ref, gates),
                    (active_ref, actives),
                )
            )
        ]
        for load in loads:
            load.start()
        at.meet(True, True)
        low[...] = error_ref[...].astype(jnp.bfloat16)
        sums = LinePieces(
            at, lambda w: parts.at[pl.ds(pl.multiple_of(w * count, count), count)], sum_scratch
        )
        gate_sum = SquareTerms(at, lambda s, h: gate_terms.at[s, h], gate_x, gate_y, gate_sems)
        down_sum = SquareTerms(at, lambda s, h: down_terms.at[s, h], down_x, down_y, down_sems)

        def place(index):
            step = lax.div(index, 2) + 1
            x = lax.rem(at.x + 1 + lax.rem(index, 2), 2)
            return step, x, at.beside(step) * 2 + x

        def column_load(index):
            s = place(index)[2]
            return pltpu.make_async_copy(
                normed_ref.at[:, pl.ds(pl.multiple_of(s * block, block), block)],
                columns.at[lax.rem(index, 2)],
                local.at[6 + lax.rem(index, 2)],
            )

        def leave(sum_, index):
            step, x, s = place(index)

            @pl.when(x != at.x)
            def _():
                sum_.first_x(lax.div(s, 2)).start()

            @pl.when(step < ys)
            def _():
                sum_.first_y(step, x).start()

        def down_job(index):
            s = place(index)[2]
            term = contract_first(
                actives[...], everyone[:, pl.ds(pl.multiple_of(s * block, block), block)]
            ).astype(jnp.bfloat16)
            down_terms[s, 0] = term[: units // 2]
            down_terms[s, 1] = term[units // 2 :]
            leave(down_sum, index)

        def gate_job(index):
            s = place(index)[2]
            column_load(index).wait()
            here = columns.at[lax.rem(index, 2)]
            for number, terms in enumerate((gate_terms, up_terms)):
                term = contract_first(here[...], back_all[number]).astype(jnp.bfloat16)
                terms[s, 0] = term[: block // 2]
                terms[s, 1] = term[block // 2 :]

            @pl.when(index + 2 < seq)
            def _():
                column_load(index + 2).start()

            leave(gate_sum, index)

        def fill(slot):
            def step(index, carry):
                job = slot * (seq // 4) + index

                @pl.when(job < seq)
                def _():
                    down_job(job)

                @pl.when(job >= seq)
                def _():
                    gate_job(job - seq)

                return carry

            lax.fori_loop(0, seq // 4, step, 0)

        def ready_first():
            column_load(0).start()
            column_load(1).start()
            for load in loads:
                load.wait()

        def rows(z):
            return pl.ds(pl.multiple_of(z * 2 * count, 2 * count), 2 * count)

        def first(z):
            active_back = contract_last(everyone[rows(z), :], downs[...])
            gate_here, up_here = gate_all[rows(z), :], up_all[rows(z), :]
            share = jax.nn.sigmoid(gate_here)
            back_all[0, rows(z), :] = (
                active_back * up_here * share * (1.0 + gate_here * (1.0 - share))
            ).astype(jnp.bfloat16)
            back_all[1, rows(z), :] = (active_back * gate_here * share).astype(jnp.bfloat16)

        def second(z, piece):
            window = pl.ds(pl.multiple_of(piece * sums.width, sums.width), sums.width)
            parts[rows(z), window] = (
                contract_last(back_all[0, rows(z), :], gates[0, window, :])
                + contract_last(back_all[1, rows(z), :], gates[1, window, :])
            ).astype(jnp.bfloat16)

        exchange(
            at,
            low,
            everyone,
            gather_sems,
            local.at[5],
            sums,
            first,
            second,
            total,
            (ready_first,),
            False,
            fill,
        )
        stores = [
            pltpu.make_async_copy(source, target, outgoing.at[index])
            for index, (source, target) in enumerate(
                ((gate_terms, gate_out), (up_terms, up_out), (down_terms, down_out))
            )
        ]
        for copy in stores:
            copy.start()
        gain_terms[...] = jnp.zeros_like(gain_terms)

        def load_rows(window):
            return attended_ref[window, :], total[window, :], error_ref[window, :]

        def store_rows(window, value):
            grad_ref[window, :] = value
            mix_ref[window, :] = value.astype(jnp.bfloat16)

        norm_back(count, load_rows, store_rows, gain_ref[...], gain_terms)
        for copy in stores:
            copy.wait()
        gate_sum.first_wait()
        down_sum.first_wait()

    def terms_of(half):
        return jax.ShapeDtypeStruct((seq, 2) + half, jnp.bfloat16)

    def first_of(half):
        return [
            jax.ShapeDtypeStruct((ys,) + half, jnp.bfloat16),
            jax.ShapeDtypeStruct((ys, 2) + half, jnp.bfloat16),
        ]

    return remote_call(
        kernel,
        "feed_back",
        3,
        [
            jax.ShapeDtypeStruct((count, width), jnp.float32),
            jax.ShapeDtypeStruct((count, width), jnp.bfloat16),
            jax.ShapeDtypeStruct((8, width), jnp.float32),
            terms_of(gate_half),
            terms_of(gate_half),
            terms_of(down_half),
        ]
        + first_of(gate_half)
        + first_of(down_half),
        [
            pltpu.VMEM((count, width), jnp.bfloat16),
            pltpu.VMEM((tokens, width), jnp.bfloat16),
            pltpu.VMEM(gate_up.shape, jnp.bfloat16),
            pltpu.VMEM((units, width), jnp.bfloat16),
            pltpu.VMEM((tokens, units), jnp.float32),
            pltpu.VMEM((tokens, units), jnp.float32),
            pltpu.VMEM((2, tokens, units), jnp.bfloat16),
            pltpu.VMEM((tokens, width), jnp.bfloat16),
            pltpu.VMEM((tokens, units), jnp.bfloat16),
            pltpu.VMEM((2, tokens, block), jnp.bfloat16),
            pltpu.VMEM((seq, 2) + gate_half, jnp.bfloat16),
            pltpu.VMEM((seq, 2) + gate_half, jnp.bfloat16),
            pltpu.VMEM((seq, 2) + down_half, jnp.bfloat16),
            pltpu.VMEM((count, width), jnp.float32),
        ]
        + LineGather.semaphores(wt)
        + LinePieces.scratch(wt, (count, width), PIECES)
        + SquareTerms.semaphores(seq)
        + SquareTerms.semaphores(seq)
        + [pltpu.SemaphoreType.DMA((8,)), pltpu.SemaphoreType.DMA((3,))],
        error,
        attended,
        gain,
        gate_up,
        down,
        gate,
        up,
        active,
        normed,
        in_specs=[VMEM] * 3 + [ANY] * 6,
        out_specs=[VMEM] * 3 + [ANY] * 7,
    )


def mixer_back(
    mix_back,
    attended_grad,
    tokens,
    gain,
    out_rows,
    qkv_columns,
    hidden,
    projected,
    mixer,
    mixed_values,
    head_outputs,
    segments,
    marks,
    taps,
    order,
    gain_terms,
    energy,
    gate_parts,
    up_parts,
    down_parts,
):
    seq, wt = lax.axis_size("seq"), lax.axis_size("wt")
    zs, ys = wt // 2, seq // 2
    count, width = mix_back.shape
    length = count * seq
    heads = mixed_values.shape[0]
    qkv_width = qkv_columns.shape[1]
    value_width = heads * DV
    rank = width // (seq * wt)
    gate_half, down_half = gate_parts[0].shape[2:], down_parts[0].shape[2:]
    rows_at_once = 256
    segment_rows = segments.reshape(1, length)
    segment_columns = segments.reshape(length, 1)
    big = [out_rows, qkv_columns, hidden, projected, mixer, mixed_values, head_outputs]
    small = [mix_back, attended_grad, tokens, gain, segment_rows, segment_columns, marks, taps, order, gain_terms, energy]
    far = list(gate_parts) + list(down_parts) + list(up_parts)

    def kernel(*refs):
        big_refs, refs = refs[: len(big)], refs[len(big) :]
        small_refs, refs = refs[: len(small)], refs[len(small) :]
        (gate_t, gate_x, gate_y, down_t, down_x, down_y, up_t), refs = refs[: len(far)], refs[len(far) :]
        (grad_out, sums_out, gate_out, up_out, down_out, qkv_out, w_out_out, up_x, up_y), refs = refs[:9], refs[9:]
        (w_out_v, w_qkv_v, hidden_v, projected_v, mixer_v, values_v, outputs_v), refs = refs[:7], refs[7:]
        (mix_all, mixer_grad, sorted_v, query_acc, key_acc, value_acc, back_sorted, back_v), refs = refs[:8], refs[8:]
        (hidden_parts, qkv_parts, out_parts, hidden_total, gain_acc, spread, taps_acc), refs = refs[:7], refs[7:]
        (room_gate0, room_gate1, room_down0, room_down1, qkv_sum, first, middle, last), refs = refs[:8], refs[8:]
        hidden_scratch, refs = refs[:8], refs[8:]
        qkv_scratch, out_scratch, refs = refs[:5], refs[5:10], refs[10:]
        gate_scratch, down_scratch, up_scratch, refs = refs[:5], refs[5:10], refs[10:15], refs[15:]
        gather_sems, up_sems, refs = refs[:3], refs[3:5], refs[5:]
        local, swap, first_sems, last_sems = refs
        (
            mix_ref,
            grad_ref,
            token_ref,
            gain_ref,
            segment_row,
            segment_column,
            mark_ref,
            tap_ref,
            order_ref,
            gain_two,
            energy_ref,
        ) = small_refs
        at = Place(seq, wt)
        loads = [
            pltpu.make_async_copy(source, target, local.at[4 + index])
            for index, (source, target) in enumerate(
                zip(big_refs, (w_out_v, w_qkv_v, hidden_v, projected_v, mixer_v, values_v, outputs_v))
            )
        ]
        for load in loads:
            load.start()
        at.meet(True, True)
        half = count // 2
        gather = SquareGather(
            at,
            lambda s, h: mix_all.at[pl.ds(pl.multiple_of(s * count + h * half, half), half)],
            lambda h: mix_ref.at[pl.ds(h * half, half)],
            gather_sems,
        )
        gather.start()
        own = pltpu.make_async_copy(
            mix_ref, mix_all.at[pl.ds(pl.multiple_of(at.s * count, count), count)], local.at[3]
        )
        own.start()

        def fetch(pairs):
            copies = [
                pltpu.make_async_copy(source, target, local.at[index])
                for index, (source, target) in enumerate(pairs)
            ]
            for copy in copies:
                copy.start()
            for copy in copies:
                copy.wait()

        gate_sum = SquareTerms(at, lambda s, h: gate_t.at[s, h], gate_x, gate_y, None, gate_scratch)
        down_sum = SquareTerms(at, lambda s, h: down_t.at[s, h], down_x, down_y, None, down_scratch)
        up_sum = SquareTerms(at, lambda s, h: up_t.at[s, h], up_x, up_y, up_sems, up_scratch)
        gate_rooms, down_rooms = (room_gate0, room_gate1), (room_down0, room_down1)
        gate_sum.second_start(fetch, gate_rooms)
        down_sum.second_start(fetch, down_rooms)
        own.wait()
        for load in loads:
            load.wait()
        sorted_v[...] = jnp.dot(
            projected_v[...], order_ref[...], preferred_element_type=jnp.float32
        ).astype(jnp.bfloat16)
        query_acc[...] = jnp.zeros_like(query_acc)
        key_acc[...] = jnp.zeros_like(key_acc)
        value_acc[...] = jnp.zeros_like(value_acc)
        gather.relay()
        gather.finish()
        gate_sum.second_go()
        down_sum.second_go()
        up_sum.first_start()
        mixer_grad[...] = contract_last(mix_all[...], w_out_v[...]).astype(jnp.bfloat16)
        out_sum = LineSum(at, lambda w: out_parts.at[w], out_scratch)
        out_rank = out_parts.shape[1]
        out_block = 512 if value_width % 512 == 0 else value_width

        def out_job(index, carry):
            window = pl.ds(pl.multiple_of(index * 512, 512), 512)
            term = contract_first(mixer_v[...], mix_all[:, window]).astype(jnp.bfloat16)
            for w in range(wt):
                out_parts[w, :, window] = term[w * out_rank : (w + 1) * out_rank]
            return carry

        lax.fori_loop(0, width // 512, out_job, 0)
        out_sum.start()

        steps = length // rows_at_once
        lanes = lax.broadcasted_iota(jnp.int32, (1, 128), 1)

        def attend(index, carry):
            head, start = lax.div(index, steps), lax.rem(index, steps) * rows_at_once
            rows = pl.ds(pl.multiple_of(start, rows_at_once), rows_at_once)
            columns = pl.ds(pl.multiple_of(head * DV, DV), DV)
            mine = ((lanes >= head * FEAT) & (lanes < head * FEAT + FEAT)).astype(jnp.float32)
            queries = sorted_v[rows, value_width : value_width + 128] * mine.astype(jnp.bfloat16)
            keys = sorted_v[:, value_width + 128 :]
            scores = contract_last(queries, keys) * 0.25
            places = start + lax.broadcasted_iota(jnp.int32, scores.shape, 0)
            allowed = (segment_column[rows, :] == segment_row[...]) & (
                places >= lax.broadcasted_iota(jnp.int32, scores.shape, 1)
            )
            kernel_values = jnp.where(allowed, 1.0 + scores + 0.5 * scores * scores, 0.0)
            denominator = jnp.sum(kernel_values, axis=1, keepdims=True)
            incoming = mixer_grad[rows, columns].astype(jnp.float32)
            numerator_back = (incoming / denominator).astype(jnp.bfloat16)
            denominator_back = (
                -jnp.sum(incoming * outputs_v[head, rows, :], axis=1, keepdims=True) / denominator
            )
            weight_back = contract_last(numerator_back, values_v[head])
            kernel_back = jnp.where(allowed, weight_back + denominator_back, 0.0)
            dots_back = (0.25 * kernel_back * (1.0 + scores)).astype(jnp.bfloat16)
            query_acc[rows, :] += jnp.dot(dots_back, keys, preferred_element_type=jnp.float32) * mine
            key_acc[...] += contract_first(dots_back, queries)
            value_acc[:, columns] += contract_first(kernel_values.astype(jnp.bfloat16), numerator_back)
            return carry

        lax.fori_loop(0, heads * steps, attend, 0)
        taps_acc[...] = jnp.zeros_like(taps_acc)

        def convolve(head, carry):
            columns = pl.ds(pl.multiple_of(head * DV, DV), DV)
            mixed_back = value_acc[:, columns]
            raw = sorted_v[:, columns].astype(jnp.float32)
            raw_back = tap_ref[0:1, columns] * mixed_back
            taps_acc[3:4, columns] = jnp.sum(mixed_back * raw, axis=0, keepdims=True)
            for tap in range(1, KCONV):
                masked = mixed_back * mark_ref[:, tap : tap + 1]
                taps_acc[3 + tap : 4 + tap, columns] = jnp.sum(
                    masked * pltpu.roll(raw, tap, 0), axis=0, keepdims=True
                )
                raw_back = raw_back + tap_ref[tap : tap + 1, columns] * pltpu.roll(masked, length - tap, 0)
            back_sorted[:, columns] = raw_back.astype(jnp.bfloat16)
            return carry

        lax.fori_loop(0, heads, convolve, 0)
        back_sorted[:, value_width : value_width + 128] = query_acc[...].astype(jnp.bfloat16)
        back_sorted[:, value_width + 128 :] = key_acc[...].astype(jnp.bfloat16)
        back_v[...] = contract_last(back_sorted[...], order_ref[...]).astype(jnp.bfloat16)
        hidden_sum = SquareSum(at, lambda s, h: hidden_parts.at[s, h], hidden_scratch)

        def hidden_job(index, carry):
            window = pl.ds(pl.multiple_of(index * 512, 512), 512)
            term = contract_last(back_v[...], w_qkv_v[window, :]).astype(jnp.bfloat16)
            for s in range(seq):
                for h in range(2):
                    begin = s * count + h * half
                    hidden_parts[s, h, :, window] = term[begin : begin + half]
            return carry

        lax.fori_loop(0, width // 512, hidden_job, 0)
        hidden_sum.start()
        qkv_sums = LineSum(at, lambda w: qkv_parts.at[:, w], qkv_scratch)
        qkv_rank = qkv_parts.shape[2]

        def qkv_job(s, carry):
            block = wt * qkv_rank
            window = pl.ds(pl.multiple_of(s * block, block), block)
            term = contract_first(hidden_v[:, window], back_v[...]).astype(jnp.bfloat16)
            for w in range(wt):
                qkv_parts[s, w] = term[w * qkv_rank : (w + 1) * qkv_rank]
            return carry

        lax.fori_loop(0, seq, qkv_job, 0)
        qkv_sums.start()
        hidden_sum.relay()
        for index in range(zs - 1):
            out_sum.step(index)
            qkv_sums.step(index)
        up_sum.first_wait()
        up_sum.second_start(fetch, gate_rooms)
        up_sum.second_go()
        hidden_sum.finish(lambda h: hidden_total.at[h])
        gain_acc[...] = jnp.zeros_like(gain_acc)
        for h in range(2):

            def shift(window):
                return pl.ds(pl.multiple_of(h * half + window.start, 16), 16)

            def load_rows(window):
                rows = shift(window)
                return token_ref[rows, :].astype(jnp.float32), hidden_total[h, window, :], grad_ref[rows, :]

            def store_rows(window, value):
                grad_out[shift(window), :] = value

            norm_back(half, load_rows, store_rows, gain_ref[...], gain_acc)
        spread[...] = jnp.zeros_like(spread)
        spread[0:1, :] = jnp.sum(gain_acc[...], axis=0, keepdims=True)
        spread[1:2, :] = jnp.sum(gain_two[...], axis=0, keepdims=True)
        spread[2:3, :] = jnp.broadcast_to(energy_ref[...], (1, width))
        copies = []
        for step in range(1, seq):
            to = lax.rem(at.s + step, seq)
            window = pl.ds(pl.multiple_of(to * value_width, value_width), value_width)
            copies.append(
                send(spread.at[:, window], first.at[at.s], first_sems.at[step, 0], first_sems.at[at.s, 1], (to, at.w))
            )
        for copy in copies:
            copy.start()
        qkv_sums.finish(qkv_sum)
        for step in range(1, seq):
            to = lax.rem(at.s + step, seq)
            copy = send(qkv_sum.at[to], qkv_out.at[at.s], swap.at[step, 0], swap.at[at.s, 1], (to, at.w))
            copy.start()
            copies.append(copy)
        add_into(qkv_out.at[at.s], [qkv_sum.at[at.s]])
        out_sum.finish(w_out_out)
        terms = [spread.at[:, pl.ds(pl.multiple_of(at.s * value_width, value_width), value_width)], taps_acc]
        for step in range(1, seq):
            s = lax.rem(at.s + step, seq)
            slot = first.at[s]
            send(slot, slot, first_sems.at[step, 0], first_sems.at[s, 1], at.across()).wait_recv()
            terms.append(slot)
        add_into(middle, terms)
        for step in range(1, wt):
            to = lax.rem(at.w + step, wt)
            copy = send(middle, last.at[at.w], last_sems.at[step, 0], last_sems.at[at.w, 1], (at.s, to))
            copy.start()
            copies.append(copy)
        gate_sum.finish(fetch, gate_rooms, lambda h: gate_out.at[h])
        down_sum.finish(fetch, down_rooms, lambda h: down_out.at[h])
        terms = [middle]
        for step in range(1, wt):
            w = lax.rem(at.w + step, wt)
            slot = last.at[w]
            send(slot, slot, last_sems.at[step, 0], last_sems.at[w, 1], at.partner()).wait_recv()
            terms.append(slot)
        add_into(sums_out, terms)
        for step in range(1, seq):
            s = lax.rem(at.s + step, seq)
            slot = qkv_out.at[s]
            send(slot, slot, swap.at[step, 0], swap.at[s, 1], at.across()).wait_recv()
        up_sum.finish(fetch, gate_rooms, lambda h: up_out.at[h])
        for copy in copies:
            copy.wait_send()

    out_rank, qkv_rank = value_width // wt, width // (seq * wt)
    f32, low = jnp.float32, jnp.bfloat16
    tile = (8, value_width)
    results = remote_call(
        kernel,
        "mixer_back",
        4,
        [
            jax.ShapeDtypeStruct((count, width), f32),
            jax.ShapeDtypeStruct(tile, f32),
            jax.ShapeDtypeStruct((2,) + gate_half, f32),
            jax.ShapeDtypeStruct((2,) + gate_half, f32),
            jax.ShapeDtypeStruct((2,) + down_half, f32),
            jax.ShapeDtypeStruct((seq, qkv_rank, qkv_width), f32),
            jax.ShapeDtypeStruct((out_rank, width), f32),
            jax.ShapeDtypeStruct((ys,) + gate_half, low),
            jax.ShapeDtypeStruct((ys, 2) + gate_half, low),
        ],
        [pltpu.VMEM(array.shape, array.dtype) for array in big]
        + [
            pltpu.VMEM((length, width), low),
            pltpu.VMEM((length, value_width), low),
            pltpu.VMEM((length, value_width + 256), low),
            pltpu.VMEM((length, 128), f32),
            pltpu.VMEM((length, 128), f32),
            pltpu.VMEM((length, value_width), f32),
            pltpu.VMEM((length, value_width + 256), low),
            pltpu.VMEM((length, qkv_width), low),
            pltpu.VMEM((seq, 2, count // 2, width), low),
            pltpu.VMEM((seq, wt, qkv_rank, qkv_width), low),
            pltpu.VMEM((wt, out_rank, width), low),
            pltpu.VMEM((2, count // 2, width), f32),
            pltpu.VMEM((8, width), f32),
            pltpu.VMEM((8, width), f32),
            pltpu.VMEM(tile, f32),
            pltpu.VMEM(gate_half, low),
            pltpu.VMEM(gate_half, low),
            pltpu.VMEM(down_half, low),
            pltpu.VMEM(down_half, low),
            pltpu.VMEM((seq, qkv_rank, qkv_width), f32),
            pltpu.VMEM((seq,) + tile, f32),
            pltpu.VMEM(tile, f32),
            pltpu.VMEM((wt,) + tile, f32),
        ]
        + SquareSum.scratch(seq, (count // 2, width))
        + LineSum.scratch(wt, (seq, qkv_rank, qkv_width))
        + LineSum.scratch(wt, (out_rank, width))
        + SquareTerms.scratch(seq, gate_half)
        + SquareTerms.scratch(seq, down_half)
        + SquareTerms.scratch(seq, gate_half)
        + SquareGather.semaphores(seq)
        + SquareTerms.semaphores(seq)
        + [
            pltpu.SemaphoreType.DMA((11,)),
            pltpu.SemaphoreType.DMA((seq, 2)),
            pltpu.SemaphoreType.DMA((seq, 2)),
            pltpu.SemaphoreType.DMA((wt, 2)),
        ],
        *big,
        *small,
        *far,
        in_specs=[ANY] * len(big) + [VMEM] * len(small) + [ANY] * len(far),
        out_specs=[VMEM] * 7 + [ANY] * 2,
    )
    return results[:7]


def column_order(heads):
    head_width = 2 * FEAT + DV
    column = jnp.arange(heads * head_width)
    head, place = column // head_width, column % head_width
    value_width = heads * DV
    target = jnp.where(
        place < FEAT,
        value_width + head * FEAT + place,
        jnp.where(place < 2 * FEAT, value_width + 128 + head * FEAT + place - FEAT, head * DV + place - 2 * FEAT),
    )
    return (target[:, None] == jnp.arange(value_width + 256)[None, :]).astype(jnp.bfloat16)


def rows_of_tile(values, row):
    pad = [(0, 0)] * (values.ndim - 1)
    return jnp.pad(values[..., None, :], pad + [(row, 7 - row), (0, 128 - values.shape[-1])])

def body(
    inputs,
    segment_ids,
    valid_lengths,
    teacher,
    w_qkv,
    conv_weight,
    w_out,
    norm_gain,
    w_gate_up,
    w_down,
    mlp_gain,
):
    seq_parts, wt_parts = lax.axis_size("seq"), lax.axis_size("wt")
    tok_count = inputs.shape[1]
    model_width = inputs.shape[2]
    length = tok_count * seq_parts
    block_rows = min(block_limit, length)
    head_count = H // seq_parts
    head_width = 2 * FEAT + DV
    qkv_width = head_count * head_width
    rows_low = inputs[0]
    rows_in = rows_low.astype(jnp.float32)
    gain_lanes = norm_gain.shape[0]
    gains = rows_of_tile(norm_gain.astype(jnp.float32), 0) + rows_of_tile(mlp_gain.astype(jnp.float32), 1)
    qkv_rows = w_qkv.reshape(w_qkv.shape[0], seq_parts, qkv_width).transpose(1, 0, 2)
    tokens_all, qkv_columns, out_rows, gains_all = gather_start(rows_low, qkv_rows, w_out, gains)
    qkv_columns = qkv_columns.reshape(model_width, qkv_width)
    out_rows = out_rows.reshape(head_count * DV, model_width)
    gain_first = gains_all[:, :, 0, :gain_lanes].reshape(model_width)
    gain_second = gains_all[:, :, 1, :gain_lanes].reshape(model_width)
    gate_up_part = lax.all_gather(w_gate_up, "seq", axis=1, tiled=True)
    hidden_low = rms_norm(tokens_all.astype(jnp.float32), gain_first).astype(jnp.bfloat16)
    projected = jnp.dot(hidden_low, qkv_columns, preferred_element_type=jnp.float32).astype(
        jnp.bfloat16
    )
    grouped = projected.reshape(length, head_count, head_width)
    head_queries = grouped[:, :, :FEAT].transpose(1, 2, 0)
    head_keys = grouped[:, :, FEAT : 2 * FEAT].transpose(1, 2, 0)
    raw_values = grouped[:, :, 2 * FEAT :].astype(jnp.float32)
    segments = segment_ids[0]
    conv_taps = conv_weight.astype(jnp.float32).reshape(KCONV, head_count, DV)
    tap_masks = [jnp.ones((length,), jnp.float32)]
    mixed_values = conv_taps[0] * raw_values
    for tap_index in range(1, KCONV):
        earlier = shift_down(segments, tap_index, -1)
        tap_masks.append((earlier == segments).astype(jnp.float32))
        mixed_values = (
            mixed_values
            + conv_taps[tap_index]
            * shift_down(raw_values, tap_index, 0.0)
            * tap_masks[tap_index][:, None, None]
        )
    conv_low = mixed_values.astype(jnp.bfloat16).transpose(1, 0, 2)
    head_outputs, denominators = attend_forward(
        head_queries, head_keys, conv_low, segments, block_rows
    )
    mixer_low = head_outputs.transpose(1, 0, 2).reshape(length, head_count * DV).astype(jnp.bfloat16)
    mixed_parts = jnp.dot(mixer_low, out_rows, preferred_element_type=jnp.float32).astype(jnp.bfloat16)
    attended = rows_in + square_sum(
        mixed_parts.reshape(seq_parts, 2, tok_count // 2, model_width), "mixed_sum", 1
    ).reshape(tok_count, model_width)
    normed_low = rms_norm(attended, gain_second).astype(jnp.bfloat16)
    branch_out, normed_all, gate_all, up_all, active_all, down_part = feed_forward(
        normed_low, gate_up_part, w_down
    )
    outputs = attended + branch_out
    sequence_length = lax.dynamic_index_in_dim(
        valid_lengths, lax.axis_index("wt"), 0, keepdims=False
    )
    positions = lax.axis_index("seq") * tok_count + jnp.arange(tok_count, dtype=jnp.int32)
    keep_mask = (positions < sequence_length).astype(jnp.float32)
    residual_error = (outputs - teacher[0].astype(jnp.float32)) * keep_mask[:, None]
    energy = 0.5 * jnp.sum(residual_error * residual_error)
    (
        attended_grad,
        mix_back,
        gain_two_terms,
        gate_terms,
        up_terms,
        down_terms,
        gate_from_x,
        gate_from_y,
        down_from_x,
        down_from_y,
    ) = feed_back(
        residual_error,
        attended,
        gain_second[None],
        gate_up_part,
        down_part,
        gate_all,
        up_all,
        active_all,
        normed_all,
    )
    marks = jnp.stack(tap_masks, axis=1) * (
        jnp.arange(length)[:, None] >= jnp.arange(KCONV)[None, :]
    ).astype(jnp.float32)
    inputs_grad, totals, gate_total, up_total, down_total, qkv_total, grad_w_out = mixer_back(
        mix_back,
        attended_grad,
        rows_low,
        gain_first[None],
        out_rows,
        qkv_columns,
        hidden_low,
        projected,
        mixer_low,
        conv_low,
        head_outputs,
        segments,
        marks,
        conv_taps.reshape(KCONV, head_count * DV),
        column_order(head_count),
        gain_two_terms,
        energy.reshape(1, 1),
        (gate_terms, gate_from_x, gate_from_y),
        (up_terms,),
        (down_terms, down_from_x, down_from_y),
    )
    grad_w_qkv = qkv_total.transpose(1, 0, 2).reshape(w_qkv.shape)
    hidden_units = gate_up_part.shape[2]
    grad_w_gate_up = jnp.stack(
        [total.reshape(model_width // seq_parts, hidden_units) for total in (gate_total, up_total)]
    )
    grad_w_down = down_total.reshape(w_down.shape)
    totals = lax.dynamic_slice_in_dim(totals, lax.axis_index("wt") * gain_lanes, gain_lanes, 1)
    grad_norm_gain, grad_mlp_gain = totals[0], totals[1]
    grad_conv = totals[3 : 3 + KCONV]
    valid_total = jnp.sum(valid_lengths).astype(jnp.float32)
    mean_loss = 2.0 * totals[2, 0] / (valid_total * model_width)
    return (
        outputs.astype(jnp.bfloat16)[None],
        inputs_grad[None],
        mean_loss,
        grad_w_qkv,
        grad_conv,
        grad_w_out,
        grad_norm_gain,
        grad_w_gate_up,
        grad_w_down,
        grad_mlp_gain,
    )


def solution(mesh):
    in_specs = (
        P("wt", "seq", None),
        P("wt", None),
        P(),
        P("wt", "seq", None),
        P(("seq", "wt"), None),
        P(None, "seq"),
        P(("seq", "wt"), None),
        P(("seq", "wt")),
        P(None, "seq", "wt"),
        P("wt", "seq"),
        P(("seq", "wt")),
    )
    out_specs = (
        P("wt", "seq", None),
        P("wt", "seq", None),
        P(),
        P(("seq", "wt"), None),
        P(None, ("seq", "wt")),
        P(("seq", "wt"), None),
        P(("seq", "wt")),
        P(None, "seq", "wt"),
        P("wt", "seq"),
        P(("seq", "wt")),
    )
    return jax.shard_map(body, mesh=mesh, in_specs=in_specs, out_specs=out_specs, check_vma=False)
```

```python
import jax
import jax.numpy as jnp
from jax import lax
from jax.experimental import pallas as pl
from jax.experimental.pallas import tpu as pltpu
from jax.sharding import PartitionSpec as P

H = 16
FEAT = 16
KCONV = 3
DV = 128


epsilon = 1e-05


def rms_norm(values, gain_vector):
    inverse_root = lax.rsqrt(jnp.mean(values * values, axis=-1, keepdims=True) + epsilon)
    return values * inverse_root * gain_vector


def contract_last(former, latter):
    return lax.dot_general(
        former, latter, (((1,), (1,)), ((), ())), preferred_element_type=jnp.float32
    )


def contract_first(former, latter):
    return lax.dot_general(
        former, latter, (((0,), (0,)), ((), ())), preferred_element_type=jnp.float32
    )


def shift_down(values, amount, filler):
    padding = jnp.full((amount,) + values.shape[1:], filler, values.dtype)
    return jnp.concatenate([padding, values[:-amount]], axis=0)


def gated_unit(gate_in, up_in):
    return jax.nn.silu(gate_in) * up_in


MESH = pl.DeviceIdType.MESH
VMEM = pl.BlockSpec(memory_space=pltpu.VMEM)
ANY = pl.BlockSpec(memory_space=pl.ANY)
VMEM_LIMIT = 63 * 1024 * 1024


class Place:
    def __init__(self, seq, wt):
        self.seq, self.wt = seq, wt
        self.ys, self.zs = seq // 2, wt // 2
        self.s, self.w = lax.axis_index("seq"), lax.axis_index("wt")
        self.y, self.x = lax.div(self.s, 2), lax.rem(self.s, 2)
        self.z, self.c = lax.div(self.w, 2), lax.rem(self.w, 2)

    def across(self):
        return (self.y * 2 + 1 - self.x, self.w)

    def beside(self, step):
        return lax.rem(self.y + step, self.ys)

    def column(self, y):
        return (y * 2 + self.x, self.w)

    def partner(self):
        return (self.s, self.z * 2 + 1 - self.c)

    def level(self, z):
        return (self.s, z * 2 + self.c)

    def meet(self, square, line):
        barrier = pltpu.get_barrier_semaphore()
        count = 0
        if square:
            for step in range(1, self.seq):
                device = (lax.rem(self.s + step, self.seq), self.w)
                pl.semaphore_signal(barrier, inc=1, device_id=device, device_id_type=MESH)
                count += 1
        if line:
            for step in range(1, self.wt):
                device = (self.s, lax.rem(self.w + step, self.wt))
                pl.semaphore_signal(barrier, inc=1, device_id=device, device_id_type=MESH)
                count += 1
        pl.semaphore_wait(barrier, count)


def send(source, target, leaving, arriving, device):
    return pltpu.make_async_remote_copy(
        src_ref=source,
        dst_ref=target,
        send_sem=leaving,
        recv_sem=arriving,
        device_id=device,
        device_id_type=MESH,
    )


def add_into(target, sources):
    if len(target.shape) == 3:
        for index in range(target.shape[0]):
            add_into(target.at[index], [source.at[index] for source in sources])
        return
    rows = target.shape[0]
    tile = next(t for t in (64, 32, 16, 8, rows) if rows % t == 0)

    def step(index, carry):
        window = pl.ds(pl.multiple_of(index * tile, tile), tile)
        total = sources[0][window, :].astype(jnp.float32)
        for source in sources[1:]:
            total = total + source[window, :].astype(jnp.float32)
        target[window, :] = total.astype(target.dtype)
        return carry

    lax.fori_loop(0, rows // tile, step, 0)


class SquareGather:
    @staticmethod
    def semaphores(seq):
        return [
            pltpu.SemaphoreType.DMA((2 + seq // 2,)),
            pltpu.SemaphoreType.DMA((seq // 2, 3)),
            pltpu.SemaphoreType.DMA((seq, 2)),
        ]

    def __init__(self, at, view, own, sems):
        self.at, self.view, self.own = at, view, own
        self.over_x, self.over_y, self.got = sems
        self.sent = []

    def go(self, source, s, half, leaving, device):
        copy = send(source, self.view(s, half), leaving, self.got.at[s, half], device)
        copy.start()
        self.sent.append(copy)

    def wait(self, s, half):
        slot = self.view(s, half)
        send(slot, slot, self.over_x.at[0], self.got.at[s, half], self.at.across()).wait_recv()

    def start(self):
        at = self.at
        for half in range(2):
            self.go(self.own(half), at.s, half, self.over_x.at[half], at.across())
            for step in range(1, at.ys):
                target = at.column(at.beside(step))
                self.go(self.own(1 - half), at.s, 1 - half, self.over_y.at[step, half], target)

    def relay(self):
        at = self.at
        other = at.y * 2 + 1 - at.x
        self.wait(other, 0)
        for step in range(1, at.ys):
            self.go(self.view(other, 0), other, 0, self.over_y.at[step, 2], at.column(at.beside(step)))
        for step in range(1, at.ys):
            s = at.beside(step) * 2 + at.x
            self.wait(s, 1)
            self.go(self.view(s, 1), s, 1, self.over_x.at[1 + step], at.across())

    def finish(self):
        at = self.at
        self.wait(at.y * 2 + 1 - at.x, 1)
        for step in range(1, at.ys):
            y = at.beside(step)
            self.wait(y * 2 + at.x, 0)
            self.wait(y * 2 + 1 - at.x, 0)
            self.wait(y * 2 + 1 - at.x, 1)
        for copy in self.sent:
            copy.wait_send()


class SquareSum:
    @staticmethod
    def scratch(seq, half_shape):
        ys = seq // 2
        return [
            pltpu.VMEM((ys,) + half_shape, jnp.bfloat16),
            pltpu.VMEM((ys, 2) + half_shape, jnp.bfloat16),
            pltpu.VMEM((ys,) + half_shape, jnp.bfloat16),
            pltpu.VMEM(half_shape, jnp.bfloat16),
            pltpu.VMEM((ys,) + half_shape, jnp.bfloat16),
            pltpu.VMEM(half_shape, jnp.bfloat16),
            pltpu.SemaphoreType.DMA((ys, 2, 2)),
            pltpu.SemaphoreType.DMA((ys, 3, 2)),
        ]

    def __init__(self, at, part, scratch):
        self.at, self.part = at, part
        self.from_x, self.from_y, self.last_y, self.last_x, self.sum_y, self.sum_x, self.xs, self.yss = scratch
        self.sent = []

    def go(self, source, target, leaving, arriving, device):
        copy = send(source, target, leaving, arriving, device)
        copy.start()
        self.sent.append(copy)

    def wait(self, slot, leaving, arriving):
        send(slot, slot, leaving, arriving, self.at.across()).wait_recv()

    def start(self):
        at = self.at
        for y in range(at.ys):
            self.go(
                self.part(y * 2 + 1 - at.x, 0),
                self.from_x.at[y],
                self.xs.at[y, 0, 0],
                self.xs.at[y, 0, 1],
                at.across(),
            )
        for step in range(1, at.ys):
            y = at.beside(step)
            for x in range(2):
                self.go(
                    self.part(y * 2 + x, 1),
                    self.from_y.at[at.y, x],
                    self.yss.at[step, x, 0],
                    self.yss.at[at.y, x, 1],
                    at.column(y),
                )

    def relay(self):
        at = self.at
        for step in range(1, at.ys):
            y = at.beside(step)
            self.wait(self.from_x.at[y], self.xs.at[y, 0, 0], self.xs.at[y, 0, 1])
            add_into(self.sum_y.at[y], [self.part(y * 2 + at.x, 0), self.from_x.at[y]])
            self.go(
                self.sum_y.at[y],
                self.last_y.at[at.y],
                self.yss.at[step, 2, 0],
                self.yss.at[at.y, 2, 1],
                at.column(y),
            )
        terms = []
        for step in range(1, at.ys):
            y = at.beside(step)
            for x in range(2):
                self.wait(self.from_y.at[y, x], self.yss.at[step, x, 0], self.yss.at[y, x, 1])
            terms.append(self.from_y.at[y, 1 - at.x])
        add_into(self.sum_x, [self.part(at.y * 2 + 1 - at.x, 1)] + terms)
        self.go(self.sum_x, self.last_x, self.xs.at[0, 1, 0], self.xs.at[0, 1, 1], at.across())

    def finish(self, total):
        at = self.at
        self.wait(self.from_x.at[at.y], self.xs.at[0, 0, 0], self.xs.at[at.y, 0, 1])
        terms = [self.part(at.s, 0), self.from_x.at[at.y]]
        for step in range(1, at.ys):
            y = at.beside(step)
            self.wait(self.last_y.at[y], self.yss.at[step, 2, 0], self.yss.at[y, 2, 1])
            terms.append(self.last_y.at[y])
        add_into(total(0), terms)
        self.wait(self.last_x, self.xs.at[0, 1, 0], self.xs.at[0, 1, 1])
        terms = [self.part(at.s, 1), self.last_x]
        for step in range(1, at.ys):
            terms.append(self.from_y.at[at.beside(step), at.x])
        add_into(total(1), terms)
        for copy in self.sent:
            copy.wait_send()


class LineGather:
    @staticmethod
    def semaphores(wt):
        return [pltpu.SemaphoreType.DMA((5, wt // 2))]

    def __init__(self, at, view, sems):
        self.at, self.view, self.sems = at, view, sems[0]

    def up(self, z, source=None):
        slot = self.view(z * 2 + self.at.c)
        source = slot if source is None else source
        return send(source, slot, self.sems.at[0, z], self.sems.at[3, z], self.at.level(self.at.z + 1))

    def down(self, z, source=None):
        slot = self.view(z * 2 + self.at.c)
        source = slot if source is None else source
        return send(source, slot, self.sems.at[1, z], self.sems.at[3, z], self.at.level(self.at.z - 1))

    def over(self, z, source=None):
        slot = self.view(z * 2 + self.at.c)
        source = slot if source is None else source
        return send(source, slot, self.sems.at[2, z], self.sems.at[4, z], self.at.partner())

    def start(self, source=None):
        at = self.at

        @pl.when(at.z + 1 < at.zs)
        def _():
            self.up(at.z, source).start()

        @pl.when(at.z > 0)
        def _():
            self.down(at.z, source).start()

        self.over(at.z, source).start()

    def step(self, index):
        at = self.at
        below, above = at.z - 1 - index, at.z + 1 + index

        @pl.when(below >= 0)
        def _():
            self.up(below).wait_recv()

            @pl.when(at.z + 1 < at.zs)
            def _():
                self.up(below).start()

            self.over(below).start()

        @pl.when(above < at.zs)
        def _():
            self.down(above).wait_recv()

            @pl.when(at.z > 0)
            def _():
                self.down(above).start()

            self.over(above).start()

    def wait_over(self, z):
        slot = self.view(z * 2 + 1 - self.at.c)
        send(slot, slot, self.sems.at[2, z], self.sems.at[4, z], self.at.partner()).wait_recv()

    def finish(self):
        for z in range(self.at.zs):
            self.wait_over(z)
        self.sent()

    def sent(self):
        at = self.at
        for z in range(at.zs):

            @pl.when((at.z >= z) & (at.z + 1 < at.zs))
            def _():
                self.up(z).wait_send()

            @pl.when((at.z <= z) & (at.z > 0))
            def _():
                self.down(z).wait_send()

            self.over(z).wait_send()


def remote_call(kernel, name, number, outs, scratch, *operands, in_specs=None, out_specs=None):
    return pl.pallas_call(
        kernel,
        name=name,
        out_shape=outs,
        in_specs=[VMEM] * len(operands) if in_specs is None else in_specs,
        out_specs=jax.tree.map(lambda _: VMEM, outs) if out_specs is None else out_specs,
        scratch_shapes=scratch,
        compiler_params=pltpu.CompilerParams(
            collective_id=number, has_side_effects=True, vmem_limit_bytes=VMEM_LIMIT
        ),
    )(*operands)


def mixer_forward(tokens, qkv_rows, out_rows, gains, gate_up, segments, marks, taps, order):
    seq, wt = lax.axis_size("seq"), lax.axis_size("wt")
    zs = wt // 2
    count, width = tokens.shape
    length = count * seq
    _, qkv_rank, qkv_width = qkv_rows.shape
    out_rank = out_rows.shape[0]
    heads = H // seq
    value_width = heads * DV
    lanes_each = width // (seq * wt)
    block, units = gate_up.shape[1:]
    early = early_rows(block)
    rows_at_once = 256
    small = [
        tokens,
        qkv_rows,
        out_rows,
        gains,
        segments.reshape(1, length),
        segments.reshape(length, 1),
        marks,
        taps,
        order,
    ]

    def kernel(*refs):
        (x_ref, qkv_ref, out_ref, gain_ref, segment_row, segment_column, mark_ref, tap_ref, order_ref), refs = (
            refs[:9],
            refs[9:],
        )
        gate_up_ref, refs = refs[0], refs[1:]
        (attended_out, normed_out, gain_rows), refs = refs[:3], refs[3:]
        (qkv_out, w_out_out, hidden_out, sorted_out, mixer_out, values_out, outputs_out, gates_out), refs = (
            refs[:8],
            refs[8:],
        )
        (xs, qkvs, outs, gains_all, hidden_v, sorted_v, mixer_v, values_v, outputs_v, parts, total, room), refs = (
            refs[:12],
            refs[12:],
        )
        sum_scratch, x_sems, gate_sems, refs = refs[:8], refs[8:11], refs[11:14], refs[14:]
        line_sems, refs = [refs[index : index + 1] for index in range(3)], refs[3:]
        swap_q, swap_g, local, outgoing = refs
        at = Place(seq, wt)
        room_load = pltpu.make_async_copy(gate_up_ref.at[:, pl.ds(0, early)], room, local.at[4])
        room_load.start()
        at.meet(True, True)
        half = count // 2
        gather_x = SquareGather(
            at,
            lambda s, h: xs.at[pl.ds(pl.multiple_of(s * count + h * half, half), half)],
            lambda h: x_ref.at[pl.ds(h * half, half)],
            x_sems,
        )
        gather_q = LineGather(at, lambda w: qkvs.at[:, w], line_sems[0])
        gather_g = LineGather(
            at, lambda w: gains_all.at[:, pl.ds(pl.multiple_of(w * 8, 8), 8)], line_sems[1]
        )
        gather_o = LineGather(at, lambda w: outs.at[w], line_sems[2])
        gates = SquareGather(
            at, lambda s, h: gates_out.at[h, s], lambda h: gate_up_ref.at[h, pl.ds(0, early)], gate_sems
        )
        gain_slot = pl.ds(pl.multiple_of(at.w * 8, 8), 8)
        swaps = []
        for step in range(1, seq):
            to = lax.rem(at.s + step, seq)
            swaps.append(
                send(gain_ref, gains_all.at[at.s, gain_slot], swap_g.at[step, 0], swap_g.at[at.s, 1], (to, at.w))
            )
            swaps.append(
                send(qkv_ref.at[to], qkvs.at[at.s, at.w], swap_q.at[step, 0], swap_q.at[at.s, 1], (to, at.w))
            )
        for copy in swaps:
            copy.start()
        gather_x.start()
        own = [
            pltpu.make_async_copy(qkv_ref.at[at.s], qkvs.at[at.s, at.w], local.at[0]),
            pltpu.make_async_copy(gain_ref, gains_all.at[at.s, gain_slot], local.at[1]),
            pltpu.make_async_copy(out_ref, outs.at[at.w], local.at[2]),
            pltpu.make_async_copy(x_ref, xs.at[pl.ds(pl.multiple_of(at.s * count, count), count)], local.at[3]),
        ]
        for copy in own:
            copy.start()
        for copy in own:
            copy.wait()
        room_load.wait()
        room_store = pltpu.make_async_copy(room, gates_out.at[:, at.s], local.at[4])
        room_store.start()
        for step in range(1, seq):
            s = lax.rem(at.s + step, seq)
            slot = gains_all.at[s, gain_slot]
            send(slot, slot, swap_g.at[step, 0], swap_g.at[s, 1], at.across()).wait_recv()
            slot = qkvs.at[s, at.w]
            send(slot, slot, swap_q.at[step, 0], swap_q.at[s, 1], at.across()).wait_recv()
        gather_g.start()
        gather_q.start()
        gather_x.relay()
        gates.start()
        for index in range(zs - 1):
            gather_g.step(index)
            gather_q.step(index)
        gather_o.start()
        gather_g.finish()

        device_rows = gains_all[...].reshape(seq * wt * 8, 128).astype(jnp.bfloat16)
        gain_rows[...] = jnp.zeros_like(gain_rows)

        def spread_gains(index, carry):
            begin = pl.multiple_of(index * 256, 256)
            lane = lax.broadcasted_iota(jnp.int32, (128, 256), 0)
            column = begin + lax.broadcasted_iota(jnp.int32, (128, 256), 1)
            copied = jnp.dot(
                device_rows,
                (lane == lax.rem(column, lanes_each)).astype(jnp.float32).astype(jnp.bfloat16),
                preferred_element_type=jnp.float32,
            )
            row = lax.broadcasted_iota(jnp.int32, copied.shape, 0)
            column = begin + lax.broadcasted_iota(jnp.int32, copied.shape, 1)
            first_row = lax.div(column, lanes_each) * 8
            for number in range(2):
                gain_rows[number : number + 1, pl.ds(begin, 256)] = jnp.sum(
                    jnp.where(row == first_row + number, copied, 0.0), axis=0, keepdims=True
                )
            return carry

        lax.fori_loop(0, width // 256, spread_gains, 0)
        gather_x.finish()

        def norm_rows(index, carry):
            window = pl.ds(pl.multiple_of(index * 32, 32), 32)
            hidden_v[window, :] = rms_norm(xs[window, :].astype(jnp.float32), gain_rows[0:1, :]).astype(
                jnp.bfloat16
            )
            return carry

        lax.fori_loop(0, length // 32, norm_rows, 0)
        gather_q.finish()
        projected = jnp.dot(
            hidden_v[...], qkvs[...].reshape(width, qkv_width), preferred_element_type=jnp.float32
        ).astype(jnp.bfloat16)
        sorted_v[...] = jnp.dot(projected, order_ref[...], preferred_element_type=jnp.float32).astype(
            jnp.bfloat16
        )
        stores = [
            pltpu.make_async_copy(source, target, outgoing.at[index])
            for index, (source, target) in enumerate(
                (
                    (qkvs, qkv_out),
                    (hidden_v, hidden_out),
                    (sorted_v, sorted_out),
                    (values_v, values_out),
                    (outputs_v, outputs_out),
                    (mixer_v, mixer_out),
                    (outs, w_out_out),
                )
            )
        ]
        for copy in stores[:3]:
            copy.start()

        def convolve(head, carry):
            columns = pl.ds(pl.multiple_of(head * DV, DV), DV)
            raw = sorted_v[:, columns].astype(jnp.float32)
            mixed = tap_ref[0:1, columns] * raw
            for tap in range(1, KCONV):
                mixed = mixed + tap_ref[tap : tap + 1, columns] * pltpu.roll(raw, tap, 0) * mark_ref[:, tap : tap + 1]
            values_v[head] = mixed.astype(jnp.bfloat16)
            return carry

        lax.fori_loop(0, heads, convolve, 0)
        stores[3].start()
        gates.relay()
        steps = length // rows_at_once
        lanes = lax.broadcasted_iota(jnp.int32, (1, 128), 1)

        def attend(index, carry):
            head, start = lax.div(index, steps), lax.rem(index, steps) * rows_at_once
            rows = pl.ds(pl.multiple_of(start, rows_at_once), rows_at_once)
            mine = ((lanes >= head * FEAT) & (lanes < head * FEAT + FEAT)).astype(jnp.float32)
            queries = sorted_v[rows, value_width : value_width + 128] * mine.astype(jnp.bfloat16)
            scores = contract_last(queries, sorted_v[:, value_width + 128 :]) * 0.25
            places = start + lax.broadcasted_iota(jnp.int32, scores.shape, 0)
            allowed = (segment_column[rows, :] == segment_row[...]) & (
                places >= lax.broadcasted_iota(jnp.int32, scores.shape, 1)
            )
            kernel_values = jnp.where(allowed, 1.0 + scores + 0.5 * scores * scores, 0.0)
            denominator = jnp.sum(kernel_values, axis=1, keepdims=True)
            mixed = (
                jnp.dot(kernel_values.astype(jnp.bfloat16), values_v[head], preferred_element_type=jnp.float32)
                / denominator
            )
            outputs_v[head, rows, :] = mixed
            mixer_v[rows, pl.ds(pl.multiple_of(head * DV, DV), DV)] = mixed.astype(jnp.bfloat16)
            return carry

        turns = heads * steps
        for index in range(zs - 1):
            lax.fori_loop(turns * index // (zs - 1), turns * (index + 1) // (zs - 1), attend, 0)
            gather_o.step(index)
        gather_o.finish()
        for copy in stores[4:]:
            copy.start()

        def out_job(index, carry):
            window = pl.ds(pl.multiple_of(index * 512, 512), 512)
            term = jnp.dot(
                mixer_v[...], outs[:, :, window].reshape(value_width, 512), preferred_element_type=jnp.float32
            ).astype(jnp.bfloat16)
            for s in range(seq):
                for h in range(2):
                    begin = s * count + h * half
                    parts[s, h, :, window] = term[begin : begin + half]
            return carry

        lax.fori_loop(0, width // 512, out_job, 0)
        work = SquareSum(at, lambda s, h: parts.at[s, h], sum_scratch)
        work.start()
        work.relay()
        work.finish(lambda h: total.at[h])

        def finish_rows(index, carry):
            for h in range(2):
                window = pl.ds(pl.multiple_of(index * 16, 16), 16)
                rows = pl.ds(pl.multiple_of(h * half + index * 16, 16), 16)
                attended = x_ref[rows, :].astype(jnp.float32) + total[h, window, :]
                attended_out[rows, :] = attended
                normed_out[rows, :] = rms_norm(attended, gain_rows[1:2, :]).astype(jnp.bfloat16)
            return carry

        lax.fori_loop(0, half // 16, finish_rows, 0)
        gates.finish()
        room_store.wait()
        for copy in swaps:
            copy.wait_send()
        for copy in stores:
            copy.wait()

    low, f32 = jnp.bfloat16, jnp.float32
    sorted_width = value_width + 256
    return remote_call(
        kernel,
        "mixer_forward",
        0,
        [
            jax.ShapeDtypeStruct((count, width), f32),
            jax.ShapeDtypeStruct((count, width), low),
            jax.ShapeDtypeStruct((8, width), f32),
            jax.ShapeDtypeStruct((seq, wt, qkv_rank, qkv_width), low),
            jax.ShapeDtypeStruct((wt, out_rank, width), low),
            jax.ShapeDtypeStruct((length, width), low),
            jax.ShapeDtypeStruct((length, sorted_width), low),
            jax.ShapeDtypeStruct((length, value_width), low),
            jax.ShapeDtypeStruct((heads, length, DV), low),
            jax.ShapeDtypeStruct((heads, length, DV), f32),
            jax.ShapeDtypeStruct((2, seq, early, units), low),
        ],
        [
            pltpu.VMEM((length, width), low),
            pltpu.VMEM((seq, wt, qkv_rank, qkv_width), low),
            pltpu.VMEM((wt, out_rank, width), low),
            pltpu.VMEM((seq, wt * 8, 128), f32),
            pltpu.VMEM((length, width), low),
            pltpu.VMEM((length, sorted_width), low),
            pltpu.VMEM((length, value_width), low),
            pltpu.VMEM((heads, length, DV), low),
            pltpu.VMEM((heads, length, DV), f32),
            pltpu.VMEM((seq, 2, count // 2, width), low),
            pltpu.VMEM((2, count // 2, width), f32),
            pltpu.VMEM((2, early, units), low),
        ]
        + SquareSum.scratch(seq, (count // 2, width))
        + SquareGather.semaphores(seq)
        + SquareGather.semaphores(seq)
        + LineGather.semaphores(wt) * 3
        + [
            pltpu.SemaphoreType.DMA((seq, 2)),
            pltpu.SemaphoreType.DMA((seq, 2)),
            pltpu.SemaphoreType.DMA((5,)),
            pltpu.SemaphoreType.DMA((7,)),
        ],
        *small,
        gate_up,
        in_specs=[VMEM] * len(small) + [ANY],
        out_specs=[VMEM] * 3 + [ANY] * 8,
    )


def early_rows(block):
    return block // 4 * 3


class LinePieces:
    @staticmethod
    def scratch(wt, shape, pieces):
        zs = wt // 2
        return [pltpu.VMEM((zs,) + shape, jnp.bfloat16)] * 3 + [pltpu.SemaphoreType.DMA((6, zs, pieces))]

    def __init__(self, at, part, scratch):
        self.at, self.part = at, part
        self.pair, self.below, self.above, self.sems = scratch
        self.pieces = self.sems.shape[2]
        self.width = self.pair.shape[-1] // self.pieces

    def cut(self, ref, piece):
        if len(ref.shape) == 3:
            return ref.at[piece]
        return ref.at[:, pl.ds(pl.multiple_of(piece * self.width, self.width), self.width)]

    def own(self, z, piece):
        return self.cut(self.part(z * 2 + self.at.c), piece)

    def over(self, z, piece):
        return send(
            self.cut(self.part(z * 2 + 1 - self.at.c), piece),
            self.cut(self.pair.at[z], piece),
            self.sems.at[0, z, piece],
            self.sems.at[1, z, piece],
            self.at.partner(),
        )

    def up(self, z, piece):
        return send(
            self.own(z, piece),
            self.cut(self.below.at[z], piece),
            self.sems.at[2, z, piece],
            self.sems.at[3, z, piece],
            self.at.level(self.at.z + 1),
        )

    def down(self, z, piece):
        return send(
            self.own(z, piece),
            self.cut(self.above.at[z], piece),
            self.sems.at[4, z, piece],
            self.sems.at[5, z, piece],
            self.at.level(self.at.z - 1),
        )

    def terms(self, z, piece):
        self.over(z, piece).wait_recv()
        return [self.own(z, piece), self.cut(self.pair.at[z], piece)]

    def ends(self, z, piece):
        at = self.at

        @pl.when((at.z == 0) & (z > 0))
        def _():
            add_into(self.own(z, piece), self.terms(z, piece))
            self.up(z, piece).start()

        @pl.when((at.z == at.zs - 1) & (z < at.zs - 1))
        def _():
            add_into(self.own(z, piece), self.terms(z, piece))
            self.down(z, piece).start()

    def begin(self):
        zs = self.at.zs

        def pairs(piece, carry):
            for index in range(zs // 2):
                self.over(index, piece).start()
                self.over(zs - 1 - index, piece).start()
            return carry

        lax.fori_loop(0, self.pieces, pairs, 0)

        def starts(index, carry):
            piece = lax.rem(index, self.pieces)
            far = zs - 1 - lax.div(index, self.pieces)
            self.ends(jnp.where(self.at.z == 0, far, zs - 1 - far), piece)
            return carry

        lax.fori_loop(0, (zs - 1) * self.pieces, starts, 0)

    def pass_on(self, index, fill=None):
        at = self.at
        upper = at.z * 2 >= at.zs
        high, low = index, at.zs - 1 - index

        def lower(piece, when):
            @pl.when((at.z > low) & (at.z < at.zs - 1) & when)
            def _():
                terms = self.terms(low, piece)
                self.down(low, piece).wait_recv()
                add_into(self.own(low, piece), terms + [self.cut(self.above.at[low], piece)])
                self.down(low, piece).start()

        def step(piece, carry):
            lower(piece, upper)

            @pl.when((at.z < high) & (at.z > 0))
            def _():
                terms = self.terms(high, piece)
                self.up(high, piece).wait_recv()
                add_into(self.own(high, piece), terms + [self.cut(self.below.at[high], piece)])
                self.up(high, piece).start()

            lower(piece, jnp.logical_not(upper))
            if fill is not None:
                fill(piece)
            return carry

        lax.fori_loop(0, self.pieces, step, 0)

    def finish(self, total, fill=None):
        at = self.at

        def step(piece, carry):
            if fill is not None:
                fill(self.pieces + piece)
            terms = self.terms(at.z, piece)
            below, above = self.cut(self.below.at[at.z], piece), self.cut(self.above.at[at.z], piece)

            @pl.when(at.z == 0)
            def _():
                self.down(at.z, piece).wait_recv()
                add_into(self.cut(total, piece), terms + [above])

            @pl.when(at.z == at.zs - 1)
            def _():
                self.up(at.z, piece).wait_recv()
                add_into(self.cut(total, piece), terms + [below])

            @pl.when((at.z > 0) & (at.z < at.zs - 1))
            def _():
                self.up(at.z, piece).wait_recv()
                self.down(at.z, piece).wait_recv()
                add_into(self.cut(total, piece), terms + [below, above])

            for z in range(at.zs):

                @pl.when(at.z < z)
                def _():
                    self.up(z, piece).wait_send()

                @pl.when(at.z > z)
                def _():
                    self.down(z, piece).wait_send()

                self.over(z, piece).wait_send()
            return carry

        lax.fori_loop(0, self.pieces, step, 0)


class SquareTerms:
    @staticmethod
    def semaphores(seq):
        return [pltpu.SemaphoreType.DMA((seq // 2, 2)), pltpu.SemaphoreType.DMA((seq // 2, 2, 2))]

    @staticmethod
    def scratch(seq, half_shape):
        ys = seq // 2
        return [
            pltpu.VMEM((ys,) + half_shape, jnp.bfloat16),
            pltpu.VMEM(half_shape, jnp.bfloat16),
            pltpu.SemaphoreType.DMA((ys + 1, 2)),
        ]

    def __init__(self, at, terms, from_x, from_y, sems=None, lasts=None, scratch=None):
        self.at, self.terms, self.from_x, self.from_y = at, terms, from_x, from_y
        if sems is not None:
            self.xs, self.ys = sems
        if scratch is not None:
            self.last_y, self.last_x = lasts
            self.sum_y, self.sum_x, self.last = scratch

    def first_x(self, y):
        at = self.at
        return send(
            self.terms(y * 2 + 1 - at.x, 0), self.from_x.at[y], self.xs.at[y, 0], self.xs.at[y, 1], at.across()
        )

    def first_y(self, step, x):
        at = self.at
        y = at.beside(step)
        return send(
            self.terms(y * 2 + x, 1),
            self.from_y.at[at.y, x],
            self.ys.at[step, x, 0],
            self.ys.at[at.y, x, 1],
            at.column(y),
        )

    def first_start(self):
        for y in range(self.at.ys):
            self.first_x(y).start()
        for step in range(1, self.at.ys):
            for x in range(2):
                self.first_y(step, x).start()

    def first_wait(self):
        at = self.at
        for y in range(at.ys):
            self.first_x(y).wait()
        for step in range(1, at.ys):
            y = at.beside(step)
            for x in range(2):
                self.first_y(step, x).wait_send()
                slot = self.from_y.at[y, x]
                send(slot, slot, self.ys.at[step, x, 0], self.ys.at[y, x, 1], at.across()).wait_recv()

    def second_y(self, step):
        at = self.at
        y = at.beside(step)
        return send(
            self.sum_y.at[y], self.last_y.at[at.y], self.last.at[step, 0], self.last.at[at.y, 1], at.column(y)
        )

    def second_x(self):
        at = self.at
        return send(self.sum_x, self.last_x, self.last.at[at.ys, 0], self.last.at[at.ys, 1], at.across())

    def second_start(self, fetch, rooms):
        at = self.at
        for step in range(1, at.ys):
            y = at.beside(step)
            fetch([(self.terms(y * 2 + at.x, 0), rooms[0]), (self.from_x.at[y], rooms[1])])
            add_into(self.sum_y.at[y], [rooms[0], rooms[1]])
        fetch([(self.terms(at.y * 2 + 1 - at.x, 1), self.sum_x)])
        for step in range(1, at.ys):
            y = at.beside(step)
            fetch([(self.from_y.at[y, 1 - at.x], rooms[0])])
            add_into(self.sum_x, [self.sum_x, rooms[0]])

    def second_go(self):
        for step in range(1, self.at.ys):
            self.second_y(step).start()
        self.second_x().start()

    def second_wait(self):
        at = self.at
        for step in range(1, at.ys):
            self.second_y(step).wait_send()
            y = at.beside(step)
            slot = self.last_y.at[y]
            send(slot, slot, self.last.at[step, 0], self.last.at[y, 1], at.across()).wait_recv()
        self.second_x().wait()


def norm_back(rows, load, store, gain, terms):
    def step(index, carry):
        window = pl.ds(pl.multiple_of(index * 16, 16), 16)
        values, incoming, base = load(window)
        root = lax.rsqrt(jnp.mean(values * values, axis=-1, keepdims=True) + epsilon)
        scaled = incoming * gain
        share = jnp.mean(values * scaled, axis=-1, keepdims=True)
        store(window, base + root * scaled - values * (root * root * root * share))
        term = incoming * values * root
        terms[...] += term[:8] + term[8:]
        return carry

    lax.fori_loop(0, rows // 16, step, 0)


def exchange(
    at, shard, everyone, gather_sems, local, sums, first, second, total, ready, wait_for_ready, fill=None
):
    count = shard.shape[0]
    gather = LineGather(
        at, lambda w: everyone.at[pl.ds(pl.multiple_of(w * count, count), count)], gather_sems
    )
    gather.start(shard)
    own = pltpu.make_async_copy(
        shard, everyone.at[pl.ds(pl.multiple_of(at.w * count, count), count)], local
    )
    own.start()
    own.wait()
    ready[0]()
    last = 2 * (at.zs - 1)
    late = 3 if wait_for_ready else 0

    def turn(index, carry):
        fresh = index <= last
        place = jnp.where(fresh, index, jnp.where(index == last + 3, 0, index - last))
        far, side = lax.div(place + 1, 2), lax.rem(place, 2)
        z = at.z + jnp.where(side == 1, -far, far)
        valid = (z >= 0) & (z < at.zs)

        @pl.when(fresh & (side == 1))
        def _():
            gather.step(far - 1)

        @pl.when(fresh & valid)
        def _():
            gather.wait_over(z)
            first(z)

        if wait_for_ready:

            @pl.when(index == late)
            def _():
                ready[1]()

        @pl.when(valid & (index >= late))
        def _():
            def step(piece, inner):
                second(z, piece)
                sums.over(z, piece).start()

                @pl.when(piece > 0)
                def _():
                    sums.ends(z, piece - 1)

                return inner

            lax.fori_loop(0, sums.pieces, step, 0)
            sums.ends(z, sums.pieces - 1)

        return carry

    lax.fori_loop(0, last + 1 + late, turn, 0)
    for index in range(2, at.zs):
        sums.pass_on(index, fill if index == at.zs - 1 else None)
    sums.finish(total, fill)
    gather.sent()


PIECES = 4


def feed_forward(normed, attended, teacher, keep, gate_early, gate_up_shard, down_shard):
    seq, wt = lax.axis_size("seq"), lax.axis_size("wt")
    count, width = normed.shape
    block, units = gate_up_shard.shape[1:]
    early = early_rows(block)
    columns = down_shard.shape[1]
    tokens = wt * count
    zs = wt // 2
    half = units // 2

    def kernel(*refs):
        (normed_ref, attended_ref, teacher_ref, keep_ref, early_ref, gate_shard_ref, shard_ref), refs = refs[:7], refs[7:]
        (final_out, error_out, energy_out), refs = refs[:3], refs[3:]
        (normed_out, gate_out, up_out, active_out, down_out, gates_out), refs = refs[:6], refs[6:]
        (everyone, gates, downs, gate_all, up_all, active_all, parts, total), refs = refs[:8], refs[8:]
        gather_sems, sum_scratch, late_sems, square_sems, (local, outgoing) = (
            refs[:1],
            refs[1:5],
            refs[5:8],
            refs[8:11],
            refs[11:],
        )
        at = Place(seq, wt)
        loads = [
            pltpu.make_async_copy(
                early_ref.at[:, s], gates.at[:, pl.ds(s * block, early)], local.at[4 + s]
            )
            for s in range(seq)
        ]
        loads.append(
            pltpu.make_async_copy(
                gate_shard_ref.at[:, pl.ds(early, block - early)],
                gates.at[:, pl.ds(pl.multiple_of(at.s * block + early, 16), block - early)],
                local.at[0],
            )
        )
        for load in loads:
            load.start()
        at.meet(True, True)
        late = SquareGather(
            at,
            lambda s, h: gates.at[h, pl.ds(pl.multiple_of(s * block + early, 16), block - early)],
            lambda h: gate_shard_ref.at[h, pl.ds(early, block - early)],
            late_sems,
        )
        weights = SquareGather(
            at,
            lambda s, h: downs.at[
                pl.ds(h * half, half), pl.ds(pl.multiple_of(s * columns, columns), columns)
            ],
            lambda h: shard_ref.at[pl.ds(h * half, half)],
            square_sems,
        )
        sums = LinePieces(
            at, lambda w: parts.at[pl.ds(pl.multiple_of(w * count, count), count)], sum_scratch
        )
        down_store = pltpu.make_async_copy(downs, down_out, local.at[2])
        gates_store = pltpu.make_async_copy(gates, gates_out, local.at[0])

        def ready_first():
            late.start()
            own = pltpu.make_async_copy(
                shard_ref, downs.at[:, pl.ds(pl.multiple_of(at.s * columns, columns), columns)], local.at[3]
            )
            own.start()
            late.relay()
            weights.start()
            own.wait()
            for load in loads:
                load.wait()
            late.finish()
            gates_store.start()

        def ready_later():
            weights.relay()
            weights.finish()
            down_store.start()

        def rows(z):
            return pl.ds(pl.multiple_of(z * 2 * count, 2 * count), 2 * count)

        def stores(z):
            return [
                pltpu.make_async_copy(source.at[rows(z)], target.at[rows(z)], outgoing.at[index, z])
                for index, (source, target) in enumerate(
                    ((everyone, normed_out), (gate_all, gate_out), (up_all, up_out), (active_all, active_out))
                )
            ]

        def first(z):
            here = everyone[rows(z), :]
            gate = jnp.dot(here, gates[0], preferred_element_type=jnp.float32)
            up = jnp.dot(here, gates[1], preferred_element_type=jnp.float32)
            gate_all[rows(z), :] = gate
            up_all[rows(z), :] = up
            active_all[rows(z), :] = gated_unit(gate, up).astype(jnp.bfloat16)
            for copy in stores(z):
                copy.start()

        def second(z, piece):
            window = pl.ds(pl.multiple_of(piece * sums.width, sums.width), sums.width)
            parts[rows(z), window] = jnp.dot(
                active_all[rows(z), :], downs[:, window], preferred_element_type=jnp.float32
            ).astype(jnp.bfloat16)

        exchange(
            at,
            normed_ref,
            everyone,
            gather_sems,
            local.at[1],
            sums,
            first,
            second,
            total,
            (ready_first, ready_later),
            True,
        )
        energy_out[...] = jnp.zeros_like(energy_out)

        def finish_rows(index, carry):
            window = pl.ds(pl.multiple_of(index * 16, 16), 16)
            final = attended_ref[window, :] + total[window, :]
            final_out[window, :] = final.astype(jnp.bfloat16)
            error = (final - teacher_ref[window, :].astype(jnp.float32)) * keep_ref[window, :]
            error_out[window, :] = error
            squares = error * error
            energy_out[...] += 0.5 * (squares[:8] + squares[8:])
            return carry

        lax.fori_loop(0, count // 16, finish_rows, 0)
        down_store.wait()
        gates_store.wait()
        for z in range(zs):
            for copy in stores(z):
                copy.wait()

    low, f32 = jnp.bfloat16, jnp.float32
    return remote_call(
        kernel,
        "feed_forward",
        2,
        [
            jax.ShapeDtypeStruct((count, width), low),
            jax.ShapeDtypeStruct((count, width), f32),
            jax.ShapeDtypeStruct((8, width), f32),
            jax.ShapeDtypeStruct((tokens, width), low),
            jax.ShapeDtypeStruct((tokens, units), f32),
            jax.ShapeDtypeStruct((tokens, units), f32),
            jax.ShapeDtypeStruct((tokens, units), low),
            jax.ShapeDtypeStruct((units, width), low),
            jax.ShapeDtypeStruct((2, width, units), low),
        ],
        [
            pltpu.VMEM((tokens, width), low),
            pltpu.VMEM((2, width, units), low),
            pltpu.VMEM((units, width), low),
            pltpu.VMEM((tokens, units), f32),
            pltpu.VMEM((tokens, units), f32),
            pltpu.VMEM((tokens, units), low),
            pltpu.VMEM((tokens, width), low),
            pltpu.VMEM((count, width), f32),
        ]
        + LineGather.semaphores(wt)
        + LinePieces.scratch(wt, (count, width), PIECES)
        + SquareGather.semaphores(seq)
        + SquareGather.semaphores(seq)
        + [pltpu.SemaphoreType.DMA((4 + seq,)), pltpu.SemaphoreType.DMA((4, zs))],
        normed,
        attended,
        teacher,
        keep,
        gate_early,
        gate_up_shard,
        down_shard,
        in_specs=[VMEM] * 4 + [ANY] * 2 + [VMEM],
        out_specs=[VMEM] * 3 + [ANY] * 6,
    )


def feed_back(error, attended, gain, gate_up, down, gate, up, active, normed):
    seq, wt = lax.axis_size("seq"), lax.axis_size("wt")
    count, width = error.shape
    units = gate_up.shape[2]
    tokens = wt * count
    zs, ys = wt // 2, seq // 2
    block = width // seq
    gate_half, down_half = (block // 2, units), (units // 2, block)

    def kernel(*refs):
        (error_ref, attended_ref, gain_ref, gate_up_ref, down_ref, gate_ref, up_ref, active_ref, normed_ref), refs = (
            refs[:9],
            refs[9:],
        )
        (grad_ref, mix_ref, gain_terms), refs = refs[:3], refs[3:]
        (gate_out, up_out, down_out, gate_x, gate_y, down_x, down_y), refs = refs[:7], refs[7:]
        (low, everyone, gates, downs, gate_all, up_all, back_all, parts, actives, columns), refs = refs[:10], refs[10:]
        (gate_terms, up_terms, down_terms, total), refs = refs[:4], refs[4:]
        gather_sems, sum_scratch, gate_sems, down_sems, (local, outgoing) = (
            refs[:1],
            refs[1:5],
            refs[5:7],
            refs[7:9],
            refs[9:],
        )
        at = Place(seq, wt)
        loads = [
            pltpu.make_async_copy(source, target, local.at[index])
            for index, (source, target) in enumerate(
                (
                    (down_ref, downs),
                    (gate_ref, gate_all),
                    (up_ref, up_all),
                    (gate_up_ref, gates),
                    (active_ref, actives),
                )
            )
        ]
        for load in loads:
            load.start()
        at.meet(True, True)
        low[...] = error_ref[...].astype(jnp.bfloat16)
        sums = LinePieces(
            at, lambda w: parts.at[pl.ds(pl.multiple_of(w * count, count), count)], sum_scratch
        )
        gate_sum = SquareTerms(at, lambda s, h: gate_terms.at[s, h], gate_x, gate_y, gate_sems)
        down_sum = SquareTerms(at, lambda s, h: down_terms.at[s, h], down_x, down_y, down_sems)

        def place(index):
            step = lax.div(index, 2) + 1
            x = lax.rem(at.x + 1 + lax.rem(index, 2), 2)
            return step, x, at.beside(step) * 2 + x

        def column_load(index):
            s = place(index)[2]
            return pltpu.make_async_copy(
                normed_ref.at[:, pl.ds(pl.multiple_of(s * block, block), block)],
                columns.at[lax.rem(index, 2)],
                local.at[6 + lax.rem(index, 2)],
            )

        def leave(sum_, index):
            step, x, s = place(index)

            @pl.when(x != at.x)
            def _():
                sum_.first_x(lax.div(s, 2)).start()

            @pl.when(step < ys)
            def _():
                sum_.first_y(step, x).start()

        def down_job(index):
            s = place(index)[2]
            term = contract_first(
                actives[...], everyone[:, pl.ds(pl.multiple_of(s * block, block), block)]
            ).astype(jnp.bfloat16)
            down_terms[s, 0] = term[: units // 2]
            down_terms[s, 1] = term[units // 2 :]
            leave(down_sum, index)

        def gate_job(index):
            s = place(index)[2]
            column_load(index).wait()
            here = columns.at[lax.rem(index, 2)]
            for number, terms in enumerate((gate_terms, up_terms)):
                term = contract_first(here[...], back_all[number]).astype(jnp.bfloat16)
                terms[s, 0] = term[: block // 2]
                terms[s, 1] = term[block // 2 :]

            @pl.when(index + 2 < seq)
            def _():
                column_load(index + 2).start()

            leave(gate_sum, index)

        def fill(slot):
            def step(index, carry):
                job = slot * (seq // 4) + index

                @pl.when(job < seq)
                def _():
                    down_job(job)

                @pl.when(job >= seq)
                def _():
                    gate_job(job - seq)

                return carry

            lax.fori_loop(0, seq // 4, step, 0)

        def ready_first():
            column_load(0).start()
            column_load(1).start()
            for load in loads:
                load.wait()

        def rows(z):
            return pl.ds(pl.multiple_of(z * 2 * count, 2 * count), 2 * count)

        def first(z):
            active_back = contract_last(everyone[rows(z), :], downs[...])
            gate_here, up_here = gate_all[rows(z), :], up_all[rows(z), :]
            share = jax.nn.sigmoid(gate_here)
            back_all[0, rows(z), :] = (
                active_back * up_here * share * (1.0 + gate_here * (1.0 - share))
            ).astype(jnp.bfloat16)
            back_all[1, rows(z), :] = (active_back * gate_here * share).astype(jnp.bfloat16)

        def second(z, piece):
            window = pl.ds(pl.multiple_of(piece * sums.width, sums.width), sums.width)
            parts[rows(z), window] = (
                contract_last(back_all[0, rows(z), :], gates[0, window, :])
                + contract_last(back_all[1, rows(z), :], gates[1, window, :])
            ).astype(jnp.bfloat16)

        exchange(
            at,
            low,
            everyone,
            gather_sems,
            local.at[5],
            sums,
            first,
            second,
            total,
            (ready_first,),
            False,
            fill,
        )
        stores = [
            pltpu.make_async_copy(source, target, outgoing.at[index])
            for index, (source, target) in enumerate(
                ((gate_terms, gate_out), (up_terms, up_out), (down_terms, down_out))
            )
        ]
        for copy in stores:
            copy.start()
        gain_terms[...] = jnp.zeros_like(gain_terms)

        def load_rows(window):
            return attended_ref[window, :], total[window, :], error_ref[window, :]

        def store_rows(window, value):
            grad_ref[window, :] = value
            mix_ref[window, :] = value.astype(jnp.bfloat16)

        norm_back(count, load_rows, store_rows, gain_ref[1:2, :], gain_terms)
        for copy in stores:
            copy.wait()
        gate_sum.first_wait()
        down_sum.first_wait()

    def terms_of(half):
        return jax.ShapeDtypeStruct((seq, 2) + half, jnp.bfloat16)

    def first_of(half):
        return [
            jax.ShapeDtypeStruct((ys,) + half, jnp.bfloat16),
            jax.ShapeDtypeStruct((ys, 2) + half, jnp.bfloat16),
        ]

    return remote_call(
        kernel,
        "feed_back",
        3,
        [
            jax.ShapeDtypeStruct((count, width), jnp.float32),
            jax.ShapeDtypeStruct((count, width), jnp.bfloat16),
            jax.ShapeDtypeStruct((8, width), jnp.float32),
            terms_of(gate_half),
            terms_of(gate_half),
            terms_of(down_half),
        ]
        + first_of(gate_half)
        + first_of(down_half),
        [
            pltpu.VMEM((count, width), jnp.bfloat16),
            pltpu.VMEM((tokens, width), jnp.bfloat16),
            pltpu.VMEM(gate_up.shape, jnp.bfloat16),
            pltpu.VMEM((units, width), jnp.bfloat16),
            pltpu.VMEM((tokens, units), jnp.float32),
            pltpu.VMEM((tokens, units), jnp.float32),
            pltpu.VMEM((2, tokens, units), jnp.bfloat16),
            pltpu.VMEM((tokens, width), jnp.bfloat16),
            pltpu.VMEM((tokens, units), jnp.bfloat16),
            pltpu.VMEM((2, tokens, block), jnp.bfloat16),
            pltpu.VMEM((seq, 2) + gate_half, jnp.bfloat16),
            pltpu.VMEM((seq, 2) + gate_half, jnp.bfloat16),
            pltpu.VMEM((seq, 2) + down_half, jnp.bfloat16),
            pltpu.VMEM((count, width), jnp.float32),
        ]
        + LineGather.semaphores(wt)
        + LinePieces.scratch(wt, (count, width), PIECES)
        + SquareTerms.semaphores(seq)
        + SquareTerms.semaphores(seq)
        + [pltpu.SemaphoreType.DMA((8,)), pltpu.SemaphoreType.DMA((3,))],
        error,
        attended,
        gain,
        gate_up,
        down,
        gate,
        up,
        active,
        normed,
        in_specs=[VMEM] * 3 + [ANY] * 6,
        out_specs=[VMEM] * 3 + [ANY] * 7,
    )


def mixer_back(
    mix_back,
    attended_grad,
    tokens,
    gain,
    out_rows,
    qkv_columns,
    hidden,
    sorted_columns,
    mixer,
    mixed_values,
    head_outputs,
    segments,
    marks,
    taps,
    order,
    gain_terms,
    energy,
    gate_parts,
    up_parts,
    down_parts,
):
    seq, wt = lax.axis_size("seq"), lax.axis_size("wt")
    zs, ys = wt // 2, seq // 2
    count, width = mix_back.shape
    length = count * seq
    heads = mixed_values.shape[0]
    qkv_width = qkv_columns.shape[1]
    value_width = heads * DV
    rank = width // (seq * wt)
    gate_half, down_half = gate_parts[0].shape[2:], down_parts[0].shape[2:]
    rows_at_once = 256
    segment_rows = segments.reshape(1, length)
    segment_columns = segments.reshape(length, 1)
    big = [out_rows, qkv_columns, hidden, sorted_columns, mixer, mixed_values, head_outputs]
    small = [mix_back, attended_grad, tokens, gain, segment_rows, segment_columns, marks, taps, order, gain_terms, energy]
    far = list(gate_parts) + list(down_parts) + list(up_parts)

    def kernel(*refs):
        big_refs, refs = refs[: len(big)], refs[len(big) :]
        small_refs, refs = refs[: len(small)], refs[len(small) :]
        (gate_t, gate_x, gate_y, down_t, down_x, down_y, up_t), refs = refs[: len(far)], refs[len(far) :]
        (grad_out, sums_out, qkv_out, w_out_out, up_x, up_y), refs = refs[:6], refs[6:]
        gate_lasts, up_lasts, down_lasts, refs = refs[:2], refs[2:4], refs[4:6], refs[6:]
        (w_out_v, w_qkv_v, hidden_v, sorted_v, mixer_v, values_v, outputs_v), refs = refs[:7], refs[7:]
        (mix_all, mixer_grad, query_acc, key_acc, value_acc, back_sorted, back_v), refs = refs[:7], refs[7:]
        (hidden_parts, qkv_parts, out_parts, hidden_total, gain_acc, spread, taps_acc), refs = refs[:7], refs[7:]
        (room_gate0, room_gate1, room_down0, room_down1, qkv_sum, first, middle, last), refs = refs[:8], refs[8:]
        hidden_scratch, refs = refs[:8], refs[8:]
        qkv_scratch, out_scratch, refs = refs[:4], refs[4:8], refs[8:]
        gate_scratch, down_scratch, up_scratch, refs = refs[:3], refs[3:6], refs[6:9], refs[9:]
        gather_sems, up_sems, refs = refs[:3], refs[3:5], refs[5:]
        local, swap, first_sems, last_sems = refs
        (
            mix_ref,
            grad_ref,
            token_ref,
            gain_ref,
            segment_row,
            segment_column,
            mark_ref,
            tap_ref,
            order_ref,
            gain_two,
            energy_ref,
        ) = small_refs
        at = Place(seq, wt)
        loads = [
            pltpu.make_async_copy(source, target, local.at[4 + index])
            for index, (source, target) in enumerate(
                zip(big_refs, (w_out_v, w_qkv_v, hidden_v, sorted_v, mixer_v, values_v, outputs_v))
            )
        ]
        for load in loads:
            load.start()
        at.meet(True, True)
        half = count // 2
        gather = SquareGather(
            at,
            lambda s, h: mix_all.at[pl.ds(pl.multiple_of(s * count + h * half, half), half)],
            lambda h: mix_ref.at[pl.ds(h * half, half)],
            gather_sems,
        )
        gather.start()
        own = pltpu.make_async_copy(
            mix_ref, mix_all.at[pl.ds(pl.multiple_of(at.s * count, count), count)], local.at[3]
        )
        own.start()

        def fetch(pairs):
            copies = [
                pltpu.make_async_copy(source, target, local.at[index])
                for index, (source, target) in enumerate(pairs)
            ]
            for copy in copies:
                copy.start()
            for copy in copies:
                copy.wait()

        gate_sum = SquareTerms(at, lambda s, h: gate_t.at[s, h], gate_x, gate_y, None, gate_lasts, gate_scratch)
        down_sum = SquareTerms(at, lambda s, h: down_t.at[s, h], down_x, down_y, None, down_lasts, down_scratch)
        up_sum = SquareTerms(at, lambda s, h: up_t.at[s, h], up_x, up_y, up_sems, up_lasts, up_scratch)
        gate_rooms, down_rooms = (room_gate0, room_gate1), (room_down0, room_down1)
        gate_sum.second_start(fetch, gate_rooms)
        down_sum.second_start(fetch, down_rooms)
        own.wait()
        for load in loads:
            load.wait()
        query_acc[...] = jnp.zeros_like(query_acc)
        key_acc[...] = jnp.zeros_like(key_acc)
        value_acc[...] = jnp.zeros_like(value_acc)
        gather.relay()
        gather.finish()
        gate_sum.second_go()
        down_sum.second_go()
        mixer_grad[...] = contract_last(mix_all[...], w_out_v[...]).astype(jnp.bfloat16)
        out_sum = LinePieces(at, lambda w: out_parts.at[w], out_scratch)
        out_rank = out_parts.shape[1]
        out_block = 512 if value_width % 512 == 0 else value_width

        def out_job(index, carry):
            window = pl.ds(pl.multiple_of(index * 512, 512), 512)
            term = contract_first(mixer_v[...], mix_all[:, window]).astype(jnp.bfloat16)
            for w in range(wt):
                out_parts[w, :, window] = term[w * out_rank : (w + 1) * out_rank]
            return carry

        lax.fori_loop(0, width // 512, out_job, 0)
        out_sum.begin()

        steps = length // rows_at_once
        lanes = lax.broadcasted_iota(jnp.int32, (1, 128), 1)

        def attend(index, carry):
            head, start = lax.div(index, steps), lax.rem(index, steps) * rows_at_once
            rows = pl.ds(pl.multiple_of(start, rows_at_once), rows_at_once)
            columns = pl.ds(pl.multiple_of(head * DV, DV), DV)
            mine = ((lanes >= head * FEAT) & (lanes < head * FEAT + FEAT)).astype(jnp.float32)
            queries = sorted_v[rows, value_width : value_width + 128] * mine.astype(jnp.bfloat16)
            keys = sorted_v[:, value_width + 128 :]
            scores = contract_last(queries, keys) * 0.25
            places = start + lax.broadcasted_iota(jnp.int32, scores.shape, 0)
            allowed = (segment_column[rows, :] == segment_row[...]) & (
                places >= lax.broadcasted_iota(jnp.int32, scores.shape, 1)
            )
            kernel_values = jnp.where(allowed, 1.0 + scores + 0.5 * scores * scores, 0.0)
            denominator = jnp.sum(kernel_values, axis=1, keepdims=True)
            incoming = mixer_grad[rows, columns].astype(jnp.float32)
            numerator_back = (incoming / denominator).astype(jnp.bfloat16)
            denominator_back = (
                -jnp.sum(incoming * outputs_v[head, rows, :], axis=1, keepdims=True) / denominator
            )
            weight_back = contract_last(numerator_back, values_v[head])
            kernel_back = jnp.where(allowed, weight_back + denominator_back, 0.0)
            dots_back = (0.25 * kernel_back * (1.0 + scores)).astype(jnp.bfloat16)
            query_acc[rows, :] += jnp.dot(dots_back, keys, preferred_element_type=jnp.float32) * mine
            key_acc[...] += contract_first(dots_back, queries)
            value_acc[:, columns] += contract_first(kernel_values.astype(jnp.bfloat16), numerator_back)
            return carry

        middle_step = heads * steps // 2
        lax.fori_loop(0, middle_step, attend, 0)
        for index in range(zs - 1, 1, -1):
            if index == zs // 2:
                lax.fori_loop(middle_step, heads * steps, attend, 0)
            out_sum.pass_on(index)
        taps_acc[...] = jnp.zeros_like(taps_acc)

        def convolve(head, carry):
            columns = pl.ds(pl.multiple_of(head * DV, DV), DV)
            mixed_back = value_acc[:, columns]
            raw = sorted_v[:, columns].astype(jnp.float32)
            raw_back = tap_ref[0:1, columns] * mixed_back
            taps_acc[3:4, columns] = jnp.sum(mixed_back * raw, axis=0, keepdims=True)
            for tap in range(1, KCONV):
                masked = mixed_back * mark_ref[:, tap : tap + 1]
                taps_acc[3 + tap : 4 + tap, columns] = jnp.sum(
                    masked * pltpu.roll(raw, tap, 0), axis=0, keepdims=True
                )
                raw_back = raw_back + tap_ref[tap : tap + 1, columns] * pltpu.roll(masked, length - tap, 0)
            back_sorted[:, columns] = raw_back.astype(jnp.bfloat16)
            return carry

        lax.fori_loop(0, heads, convolve, 0)
        back_sorted[:, value_width : value_width + 128] = query_acc[...].astype(jnp.bfloat16)
        back_sorted[:, value_width + 128 :] = key_acc[...].astype(jnp.bfloat16)
        back_v[...] = contract_last(back_sorted[...], order_ref[...]).astype(jnp.bfloat16)
        hidden_sum = SquareSum(at, lambda s, h: hidden_parts.at[s, h], hidden_scratch)

        def hidden_job(index, carry):
            window = pl.ds(pl.multiple_of(index * 512, 512), 512)
            term = contract_last(back_v[...], w_qkv_v[window, :]).astype(jnp.bfloat16)
            for s in range(seq):
                for h in range(2):
                    begin = s * count + h * half
                    hidden_parts[s, h, :, window] = term[begin : begin + half]
            return carry

        lax.fori_loop(0, width // 512, hidden_job, 0)
        hidden_sum.start()
        qkv_sums = LinePieces(at, lambda w: qkv_parts.at[:, w], qkv_scratch)
        qkv_rank = qkv_parts.shape[2]

        def qkv_job(s, carry):
            block = wt * qkv_rank
            window = pl.ds(pl.multiple_of(s * block, block), block)
            term = contract_first(hidden_v[:, window], back_v[...]).astype(jnp.bfloat16)
            for w in range(wt):
                qkv_parts[s, w] = term[w * qkv_rank : (w + 1) * qkv_rank]
            return carry

        lax.fori_loop(0, seq, qkv_job, 0)
        qkv_sums.begin()
        qkv_sums.pass_on(zs - 1)
        hidden_sum.relay()
        up_sum.first_start()
        for index in range(zs - 2, 1, -1):
            qkv_sums.pass_on(index)
        hidden_sum.finish(lambda h: hidden_total.at[h])
        gain_acc[...] = jnp.zeros_like(gain_acc)
        for h in range(2):

            def shift(window):
                return pl.ds(pl.multiple_of(h * half + window.start, 16), 16)

            def load_rows(window):
                rows = shift(window)
                return token_ref[rows, :].astype(jnp.float32), hidden_total[h, window, :], grad_ref[rows, :]

            def store_rows(window, value):
                grad_out[shift(window), :] = value

            norm_back(half, load_rows, store_rows, gain_ref[0:1, :], gain_acc)
        spread[...] = jnp.zeros_like(spread)
        spread[0:1, :] = jnp.sum(gain_acc[...], axis=0, keepdims=True)
        spread[1:2, :] = jnp.sum(gain_two[...], axis=0, keepdims=True)
        energy = jnp.sum(jnp.sum(energy_ref[...], axis=0, keepdims=True), axis=1, keepdims=True)
        spread[2:3, :] = jnp.broadcast_to(energy, (1, width))
        copies = []
        for step in range(1, seq):
            to = lax.rem(at.s + step, seq)
            window = pl.ds(pl.multiple_of(to * value_width, value_width), value_width)
            copies.append(
                send(spread.at[:, window], first.at[at.s], first_sems.at[step, 0], first_sems.at[at.s, 1], (to, at.w))
            )
        for copy in copies:
            copy.start()
        qkv_sums.finish(qkv_sum)
        for step in range(1, seq):
            to = lax.rem(at.s + step, seq)
            copy = send(qkv_sum.at[to], qkv_out.at[at.s], swap.at[step, 0], swap.at[at.s, 1], (to, at.w))
            copy.start()
            copies.append(copy)
        add_into(qkv_out.at[at.s], [qkv_sum.at[at.s]])
        out_sum.finish(w_out_out)
        terms = [spread.at[:, pl.ds(pl.multiple_of(at.s * value_width, value_width), value_width)], taps_acc]
        for step in range(1, seq):
            s = lax.rem(at.s + step, seq)
            slot = first.at[s]
            send(slot, slot, first_sems.at[step, 0], first_sems.at[s, 1], at.across()).wait_recv()
            terms.append(slot)
        add_into(middle, terms)
        for step in range(1, wt):
            to = lax.rem(at.w + step, wt)
            copy = send(middle, last.at[at.w], last_sems.at[step, 0], last_sems.at[at.w, 1], (at.s, to))
            copy.start()
            copies.append(copy)
        up_sum.first_wait()
        up_sum.second_start(fetch, gate_rooms)
        up_sum.second_go()
        gate_sum.second_wait()
        down_sum.second_wait()
        terms = [middle]
        for step in range(1, wt):
            w = lax.rem(at.w + step, wt)
            slot = last.at[w]
            send(slot, slot, last_sems.at[step, 0], last_sems.at[w, 1], at.partner()).wait_recv()
            terms.append(slot)
        add_into(sums_out, terms)
        for step in range(1, seq):
            s = lax.rem(at.s + step, seq)
            slot = qkv_out.at[s]
            send(slot, slot, swap.at[step, 0], swap.at[s, 1], at.across()).wait_recv()
        up_sum.second_wait()
        for copy in copies:
            copy.wait_send()

    out_rank, qkv_rank = value_width // wt, width // (seq * wt)
    f32, low = jnp.float32, jnp.bfloat16
    tile = (8, value_width)
    results = remote_call(
        kernel,
        "mixer_back",
        4,
        [
            jax.ShapeDtypeStruct((count, width), f32),
            jax.ShapeDtypeStruct(tile, f32),
            jax.ShapeDtypeStruct((seq, qkv_rank, qkv_width), f32),
            jax.ShapeDtypeStruct((out_rank, width), f32),
            jax.ShapeDtypeStruct((ys,) + gate_half, low),
            jax.ShapeDtypeStruct((ys, 2) + gate_half, low),
        ]
        + [
            jax.ShapeDtypeStruct(shape, low)
            for shape_half in (gate_half, gate_half, down_half)
            for shape in ((ys,) + shape_half, shape_half)
        ],
        [pltpu.VMEM(array.shape, array.dtype) for array in big]
        + [
            pltpu.VMEM((length, width), low),
            pltpu.VMEM((length, value_width), low),
            pltpu.VMEM((length, 128), f32),
            pltpu.VMEM((length, 128), f32),
            pltpu.VMEM((length, value_width), f32),
            pltpu.VMEM((length, value_width + 256), low),
            pltpu.VMEM((length, qkv_width), low),
            pltpu.VMEM((seq, 2, count // 2, width), low),
            pltpu.VMEM((seq, wt, qkv_rank, qkv_width), low),
            pltpu.VMEM((wt, out_rank, width), low),
            pltpu.VMEM((2, count // 2, width), f32),
            pltpu.VMEM((8, width), f32),
            pltpu.VMEM((8, width), f32),
            pltpu.VMEM(tile, f32),
            pltpu.VMEM(gate_half, low),
            pltpu.VMEM(gate_half, low),
            pltpu.VMEM(down_half, low),
            pltpu.VMEM(down_half, low),
            pltpu.VMEM((seq, qkv_rank, qkv_width), f32),
            pltpu.VMEM((seq,) + tile, f32),
            pltpu.VMEM(tile, f32),
            pltpu.VMEM((wt,) + tile, f32),
        ]
        + SquareSum.scratch(seq, (count // 2, width))
        + LinePieces.scratch(wt, (seq, qkv_rank, qkv_width), seq)
        + LinePieces.scratch(wt, (out_rank, width), PIECES)
        + SquareTerms.scratch(seq, gate_half)
        + SquareTerms.scratch(seq, down_half)
        + SquareTerms.scratch(seq, gate_half)
        + SquareGather.semaphores(seq)
        + SquareTerms.semaphores(seq)
        + [
            pltpu.SemaphoreType.DMA((11,)),
            pltpu.SemaphoreType.DMA((seq, 2)),
            pltpu.SemaphoreType.DMA((seq, 2)),
            pltpu.SemaphoreType.DMA((wt, 2)),
        ],
        *big,
        *small,
        *far,
        in_specs=[ANY] * len(big) + [VMEM] * len(small) + [ANY] * len(far),
        out_specs=[VMEM] * 4 + [ANY] * 8,
    )
    grad, totals, qkv_total, out_total, up_x, up_y = results[:6]
    gate = tuple(gate_parts) + tuple(results[6:8])
    up = tuple(up_parts) + (up_x, up_y) + tuple(results[8:10])
    down = tuple(down_parts) + tuple(results[10:12])
    return grad, totals, gate, up, down, qkv_total, out_total


def column_order(heads):
    head_width = 2 * FEAT + DV
    column = jnp.arange(heads * head_width)
    head, place = column // head_width, column % head_width
    value_width = heads * DV
    target = jnp.where(
        place < FEAT,
        value_width + head * FEAT + place,
        jnp.where(place < 2 * FEAT, value_width + 128 + head * FEAT + place - FEAT, head * DV + place - 2 * FEAT),
    )
    return (target[:, None] == jnp.arange(value_width + 256)[None, :]).astype(jnp.bfloat16)


def last_sums(gate, up, down, qkv_total, out_total, grad, final, qkv_shape):
    seq = lax.axis_size("seq")
    ys = seq // 2
    f32, low = jnp.float32, jnp.bfloat16
    gate_half, down_half = gate[0].shape[2:], down[0].shape[2:]
    qkv_width = qkv_total.shape[2]
    operands = list(gate) + list(up) + list(down)
    passed = [out_total, grad, final]

    def kernel(*refs):
        groups, refs = [refs[5 * index : 5 * index + 5] for index in range(3)], refs[15:]
        qkv_ref, passed_refs, refs = refs[0], refs[1:4], refs[4:]
        (gate_up_out, down_out, qkv_out), refs = refs[:3], refs[3:]
        passed_outs, refs = refs[:3], refs[3:]
        totals, refs = refs[:2], refs[2:]
        passed_rooms, refs = refs[:3], refs[3:]
        rooms, (loads, stores, pass_sems) = [refs[5 * index : 5 * index + 5] for index in range(3)], refs[15:]
        s = lax.axis_index("seq")
        y, x = lax.div(s, 2), lax.rem(s, 2)
        copies = []
        for number, (group, room) in enumerate(zip(groups, rooms)):
            terms, from_x, from_y, last_y, last_x = group
            sources = (terms.at[s], from_x.at[y], from_y.at[:, x], last_y, last_x)
            mine = [
                pltpu.make_async_copy(source, target, loads.at[number, index])
                for index, (source, target) in enumerate(zip(sources, room))
            ]
            for copy in mine:
                copy.start()
            copies.append(mine)
        ins = [
            pltpu.make_async_copy(source, room, pass_sems.at[index, 0])
            for index, (source, room) in enumerate(zip(passed_refs, passed_rooms))
        ]
        for copy in ins:
            copy.start()
        for index in range(seq):
            qkv_out[:, index * qkv_width : (index + 1) * qkv_width] = qkv_ref[index]
        outs = []
        for index, (room, target) in enumerate(zip(passed_rooms, passed_outs)):
            ins[index].wait()
            copy = pltpu.make_async_copy(room, target, pass_sems.at[index, 1])
            copy.start()
            outs.append(copy)
        for number, room in enumerate(rooms):
            own, near_x, near_y, last_y, last_x = room
            total = totals[number // 2]
            base = 2 * (number % 2)
            for copy in copies[number]:
                copy.wait()
            rows = own.shape[1]
            tile = next(t for t in (64, 32, 16) if rows % t == 0)

            def step(index, carry):
                window = pl.ds(pl.multiple_of(index * tile, tile), tile)
                first = own[0, window, :].astype(f32) + near_x[window, :].astype(f32)
                second = own[1, window, :].astype(f32) + last_x[window, :].astype(f32)
                for other in range(1, ys):
                    place = lax.rem(y + other, ys)
                    first = first + last_y[place, window, :].astype(f32)
                    second = second + near_y[place, window, :].astype(f32)
                total[base, window, :] = first
                total[base + 1, window, :] = second
                return carry

            lax.fori_loop(0, rows // tile, step, 0)
            target = gate_up_out.at[pl.ds(base, 2)] if number < 2 else down_out
            copy = pltpu.make_async_copy(total.at[pl.ds(base, 2)], target, stores.at[number])
            copy.start()
            outs.append(copy)
        for copy in outs:
            copy.wait()

    def rooms(half):
        return [
            pltpu.VMEM((2,) + half, low),
            pltpu.VMEM(half, low),
            pltpu.VMEM((ys,) + half, low),
            pltpu.VMEM((ys,) + half, low),
            pltpu.VMEM(half, low),
        ]

    return pl.pallas_call(
        kernel,
        name="last_sums",
        out_shape=[
            jax.ShapeDtypeStruct((4,) + gate_half, f32),
            jax.ShapeDtypeStruct((2,) + down_half, f32),
            jax.ShapeDtypeStruct(qkv_shape, f32),
        ]
        + [jax.ShapeDtypeStruct(array.shape, array.dtype) for array in passed],
        in_specs=[ANY] * 15 + [VMEM] + [ANY] * 3,
        out_specs=[ANY] * 2 + [VMEM] + [ANY] * 3,
        scratch_shapes=[pltpu.VMEM((4,) + gate_half, f32), pltpu.VMEM((2,) + down_half, f32)]
        + [pltpu.VMEM(array.shape, array.dtype) for array in passed]
        + rooms(gate_half) * 2
        + rooms(down_half)
        + [
            pltpu.SemaphoreType.DMA((3, 5)),
            pltpu.SemaphoreType.DMA((3,)),
            pltpu.SemaphoreType.DMA((3, 2)),
        ],
        compiler_params=pltpu.CompilerParams(vmem_limit_bytes=VMEM_LIMIT),
    )(*operands, qkv_total, *passed)


def rows_of_tile(values, row):
    return jnp.pad(values[None, :], [(row, 7 - row), (0, 128 - values.shape[0])])


def body(
    inputs,
    segment_ids,
    valid_lengths,
    teacher,
    w_qkv,
    conv_weight,
    w_out,
    norm_gain,
    w_gate_up,
    w_down,
    mlp_gain,
):
    seq_parts = lax.axis_size("seq")
    tok_count = inputs.shape[1]
    model_width = inputs.shape[2]
    length = tok_count * seq_parts
    head_count = H // seq_parts
    qkv_width = head_count * (2 * FEAT + DV)
    rows_low = inputs[0]
    gain_lanes = norm_gain.shape[0]
    gains = rows_of_tile(norm_gain.astype(jnp.float32), 0) + rows_of_tile(mlp_gain.astype(jnp.float32), 1)
    qkv_rows = w_qkv.reshape(w_qkv.shape[0], seq_parts, qkv_width).transpose(1, 0, 2)
    segments = segment_ids[0]
    tap_masks = [jnp.ones((length,), jnp.float32)]
    for tap_index in range(1, KCONV):
        tap_masks.append((shift_down(segments, tap_index, -1) == segments).astype(jnp.float32))
    marks = jnp.stack(tap_masks, axis=1)
    taps = conv_weight.astype(jnp.float32)
    order = column_order(head_count)
    (
        attended,
        normed_low,
        gain_rows,
        qkv_columns,
        out_rows,
        hidden_low,
        sorted_columns,
        mixer_low,
        mixed_values,
        head_outputs,
        gate_early,
    ) = mixer_forward(rows_low, qkv_rows, w_out, gains, w_gate_up, segments, marks, taps, order)
    sequence_length = lax.dynamic_index_in_dim(
        valid_lengths, lax.axis_index("wt"), 0, keepdims=False
    )
    positions = lax.axis_index("seq") * tok_count + jnp.arange(tok_count, dtype=jnp.int32)
    keep_mask = (positions < sequence_length).astype(jnp.float32)[:, None]
    (
        final_low,
        residual_error,
        energy,
        normed_all,
        gate_all,
        up_all,
        active_all,
        down_part,
        gate_up_part,
    ) = feed_forward(normed_low, attended, teacher[0], keep_mask, gate_early, w_gate_up, w_down)
    (
        attended_grad,
        mix_back,
        gain_two_terms,
        gate_terms,
        up_terms,
        down_terms,
        gate_from_x,
        gate_from_y,
        down_from_x,
        down_from_y,
    ) = feed_back(
        residual_error,
        attended,
        gain_rows,
        gate_up_part,
        down_part,
        gate_all,
        up_all,
        active_all,
        normed_all,
    )
    inputs_grad, totals, gate, up, down, qkv_total, out_total = mixer_back(
        mix_back,
        attended_grad,
        rows_low,
        gain_rows,
        out_rows.reshape(head_count * DV, model_width),
        qkv_columns.reshape(model_width, qkv_width),
        hidden_low,
        sorted_columns,
        mixer_low,
        mixed_values,
        head_outputs,
        segments,
        marks,
        taps,
        order,
        gain_two_terms,
        energy,
        (gate_terms, gate_from_x, gate_from_y),
        (up_terms,),
        (down_terms, down_from_x, down_from_y),
    )
    grad_w_gate_up, grad_w_down, grad_w_qkv, grad_w_out, inputs_grad, outputs = last_sums(
        gate, up, down, qkv_total, out_total, inputs_grad, final_low, w_qkv.shape
    )
    totals = lax.dynamic_slice_in_dim(totals, lax.axis_index("wt") * gain_lanes, gain_lanes, 1)
    grad_norm_gain, grad_mlp_gain = totals[0], totals[1]
    grad_conv = totals[3 : 3 + KCONV]
    valid_total = jnp.sum(valid_lengths).astype(jnp.float32)
    mean_loss = 2.0 * totals[2, 0] / (valid_total * model_width)
    return (
        outputs[None],
        inputs_grad[None],
        mean_loss,
        grad_w_qkv,
        grad_conv,
        grad_w_out,
        grad_norm_gain,
        grad_w_gate_up.reshape(w_gate_up.shape),
        grad_w_down.reshape(w_down.shape),
        grad_mlp_gain,
    )


def solution(mesh):
    in_specs = (
        P("wt", "seq", None),
        P("wt", None),
        P(),
        P("wt", "seq", None),
        P(("seq", "wt"), None),
        P(None, "seq"),
        P(("seq", "wt"), None),
        P(("seq", "wt")),
        P(None, "seq", "wt"),
        P("wt", "seq"),
        P(("seq", "wt")),
    )
    out_specs = (
        P("wt", "seq", None),
        P("wt", "seq", None),
        P(),
        P(("seq", "wt"), None),
        P(None, ("seq", "wt")),
        P(("seq", "wt"), None),
        P(("seq", "wt")),
        P(None, "seq", "wt"),
        P("wt", "seq"),
        P(("seq", "wt")),
    )
    return jax.shard_map(body, mesh=mesh, in_specs=in_specs, out_specs=out_specs, check_vma=False)
```

```python
import jax
import jax.numpy as jnp
from jax import lax
from jax.experimental import pallas as pl
from jax.experimental.pallas import tpu as pltpu
from jax.sharding import PartitionSpec as P

H = 16
FEAT = 16
KCONV = 3
DV = 128


epsilon = 1e-05


def rms_norm(values, gain_vector):
    inverse_root = lax.rsqrt(jnp.mean(values * values, axis=-1, keepdims=True) + epsilon)
    return values * inverse_root * gain_vector


def contract_last(former, latter):
    return lax.dot_general(
        former, latter, (((1,), (1,)), ((), ())), preferred_element_type=jnp.float32
    )


def contract_first(former, latter):
    return lax.dot_general(
        former, latter, (((0,), (0,)), ((), ())), preferred_element_type=jnp.float32
    )


def shift_down(values, amount, filler):
    padding = jnp.full((amount,) + values.shape[1:], filler, values.dtype)
    return jnp.concatenate([padding, values[:-amount]], axis=0)


def gated_unit(gate_in, up_in):
    return jax.nn.silu(gate_in) * up_in


MESH = pl.DeviceIdType.MESH
VMEM = pl.BlockSpec(memory_space=pltpu.VMEM)
ANY = pl.BlockSpec(memory_space=pl.ANY)
SMEM = pl.BlockSpec(memory_space=pltpu.SMEM)
VMEM_LIMIT = 63 * 1024 * 1024


class Place:
    def __init__(self, seq, wt):
        self.seq, self.wt = seq, wt
        self.ys, self.zs = seq // 2, wt // 2
        self.s, self.w = lax.axis_index("seq"), lax.axis_index("wt")
        self.y, self.x = lax.div(self.s, 2), lax.rem(self.s, 2)
        self.z, self.c = lax.div(self.w, 2), lax.rem(self.w, 2)

    def across(self):
        return (self.y * 2 + 1 - self.x, self.w)

    def beside(self, step):
        return lax.rem(self.y + step, self.ys)

    def column(self, y):
        return (y * 2 + self.x, self.w)

    def partner(self):
        return (self.s, self.z * 2 + 1 - self.c)

    def level(self, z):
        return (self.s, z * 2 + self.c)

    def meet(self, square, line):
        barrier = pltpu.get_barrier_semaphore()
        count = 0
        if square:
            for step in range(1, self.seq):
                device = (lax.rem(self.s + step, self.seq), self.w)
                pl.semaphore_signal(barrier, inc=1, device_id=device, device_id_type=MESH)
                count += 1
        if line:
            for step in range(1, self.wt):
                device = (self.s, lax.rem(self.w + step, self.wt))
                pl.semaphore_signal(barrier, inc=1, device_id=device, device_id_type=MESH)
                count += 1
        pl.semaphore_wait(barrier, count)


def send(source, target, leaving, arriving, device):
    return pltpu.make_async_remote_copy(
        src_ref=source,
        dst_ref=target,
        send_sem=leaving,
        recv_sem=arriving,
        device_id=device,
        device_id_type=MESH,
    )


def add_into(target, sources):
    if len(target.shape) == 3:
        for index in range(target.shape[0]):
            add_into(target.at[index], [source.at[index] for source in sources])
        return
    rows = target.shape[0]
    tile = next(t for t in (64, 32, 16, 8, rows) if rows % t == 0)

    def step(index, carry):
        window = pl.ds(pl.multiple_of(index * tile, tile), tile)
        total = sources[0][window, :].astype(jnp.float32)
        for source in sources[1:]:
            total = total + source[window, :].astype(jnp.float32)
        target[window, :] = total.astype(target.dtype)
        return carry

    lax.fori_loop(0, rows // tile, step, 0)


class SquareGather:
    @staticmethod
    def semaphores(seq):
        return [
            pltpu.SemaphoreType.DMA((2 + seq // 2,)),
            pltpu.SemaphoreType.DMA((seq // 2, 3)),
            pltpu.SemaphoreType.DMA((seq, 2)),
        ]

    def __init__(self, at, view, own, sems):
        self.at, self.view, self.own = at, view, own
        self.over_x, self.over_y, self.got = sems
        self.sent = []

    def go(self, source, s, half, leaving, device):
        copy = send(source, self.view(s, half), leaving, self.got.at[s, half], device)
        copy.start()
        self.sent.append(copy)

    def wait(self, s, half):
        slot = self.view(s, half)
        send(slot, slot, self.over_x.at[0], self.got.at[s, half], self.at.across()).wait_recv()

    def start(self):
        at = self.at
        for half in range(2):
            self.go(self.own(half), at.s, half, self.over_x.at[half], at.across())
            for step in range(1, at.ys):
                target = at.column(at.beside(step))
                self.go(self.own(1 - half), at.s, 1 - half, self.over_y.at[step, half], target)

    def relay(self):
        at = self.at
        other = at.y * 2 + 1 - at.x
        self.wait(other, 0)
        for step in range(1, at.ys):
            self.go(self.view(other, 0), other, 0, self.over_y.at[step, 2], at.column(at.beside(step)))
        for step in range(1, at.ys):
            s = at.beside(step) * 2 + at.x
            self.wait(s, 1)
            self.go(self.view(s, 1), s, 1, self.over_x.at[1 + step], at.across())

    def finish(self):
        at = self.at
        self.wait(at.y * 2 + 1 - at.x, 1)
        for step in range(1, at.ys):
            y = at.beside(step)
            self.wait(y * 2 + at.x, 0)
            self.wait(y * 2 + 1 - at.x, 0)
            self.wait(y * 2 + 1 - at.x, 1)
        for copy in self.sent:
            copy.wait_send()


class SquareSum:
    @staticmethod
    def scratch(seq, half_shape):
        ys = seq // 2
        return [
            pltpu.VMEM((ys,) + half_shape, jnp.bfloat16),
            pltpu.VMEM((ys, 2) + half_shape, jnp.bfloat16),
            pltpu.VMEM((ys,) + half_shape, jnp.bfloat16),
            pltpu.VMEM(half_shape, jnp.bfloat16),
            pltpu.VMEM((ys,) + half_shape, jnp.bfloat16),
            pltpu.VMEM(half_shape, jnp.bfloat16),
            pltpu.SemaphoreType.DMA((ys, 2, 2)),
            pltpu.SemaphoreType.DMA((ys, 3, 2)),
        ]

    def __init__(self, at, part, scratch):
        self.at, self.part = at, part
        self.from_x, self.from_y, self.last_y, self.last_x, self.sum_y, self.sum_x, self.xs, self.yss = scratch
        self.sent = []

    def go(self, source, target, leaving, arriving, device):
        copy = send(source, target, leaving, arriving, device)
        copy.start()
        self.sent.append(copy)

    def wait(self, slot, leaving, arriving):
        send(slot, slot, leaving, arriving, self.at.across()).wait_recv()

    def start(self):
        at = self.at
        for y in range(at.ys):
            self.go(
                self.part(y * 2 + 1 - at.x, 0),
                self.from_x.at[y],
                self.xs.at[y, 0, 0],
                self.xs.at[y, 0, 1],
                at.across(),
            )
        for step in range(1, at.ys):
            y = at.beside(step)
            for x in range(2):
                self.go(
                    self.part(y * 2 + x, 1),
                    self.from_y.at[at.y, x],
                    self.yss.at[step, x, 0],
                    self.yss.at[at.y, x, 1],
                    at.column(y),
                )

    def relay(self):
        at = self.at
        for step in range(1, at.ys):
            y = at.beside(step)
            self.wait(self.from_x.at[y], self.xs.at[y, 0, 0], self.xs.at[y, 0, 1])
            add_into(self.sum_y.at[y], [self.part(y * 2 + at.x, 0), self.from_x.at[y]])
            self.go(
                self.sum_y.at[y],
                self.last_y.at[at.y],
                self.yss.at[step, 2, 0],
                self.yss.at[at.y, 2, 1],
                at.column(y),
            )
        terms = []
        for step in range(1, at.ys):
            y = at.beside(step)
            for x in range(2):
                self.wait(self.from_y.at[y, x], self.yss.at[step, x, 0], self.yss.at[y, x, 1])
            terms.append(self.from_y.at[y, 1 - at.x])
        add_into(self.sum_x, [self.part(at.y * 2 + 1 - at.x, 1)] + terms)
        self.go(self.sum_x, self.last_x, self.xs.at[0, 1, 0], self.xs.at[0, 1, 1], at.across())

    def finish(self, total):
        at = self.at
        self.wait(self.from_x.at[at.y], self.xs.at[0, 0, 0], self.xs.at[at.y, 0, 1])
        terms = [self.part(at.s, 0), self.from_x.at[at.y]]
        for step in range(1, at.ys):
            y = at.beside(step)
            self.wait(self.last_y.at[y], self.yss.at[step, 2, 0], self.yss.at[y, 2, 1])
            terms.append(self.last_y.at[y])
        add_into(total(0), terms)
        self.wait(self.last_x, self.xs.at[0, 1, 0], self.xs.at[0, 1, 1])
        terms = [self.part(at.s, 1), self.last_x]
        for step in range(1, at.ys):
            terms.append(self.from_y.at[at.beside(step), at.x])
        add_into(total(1), terms)
        for copy in self.sent:
            copy.wait_send()


class LineGather:
    @staticmethod
    def semaphores(wt, cuts=1):
        return [pltpu.SemaphoreType.DMA((5, wt // 2, cuts))]

    def __init__(self, at, view, sems):
        self.at, self.view, self.sems = at, view, sems[0]
        self.cuts = self.sems.shape[2]

    def cut(self, ref, part):
        if self.cuts == 1:
            return ref
        rows = ref.shape[0] // self.cuts
        return ref.at[pl.ds(part * rows, rows)]

    def hop(self, z, part, kind, device, source):
        slot = self.view(z * 2 + self.at.c)
        source = slot if source is None else source
        arriving = 4 if kind == 2 else 3
        return send(
            self.cut(source, part),
            self.cut(slot, part),
            self.sems.at[kind, z, part],
            self.sems.at[arriving, z, part],
            device,
        )

    def up(self, z, part, source=None):
        return self.hop(z, part, 0, self.at.level(self.at.z + 1), source)

    def down(self, z, part, source=None):
        return self.hop(z, part, 1, self.at.level(self.at.z - 1), source)

    def over(self, z, part, source=None):
        return self.hop(z, part, 2, self.at.partner(), source)

    def start(self, source=None):
        at = self.at
        for part in range(self.cuts):

            @pl.when(at.z + 1 < at.zs)
            def _():
                self.up(at.z, part, source).start()

            @pl.when(at.z > 0)
            def _():
                self.down(at.z, part, source).start()

            self.over(at.z, part, source).start()

    def step(self, index):
        at = self.at
        below, above = at.z - 1 - index, at.z + 1 + index
        for part in range(self.cuts):

            @pl.when(below >= 0)
            def _():
                self.up(below, part).wait_recv()

                @pl.when(at.z + 1 < at.zs)
                def _():
                    self.up(below, part).start()

                self.over(below, part).start()

            @pl.when(above < at.zs)
            def _():
                self.down(above, part).wait_recv()

                @pl.when(at.z > 0)
                def _():
                    self.down(above, part).start()

                self.over(above, part).start()

    def wait_over(self, z):
        for part in range(self.cuts):
            slot = self.cut(self.view(z * 2 + 1 - self.at.c), part)
            send(slot, slot, self.sems.at[2, z, part], self.sems.at[4, z, part], self.at.partner()).wait_recv()

    def finish(self):
        for z in range(self.at.zs):
            self.wait_over(z)
        self.sent()

    def sent(self):
        at = self.at
        for z in range(at.zs):
            for part in range(self.cuts):

                @pl.when((at.z >= z) & (at.z + 1 < at.zs))
                def _():
                    self.up(z, part).wait_send()

                @pl.when((at.z <= z) & (at.z > 0))
                def _():
                    self.down(z, part).wait_send()

                self.over(z, part).wait_send()


def remote_call(kernel, name, number, outs, scratch, *operands, in_specs=None, out_specs=None):
    return pl.pallas_call(
        kernel,
        name=name,
        out_shape=outs,
        in_specs=[VMEM] * len(operands) if in_specs is None else in_specs,
        out_specs=jax.tree.map(lambda _: VMEM, outs) if out_specs is None else out_specs,
        scratch_shapes=scratch,
        compiler_params=pltpu.CompilerParams(
            collective_id=number, has_side_effects=True, vmem_limit_bytes=VMEM_LIMIT
        ),
    )(*operands)


def mixer_forward(tokens, qkv_rows, out_rows, gains, gate_up, segments, taps):
    seq, wt = lax.axis_size("seq"), lax.axis_size("wt")
    zs = wt // 2
    count, width = tokens.shape
    length = count * seq
    out_rank = out_rows.shape[0]
    heads = H // seq
    value_width = heads * DV
    qkv_width = value_width + 2 * FEAT * heads
    qkv_rank = width // (seq * wt)
    lanes_each = width // (seq * wt)
    units, block = gate_up.shape[1:]
    early = early_rows(units)
    rows_at_once = 256
    small = [
        tokens,
        qkv_rows,
        out_rows,
        gains,
        segments,
        taps,
    ]

    def kernel(*refs):
        (x_ref, qkv_ref, out_ref, gain_ref, segment_ref, tap_ref), refs = refs[:6], refs[6:]
        gate_up_ref, refs = refs[0], refs[1:]
        (attended_out, normed_out, gain_rows), refs = refs[:3], refs[3:]
        (qkv_out, w_out_out, hidden_out, sorted_out, mixer_out, values_out, outputs_out, gates_out, order_out), refs = (
            refs[:9],
            refs[9:],
        )
        (xs, qkvs, outs, gains_all, hidden_v, sorted_v, mixer_v, values_v, outputs_v, parts, total, room), refs = (
            refs[:12],
            refs[12:],
        )
        (order_v, segment_column, tap_v), refs = refs[:3], refs[3:]
        sum_scratch, x_sems, gate_sems, refs = refs[:8], refs[8:11], refs[11:14], refs[14:]
        line_sems, refs = [refs[index : index + 1] for index in range(3)], refs[3:]
        swap_q, swap_g, local, outgoing = refs
        at = Place(seq, wt)
        room_load = pltpu.make_async_copy(gate_up_ref.at[:, pl.ds(0, early)], room, local.at[4])
        room_load.start()
        at.meet(True, True)
        half = count // 2
        gather_x = SquareGather(
            at,
            lambda s, h: xs.at[pl.ds(pl.multiple_of(s * count + h * half, half), half)],
            lambda h: x_ref.at[pl.ds(h * half, half)],
            x_sems,
        )
        gather_q = LineGather(at, lambda w: qkvs.at[:, w], line_sems[0])
        gather_g = LineGather(
            at, lambda w: gains_all.at[:, pl.ds(pl.multiple_of(w * 8, 8), 8)], line_sems[1]
        )
        gather_o = LineGather(at, lambda w: outs.at[w], line_sems[2])
        gates = SquareGather(
            at,
            lambda s, h: gates_out.at[h, :, pl.ds(pl.multiple_of(s * block, block), block)],
            lambda h: gate_up_ref.at[h, pl.ds(0, early)],
            gate_sems,
        )
        gain_slot = pl.ds(pl.multiple_of(at.w * 8, 8), 8)

        def qkv_part(s):
            if len(qkv_ref.shape) == 3:
                return qkv_ref.at[s]
            return qkv_ref.at[:, pl.ds(pl.multiple_of(s * qkv_width, qkv_width), qkv_width)]

        swaps = []
        for step in range(1, seq):
            to = lax.rem(at.s + step, seq)
            swaps.append(
                send(gain_ref, gains_all.at[at.s, gain_slot], swap_g.at[step, 0], swap_g.at[at.s, 1], (to, at.w))
            )
            swaps.append(
                send(qkv_part(to), qkvs.at[at.s, at.w], swap_q.at[step, 0], swap_q.at[at.s, 1], (to, at.w))
            )
        for copy in swaps:
            copy.start()
        gather_x.start()
        own = [
            pltpu.make_async_copy(qkv_part(at.s), qkvs.at[at.s, at.w], local.at[0]),
            pltpu.make_async_copy(gain_ref, gains_all.at[at.s, gain_slot], local.at[1]),
            pltpu.make_async_copy(out_ref, outs.at[at.w], local.at[2]),
            pltpu.make_async_copy(x_ref, xs.at[pl.ds(pl.multiple_of(at.s * count, count), count)], local.at[3]),
        ]
        for copy in own:
            copy.start()
        for copy in own:
            copy.wait()
        room_load.wait()
        room_store = pltpu.make_async_copy(
            room, gates_out.at[:, :, pl.ds(pl.multiple_of(at.s * block, block), block)], local.at[4]
        )
        room_store.start()
        for step in range(1, seq):
            s = lax.rem(at.s + step, seq)
            slot = gains_all.at[s, gain_slot]
            send(slot, slot, swap_g.at[step, 0], swap_g.at[s, 1], at.across()).wait_recv()
            slot = qkvs.at[s, at.w]
            send(slot, slot, swap_q.at[step, 0], swap_q.at[s, 1], at.across()).wait_recv()
        gather_g.start()
        gather_q.start()
        tap_v[...] = tap_ref[...].astype(jnp.float32)
        segment_row = segment_ref[...].astype(jnp.float32)
        segment_column[...] = jnp.broadcast_to(segment_row, (128, length)).T
        write_order(order_v, heads)
        gather_x.relay()
        gates.start()
        for index in range(zs - 1):
            if index == zs - 2:
                gather_o.start()
            gather_g.step(index)
            gather_q.step(index)
        gather_g.finish()

        device_rows = gains_all[...].reshape(seq * wt * 8, 128).astype(jnp.bfloat16)
        gain_rows[...] = jnp.zeros_like(gain_rows)

        def spread_gains(index, carry):
            begin = pl.multiple_of(index * 256, 256)
            lane = lax.broadcasted_iota(jnp.int32, (128, 256), 0)
            column = begin + lax.broadcasted_iota(jnp.int32, (128, 256), 1)
            copied = jnp.dot(
                device_rows,
                (lane == lax.rem(column, lanes_each)).astype(jnp.float32).astype(jnp.bfloat16),
                preferred_element_type=jnp.float32,
            )
            row = lax.broadcasted_iota(jnp.int32, copied.shape, 0)
            column = begin + lax.broadcasted_iota(jnp.int32, copied.shape, 1)
            first_row = lax.div(column, lanes_each) * 8
            for number in range(2):
                gain_rows[number : number + 1, pl.ds(begin, 256)] = jnp.sum(
                    jnp.where(row == first_row + number, copied, 0.0), axis=0, keepdims=True
                )
            return carry

        lax.fori_loop(0, width // 256, spread_gains, 0)
        gather_x.finish()

        def norm_rows(index, carry):
            window = pl.ds(pl.multiple_of(index * 32, 32), 32)
            hidden_v[window, :] = rms_norm(xs[window, :].astype(jnp.float32), gain_rows[0:1, :]).astype(
                jnp.bfloat16
            )
            return carry

        lax.fori_loop(0, length // 32, norm_rows, 0)
        gather_q.finish()
        projected = jnp.dot(
            hidden_v[...], qkvs[...].reshape(width, qkv_width), preferred_element_type=jnp.float32
        ).astype(jnp.bfloat16)
        sorted_v[...] = jnp.dot(projected, order_v[...], preferred_element_type=jnp.float32).astype(
            jnp.bfloat16
        )
        stores = [
            pltpu.make_async_copy(source, target, outgoing.at[index])
            for index, (source, target) in enumerate(
                (
                    (qkvs, qkv_out),
                    (hidden_v, hidden_out),
                    (sorted_v, sorted_out),
                    (values_v, values_out),
                    (outputs_v, outputs_out),
                    (mixer_v, mixer_out),
                    (outs, w_out_out),
                    (order_v, order_out),
                )
            )
        ]
        for copy in stores[:3]:
            copy.start()
        marks = tap_marks(segment_column)

        def convolve(head, carry):
            columns = pl.ds(pl.multiple_of(head * DV, DV), DV)
            raw = sorted_v[:, columns].astype(jnp.float32)
            mixed = tap_v[0:1, columns] * raw
            for tap in range(1, KCONV):
                mixed = mixed + tap_v[tap : tap + 1, columns] * pltpu.roll(raw, tap, 0) * marks[tap]
            values_v[head] = mixed.astype(jnp.bfloat16)
            return carry

        lax.fori_loop(0, heads, convolve, 0)
        stores[3].start()
        gates.relay()
        steps = length // rows_at_once
        lanes = lax.broadcasted_iota(jnp.int32, (1, 128), 1)

        def attend(index, carry):
            head, start = lax.div(index, steps), lax.rem(index, steps) * rows_at_once
            rows = pl.ds(pl.multiple_of(start, rows_at_once), rows_at_once)
            mine = ((lanes >= head * FEAT) & (lanes < head * FEAT + FEAT)).astype(jnp.float32)
            queries = sorted_v[rows, value_width : value_width + 128] * mine.astype(jnp.bfloat16)
            scores = contract_last(queries, sorted_v[:, value_width + 128 :]) * 0.25
            places = start + lax.broadcasted_iota(jnp.int32, scores.shape, 0)
            allowed = (segment_column[rows, :1] == segment_row) & (
                places >= lax.broadcasted_iota(jnp.int32, scores.shape, 1)
            )
            kernel_values = jnp.where(allowed, 1.0 + scores + 0.5 * scores * scores, 0.0)
            denominator = jnp.sum(kernel_values, axis=1, keepdims=True)
            mixed = (
                jnp.dot(kernel_values.astype(jnp.bfloat16), values_v[head], preferred_element_type=jnp.float32)
                / denominator
            )
            outputs_v[head, rows, :] = mixed
            mixer_v[rows, pl.ds(pl.multiple_of(head * DV, DV), DV)] = mixed.astype(jnp.bfloat16)
            return carry

        turns = heads * steps
        for index in range(zs - 1):
            lax.fori_loop(turns * index // (zs - 1), turns * (index + 1) // (zs - 1), attend, 0)
            gather_o.step(index)
        gather_o.finish()
        for copy in stores[4:]:
            copy.start()

        def out_job(index, carry):
            window = pl.ds(pl.multiple_of(index * 512, 512), 512)
            term = jnp.dot(
                mixer_v[...], outs[:, :, window].reshape(value_width, 512), preferred_element_type=jnp.float32
            ).astype(jnp.bfloat16)
            for s in range(seq):
                for h in range(2):
                    begin = s * count + h * half
                    parts[s, h, :, window] = term[begin : begin + half]
            return carry

        lax.fori_loop(0, width // 512, out_job, 0)
        work = SquareSum(at, lambda s, h: parts.at[s, h], sum_scratch)
        work.start()
        work.relay()
        work.finish(lambda h: total.at[h])

        def finish_rows(index, carry):
            for h in range(2):
                window = pl.ds(pl.multiple_of(index * 16, 16), 16)
                rows = pl.ds(pl.multiple_of(h * half + index * 16, 16), 16)
                attended = x_ref[rows, :].astype(jnp.float32) + total[h, window, :]
                attended_out[rows, :] = attended
                normed_out[rows, :] = rms_norm(attended, gain_rows[1:2, :]).astype(jnp.bfloat16)
            return carry

        lax.fori_loop(0, half // 16, finish_rows, 0)
        gates.finish()
        room_store.wait()
        for copy in swaps:
            copy.wait_send()
        for copy in stores:
            copy.wait()

    low, f32 = jnp.bfloat16, jnp.float32
    sorted_width = value_width + 256
    return remote_call(
        kernel,
        "mixer_forward",
        0,
        [
            jax.ShapeDtypeStruct((count, width), f32),
            jax.ShapeDtypeStruct((count, width), low),
            jax.ShapeDtypeStruct((8, width), f32),
            jax.ShapeDtypeStruct((seq, wt, qkv_rank, qkv_width), low),
            jax.ShapeDtypeStruct((wt, out_rank, width), low),
            jax.ShapeDtypeStruct((length, width), low),
            jax.ShapeDtypeStruct((length, sorted_width), low),
            jax.ShapeDtypeStruct((length, value_width), low),
            jax.ShapeDtypeStruct((heads, length, DV), low),
            jax.ShapeDtypeStruct((heads, length, DV), f32),
            jax.ShapeDtypeStruct((2, early, width), low),
            jax.ShapeDtypeStruct((qkv_width, sorted_width), low),
        ],
        [
            pltpu.VMEM((length, width), low),
            pltpu.VMEM((seq, wt, qkv_rank, qkv_width), low),
            pltpu.VMEM((wt, out_rank, width), low),
            pltpu.VMEM((seq, wt * 8, 128), f32),
            pltpu.VMEM((length, width), low),
            pltpu.VMEM((length, sorted_width), low),
            pltpu.VMEM((length, value_width), low),
            pltpu.VMEM((heads, length, DV), low),
            pltpu.VMEM((heads, length, DV), f32),
            pltpu.VMEM((seq, 2, count // 2, width), low),
            pltpu.VMEM((2, count // 2, width), f32),
            pltpu.VMEM((2, early, block), low),
            pltpu.VMEM((qkv_width, sorted_width), low),
            pltpu.VMEM((length, 128), f32),
            pltpu.VMEM((KCONV, value_width), f32),
        ]
        + SquareSum.scratch(seq, (count // 2, width))
        + SquareGather.semaphores(seq)
        + SquareGather.semaphores(seq)
        + LineGather.semaphores(wt) * 3
        + [
            pltpu.SemaphoreType.DMA((seq, 2)),
            pltpu.SemaphoreType.DMA((seq, 2)),
            pltpu.SemaphoreType.DMA((5,)),
            pltpu.SemaphoreType.DMA((8,)),
        ],
        *small,
        gate_up,
        in_specs=[VMEM] * len(small) + [ANY],
        out_specs=[VMEM] * 3 + [ANY] * 9,
    )


def write_order(ref, heads):
    head_width, value_width = 2 * FEAT + DV, heads * DV

    def step(index, carry):
        window = pl.ds(pl.multiple_of(index * 32, 32), 32)
        shape = (32, ref.shape[1])
        column = index * 32 + lax.broadcasted_iota(jnp.int32, shape, 0)
        head = lax.div(column, head_width)
        place = lax.rem(column, head_width)
        target = jnp.where(
            place < FEAT,
            value_width + head * FEAT + place,
            jnp.where(
                place < 2 * FEAT, value_width + 128 + head * FEAT + place - FEAT, head * DV + place - 2 * FEAT
            ),
        )
        hit = target == lax.broadcasted_iota(jnp.int32, shape, 1)
        ref[window, :] = hit.astype(jnp.float32).astype(jnp.bfloat16)
        return carry

    lax.fori_loop(0, ref.shape[0] // 32, step, 0)


def tap_marks(segment_column):
    segment = segment_column[:, :1]
    place = lax.broadcasted_iota(jnp.int32, segment_column.shape, 0)[:, :1]
    marks = [None]
    for tap in range(1, KCONV):
        same = (pltpu.roll(segment_column[...], tap, 0)[:, :1] == segment) & (place >= tap)
        marks.append(same.astype(jnp.float32))
    return marks


def early_rows(units):
    return units * 3 // 4 // 16 * 16


class LinePieces:
    @staticmethod
    def scratch(wt, shape, pieces):
        zs = wt // 2
        return [pltpu.VMEM((zs,) + shape, jnp.bfloat16)] * 3 + [pltpu.SemaphoreType.DMA((6, zs, pieces))]

    def __init__(self, at, part, scratch):
        self.at, self.part = at, part
        self.pair, self.below, self.above, self.sems = scratch
        self.pieces = self.sems.shape[2]
        self.width = self.pair.shape[-1] // self.pieces

    def cut(self, ref, piece):
        if len(ref.shape) == 3:
            return ref.at[piece]
        return ref.at[:, pl.ds(pl.multiple_of(piece * self.width, self.width), self.width)]

    def own(self, z, piece):
        return self.cut(self.part(z * 2 + self.at.c), piece)

    def over(self, z, piece):
        return send(
            self.cut(self.part(z * 2 + 1 - self.at.c), piece),
            self.cut(self.pair.at[z], piece),
            self.sems.at[0, z, piece],
            self.sems.at[1, z, piece],
            self.at.partner(),
        )

    def up(self, z, piece):
        return send(
            self.own(z, piece),
            self.cut(self.below.at[z], piece),
            self.sems.at[2, z, piece],
            self.sems.at[3, z, piece],
            self.at.level(self.at.z + 1),
        )

    def down(self, z, piece):
        return send(
            self.own(z, piece),
            self.cut(self.above.at[z], piece),
            self.sems.at[4, z, piece],
            self.sems.at[5, z, piece],
            self.at.level(self.at.z - 1),
        )

    def terms(self, z, piece):
        self.over(z, piece).wait_recv()
        return [self.own(z, piece), self.cut(self.pair.at[z], piece)]

    def ends(self, z, piece):
        at = self.at

        @pl.when((at.z == 0) & (z > 0))
        def _():
            add_into(self.own(z, piece), self.terms(z, piece))
            self.up(z, piece).start()

        @pl.when((at.z == at.zs - 1) & (z < at.zs - 1))
        def _():
            add_into(self.own(z, piece), self.terms(z, piece))
            self.down(z, piece).start()

    def begin(self):
        zs = self.at.zs

        def pairs(piece, carry):
            for index in range(zs // 2):
                self.over(index, piece).start()
                self.over(zs - 1 - index, piece).start()
            return carry

        lax.fori_loop(0, self.pieces, pairs, 0)

        def starts(index, carry):
            piece = lax.rem(index, self.pieces)
            far = zs - 1 - lax.div(index, self.pieces)
            self.ends(jnp.where(self.at.z == 0, far, zs - 1 - far), piece)
            return carry

        lax.fori_loop(0, (zs - 1) * self.pieces, starts, 0)

    def pass_on(self, index, fill=None):
        at = self.at
        upper = at.z * 2 >= at.zs
        high, low = index, at.zs - 1 - index

        def lower(piece, when):
            @pl.when((at.z > low) & (at.z < at.zs - 1) & when)
            def _():
                terms = self.terms(low, piece)
                self.down(low, piece).wait_recv()
                add_into(self.own(low, piece), terms + [self.cut(self.above.at[low], piece)])
                self.down(low, piece).start()

        def step(piece, carry):
            lower(piece, upper)

            @pl.when((at.z < high) & (at.z > 0))
            def _():
                terms = self.terms(high, piece)
                self.up(high, piece).wait_recv()
                add_into(self.own(high, piece), terms + [self.cut(self.below.at[high], piece)])
                self.up(high, piece).start()

            lower(piece, jnp.logical_not(upper))
            if fill is not None:
                fill(piece, self.pieces)
            return carry

        lax.fori_loop(0, self.pieces, step, 0)

    def finish(self, total):
        at = self.at

        def step(piece, carry):
            terms = self.terms(at.z, piece)
            below, above = self.cut(self.below.at[at.z], piece), self.cut(self.above.at[at.z], piece)

            @pl.when(at.z == 0)
            def _():
                self.down(at.z, piece).wait_recv()
                add_into(self.cut(total, piece), terms + [above])

            @pl.when(at.z == at.zs - 1)
            def _():
                self.up(at.z, piece).wait_recv()
                add_into(self.cut(total, piece), terms + [below])

            @pl.when((at.z > 0) & (at.z < at.zs - 1))
            def _():
                self.up(at.z, piece).wait_recv()
                self.down(at.z, piece).wait_recv()
                add_into(self.cut(total, piece), terms + [below, above])

            for z in range(at.zs):

                @pl.when(at.z < z)
                def _():
                    self.up(z, piece).wait_send()

                @pl.when(at.z > z)
                def _():
                    self.down(z, piece).wait_send()

                self.over(z, piece).wait_send()
            return carry

        lax.fori_loop(0, self.pieces, step, 0)


class SquareTerms:
    @staticmethod
    def semaphores(seq):
        return [pltpu.SemaphoreType.DMA((seq // 2, 2)), pltpu.SemaphoreType.DMA((seq // 2, 2, 2))]

    @staticmethod
    def scratch(seq, half_shape):
        ys = seq // 2
        return [
            pltpu.VMEM((ys,) + half_shape, jnp.bfloat16),
            pltpu.VMEM(half_shape, jnp.bfloat16),
            pltpu.SemaphoreType.DMA((ys + 1, 2)),
        ]

    def __init__(self, at, terms, from_x, from_y, sems=None, lasts=None, scratch=None):
        self.at, self.terms, self.from_x, self.from_y = at, terms, from_x, from_y
        if sems is not None:
            self.xs, self.ys = sems
        if scratch is not None:
            self.last_y, self.last_x = lasts
            self.sum_y, self.sum_x, self.last = scratch

    def first_x(self, y):
        at = self.at
        return send(
            self.terms(y * 2 + 1 - at.x, 0), self.from_x.at[y], self.xs.at[y, 0], self.xs.at[y, 1], at.across()
        )

    def first_y(self, step, x):
        at = self.at
        y = at.beside(step)
        return send(
            self.terms(y * 2 + x, 1),
            self.from_y.at[at.y, x],
            self.ys.at[step, x, 0],
            self.ys.at[at.y, x, 1],
            at.column(y),
        )

    def first_start(self):
        for y in range(self.at.ys):
            self.first_x(y).start()
        for step in range(1, self.at.ys):
            for x in range(2):
                self.first_y(step, x).start()

    def first_wait(self):
        at = self.at
        for y in range(at.ys):
            self.first_x(y).wait()
        for step in range(1, at.ys):
            y = at.beside(step)
            for x in range(2):
                self.first_y(step, x).wait_send()
                slot = self.from_y.at[y, x]
                send(slot, slot, self.ys.at[step, x, 0], self.ys.at[y, x, 1], at.across()).wait_recv()

    def second_y(self, step):
        at = self.at
        y = at.beside(step)
        return send(
            self.sum_y.at[y], self.last_y.at[at.y], self.last.at[step, 0], self.last.at[at.y, 1], at.column(y)
        )

    def second_x(self):
        at = self.at
        return send(self.sum_x, self.last_x, self.last.at[at.ys, 0], self.last.at[at.ys, 1], at.across())

    def second_start(self, fetch, rooms):
        at = self.at
        for step in range(1, at.ys):
            y = at.beside(step)
            fetch([(self.terms(y * 2 + at.x, 0), rooms[0]), (self.from_x.at[y], rooms[1])])
            add_into(self.sum_y.at[y], [rooms[0], rooms[1]])
        fetch([(self.terms(at.y * 2 + 1 - at.x, 1), self.sum_x)])
        for step in range(1, at.ys):
            y = at.beside(step)
            fetch([(self.from_y.at[y, 1 - at.x], rooms[0])])
            add_into(self.sum_x, [self.sum_x, rooms[0]])

    def second_load(self, fetch):
        at = self.at
        pairs = [(self.terms(at.y * 2 + 1 - at.x, 1), self.sum_x)]
        for step in range(1, at.ys):
            y = at.beside(step)
            pairs.append((self.terms(y * 2 + at.x, 0), self.sum_y.at[y]))
        fetch(pairs)

    def second_arrived(self):
        at = self.at
        terms = [self.sum_x]
        for step in range(1, at.ys):
            y = at.beside(step)
            add_into(self.sum_y.at[y], [self.sum_y.at[y], self.from_x.at[y]])
            terms.append(self.from_y.at[y, 1 - at.x])
        add_into(self.sum_x, terms)

    def second_go(self):
        for step in range(1, self.at.ys):
            self.second_y(step).start()
        self.second_x().start()

    def second_wait(self):
        at = self.at
        for step in range(1, at.ys):
            self.second_y(step).wait_send()
            y = at.beside(step)
            slot = self.last_y.at[y]
            send(slot, slot, self.last.at[step, 0], self.last.at[y, 1], at.across()).wait_recv()
        self.second_x().wait()


def norm_back(rows, load, store, gain, terms):
    def step(index, carry):
        window = pl.ds(pl.multiple_of(index * 16, 16), 16)
        values, incoming, base = load(window)
        root = lax.rsqrt(jnp.mean(values * values, axis=-1, keepdims=True) + epsilon)
        scaled = incoming * gain
        share = jnp.mean(values * scaled, axis=-1, keepdims=True)
        store(window, base + root * scaled - values * (root * root * root * share))
        term = incoming * values * root
        terms[...] += term[:8] + term[8:]
        return carry

    lax.fori_loop(0, rows // 16, step, 0)


def exchange(
    at, shard, everyone, gather_sems, local, sums, first, second, total, ready, wait_for_ready, fill=None
):
    count = shard.shape[0]
    gather = LineGather(
        at, lambda w: everyone.at[pl.ds(pl.multiple_of(w * count, count), count)], gather_sems
    )
    gather.start(shard)
    own = pltpu.make_async_copy(
        shard, everyone.at[pl.ds(pl.multiple_of(at.w * count, count), count)], local
    )
    own.start()
    own.wait()
    ready[0]()
    last = 2 * (at.zs - 1)
    late = 3 if wait_for_ready else 0

    def turn(index, carry):
        fresh = index <= last
        place = jnp.where(fresh, index, jnp.where(index == last + 3, 0, index - last))
        far, side = lax.div(place + 1, 2), lax.rem(place, 2)
        z = at.z + jnp.where(side == 1, -far, far)
        valid = (z >= 0) & (z < at.zs)

        @pl.when(fresh & (side == 1))
        def _():
            gather.step(far - 1)

        @pl.when(fresh & valid)
        def _():
            gather.wait_over(z)
            first(z)

        if wait_for_ready:

            @pl.when(index == late)
            def _():
                ready[1]()

        @pl.when(valid & (index >= late))
        def _():
            def step(piece, inner):
                second(z, piece)
                sums.over(z, piece).start()

                @pl.when(piece > 0)
                def _():
                    sums.ends(z, piece - 1)

                return inner

            lax.fori_loop(0, sums.pieces, step, 0)
            sums.ends(z, sums.pieces - 1)

        return carry

    lax.fori_loop(0, last + 1 + late, turn, 0)
    if fill is not None:
        fill(None, PIECES)
    for index in range(2, at.zs):
        sums.pass_on(index, fill if index == 2 else None)
    sums.finish(total)
    gather.sent()


PIECES = 4


def feed_forward(normed, attended, teacher, lengths, gate_early, gate_up_shard, down_shard):
    seq, wt = lax.axis_size("seq"), lax.axis_size("wt")
    count, width = normed.shape
    units, block = gate_up_shard.shape[1:]
    early = early_rows(units)
    columns = down_shard.shape[1]
    tokens = wt * count
    zs = wt // 2
    half = units // 2

    def kernel(*refs):
        (normed_ref, attended_ref, teacher_ref, length_ref, early_ref, gate_shard_ref, shard_ref), refs = refs[:7], refs[7:]
        (final_out, error_out, energy_out), refs = refs[:3], refs[3:]
        (normed_out, gate_out, up_out, active_out, down_out, gates_out), refs = refs[:6], refs[6:]
        (everyone, gates, downs, gate_all, up_all, active_all, parts, total), refs = refs[:8], refs[8:]
        gather_sems, sum_scratch, late_sems, square_sems, (local, outgoing) = (
            refs[:1],
            refs[1:5],
            refs[5:8],
            refs[8:11],
            refs[11:],
        )
        at = Place(seq, wt)
        loads = [
            pltpu.make_async_copy(early_ref, gates.at[:, pl.ds(0, early)], local.at[4]),
            pltpu.make_async_copy(
                gate_shard_ref.at[:, pl.ds(early, units - early)],
                gates.at[:, pl.ds(early, units - early), pl.ds(pl.multiple_of(at.s * block, block), block)],
                local.at[0],
            ),
        ]
        for load in loads:
            load.start()
        at.meet(True, True)
        late = SquareGather(
            at,
            lambda s, h: gates.at[
                h, pl.ds(early, units - early), pl.ds(pl.multiple_of(s * block, block), block)
            ],
            lambda h: gate_shard_ref.at[h, pl.ds(early, units - early)],
            late_sems,
        )
        weights = SquareGather(
            at,
            lambda s, h: downs.at[
                pl.ds(h * half, half), pl.ds(pl.multiple_of(s * columns, columns), columns)
            ],
            lambda h: shard_ref.at[pl.ds(h * half, half)],
            square_sems,
        )
        sums = LinePieces(
            at, lambda w: parts.at[pl.ds(pl.multiple_of(w * count, count), count)], sum_scratch
        )
        down_store = pltpu.make_async_copy(downs, down_out, local.at[2])
        gates_store = pltpu.make_async_copy(gates, gates_out, local.at[0])

        def ready_first():
            late.start()
            own = pltpu.make_async_copy(
                shard_ref, downs.at[:, pl.ds(pl.multiple_of(at.s * columns, columns), columns)], local.at[3]
            )
            own.start()
            late.relay()
            weights.start()
            own.wait()
            for load in loads:
                load.wait()
            late.finish()
            gates_store.start()

        def ready_later():
            weights.relay()
            weights.finish()
            down_store.start()

        def rows(z):
            return pl.ds(pl.multiple_of(z * 2 * count, 2 * count), 2 * count)

        def stores(z):
            return [
                pltpu.make_async_copy(source.at[rows(z)], target.at[rows(z)], outgoing.at[index, z])
                for index, (source, target) in enumerate(
                    ((everyone, normed_out), (gate_all, gate_out), (up_all, up_out), (active_all, active_out))
                )
            ]

        def first(z):
            here = everyone[rows(z), :]
            gate = contract_last(here, gates[0])
            up = contract_last(here, gates[1])
            gate_all[rows(z), :] = gate
            up_all[rows(z), :] = up
            active_all[rows(z), :] = gated_unit(gate, up).astype(jnp.bfloat16)
            for copy in stores(z):
                copy.start()

        def second(z, piece):
            window = pl.ds(pl.multiple_of(piece * sums.width, sums.width), sums.width)
            parts[rows(z), window] = jnp.dot(
                active_all[rows(z), :], downs[:, window], preferred_element_type=jnp.float32
            ).astype(jnp.bfloat16)

        exchange(
            at,
            normed_ref,
            everyone,
            gather_sems,
            local.at[1],
            sums,
            first,
            second,
            total,
            (ready_first, ready_later),
            True,
        )
        energy_out[...] = jnp.zeros_like(energy_out)
        valid = length_ref[at.w]

        def finish_rows(index, carry):
            window = pl.ds(pl.multiple_of(index * 16, 16), 16)
            final = attended_ref[window, :] + total[window, :]
            final_out[window, :] = final.astype(jnp.bfloat16)
            place = at.s * count + index * 16 + lax.broadcasted_iota(jnp.int32, final.shape, 0)
            keep = (place < valid).astype(jnp.float32)
            error = (final - teacher_ref[window, :].astype(jnp.float32)) * keep
            error_out[window, :] = error
            squares = error * error
            energy_out[...] += 0.5 * (squares[:8] + squares[8:])
            return carry

        lax.fori_loop(0, count // 16, finish_rows, 0)
        down_store.wait()
        gates_store.wait()
        for z in range(zs):
            for copy in stores(z):
                copy.wait()

    low, f32 = jnp.bfloat16, jnp.float32
    return remote_call(
        kernel,
        "feed_forward",
        2,
        [
            jax.ShapeDtypeStruct((count, width), low),
            jax.ShapeDtypeStruct((count, width), f32),
            jax.ShapeDtypeStruct((8, width), f32),
            jax.ShapeDtypeStruct((tokens, width), low),
            jax.ShapeDtypeStruct((tokens, units), f32),
            jax.ShapeDtypeStruct((tokens, units), f32),
            jax.ShapeDtypeStruct((tokens, units), low),
            jax.ShapeDtypeStruct((units, width), low),
            jax.ShapeDtypeStruct((2, units, width), low),
        ],
        [
            pltpu.VMEM((tokens, width), low),
            pltpu.VMEM((2, units, width), low),
            pltpu.VMEM((units, width), low),
            pltpu.VMEM((tokens, units), f32),
            pltpu.VMEM((tokens, units), f32),
            pltpu.VMEM((tokens, units), low),
            pltpu.VMEM((tokens, width), low),
            pltpu.VMEM((count, width), f32),
        ]
        + LineGather.semaphores(wt, 2)
        + LinePieces.scratch(wt, (count, width), PIECES)
        + SquareGather.semaphores(seq)
        + SquareGather.semaphores(seq)
        + [pltpu.SemaphoreType.DMA((5,)), pltpu.SemaphoreType.DMA((4, zs))],
        normed,
        attended,
        teacher,
        lengths,
        gate_early,
        gate_up_shard,
        down_shard,
        in_specs=[VMEM] * 3 + [SMEM] + [ANY] * 2 + [VMEM],
        out_specs=[VMEM] * 3 + [ANY] * 6,
    )


def feed_back(error, attended, gain, gate_up, down, gate, up, active, normed):
    seq, wt = lax.axis_size("seq"), lax.axis_size("wt")
    count, width = error.shape
    units = gate_up.shape[1]
    tokens = wt * count
    ys = seq // 2
    block = width // seq
    half = (units // 2, block)

    def kernel(*refs):
        (error_ref, attended_ref, gain_ref, gate_up_ref, down_ref, gate_ref, up_ref, active_ref, normed_ref), refs = (
            refs[:9],
            refs[9:],
        )
        (grad_ref, mix_ref, gain_terms), refs = refs[:3], refs[3:]
        (gate_out, up_out, down_out, gate_x, gate_y, down_x, down_y), refs = refs[:7], refs[7:]
        (low, everyone, gates, downs, gate_all, up_all, back_all, parts, actives, columns), refs = refs[:10], refs[10:]
        (gate_terms, up_terms, down_terms, total), refs = refs[:4], refs[4:]
        gather_sems, sum_scratch, gate_sems, down_sems, (local, outgoing) = (
            refs[:1],
            refs[1:5],
            refs[5:7],
            refs[7:9],
            refs[9:],
        )
        at = Place(seq, wt)
        loads = [
            pltpu.make_async_copy(source, target, local.at[index])
            for index, (source, target) in enumerate(
                (
                    (down_ref, downs),
                    (gate_ref, gate_all),
                    (up_ref, up_all),
                    (gate_up_ref, gates),
                    (active_ref, actives),
                )
            )
        ]
        for load in loads:
            load.start()
        at.meet(True, True)
        low[...] = error_ref[...].astype(jnp.bfloat16)
        sums = LinePieces(
            at, lambda w: parts.at[pl.ds(pl.multiple_of(w * count, count), count)], sum_scratch
        )
        gate_sum = SquareTerms(at, lambda s, h: gate_terms.at[s, h], gate_x, gate_y, gate_sems)
        down_sum = SquareTerms(at, lambda s, h: down_terms.at[s, h], down_x, down_y, down_sems)

        def place(index):
            step = lax.div(index, 2) + 1
            x = lax.rem(at.x + 1 + lax.rem(index, 2), 2)
            return step, x, at.beside(step) * 2 + x

        def column_load(index):
            s = place(index)[2]
            return pltpu.make_async_copy(
                normed_ref.at[:, pl.ds(pl.multiple_of(s * block, block), block)],
                columns.at[lax.rem(index, 2)],
                local.at[6 + lax.rem(index, 2)],
            )

        def leave(sum_, index):
            step, x, s = place(index)

            @pl.when(x != at.x)
            def _():
                sum_.first_x(lax.div(s, 2)).start()

            @pl.when(step < ys)
            def _():
                sum_.first_y(step, x).start()

        def down_job(index):
            s = place(index)[2]
            term = contract_first(
                actives[...], everyone[:, pl.ds(pl.multiple_of(s * block, block), block)]
            ).astype(jnp.bfloat16)
            down_terms[s, 0] = term[: units // 2]
            down_terms[s, 1] = term[units // 2 :]
            leave(down_sum, index)

        def gate_job(index):
            s = place(index)[2]
            column_load(index).wait()
            here = columns.at[lax.rem(index, 2)]
            for number, terms in enumerate((gate_terms, up_terms)):
                term = contract_first(back_all[number], here[...]).astype(jnp.bfloat16)
                terms[s, 0] = term[: units // 2]
                terms[s, 1] = term[units // 2 :]

            @pl.when(index + 2 < seq)
            def _():
                column_load(index + 2).start()

            leave(gate_sum, index)

        def fill(slot, slots):
            if slot is None:
                lax.fori_loop(0, seq, lambda index, carry: (down_job(index), carry)[1], 0)
                return

            def step(index, carry):
                gate_job(slot * (seq // slots) + index)
                return carry

            lax.fori_loop(0, seq // slots, step, 0)

        def ready_first():
            column_load(0).start()
            column_load(1).start()
            for load in loads:
                load.wait()

        def rows(z):
            return pl.ds(pl.multiple_of(z * 2 * count, 2 * count), 2 * count)

        def first(z):
            active_back = contract_last(everyone[rows(z), :], downs[...])
            gate_here, up_here = gate_all[rows(z), :], up_all[rows(z), :]
            share = jax.nn.sigmoid(gate_here)
            back_all[0, rows(z), :] = (
                active_back * up_here * share * (1.0 + gate_here * (1.0 - share))
            ).astype(jnp.bfloat16)
            back_all[1, rows(z), :] = (active_back * gate_here * share).astype(jnp.bfloat16)

        def second(z, piece):
            window = pl.ds(pl.multiple_of(piece * sums.width, sums.width), sums.width)
            parts[rows(z), window] = (
                jnp.dot(back_all[0, rows(z), :], gates[0, :, window], preferred_element_type=jnp.float32)
                + jnp.dot(back_all[1, rows(z), :], gates[1, :, window], preferred_element_type=jnp.float32)
            ).astype(jnp.bfloat16)

        exchange(
            at,
            low,
            everyone,
            gather_sems,
            local.at[5],
            sums,
            first,
            second,
            total,
            (ready_first,),
            False,
            fill,
        )
        stores = [
            pltpu.make_async_copy(source, target, outgoing.at[index])
            for index, (source, target) in enumerate(
                ((gate_terms, gate_out), (up_terms, up_out), (down_terms, down_out))
            )
        ]
        for copy in stores:
            copy.start()
        gain_terms[...] = jnp.zeros_like(gain_terms)

        def load_rows(window):
            return attended_ref[window, :], total[window, :], error_ref[window, :]

        def store_rows(window, value):
            grad_ref[window, :] = value
            mix_ref[window, :] = value.astype(jnp.bfloat16)

        norm_back(count, load_rows, store_rows, gain_ref[1:2, :], gain_terms)
        for copy in stores:
            copy.wait()
        gate_sum.first_wait()
        down_sum.first_wait()

    def terms_of(half):
        return jax.ShapeDtypeStruct((seq, 2) + half, jnp.bfloat16)

    def first_of(half):
        return [
            jax.ShapeDtypeStruct((ys,) + half, jnp.bfloat16),
            jax.ShapeDtypeStruct((ys, 2) + half, jnp.bfloat16),
        ]

    return remote_call(
        kernel,
        "feed_back",
        3,
        [
            jax.ShapeDtypeStruct((count, width), jnp.float32),
            jax.ShapeDtypeStruct((count, width), jnp.bfloat16),
            jax.ShapeDtypeStruct((8, width), jnp.float32),
            terms_of(half),
            terms_of(half),
            terms_of(half),
        ]
        + first_of(half)
        + first_of(half),
        [
            pltpu.VMEM((count, width), jnp.bfloat16),
            pltpu.VMEM((tokens, width), jnp.bfloat16),
            pltpu.VMEM(gate_up.shape, jnp.bfloat16),
            pltpu.VMEM((units, width), jnp.bfloat16),
            pltpu.VMEM((tokens, units), jnp.float32),
            pltpu.VMEM((tokens, units), jnp.float32),
            pltpu.VMEM((2, tokens, units), jnp.bfloat16),
            pltpu.VMEM((tokens, width), jnp.bfloat16),
            pltpu.VMEM((tokens, units), jnp.bfloat16),
            pltpu.VMEM((2, tokens, block), jnp.bfloat16),
            pltpu.VMEM((seq, 2) + half, jnp.bfloat16),
            pltpu.VMEM((seq, 2) + half, jnp.bfloat16),
            pltpu.VMEM((seq, 2) + half, jnp.bfloat16),
            pltpu.VMEM((count, width), jnp.float32),
        ]
        + LineGather.semaphores(wt, 2)
        + LinePieces.scratch(wt, (count, width), PIECES)
        + SquareTerms.semaphores(seq)
        + SquareTerms.semaphores(seq)
        + [pltpu.SemaphoreType.DMA((8,)), pltpu.SemaphoreType.DMA((3,))],
        error,
        attended,
        gain,
        gate_up,
        down,
        gate,
        up,
        active,
        normed,
        in_specs=[VMEM] * 3 + [ANY] * 6,
        out_specs=[VMEM] * 3 + [ANY] * 7,
    )


def mixer_back(
    mix_back,
    attended_grad,
    tokens,
    gain,
    out_rows,
    qkv_columns,
    hidden,
    sorted_columns,
    mixer,
    mixed_values,
    head_outputs,
    segments,
    taps,
    order,
    gain_terms,
    energy,
    gate_parts,
    up_parts,
    down_parts,
):
    seq, wt = lax.axis_size("seq"), lax.axis_size("wt")
    zs, ys = wt // 2, seq // 2
    count, width = mix_back.shape
    length = count * seq
    heads = mixed_values.shape[0]
    qkv_width = qkv_columns.shape[1]
    value_width = heads * DV
    rank = width // (seq * wt)
    gate_half, down_half = gate_parts[0].shape[2:], down_parts[0].shape[2:]
    rows_at_once = 256
    big = [out_rows, qkv_columns, hidden, sorted_columns, mixer, mixed_values, head_outputs]
    small = [mix_back, attended_grad, tokens, gain, segments, taps, order, gain_terms, energy]
    far = list(gate_parts) + list(down_parts) + list(up_parts)

    def kernel(*refs):
        big_refs, refs = refs[: len(big)], refs[len(big) :]
        small_refs, refs = refs[: len(small)], refs[len(small) :]
        (gate_t, gate_x, gate_y, down_t, down_x, down_y, up_t), refs = refs[: len(far)], refs[len(far) :]
        (grad_out, sums_out, qkv_out, w_out_out, up_x, up_y), refs = refs[:6], refs[6:]
        gate_lasts, up_lasts, down_lasts, refs = refs[:2], refs[2:4], refs[4:6], refs[6:]
        (w_out_v, w_qkv_v, hidden_v, sorted_v, mixer_v, values_v, outputs_v), refs = refs[:7], refs[7:]
        (mix_all, mixer_grad, query_acc, key_acc, value_acc, back_sorted, back_v), refs = refs[:7], refs[7:]
        (hidden_parts, qkv_parts, out_parts, hidden_total, gain_acc, spread, taps_acc), refs = refs[:7], refs[7:]
        (segment_column, tap_v), refs = refs[:2], refs[2:]
        (room_gate0, room_gate1, room_down0, room_down1, qkv_sum, first, middle, last), refs = refs[:8], refs[8:]
        hidden_scratch, refs = refs[:8], refs[8:]
        qkv_scratch, out_scratch, refs = refs[:4], refs[4:8], refs[8:]
        gate_scratch, down_scratch, up_scratch, refs = refs[:3], refs[3:6], refs[6:9], refs[9:]
        gather_sems, up_sems, refs = refs[:3], refs[3:5], refs[5:]
        local, swap, first_sems, last_sems = refs
        (
            mix_ref,
            grad_ref,
            token_ref,
            gain_ref,
            segment_ref,
            tap_ref,
            order_ref,
            gain_two,
            energy_ref,
        ) = small_refs
        at = Place(seq, wt)
        loads = [
            pltpu.make_async_copy(source, target, local.at[4 + index])
            for index, (source, target) in enumerate(
                zip(big_refs, (w_out_v, w_qkv_v, hidden_v, sorted_v, mixer_v, values_v, outputs_v))
            )
        ]
        for load in loads:
            load.start()
        at.meet(True, True)
        half = count // 2
        gather = SquareGather(
            at,
            lambda s, h: mix_all.at[pl.ds(pl.multiple_of(s * count + h * half, half), half)],
            lambda h: mix_ref.at[pl.ds(h * half, half)],
            gather_sems,
        )
        gather.start()
        own = pltpu.make_async_copy(
            mix_ref, mix_all.at[pl.ds(pl.multiple_of(at.s * count, count), count)], local.at[3]
        )
        own.start()

        def fetch(pairs):
            copies = [
                pltpu.make_async_copy(source, target, local.at[index])
                for index, (source, target) in enumerate(pairs)
            ]
            for copy in copies:
                copy.start()
            for copy in copies:
                copy.wait()

        gate_sum = SquareTerms(at, lambda s, h: gate_t.at[s, h], gate_x, gate_y, None, gate_lasts, gate_scratch)
        down_sum = SquareTerms(at, lambda s, h: down_t.at[s, h], down_x, down_y, None, down_lasts, down_scratch)
        up_sum = SquareTerms(at, lambda s, h: up_t.at[s, h], up_x, up_y, up_sems, up_lasts, up_scratch)
        gate_rooms, down_rooms = (room_gate0, room_gate1), (room_down0, room_down1)
        gate_sum.second_start(fetch, gate_rooms)
        down_sum.second_start(fetch, down_rooms)
        up_sum.second_load(fetch)
        tap_v[...] = tap_ref[...].astype(jnp.float32)
        segment_row = segment_ref[...].astype(jnp.float32)
        segment_column[...] = jnp.broadcast_to(segment_row, (128, length)).T
        own.wait()
        for load in loads:
            load.wait()
        query_acc[...] = jnp.zeros_like(query_acc)
        key_acc[...] = jnp.zeros_like(key_acc)
        value_acc[...] = jnp.zeros_like(value_acc)
        gather.relay()
        gather.finish()
        gate_sum.second_go()
        down_sum.second_go()
        up_sum.first_start()
        mixer_grad[...] = contract_last(mix_all[...], w_out_v[...]).astype(jnp.bfloat16)
        out_sum = LinePieces(at, lambda w: out_parts.at[w], out_scratch)
        out_rank = out_parts.shape[1]
        out_block = 512 if value_width % 512 == 0 else value_width

        def out_job(index, carry):
            window = pl.ds(pl.multiple_of(index * 512, 512), 512)
            term = contract_first(mixer_v[...], mix_all[:, window]).astype(jnp.bfloat16)
            for w in range(wt):
                out_parts[w, :, window] = term[w * out_rank : (w + 1) * out_rank]
            return carry

        lax.fori_loop(0, width // 512, out_job, 0)
        out_sum.begin()

        steps = length // rows_at_once
        lanes = lax.broadcasted_iota(jnp.int32, (1, 128), 1)

        def attend(index, carry):
            head, start = lax.div(index, steps), lax.rem(index, steps) * rows_at_once
            rows = pl.ds(pl.multiple_of(start, rows_at_once), rows_at_once)
            columns = pl.ds(pl.multiple_of(head * DV, DV), DV)
            mine = ((lanes >= head * FEAT) & (lanes < head * FEAT + FEAT)).astype(jnp.float32)
            queries = sorted_v[rows, value_width : value_width + 128] * mine.astype(jnp.bfloat16)
            keys = sorted_v[:, value_width + 128 :]
            scores = contract_last(queries, keys) * 0.25
            places = start + lax.broadcasted_iota(jnp.int32, scores.shape, 0)
            allowed = (segment_column[rows, :1] == segment_row) & (
                places >= lax.broadcasted_iota(jnp.int32, scores.shape, 1)
            )
            kernel_values = jnp.where(allowed, 1.0 + scores + 0.5 * scores * scores, 0.0)
            denominator = jnp.sum(kernel_values, axis=1, keepdims=True)
            incoming = mixer_grad[rows, columns].astype(jnp.float32)
            numerator_back = (incoming / denominator).astype(jnp.bfloat16)
            denominator_back = (
                -jnp.sum(incoming * outputs_v[head, rows, :], axis=1, keepdims=True) / denominator
            )
            weight_back = contract_last(numerator_back, values_v[head])
            kernel_back = jnp.where(allowed, weight_back + denominator_back, 0.0)
            dots_back = (0.25 * kernel_back * (1.0 + scores)).astype(jnp.bfloat16)
            query_acc[rows, :] += jnp.dot(dots_back, keys, preferred_element_type=jnp.float32) * mine
            key_acc[...] += contract_first(dots_back, queries)
            value_acc[:, columns] += contract_first(kernel_values.astype(jnp.bfloat16), numerator_back)
            return carry

        middle_step = heads * steps // 2
        lax.fori_loop(0, middle_step, attend, 0)
        for index in range(zs - 1, 1, -1):
            if index == zs // 2:
                lax.fori_loop(middle_step, heads * steps, attend, 0)
            out_sum.pass_on(index)
        taps_acc[...] = jnp.zeros_like(taps_acc)
        marks = tap_marks(segment_column)

        def convolve(head, carry):
            columns = pl.ds(pl.multiple_of(head * DV, DV), DV)
            mixed_back = value_acc[:, columns]
            raw = sorted_v[:, columns].astype(jnp.float32)
            raw_back = tap_v[0:1, columns] * mixed_back
            taps_acc[3:4, columns] = jnp.sum(mixed_back * raw, axis=0, keepdims=True)
            for tap in range(1, KCONV):
                masked = mixed_back * marks[tap]
                taps_acc[3 + tap : 4 + tap, columns] = jnp.sum(
                    masked * pltpu.roll(raw, tap, 0), axis=0, keepdims=True
                )
                raw_back = raw_back + tap_v[tap : tap + 1, columns] * pltpu.roll(masked, length - tap, 0)
            back_sorted[:, columns] = raw_back.astype(jnp.bfloat16)
            return carry

        lax.fori_loop(0, heads, convolve, 0)
        back_sorted[:, value_width : value_width + 128] = query_acc[...].astype(jnp.bfloat16)
        back_sorted[:, value_width + 128 :] = key_acc[...].astype(jnp.bfloat16)
        back_v[...] = contract_last(back_sorted[...], order_ref[...]).astype(jnp.bfloat16)
        hidden_sum = SquareSum(at, lambda s, h: hidden_parts.at[s, h], hidden_scratch)

        def hidden_job(index, carry):
            window = pl.ds(pl.multiple_of(index * 512, 512), 512)
            term = contract_last(back_v[...], w_qkv_v[window, :]).astype(jnp.bfloat16)
            for s in range(seq):
                for h in range(2):
                    begin = s * count + h * half
                    hidden_parts[s, h, :, window] = term[begin : begin + half]
            return carry

        lax.fori_loop(0, width // 512, hidden_job, 0)
        hidden_sum.start()
        qkv_sums = LinePieces(at, lambda w: qkv_parts.at[:, w], qkv_scratch)
        qkv_rank = qkv_parts.shape[2]

        def qkv_job(s, carry):
            block = wt * qkv_rank
            window = pl.ds(pl.multiple_of(s * block, block), block)
            term = contract_first(hidden_v[:, window], back_v[...]).astype(jnp.bfloat16)
            for w in range(wt):
                qkv_parts[s, w] = term[w * qkv_rank : (w + 1) * qkv_rank]
            return carry

        lax.fori_loop(0, seq, qkv_job, 0)
        qkv_sums.begin()
        qkv_sums.pass_on(zs - 1)
        hidden_sum.relay()
        up_sum.first_wait()
        up_sum.second_arrived()
        up_sum.second_go()
        for index in range(zs - 2, 1, -1):
            qkv_sums.pass_on(index)
        hidden_sum.finish(lambda h: hidden_total.at[h])
        gain_acc[...] = jnp.zeros_like(gain_acc)
        for h in range(2):

            def shift(window):
                return pl.ds(pl.multiple_of(h * half + window.start, 16), 16)

            def load_rows(window):
                rows = shift(window)
                return token_ref[rows, :].astype(jnp.float32), hidden_total[h, window, :], grad_ref[rows, :]

            def store_rows(window, value):
                grad_out[shift(window), :] = value

            norm_back(half, load_rows, store_rows, gain_ref[0:1, :], gain_acc)
        spread[...] = jnp.zeros_like(spread)
        spread[0:1, :] = jnp.sum(gain_acc[...], axis=0, keepdims=True)
        spread[1:2, :] = jnp.sum(gain_two[...], axis=0, keepdims=True)
        energy = jnp.sum(jnp.sum(energy_ref[...], axis=0, keepdims=True), axis=1, keepdims=True)
        spread[2:3, :] = jnp.broadcast_to(energy, (1, width))
        copies = []
        for step in range(1, seq):
            to = lax.rem(at.s + step, seq)
            window = pl.ds(pl.multiple_of(to * value_width, value_width), value_width)
            copies.append(
                send(spread.at[:, window], first.at[at.s], first_sems.at[step, 0], first_sems.at[at.s, 1], (to, at.w))
            )
        for copy in copies:
            copy.start()
        qkv_sums.finish(qkv_sum)
        for step in range(1, seq):
            to = lax.rem(at.s + step, seq)
            copy = send(qkv_sum.at[to], qkv_out.at[at.s], swap.at[step, 0], swap.at[at.s, 1], (to, at.w))
            copy.start()
            copies.append(copy)
        add_into(qkv_out.at[at.s], [qkv_sum.at[at.s]])
        out_sum.finish(w_out_out)
        terms = [spread.at[:, pl.ds(pl.multiple_of(at.s * value_width, value_width), value_width)], taps_acc]
        for step in range(1, seq):
            s = lax.rem(at.s + step, seq)
            slot = first.at[s]
            send(slot, slot, first_sems.at[step, 0], first_sems.at[s, 1], at.across()).wait_recv()
            terms.append(slot)
        add_into(middle, terms)
        for step in range(1, wt):
            to = lax.rem(at.w + step, wt)
            copy = send(middle, last.at[at.w], last_sems.at[step, 0], last_sems.at[at.w, 1], (at.s, to))
            copy.start()
            copies.append(copy)
        gate_sum.second_wait()
        down_sum.second_wait()
        terms = [middle]
        for step in range(1, wt):
            w = lax.rem(at.w + step, wt)
            slot = last.at[w]
            send(slot, slot, last_sems.at[step, 0], last_sems.at[w, 1], at.partner()).wait_recv()
            terms.append(slot)
        add_into(sums_out, terms)
        for step in range(1, seq):
            s = lax.rem(at.s + step, seq)
            slot = qkv_out.at[s]
            send(slot, slot, swap.at[step, 0], swap.at[s, 1], at.across()).wait_recv()
        up_sum.second_wait()
        for copy in copies:
            copy.wait_send()

    out_rank, qkv_rank = value_width // wt, width // (seq * wt)
    f32, low = jnp.float32, jnp.bfloat16
    tile = (8, value_width)
    results = remote_call(
        kernel,
        "mixer_back",
        4,
        [
            jax.ShapeDtypeStruct((count, width), f32),
            jax.ShapeDtypeStruct(tile, f32),
            jax.ShapeDtypeStruct((seq, qkv_rank, qkv_width), f32),
            jax.ShapeDtypeStruct((out_rank, width), f32),
            jax.ShapeDtypeStruct((ys,) + gate_half, low),
            jax.ShapeDtypeStruct((ys, 2) + gate_half, low),
        ]
        + [
            jax.ShapeDtypeStruct(shape, low)
            for shape_half in (gate_half, gate_half, down_half)
            for shape in ((ys,) + shape_half, shape_half)
        ],
        [pltpu.VMEM(array.shape, array.dtype) for array in big]
        + [
            pltpu.VMEM((length, width), low),
            pltpu.VMEM((length, value_width), low),
            pltpu.VMEM((length, 128), f32),
            pltpu.VMEM((length, 128), f32),
            pltpu.VMEM((length, value_width), f32),
            pltpu.VMEM((length, value_width + 256), low),
            pltpu.VMEM((length, qkv_width), low),
            pltpu.VMEM((seq, 2, count // 2, width), low),
            pltpu.VMEM((seq, wt, qkv_rank, qkv_width), low),
            pltpu.VMEM((wt, out_rank, width), low),
            pltpu.VMEM((2, count // 2, width), f32),
            pltpu.VMEM((8, width), f32),
            pltpu.VMEM((8, width), f32),
            pltpu.VMEM(tile, f32),
            pltpu.VMEM((length, 128), f32),
            pltpu.VMEM((KCONV, value_width), f32),
            pltpu.VMEM(gate_half, low),
            pltpu.VMEM(gate_half, low),
            pltpu.VMEM(down_half, low),
            pltpu.VMEM(down_half, low),
            pltpu.VMEM((seq, qkv_rank, qkv_width), f32),
            pltpu.VMEM((seq,) + tile, f32),
            pltpu.VMEM(tile, f32),
            pltpu.VMEM((wt,) + tile, f32),
        ]
        + SquareSum.scratch(seq, (count // 2, width))
        + LinePieces.scratch(wt, (seq, qkv_rank, qkv_width), seq)
        + LinePieces.scratch(wt, (out_rank, width), PIECES)
        + SquareTerms.scratch(seq, gate_half)
        + SquareTerms.scratch(seq, down_half)
        + SquareTerms.scratch(seq, gate_half)
        + SquareGather.semaphores(seq)
        + SquareTerms.semaphores(seq)
        + [
            pltpu.SemaphoreType.DMA((11,)),
            pltpu.SemaphoreType.DMA((seq, 2)),
            pltpu.SemaphoreType.DMA((seq, 2)),
            pltpu.SemaphoreType.DMA((wt, 2)),
        ],
        *big,
        *small,
        *far,
        in_specs=[ANY] * len(big) + [VMEM] * len(small) + [ANY] * len(far),
        out_specs=[VMEM] * 6 + [ANY] * 6,
    )
    grad, totals, qkv_total, out_total, up_x, up_y = results[:6]
    gate = tuple(gate_parts) + tuple(results[6:8])
    up = tuple(up_parts) + (up_x, up_y) + tuple(results[8:10])
    down = tuple(down_parts) + tuple(results[10:12])
    return grad, totals, gate, up, down, qkv_total, out_total


def last_sums(gate, up, down, qkv_total, totals, lengths, out_total, grad, final, qkv_shape):
    seq, wt = lax.axis_size("seq"), lax.axis_size("wt")
    ys = seq // 2
    f32, low = jnp.float32, jnp.bfloat16
    gate_half, down_half = gate[0].shape[2:], down[0].shape[2:]
    total_width = totals.shape[1]
    lanes_each = total_width // wt
    width = grad.shape[1]
    qkv_width = qkv_total.shape[2]
    operands = list(gate) + list(up) + list(down)
    passed = [out_total, grad, final]

    def kernel(*refs):
        groups, refs = [refs[5 * index : 5 * index + 5] for index in range(3)], refs[15:]
        (qkv_ref, totals_ref, length_ref), passed_refs, refs = refs[:3], refs[3:6], refs[6:]
        (gate_up_out, down_out, qkv_out, first_gain, second_gain, taps_out, loss_out), refs = refs[:7], refs[7:]
        passed_outs, refs = refs[:3], refs[3:]
        totals, refs = refs[:2], refs[2:]
        passed_rooms, refs = refs[:3], refs[3:]
        rooms, (loads, stores, pass_sems) = [refs[5 * index : 5 * index + 5] for index in range(3)], refs[15:]
        s = lax.axis_index("seq")
        y, x = lax.div(s, 2), lax.rem(s, 2)
        copies = []
        for number, (group, room) in enumerate(zip(groups, rooms)):
            terms, from_x, from_y, last_y, last_x = group
            sources = (terms.at[s], from_x.at[y], from_y.at[:, x], last_y, last_x)
            mine = [
                pltpu.make_async_copy(source, target, loads.at[number, index])
                for index, (source, target) in enumerate(zip(sources, room))
            ]
            for copy in mine:
                copy.start()
            copies.append(mine)
        ins = [
            pltpu.make_async_copy(source, room, pass_sems.at[index, 0])
            for index, (source, room) in enumerate(zip(passed_refs, passed_rooms))
        ]
        for copy in ins:
            copy.start()
        shift = lax.rem(total_width - lax.axis_index("wt") * lanes_each, total_width)
        mine = pltpu.roll(totals_ref[...], shift, 1)[:, :lanes_each]
        first_gain[...] = mine[0:1]
        second_gain[...] = mine[1:2]
        taps_out[...] = mine[3 : 3 + KCONV]
        counted = length_ref[0]
        for index in range(1, length_ref.shape[0]):
            counted = counted + length_ref[index]
        loss_out[...] = 2.0 * totals_ref[2:3, :1] / (jnp.full((1, 1), counted, jnp.int32).astype(f32) * width)
        for index in range(seq):
            qkv_out[:, index * qkv_width : (index + 1) * qkv_width] = qkv_ref[index]
        outs = []
        for index, (room, target) in enumerate(zip(passed_rooms, passed_outs)):
            ins[index].wait()
            copy = pltpu.make_async_copy(room, target, pass_sems.at[index, 1])
            copy.start()
            outs.append(copy)
        for number, room in enumerate(rooms):
            own, near_x, near_y, last_y, last_x = room
            total = totals[number // 2]
            base = 2 * (number % 2)
            for copy in copies[number]:
                copy.wait()
            rows = own.shape[1]
            tile = next(t for t in (64, 32, 16) if rows % t == 0)

            def step(index, carry):
                window = pl.ds(pl.multiple_of(index * tile, tile), tile)
                first = own[0, window, :].astype(f32) + near_x[window, :].astype(f32)
                second = own[1, window, :].astype(f32) + last_x[window, :].astype(f32)
                for other in range(1, ys):
                    place = lax.rem(y + other, ys)
                    first = first + last_y[place, window, :].astype(f32)
                    second = second + near_y[place, window, :].astype(f32)
                total[base, window, :] = first
                total[base + 1, window, :] = second
                return carry

            lax.fori_loop(0, rows // tile, step, 0)
            target = gate_up_out.at[pl.ds(base, 2)] if number < 2 else down_out
            copy = pltpu.make_async_copy(total.at[pl.ds(base, 2)], target, stores.at[number])
            copy.start()
            outs.append(copy)
        for copy in outs:
            copy.wait()

    def rooms(half):
        return [
            pltpu.VMEM((2,) + half, low),
            pltpu.VMEM(half, low),
            pltpu.VMEM((ys,) + half, low),
            pltpu.VMEM((ys,) + half, low),
            pltpu.VMEM(half, low),
        ]

    return pl.pallas_call(
        kernel,
        name="last_sums",
        out_shape=[
            jax.ShapeDtypeStruct((4,) + gate_half, f32),
            jax.ShapeDtypeStruct((2,) + down_half, f32),
            jax.ShapeDtypeStruct(qkv_shape, f32),
            jax.ShapeDtypeStruct((1, lanes_each), f32),
            jax.ShapeDtypeStruct((1, lanes_each), f32),
            jax.ShapeDtypeStruct((KCONV, lanes_each), f32),
            jax.ShapeDtypeStruct((1, 1), f32),
        ]
        + [jax.ShapeDtypeStruct(array.shape, array.dtype) for array in passed],
        in_specs=[ANY] * 15 + [VMEM] * 2 + [SMEM] + [ANY] * 3,
        out_specs=[ANY] * 2 + [VMEM] * 5 + [ANY] * 3,
        scratch_shapes=[pltpu.VMEM((4,) + gate_half, f32), pltpu.VMEM((2,) + down_half, f32)]
        + [pltpu.VMEM(array.shape, array.dtype) for array in passed]
        + rooms(gate_half) * 2
        + rooms(down_half)
        + [
            pltpu.SemaphoreType.DMA((3, 5)),
            pltpu.SemaphoreType.DMA((3,)),
            pltpu.SemaphoreType.DMA((3, 2)),
        ],
        compiler_params=pltpu.CompilerParams(vmem_limit_bytes=VMEM_LIMIT),
    )(*operands, qkv_total, totals, lengths, *passed)


def rows_of_tile(values, row):
    return jnp.pad(values[None, :], [(row, 7 - row), (0, 128 - values.shape[0])])


def body(
    inputs,
    segment_ids,
    valid_lengths,
    teacher,
    w_qkv,
    conv_weight,
    w_out,
    norm_gain,
    w_gate_up,
    w_down,
    mlp_gain,
):
    seq_parts = lax.axis_size("seq")
    tok_count = inputs.shape[1]
    model_width = inputs.shape[2]
    length = tok_count * seq_parts
    head_count = H // seq_parts
    qkv_width = head_count * (2 * FEAT + DV)
    rows_low = inputs[0]
    gain_lanes = norm_gain.shape[0]
    gains = rows_of_tile(norm_gain.astype(jnp.float32), 0) + rows_of_tile(mlp_gain.astype(jnp.float32), 1)
    qkv_rows = w_qkv
    if qkv_width % 128:
        qkv_rows = w_qkv.reshape(w_qkv.shape[0], seq_parts, qkv_width).transpose(1, 0, 2)
    gate_up_low = w_gate_up.swapaxes(1, 2)
    segments = segment_ids
    (
        attended,
        normed_low,
        gain_rows,
        qkv_columns,
        out_rows,
        hidden_low,
        sorted_columns,
        mixer_low,
        mixed_values,
        head_outputs,
        gate_early,
        order,
    ) = mixer_forward(rows_low, qkv_rows, w_out, gains, gate_up_low, segments, conv_weight)
    (
        final_low,
        residual_error,
        energy,
        normed_all,
        gate_all,
        up_all,
        active_all,
        down_part,
        gate_up_part,
    ) = feed_forward(normed_low, attended, teacher[0], valid_lengths, gate_early, gate_up_low, w_down)
    (
        attended_grad,
        mix_back,
        gain_two_terms,
        gate_terms,
        up_terms,
        down_terms,
        gate_from_x,
        gate_from_y,
        down_from_x,
        down_from_y,
    ) = feed_back(
        residual_error,
        attended,
        gain_rows,
        gate_up_part,
        down_part,
        gate_all,
        up_all,
        active_all,
        normed_all,
    )
    inputs_grad, totals, gate, up, down, qkv_total, out_total = mixer_back(
        mix_back,
        attended_grad,
        rows_low,
        gain_rows,
        out_rows.reshape(head_count * DV, model_width),
        qkv_columns.reshape(model_width, qkv_width),
        hidden_low,
        sorted_columns,
        mixer_low,
        mixed_values,
        head_outputs,
        segments,
        conv_weight,
        order,
        gain_two_terms,
        energy,
        (gate_terms, gate_from_x, gate_from_y),
        (up_terms,),
        (down_terms, down_from_x, down_from_y),
    )
    (
        grad_w_gate_up,
        grad_w_down,
        grad_w_qkv,
        grad_norm_gain,
        grad_mlp_gain,
        grad_conv,
        mean_loss,
        grad_w_out,
        inputs_grad,
        outputs,
    ) = last_sums(
        gate, up, down, qkv_total, totals, valid_lengths, out_total, inputs_grad, final_low, w_qkv.shape
    )
    return (
        outputs[None],
        inputs_grad[None],
        mean_loss.reshape(()),
        grad_w_qkv,
        grad_conv,
        grad_w_out,
        grad_norm_gain.reshape(norm_gain.shape),
        grad_w_gate_up.reshape(gate_up_low.shape).swapaxes(1, 2),
        grad_w_down.reshape(w_down.shape),
        grad_mlp_gain.reshape(mlp_gain.shape),
    )


def solution(mesh):
    in_specs = (
        P("wt", "seq", None),
        P("wt", None),
        P(),
        P("wt", "seq", None),
        P(("seq", "wt"), None),
        P(None, "seq"),
        P(("seq", "wt"), None),
        P(("seq", "wt")),
        P(None, "seq", "wt"),
        P("wt", "seq"),
        P(("seq", "wt")),
    )
    out_specs = (
        P("wt", "seq", None),
        P("wt", "seq", None),
        P(),
        P(("seq", "wt"), None),
        P(None, ("seq", "wt")),
        P(("seq", "wt"), None),
        P(("seq", "wt")),
        P(None, "seq", "wt"),
        P("wt", "seq"),
        P(("seq", "wt")),
    )
    return jax.shard_map(body, mesh=mesh, in_specs=in_specs, out_specs=out_specs, check_vma=False)
```

```python
from functools import partial

import jax
import jax.numpy as jnp
from jax import lax
from jax.experimental import pallas as pl
from jax.experimental.pallas import tpu as pltpu
from jax.sharding import PartitionSpec as P

H = 16
FEAT = 16
KCONV = 3
DV = 128


epsilon = 1e-05


def rms_norm(values, gain_vector):
    inverse_root = lax.rsqrt(jnp.mean(values * values, axis=-1, keepdims=True) + epsilon)
    return values * inverse_root * gain_vector


def contract_last(former, latter):
    return lax.dot_general(
        former, latter, (((1,), (1,)), ((), ())), preferred_element_type=jnp.float32
    )


def contract_first(former, latter):
    return lax.dot_general(
        former, latter, (((0,), (0,)), ((), ())), preferred_element_type=jnp.float32
    )


def shift_down(values, amount, filler):
    padding = jnp.full((amount,) + values.shape[1:], filler, values.dtype)
    return jnp.concatenate([padding, values[:-amount]], axis=0)


def gated_unit(gate_in, up_in):
    return jax.nn.silu(gate_in) * up_in


MESH = pl.DeviceIdType.MESH
VMEM = pl.BlockSpec(memory_space=pltpu.VMEM)
ANY = pl.BlockSpec(memory_space=pl.ANY)
SMEM = pl.BlockSpec(memory_space=pltpu.SMEM)
VMEM_LIMIT = 63 * 1024 * 1024


class Place:
    def __init__(self, seq, wt):
        self.seq, self.wt = seq, wt
        self.ys, self.zs = seq // 2, wt // 2
        self.s, self.w = lax.axis_index("seq"), lax.axis_index("wt")
        self.y, self.x = lax.div(self.s, 2), lax.rem(self.s, 2)
        self.z, self.c = lax.div(self.w, 2), lax.rem(self.w, 2)

    def across(self):
        return (self.y * 2 + 1 - self.x, self.w)

    def beside(self, step):
        return lax.rem(self.y + step, self.ys)

    def column(self, y):
        return (y * 2 + self.x, self.w)

    def partner(self):
        return (self.s, self.z * 2 + 1 - self.c)

    def level(self, z):
        return (self.s, z * 2 + self.c)

    def meet(self, square, line):
        barrier = pltpu.get_barrier_semaphore()
        count = 0
        if square:
            for step in range(1, self.seq):
                device = (lax.rem(self.s + step, self.seq), self.w)
                pl.semaphore_signal(barrier, inc=1, device_id=device, device_id_type=MESH)
                count += 1
        if line:
            for step in range(1, self.wt):
                device = (self.s, lax.rem(self.w + step, self.wt))
                pl.semaphore_signal(barrier, inc=1, device_id=device, device_id_type=MESH)
                count += 1
        pl.semaphore_wait(barrier, count)


def send(source, target, leaving, arriving, device):
    return pltpu.make_async_remote_copy(
        src_ref=source,
        dst_ref=target,
        send_sem=leaving,
        recv_sem=arriving,
        device_id=device,
        device_id_type=MESH,
    )


def add_into(target, sources):
    if len(target.shape) == 3:
        for index in range(target.shape[0]):
            add_into(target.at[index], [source.at[index] for source in sources])
        return
    rows = target.shape[0]
    tile = next(t for t in (64, 32, 16, 8, rows) if rows % t == 0)

    def step(index, carry):
        window = pl.ds(pl.multiple_of(index * tile, tile), tile)
        total = sources[0][window, :].astype(jnp.float32)
        for source in sources[1:]:
            total = total + source[window, :].astype(jnp.float32)
        target[window, :] = total.astype(target.dtype)
        return carry

    lax.fori_loop(0, rows // tile, step, 0)


class SquareGather:
    @staticmethod
    def semaphores(seq):
        return [
            pltpu.SemaphoreType.DMA((2 + seq // 2,)),
            pltpu.SemaphoreType.DMA((seq // 2, 3)),
            pltpu.SemaphoreType.DMA((seq, 2)),
        ]

    def __init__(self, at, view, own, sems):
        self.at, self.view, self.own = at, view, own
        self.over_x, self.over_y, self.got = sems
        self.sent = []

    def go(self, copy):
        copy().start()
        self.sent.append(copy)

    def own_x(self, half):
        at = self.at
        target = self.view(at.s, half)
        return send(self.own(half), target, self.over_x.at[half], self.got.at[at.s, half], at.across())

    def own_y(self, step, half):
        at = self.at
        target, device = self.view(at.s, half), at.column(at.beside(step))
        return send(self.own(half), target, self.over_y.at[step, half], self.got.at[at.s, half], device)

    def pass_y(self, step):
        at = self.at
        s = at.y * 2 + 1 - at.x
        slot, device = self.view(s, 0), at.column(at.beside(step))
        return send(slot, slot, self.over_y.at[step, 2], self.got.at[s, 0], device)

    def pass_x(self, step):
        s = self.at.beside(step) * 2 + self.at.x
        slot = self.view(s, 1)
        return send(slot, slot, self.over_x.at[1 + step], self.got.at[s, 1], self.at.across())

    def wait(self, s, half):
        slot = self.view(s, half)
        send(slot, slot, self.over_x.at[0], self.got.at[s, half], self.at.across()).wait_recv()

    def start(self):
        for half in range(2):
            self.go(partial(self.own_x, half))
            for step in range(1, self.at.ys):
                self.go(partial(self.own_y, step, 1 - half))

    def relay(self):
        at = self.at
        self.wait(at.y * 2 + 1 - at.x, 0)
        for step in range(1, at.ys):
            self.go(partial(self.pass_y, step))
        for step in range(1, at.ys):
            self.wait(at.beside(step) * 2 + at.x, 1)
            self.go(partial(self.pass_x, step))

    def direct(self):
        at = self.at
        self.wait(at.y * 2 + 1 - at.x, 1)
        for step in range(1, at.ys):
            self.wait(at.beside(step) * 2 + at.x, 0)

    def relayed(self):
        at = self.at
        for step in range(1, at.ys):
            y = at.beside(step)
            self.wait(y * 2 + 1 - at.x, 0)
            self.wait(y * 2 + 1 - at.x, 1)
        for copy in self.sent:
            copy().wait_send()

    def finish(self):
        self.direct()
        self.relayed()


class SquareSum:
    @staticmethod
    def scratch(seq, half_shape):
        ys = seq // 2
        return [
            pltpu.VMEM((ys,) + half_shape, jnp.bfloat16),
            pltpu.VMEM((ys, 2) + half_shape, jnp.bfloat16),
            pltpu.VMEM((ys,) + half_shape, jnp.bfloat16),
            pltpu.VMEM(half_shape, jnp.bfloat16),
            pltpu.VMEM((ys,) + half_shape, jnp.bfloat16),
            pltpu.VMEM(half_shape, jnp.bfloat16),
            pltpu.SemaphoreType.DMA((ys, 2, 2)),
            pltpu.SemaphoreType.DMA((ys, 3, 2)),
        ]

    def __init__(self, at, part, scratch):
        self.at, self.part = at, part
        self.from_x, self.from_y, self.last_y, self.last_x, self.sum_y, self.sum_x, self.xs, self.yss = scratch
        self.sent = []

    def go(self, source, target, leaving, arriving, device):
        copy = send(source, target, leaving, arriving, device)
        copy.start()
        self.sent.append(copy)

    def wait(self, slot, leaving, arriving):
        send(slot, slot, leaving, arriving, self.at.across()).wait_recv()

    def start(self):
        at = self.at
        for y in range(at.ys):
            self.go(
                self.part(y * 2 + 1 - at.x, 0),
                self.from_x.at[y],
                self.xs.at[y, 0, 0],
                self.xs.at[y, 0, 1],
                at.across(),
            )
        for step in range(1, at.ys):
            y = at.beside(step)
            for x in range(2):
                self.go(
                    self.part(y * 2 + x, 1),
                    self.from_y.at[at.y, x],
                    self.yss.at[step, x, 0],
                    self.yss.at[at.y, x, 1],
                    at.column(y),
                )

    def relay(self):
        at = self.at
        for step in range(1, at.ys):
            y = at.beside(step)
            self.wait(self.from_x.at[y], self.xs.at[y, 0, 0], self.xs.at[y, 0, 1])
            add_into(self.sum_y.at[y], [self.part(y * 2 + at.x, 0), self.from_x.at[y]])
            self.go(
                self.sum_y.at[y],
                self.last_y.at[at.y],
                self.yss.at[step, 2, 0],
                self.yss.at[at.y, 2, 1],
                at.column(y),
            )
        terms = []
        for step in range(1, at.ys):
            y = at.beside(step)
            for x in range(2):
                self.wait(self.from_y.at[y, x], self.yss.at[step, x, 0], self.yss.at[y, x, 1])
            terms.append(self.from_y.at[y, 1 - at.x])
        add_into(self.sum_x, [self.part(at.y * 2 + 1 - at.x, 1)] + terms)
        self.go(self.sum_x, self.last_x, self.xs.at[0, 1, 0], self.xs.at[0, 1, 1], at.across())

    def finish(self, total):
        at = self.at
        self.wait(self.from_x.at[at.y], self.xs.at[0, 0, 0], self.xs.at[at.y, 0, 1])
        terms = [self.part(at.s, 0), self.from_x.at[at.y]]
        for step in range(1, at.ys):
            y = at.beside(step)
            self.wait(self.last_y.at[y], self.yss.at[step, 2, 0], self.yss.at[y, 2, 1])
            terms.append(self.last_y.at[y])
        add_into(total(0), terms)
        self.wait(self.last_x, self.xs.at[0, 1, 0], self.xs.at[0, 1, 1])
        terms = [self.part(at.s, 1), self.last_x]
        for step in range(1, at.ys):
            terms.append(self.from_y.at[at.beside(step), at.x])
        add_into(total(1), terms)
        for copy in self.sent:
            copy.wait_send()


class LineGather:
    @staticmethod
    def semaphores(wt, cuts=1):
        return [pltpu.SemaphoreType.DMA((5, wt // 2, cuts))]

    def __init__(self, at, view, sems):
        self.at, self.view, self.sems = at, view, sems[0]
        self.cuts = self.sems.shape[2]

    def cut(self, ref, part):
        if self.cuts == 1:
            return ref
        rows = ref.shape[0] // self.cuts
        return ref.at[pl.ds(part * rows, rows)]

    def hop(self, z, part, kind, device, source):
        slot = self.view(z * 2 + self.at.c)
        source = slot if source is None else source
        arriving = 4 if kind == 2 else 3
        return send(
            self.cut(source, part),
            self.cut(slot, part),
            self.sems.at[kind, z, part],
            self.sems.at[arriving, z, part],
            device,
        )

    def up(self, z, part, source=None):
        return self.hop(z, part, 0, self.at.level(self.at.z + 1), source)

    def down(self, z, part, source=None):
        return self.hop(z, part, 1, self.at.level(self.at.z - 1), source)

    def over(self, z, part, source=None):
        return self.hop(z, part, 2, self.at.partner(), source)

    def start(self, source=None):
        at = self.at
        for part in range(self.cuts):

            @pl.when(at.z + 1 < at.zs)
            def _():
                self.up(at.z, part, source).start()

            @pl.when(at.z > 0)
            def _():
                self.down(at.z, part, source).start()

            self.over(at.z, part, source).start()

    def step(self, index):
        at = self.at
        below, above = at.z - 1 - index, at.z + 1 + index
        for part in range(self.cuts):

            @pl.when(below >= 0)
            def _():
                self.up(below, part).wait_recv()

                @pl.when(at.z + 1 < at.zs)
                def _():
                    self.up(below, part).start()

                self.over(below, part).start()

            @pl.when(above < at.zs)
            def _():
                self.down(above, part).wait_recv()

                @pl.when(at.z > 0)
                def _():
                    self.down(above, part).start()

                self.over(above, part).start()

    def wait_over(self, z):
        for part in range(self.cuts):
            slot = self.cut(self.view(z * 2 + 1 - self.at.c), part)
            send(slot, slot, self.sems.at[2, z, part], self.sems.at[4, z, part], self.at.partner()).wait_recv()

    def finish(self):
        for z in range(self.at.zs):
            self.wait_over(z)
        self.sent()

    def sent(self):
        at = self.at
        for z in range(at.zs):
            for part in range(self.cuts):

                @pl.when((at.z >= z) & (at.z + 1 < at.zs))
                def _():
                    self.up(z, part).wait_send()

                @pl.when((at.z <= z) & (at.z > 0))
                def _():
                    self.down(z, part).wait_send()

                self.over(z, part).wait_send()


def remote_call(kernel, name, number, outs, scratch, *operands, in_specs=None, out_specs=None):
    return pl.pallas_call(
        kernel,
        name=name,
        out_shape=outs,
        in_specs=[VMEM] * len(operands) if in_specs is None else in_specs,
        out_specs=jax.tree.map(lambda _: VMEM, outs) if out_specs is None else out_specs,
        scratch_shapes=scratch,
        compiler_params=pltpu.CompilerParams(
            collective_id=number, has_side_effects=True, vmem_limit_bytes=VMEM_LIMIT
        ),
    )(*operands)


def mixer_forward(tokens, qkv_rows, out_rows, gains, gate_up, segments, taps):
    seq, wt = lax.axis_size("seq"), lax.axis_size("wt")
    zs = wt // 2
    count, width = tokens.shape
    length = count * seq
    out_rank = out_rows.shape[0]
    heads = H // seq
    value_width = heads * DV
    qkv_width = value_width + 2 * FEAT * heads
    qkv_rank = width // (seq * wt)
    lanes_each = width // (seq * wt)
    units, block = gate_up.shape[1:]
    early = early_rows(units)
    rows_at_once = 256
    small = [
        tokens,
        qkv_rows,
        out_rows,
        gains,
        segments,
        taps,
    ]

    def kernel(*refs):
        (x_ref, qkv_ref, out_ref, gain_ref, segment_ref, tap_ref), refs = refs[:6], refs[6:]
        gate_up_ref, refs = refs[0], refs[1:]
        (attended_out, normed_out, gain_rows), refs = refs[:3], refs[3:]
        (qkv_out, w_out_out, hidden_out, sorted_out, mixer_out, values_out, outputs_out, gates_out, order_out), refs = (
            refs[:9],
            refs[9:],
        )
        (xs, qkvs, outs, gains_all, hidden_v, sorted_v, mixer_v, values_v, outputs_v, parts, total, room), refs = (
            refs[:12],
            refs[12:],
        )
        (order_v, segment_column, tap_v), refs = refs[:3], refs[3:]
        sum_scratch, x_sems, gate_sems, refs = refs[:8], refs[8:11], refs[11:14], refs[14:]
        line_sems, refs = [refs[index : index + 1] for index in range(3)], refs[3:]
        swap_q, swap_g, local, outgoing = refs
        at = Place(seq, wt)
        room_load = pltpu.make_async_copy(gate_up_ref.at[:, pl.ds(0, early)], room, local.at[4])
        room_load.start()
        at.meet(True, True)
        half = count // 2
        gather_x = SquareGather(
            at,
            lambda s, h: xs.at[pl.ds(pl.multiple_of(s * count + h * half, half), half)],
            lambda h: x_ref.at[pl.ds(h * half, half)],
            x_sems,
        )
        gather_q = LineGather(at, lambda w: qkvs.at[:, w], line_sems[0])
        gather_g = LineGather(
            at, lambda w: gains_all.at[:, pl.ds(pl.multiple_of(w * 8, 8), 8)], line_sems[1]
        )
        gather_o = LineGather(at, lambda w: outs.at[w], line_sems[2])
        gates = SquareGather(
            at,
            lambda s, h: gates_out.at[h, :, pl.ds(pl.multiple_of(s * block, block), block)],
            lambda h: gate_up_ref.at[h, pl.ds(0, early)],
            gate_sems,
        )
        gain_slot = pl.ds(pl.multiple_of(at.w * 8, 8), 8)

        def qkv_part(s):
            if len(qkv_ref.shape) == 3:
                return qkv_ref.at[s]
            return qkv_ref.at[:, pl.ds(pl.multiple_of(s * qkv_width, qkv_width), qkv_width)]

        swaps = []
        for step in range(1, seq):
            to = lax.rem(at.s + step, seq)
            swaps.append(
                send(gain_ref, gains_all.at[at.s, gain_slot], swap_g.at[step, 0], swap_g.at[at.s, 1], (to, at.w))
            )
            swaps.append(
                send(qkv_part(to), qkvs.at[at.s, at.w], swap_q.at[step, 0], swap_q.at[at.s, 1], (to, at.w))
            )
        for copy in swaps:
            copy.start()
        gather_x.start()
        own = [
            pltpu.make_async_copy(qkv_part(at.s), qkvs.at[at.s, at.w], local.at[0]),
            pltpu.make_async_copy(gain_ref, gains_all.at[at.s, gain_slot], local.at[1]),
            pltpu.make_async_copy(out_ref, outs.at[at.w], local.at[2]),
            pltpu.make_async_copy(x_ref, xs.at[pl.ds(pl.multiple_of(at.s * count, count), count)], local.at[3]),
        ]
        for copy in own:
            copy.start()
        for copy in own:
            copy.wait()
        room_load.wait()
        room_store = pltpu.make_async_copy(
            room, gates_out.at[:, :, pl.ds(pl.multiple_of(at.s * block, block), block)], local.at[4]
        )
        room_store.start()
        for step in range(1, seq):
            s = lax.rem(at.s + step, seq)
            slot = gains_all.at[s, gain_slot]
            send(slot, slot, swap_g.at[step, 0], swap_g.at[s, 1], at.across()).wait_recv()
            slot = qkvs.at[s, at.w]
            send(slot, slot, swap_q.at[step, 0], swap_q.at[s, 1], at.across()).wait_recv()
        gather_g.start()
        gather_q.start()
        tap_v[...] = tap_ref[...].astype(jnp.float32)
        segment_row = segment_ref[...].astype(jnp.float32)
        segment_column[...] = jnp.broadcast_to(segment_row, (128, length)).T
        write_order(order_v, heads)
        gather_x.relay()
        gates.start()
        for index in range(zs - 1):
            if index == zs - 2:
                gather_o.start()
            gather_g.step(index)
            gather_q.step(index)
        gather_g.finish()

        device_rows = gains_all[...].reshape(seq * wt * 8, 128).astype(jnp.bfloat16)
        gain_rows[...] = jnp.zeros_like(gain_rows)

        def spread_gains(index, carry):
            begin = pl.multiple_of(index * 256, 256)
            lane = lax.broadcasted_iota(jnp.int32, (128, 256), 0)
            column = begin + lax.broadcasted_iota(jnp.int32, (128, 256), 1)
            copied = jnp.dot(
                device_rows,
                (lane == lax.rem(column, lanes_each)).astype(jnp.float32).astype(jnp.bfloat16),
                preferred_element_type=jnp.float32,
            )
            row = lax.broadcasted_iota(jnp.int32, copied.shape, 0)
            column = begin + lax.broadcasted_iota(jnp.int32, copied.shape, 1)
            first_row = lax.div(column, lanes_each) * 8
            for number in range(2):
                gain_rows[number : number + 1, pl.ds(begin, 256)] = jnp.sum(
                    jnp.where(row == first_row + number, copied, 0.0), axis=0, keepdims=True
                )
            return carry

        lax.fori_loop(0, width // 256, spread_gains, 0)
        gather_x.finish()

        def norm_rows(index, carry):
            window = pl.ds(pl.multiple_of(index * 32, 32), 32)
            hidden_v[window, :] = rms_norm(xs[window, :].astype(jnp.float32), gain_rows[0:1, :]).astype(
                jnp.bfloat16
            )
            return carry

        lax.fori_loop(0, length // 32, norm_rows, 0)
        gather_q.finish()
        projected = jnp.dot(
            hidden_v[...], qkvs[...].reshape(width, qkv_width), preferred_element_type=jnp.float32
        ).astype(jnp.bfloat16)
        sorted_v[...] = jnp.dot(projected, order_v[...], preferred_element_type=jnp.float32).astype(
            jnp.bfloat16
        )
        stores = [
            pltpu.make_async_copy(source, target, outgoing.at[index])
            for index, (source, target) in enumerate(
                (
                    (qkvs, qkv_out),
                    (hidden_v, hidden_out),
                    (sorted_v, sorted_out),
                    (values_v, values_out),
                    (outputs_v, outputs_out),
                    (mixer_v, mixer_out),
                    (outs, w_out_out),
                    (order_v, order_out),
                )
            )
        ]
        for copy in stores[:3]:
            copy.start()
        marks = tap_marks(segment_column)

        def convolve(head, carry):
            columns = pl.ds(pl.multiple_of(head * DV, DV), DV)
            raw = sorted_v[:, columns].astype(jnp.float32)
            mixed = tap_v[0:1, columns] * raw
            for tap in range(1, KCONV):
                mixed = mixed + tap_v[tap : tap + 1, columns] * pltpu.roll(raw, tap, 0) * marks[tap]
            values_v[head] = mixed.astype(jnp.bfloat16)
            return carry

        lax.fori_loop(0, heads, convolve, 0)
        stores[3].start()
        gates.relay()
        steps = length // rows_at_once
        lanes = lax.broadcasted_iota(jnp.int32, (1, 128), 1)

        def attend(index, carry):
            head, start = lax.div(index, steps), lax.rem(index, steps) * rows_at_once
            rows = pl.ds(pl.multiple_of(start, rows_at_once), rows_at_once)
            mine = ((lanes >= head * FEAT) & (lanes < head * FEAT + FEAT)).astype(jnp.float32)
            queries = sorted_v[rows, value_width : value_width + 128] * mine.astype(jnp.bfloat16)
            scores = contract_last(queries, sorted_v[:, value_width + 128 :]) * 0.25
            places = start + lax.broadcasted_iota(jnp.int32, scores.shape, 0)
            allowed = (segment_column[rows, :1] == segment_row) & (
                places >= lax.broadcasted_iota(jnp.int32, scores.shape, 1)
            )
            kernel_values = jnp.where(allowed, 1.0 + scores + 0.5 * scores * scores, 0.0)
            denominator = jnp.sum(kernel_values, axis=1, keepdims=True)
            mixed = (
                jnp.dot(kernel_values.astype(jnp.bfloat16), values_v[head], preferred_element_type=jnp.float32)
                / denominator
            )
            outputs_v[head, rows, :] = mixed
            mixer_v[rows, pl.ds(pl.multiple_of(head * DV, DV), DV)] = mixed.astype(jnp.bfloat16)
            return carry

        turns = heads * steps
        for index in range(zs - 1):
            lax.fori_loop(turns * index // (zs - 1), turns * (index + 1) // (zs - 1), attend, 0)
            gather_o.step(index)
        gather_o.finish()
        for copy in stores[4:]:
            copy.start()

        def out_job(index, carry):
            window = pl.ds(pl.multiple_of(index * 512, 512), 512)
            term = jnp.dot(
                mixer_v[...], outs[:, :, window].reshape(value_width, 512), preferred_element_type=jnp.float32
            ).astype(jnp.bfloat16)
            for s in range(seq):
                for h in range(2):
                    begin = s * count + h * half
                    parts[s, h, :, window] = term[begin : begin + half]
            return carry

        lax.fori_loop(0, width // 512, out_job, 0)
        work = SquareSum(at, lambda s, h: parts.at[s, h], sum_scratch)
        work.start()
        work.relay()
        work.finish(lambda h: total.at[h])

        def finish_rows(index, carry):
            for h in range(2):
                window = pl.ds(pl.multiple_of(index * 16, 16), 16)
                rows = pl.ds(pl.multiple_of(h * half + index * 16, 16), 16)
                attended = x_ref[rows, :].astype(jnp.float32) + total[h, window, :]
                attended_out[rows, :] = attended
                normed_out[rows, :] = rms_norm(attended, gain_rows[1:2, :]).astype(jnp.bfloat16)
            return carry

        lax.fori_loop(0, half // 16, finish_rows, 0)
        gates.finish()
        room_store.wait()
        for copy in swaps:
            copy.wait_send()
        for copy in stores:
            copy.wait()

    low, f32 = jnp.bfloat16, jnp.float32
    sorted_width = value_width + 256
    return remote_call(
        kernel,
        "mixer_forward",
        0,
        [
            jax.ShapeDtypeStruct((count, width), f32),
            jax.ShapeDtypeStruct((count, width), low),
            jax.ShapeDtypeStruct((8, width), f32),
            jax.ShapeDtypeStruct((seq, wt, qkv_rank, qkv_width), low),
            jax.ShapeDtypeStruct((wt, out_rank, width), low),
            jax.ShapeDtypeStruct((length, width), low),
            jax.ShapeDtypeStruct((length, sorted_width), low),
            jax.ShapeDtypeStruct((length, value_width), low),
            jax.ShapeDtypeStruct((heads, length, DV), low),
            jax.ShapeDtypeStruct((heads, length, DV), f32),
            jax.ShapeDtypeStruct((2, early, width), low),
            jax.ShapeDtypeStruct((qkv_width, sorted_width), low),
        ],
        [
            pltpu.VMEM((length, width), low),
            pltpu.VMEM((seq, wt, qkv_rank, qkv_width), low),
            pltpu.VMEM((wt, out_rank, width), low),
            pltpu.VMEM((seq, wt * 8, 128), f32),
            pltpu.VMEM((length, width), low),
            pltpu.VMEM((length, sorted_width), low),
            pltpu.VMEM((length, value_width), low),
            pltpu.VMEM((heads, length, DV), low),
            pltpu.VMEM((heads, length, DV), f32),
            pltpu.VMEM((seq, 2, count // 2, width), low),
            pltpu.VMEM((2, count // 2, width), f32),
            pltpu.VMEM((2, early, block), low),
            pltpu.VMEM((qkv_width, sorted_width), low),
            pltpu.VMEM((length, 128), f32),
            pltpu.VMEM((KCONV, value_width), f32),
        ]
        + SquareSum.scratch(seq, (count // 2, width))
        + SquareGather.semaphores(seq)
        + SquareGather.semaphores(seq)
        + LineGather.semaphores(wt) * 3
        + [
            pltpu.SemaphoreType.DMA((seq, 2)),
            pltpu.SemaphoreType.DMA((seq, 2)),
            pltpu.SemaphoreType.DMA((5,)),
            pltpu.SemaphoreType.DMA((8,)),
        ],
        *small,
        gate_up,
        in_specs=[VMEM] * len(small) + [ANY],
        out_specs=[VMEM] * 3 + [ANY] * 9,
    )


def write_order(ref, heads):
    head_width, value_width = 2 * FEAT + DV, heads * DV

    def step(index, carry):
        window = pl.ds(pl.multiple_of(index * 32, 32), 32)
        shape = (32, ref.shape[1])
        column = index * 32 + lax.broadcasted_iota(jnp.int32, shape, 0)
        head = lax.div(column, head_width)
        place = lax.rem(column, head_width)
        target = jnp.where(
            place < FEAT,
            value_width + head * FEAT + place,
            jnp.where(
                place < 2 * FEAT, value_width + 128 + head * FEAT + place - FEAT, head * DV + place - 2 * FEAT
            ),
        )
        hit = target == lax.broadcasted_iota(jnp.int32, shape, 1)
        ref[window, :] = hit.astype(jnp.float32).astype(jnp.bfloat16)
        return carry

    lax.fori_loop(0, ref.shape[0] // 32, step, 0)


def tap_marks(segment_column):
    segment = segment_column[:, :1]
    place = lax.broadcasted_iota(jnp.int32, segment_column.shape, 0)[:, :1]
    marks = [None]
    for tap in range(1, KCONV):
        same = (pltpu.roll(segment_column[...], tap, 0)[:, :1] == segment) & (place >= tap)
        marks.append(same.astype(jnp.float32))
    return marks


def early_rows(units):
    return units * 3 // 4 // 16 * 16


class LinePieces:
    @staticmethod
    def scratch(wt, shape, pieces):
        zs = wt // 2
        return [pltpu.VMEM((zs,) + shape, jnp.bfloat16)] * 3 + [pltpu.SemaphoreType.DMA((6, zs, pieces))]

    def __init__(self, at, part, scratch, order=None):
        self.at, self.part, self.order = at, part, order
        self.pair, self.below, self.above, self.sems = scratch
        self.pieces = self.sems.shape[2]
        self.width = self.pair.shape[-1] // self.pieces

    def cut(self, ref, piece):
        if len(ref.shape) == 3:
            return ref.at[piece]
        return ref.at[:, self.columns(piece)]

    def columns(self, piece):
        block = piece if self.order is None else self.order(piece)
        return pl.ds(pl.multiple_of(block * self.width, self.width), self.width)

    def own(self, z, piece):
        return self.cut(self.part(z * 2 + self.at.c), piece)

    def over(self, z, piece):
        return send(
            self.cut(self.part(z * 2 + 1 - self.at.c), piece),
            self.cut(self.pair.at[z], piece),
            self.sems.at[0, z, piece],
            self.sems.at[1, z, piece],
            self.at.partner(),
        )

    def up(self, z, piece):
        return send(
            self.own(z, piece),
            self.cut(self.below.at[z], piece),
            self.sems.at[2, z, piece],
            self.sems.at[3, z, piece],
            self.at.level(self.at.z + 1),
        )

    def down(self, z, piece):
        return send(
            self.own(z, piece),
            self.cut(self.above.at[z], piece),
            self.sems.at[4, z, piece],
            self.sems.at[5, z, piece],
            self.at.level(self.at.z - 1),
        )

    def terms(self, z, piece):
        self.over(z, piece).wait_recv()
        return [self.own(z, piece), self.cut(self.pair.at[z], piece)]

    def ends(self, z, piece):
        at = self.at

        @pl.when((at.z == 0) & (z > 0))
        def _():
            add_into(self.own(z, piece), self.terms(z, piece))
            self.up(z, piece).start()

        @pl.when((at.z == at.zs - 1) & (z < at.zs - 1))
        def _():
            add_into(self.own(z, piece), self.terms(z, piece))
            self.down(z, piece).start()

    def begin(self):
        zs = self.at.zs

        def pairs(piece, carry):
            for index in range(zs // 2):
                self.over(index, piece).start()
                self.over(zs - 1 - index, piece).start()
            return carry

        lax.fori_loop(0, self.pieces, pairs, 0)

        def starts(index, carry):
            piece = lax.rem(index, self.pieces)
            far = zs - 1 - lax.div(index, self.pieces)
            self.ends(jnp.where(self.at.z == 0, far, zs - 1 - far), piece)
            return carry

        lax.fori_loop(0, (zs - 1) * self.pieces, starts, 0)

    def pass_on(self, index, fill=None, begin=0, end=None):
        at = self.at
        upper = at.z * 2 >= at.zs
        high, low = index, at.zs - 1 - index

        def lower(piece, when):
            @pl.when((at.z > low) & (at.z < at.zs - 1) & when)
            def _():
                terms = self.terms(low, piece)
                self.down(low, piece).wait_recv()
                add_into(self.own(low, piece), terms + [self.cut(self.above.at[low], piece)])
                self.down(low, piece).start()

        def step(piece, carry):
            lower(piece, upper)

            @pl.when((at.z < high) & (at.z > 0))
            def _():
                terms = self.terms(high, piece)
                self.up(high, piece).wait_recv()
                add_into(self.own(high, piece), terms + [self.cut(self.below.at[high], piece)])
                self.up(high, piece).start()

            lower(piece, jnp.logical_not(upper))
            if fill is not None:
                fill(piece, self.pieces)
            return carry

        end = self.pieces if end is None else end
        if end - begin == 1:
            step(begin, 0)
        else:
            lax.fori_loop(begin, end, step, 0)

    def finish(self, total):
        at = self.at

        def step(piece, carry):
            terms = self.terms(at.z, piece)
            below, above = self.cut(self.below.at[at.z], piece), self.cut(self.above.at[at.z], piece)

            @pl.when(at.z == 0)
            def _():
                self.down(at.z, piece).wait_recv()
                add_into(self.cut(total, piece), terms + [above])

            @pl.when(at.z == at.zs - 1)
            def _():
                self.up(at.z, piece).wait_recv()
                add_into(self.cut(total, piece), terms + [below])

            @pl.when((at.z > 0) & (at.z < at.zs - 1))
            def _():
                self.up(at.z, piece).wait_recv()
                self.down(at.z, piece).wait_recv()
                add_into(self.cut(total, piece), terms + [below, above])

            for z in range(at.zs):

                @pl.when(at.z < z)
                def _():
                    self.up(z, piece).wait_send()

                @pl.when(at.z > z)
                def _():
                    self.down(z, piece).wait_send()

                self.over(z, piece).wait_send()
            return carry

        lax.fori_loop(0, self.pieces, step, 0)


class SquareTerms:
    @staticmethod
    def semaphores(seq):
        return [pltpu.SemaphoreType.DMA((seq // 2, 2)), pltpu.SemaphoreType.DMA((seq // 2, 2, 2))]

    @staticmethod
    def scratch(seq, half_shape):
        ys = seq // 2
        return [
            pltpu.VMEM((ys,) + half_shape, jnp.bfloat16),
            pltpu.VMEM(half_shape, jnp.bfloat16),
            pltpu.SemaphoreType.DMA((ys + 1, 2)),
        ]

    def __init__(self, at, terms, from_x, from_y, sems=None, lasts=None, scratch=None):
        self.at, self.terms, self.from_x, self.from_y = at, terms, from_x, from_y
        if sems is not None:
            self.xs, self.ys = sems
        if scratch is not None:
            self.last_y, self.last_x = lasts
            self.sum_y, self.sum_x, self.last = scratch

    def first_x(self, y):
        at = self.at
        return send(
            self.terms(y * 2 + 1 - at.x, 0), self.from_x.at[y], self.xs.at[y, 0], self.xs.at[y, 1], at.across()
        )

    def first_y(self, step, x):
        at = self.at
        y = at.beside(step)
        return send(
            self.terms(y * 2 + x, 1),
            self.from_y.at[at.y, x],
            self.ys.at[step, x, 0],
            self.ys.at[at.y, x, 1],
            at.column(y),
        )

    def first_start(self):
        for y in range(self.at.ys):
            self.first_x(y).start()
        for step in range(1, self.at.ys):
            for x in range(2):
                self.first_y(step, x).start()

    def first_wait(self):
        at = self.at
        for y in range(at.ys):
            self.first_x(y).wait()
        for step in range(1, at.ys):
            y = at.beside(step)
            for x in range(2):
                self.first_y(step, x).wait_send()
                slot = self.from_y.at[y, x]
                send(slot, slot, self.ys.at[step, x, 0], self.ys.at[y, x, 1], at.across()).wait_recv()

    def second_y(self, step):
        at = self.at
        y = at.beside(step)
        return send(
            self.sum_y.at[y], self.last_y.at[at.y], self.last.at[step, 0], self.last.at[at.y, 1], at.column(y)
        )

    def second_x(self):
        at = self.at
        return send(self.sum_x, self.last_x, self.last.at[at.ys, 0], self.last.at[at.ys, 1], at.across())

    def second_start(self, fetch, rooms):
        at = self.at
        for step in range(1, at.ys):
            y = at.beside(step)
            fetch([(self.terms(y * 2 + at.x, 0), rooms[0]), (self.from_x.at[y], rooms[1])])
            add_into(self.sum_y.at[y], [rooms[0], rooms[1]])
        fetch([(self.terms(at.y * 2 + 1 - at.x, 1), self.sum_x)])
        for step in range(1, at.ys):
            y = at.beside(step)
            fetch([(self.from_y.at[y, 1 - at.x], rooms[0])])
            add_into(self.sum_x, [self.sum_x, rooms[0]])

    def second_load(self, fetch):
        at = self.at
        pairs = [(self.terms(at.y * 2 + 1 - at.x, 1), self.sum_x)]
        for step in range(1, at.ys):
            y = at.beside(step)
            pairs.append((self.terms(y * 2 + at.x, 0), self.sum_y.at[y]))
        fetch(pairs)

    def second_arrived(self):
        at = self.at
        terms = [self.sum_x]
        for step in range(1, at.ys):
            y = at.beside(step)
            add_into(self.sum_y.at[y], [self.sum_y.at[y], self.from_x.at[y]])
            terms.append(self.from_y.at[y, 1 - at.x])
        add_into(self.sum_x, terms)

    def second_go(self):
        for step in range(1, self.at.ys):
            self.second_y(step).start()
        self.second_x().start()

    def second_wait(self):
        at = self.at
        for step in range(1, at.ys):
            self.second_y(step).wait_send()
            y = at.beside(step)
            slot = self.last_y.at[y]
            send(slot, slot, self.last.at[step, 0], self.last.at[y, 1], at.across()).wait_recv()
        self.second_x().wait()


def norm_back(rows, load, store, gain, terms):
    def step(index, carry):
        window = pl.ds(pl.multiple_of(index * 16, 16), 16)
        values, incoming, base = load(window)
        root = lax.rsqrt(jnp.mean(values * values, axis=-1, keepdims=True) + epsilon)
        scaled = incoming * gain
        share = jnp.mean(values * scaled, axis=-1, keepdims=True)
        store(window, base + root * scaled - values * (root * root * root * share))
        term = incoming * values * root
        terms[...] += term[:8] + term[8:]
        return carry

    lax.fori_loop(0, rows // 16, step, 0)


class Exchange:
    def __init__(self, at, shard, everyone, gather_sems, local, sums, first, second):
        self.at, self.sums, self.first, self.second = at, sums, first, second
        count = shard.shape[0]
        slot = lambda w: everyone.at[pl.ds(pl.multiple_of(w * count, count), count)]
        self.gather = LineGather(at, slot, gather_sems)
        self.gather.start(shard)
        own = pltpu.make_async_copy(shard, slot(at.w), local)
        own.start()
        own.wait()
        self.last = 2 * (at.zs - 1)

    def level(self, index):
        at = self.at
        far, side = lax.div(index + 1, 2), lax.rem(index, 2)
        z = at.z + jnp.where(side == 1, -far, far)
        return far, side, z, (z >= 0) & (z < at.zs)

    def arrive(self, index):
        far, side, z, valid = self.level(index)

        @pl.when(side == 1)
        def _():
            self.gather.step(far - 1)

        @pl.when(valid)
        def _():
            self.gather.wait_over(z)
            self.first(z)

        return z, valid

    def put(self, z, begin, end):
        def step(piece, inner):
            self.second(z, piece)
            self.sums.over(z, piece).start()

            @pl.when(piece > begin)
            def _():
                self.sums.ends(z, piece - 1)

            return inner

        lax.fori_loop(begin, end, step, 0)
        self.sums.ends(z, end - 1)

    def whole(self, total, fill):
        at, sums = self.at, self.sums

        def turn(index, carry):
            z, valid = self.arrive(index)

            @pl.when(valid)
            def _():
                self.put(z, 0, sums.pieces)

            return carry

        lax.fori_loop(0, self.last + 1, turn, 0)
        fill(None, sums.pieces)
        for index in range(2, at.zs):
            sums.pass_on(index, fill if index == 2 else None)
        sums.finish(total)
        self.gather.sent()

    def by_columns(self, total, direct, relayed, near):
        at, sums = self.at, self.sums
        begin = min(3, self.last)

        def turn(index, carry):
            z, valid = self.arrive(index)

            @pl.when(index == begin)
            def _():
                direct()

            @pl.when(valid & (index >= begin))
            def _():
                self.put(z, 0, near)

            return carry

        lax.fori_loop(0, self.last + 1, turn, 0)

        def earlier(index, carry):
            _, _, z, valid = self.level(index)

            @pl.when(valid)
            def _():
                self.put(z, 0, near)

            return carry

        lax.fori_loop(1, begin, earlier, 0)
        if at.zs > 2:
            sums.pass_on(2, None, 0, near)
        relayed()

        def over(index, carry):
            _, _, z, valid = self.level(self.last - index)

            @pl.when(valid)
            def _():
                for piece in range(near, sums.pieces):
                    self.second(z, piece)
                    sums.over(z, piece).start()

            return carry

        lax.fori_loop(0, self.last, over, 0)

        def start(index, carry):
            _, _, z, valid = self.level(self.last - index)

            @pl.when(valid)
            def _():
                for piece in range(near, sums.pieces):
                    sums.ends(z, piece)

            return carry

        lax.fori_loop(0, self.last, start, 0)
        self.put(at.z, 0, sums.pieces)
        for index in range(3, at.zs):
            sums.pass_on(index, None, 0, near)
        for index in range(at.zs - 1, 1, -1):
            sums.pass_on(index, None, near, sums.pieces)
        sums.finish(total)
        self.gather.sent()


PIECES = 2


def feed_forward(normed, attended, teacher, lengths, gate_early, gate_up_shard, down_shard):
    seq, wt = lax.axis_size("seq"), lax.axis_size("wt")
    count, width = normed.shape
    units, block = gate_up_shard.shape[1:]
    early = early_rows(units)
    columns = down_shard.shape[1]
    tokens = wt * count
    zs = wt // 2
    half = units // 2

    def kernel(*refs):
        (normed_ref, attended_ref, teacher_ref, length_ref, early_ref, gate_shard_ref, shard_ref), refs = refs[:7], refs[7:]
        (final_out, error_out, energy_out), refs = refs[:3], refs[3:]
        (normed_out, gate_out, up_out, active_out, down_out, gates_out), refs = refs[:6], refs[6:]
        (everyone, gates, downs, gate_all, up_all, active_all, parts, total), refs = refs[:8], refs[8:]
        gather_sems, sum_scratch, late_sems, square_sems, (local, outgoing) = (
            refs[:1],
            refs[1:5],
            refs[5:8],
            refs[8:11],
            refs[11:],
        )
        at = Place(seq, wt)
        loads = [
            pltpu.make_async_copy(early_ref, gates.at[:, pl.ds(0, early)], local.at[4]),
            pltpu.make_async_copy(
                gate_shard_ref.at[:, pl.ds(early, units - early)],
                gates.at[:, pl.ds(early, units - early), pl.ds(pl.multiple_of(at.s * block, block), block)],
                local.at[0],
            ),
        ]
        for load in loads:
            load.start()
        at.meet(True, True)
        late = SquareGather(
            at,
            lambda s, h: gates.at[
                h, pl.ds(early, units - early), pl.ds(pl.multiple_of(s * block, block), block)
            ],
            lambda h: gate_shard_ref.at[h, pl.ds(early, units - early)],
            late_sems,
        )
        weights = SquareGather(
            at,
            lambda s, h: downs.at[
                pl.ds(h * half, half), pl.ds(pl.multiple_of(s * columns, columns), columns)
            ],
            lambda h: shard_ref.at[pl.ds(h * half, half)],
            square_sems,
        )
        ys = seq // 2

        def column_block(piece):
            if isinstance(piece, int):
                step = 0 if piece < 2 else piece - 1 if piece <= ys else piece - ys
                return at.beside(step) * 2 + (1 - at.x if piece == 1 or piece > ys else at.x)
            step = jnp.where(piece < 2, 0, jnp.where(piece <= ys, piece - 1, piece - ys))
            other = (piece == 1) | (piece > ys)
            return at.beside(step) * 2 + jnp.where(other, 1 - at.x, at.x)

        sums = LinePieces(
            at,
            lambda w: parts.at[pl.ds(pl.multiple_of(w * count, count), count)],
            sum_scratch,
            column_block,
        )
        down_store = pltpu.make_async_copy(downs, down_out, local.at[2])
        gates_store = pltpu.make_async_copy(gates, gates_out, local.at[0])

        def prepare():
            late.start()
            own = pltpu.make_async_copy(
                shard_ref, downs.at[:, pl.ds(pl.multiple_of(at.s * columns, columns), columns)], local.at[3]
            )
            own.start()
            late.relay()
            weights.start()
            own.wait()
            for load in loads:
                load.wait()
            late.finish()
            gates_store.start()

        def direct():
            weights.relay()
            weights.direct()

        def relayed():
            weights.relayed()
            down_store.start()

        def rows(z):
            return pl.ds(pl.multiple_of(z * 2 * count, 2 * count), 2 * count)

        def stores(z):
            return [
                pltpu.make_async_copy(source.at[rows(z)], target.at[rows(z)], outgoing.at[index, z])
                for index, (source, target) in enumerate(
                    ((everyone, normed_out), (gate_all, gate_out), (up_all, up_out), (active_all, active_out))
                )
            ]

        def first(z):
            here = everyone[rows(z), :]
            gate = contract_last(here, gates[0])
            up = contract_last(here, gates[1])
            gate_all[rows(z), :] = gate
            up_all[rows(z), :] = up
            active_all[rows(z), :] = gated_unit(gate, up).astype(jnp.bfloat16)
            for copy in stores(z):
                copy.start()

        def second(z, piece):
            window = sums.columns(piece)
            parts[rows(z), window] = jnp.dot(
                active_all[rows(z), :], downs[:, window], preferred_element_type=jnp.float32
            ).astype(jnp.bfloat16)

        work = Exchange(at, normed_ref, everyone, gather_sems, local.at[1], sums, first, second)
        prepare()
        work.by_columns(total, direct, relayed, ys + 1)
        energy_out[...] = jnp.zeros_like(energy_out)
        valid = length_ref[at.w]

        def finish_rows(index, carry):
            window = pl.ds(pl.multiple_of(index * 16, 16), 16)
            final = attended_ref[window, :] + total[window, :]
            final_out[window, :] = final.astype(jnp.bfloat16)
            place = at.s * count + index * 16 + lax.broadcasted_iota(jnp.int32, final.shape, 0)
            keep = (place < valid).astype(jnp.float32)
            error = (final - teacher_ref[window, :].astype(jnp.float32)) * keep
            error_out[window, :] = error
            squares = error * error
            energy_out[...] += 0.5 * (squares[:8] + squares[8:])
            return carry

        lax.fori_loop(0, count // 16, finish_rows, 0)
        down_store.wait()
        gates_store.wait()
        for z in range(zs):
            for copy in stores(z):
                copy.wait()

    low, f32 = jnp.bfloat16, jnp.float32
    return remote_call(
        kernel,
        "feed_forward",
        2,
        [
            jax.ShapeDtypeStruct((count, width), low),
            jax.ShapeDtypeStruct((count, width), f32),
            jax.ShapeDtypeStruct((8, width), f32),
            jax.ShapeDtypeStruct((tokens, width), low),
            jax.ShapeDtypeStruct((tokens, units), f32),
            jax.ShapeDtypeStruct((tokens, units), f32),
            jax.ShapeDtypeStruct((tokens, units), low),
            jax.ShapeDtypeStruct((units, width), low),
            jax.ShapeDtypeStruct((2, units, width), low),
        ],
        [
            pltpu.VMEM((tokens, width), low),
            pltpu.VMEM((2, units, width), low),
            pltpu.VMEM((units, width), low),
            pltpu.VMEM((tokens, units), f32),
            pltpu.VMEM((tokens, units), f32),
            pltpu.VMEM((tokens, units), low),
            pltpu.VMEM((tokens, width), low),
            pltpu.VMEM((count, width), f32),
        ]
        + LineGather.semaphores(wt, 2)
        + LinePieces.scratch(wt, (count, width), seq)
        + SquareGather.semaphores(seq)
        + SquareGather.semaphores(seq)
        + [pltpu.SemaphoreType.DMA((5,)), pltpu.SemaphoreType.DMA((4, zs))],
        normed,
        attended,
        teacher,
        lengths,
        gate_early,
        gate_up_shard,
        down_shard,
        in_specs=[VMEM] * 3 + [SMEM] + [ANY] * 2 + [VMEM],
        out_specs=[VMEM] * 3 + [ANY] * 6,
    )


def feed_back(error, attended, gain, gate_up, down, gate, up, active, normed):
    seq, wt = lax.axis_size("seq"), lax.axis_size("wt")
    count, width = error.shape
    units = gate_up.shape[1]
    tokens = wt * count
    ys = seq // 2
    block = width // seq
    half = (units // 2, block)

    def kernel(*refs):
        (error_ref, attended_ref, gain_ref, gate_up_ref, down_ref, gate_ref, up_ref, active_ref, normed_ref), refs = (
            refs[:9],
            refs[9:],
        )
        (grad_ref, mix_ref, gain_terms), refs = refs[:3], refs[3:]
        (gate_out, up_out, down_out, gate_x, gate_y, down_x, down_y), refs = refs[:7], refs[7:]
        (low, everyone, gates, downs, gate_all, up_all, back_all, parts, actives, columns), refs = refs[:10], refs[10:]
        (gate_terms, up_terms, down_terms, total), refs = refs[:4], refs[4:]
        gather_sems, sum_scratch, gate_sems, down_sems, (local, outgoing) = (
            refs[:1],
            refs[1:5],
            refs[5:7],
            refs[7:9],
            refs[9:],
        )
        at = Place(seq, wt)
        loads = [
            pltpu.make_async_copy(source, target, local.at[index])
            for index, (source, target) in enumerate(
                (
                    (down_ref, downs),
                    (gate_ref, gate_all),
                    (up_ref, up_all),
                    (gate_up_ref, gates),
                    (active_ref, actives),
                )
            )
        ]
        for load in loads:
            load.start()
        at.meet(True, True)
        low[...] = error_ref[...].astype(jnp.bfloat16)
        sums = LinePieces(
            at, lambda w: parts.at[pl.ds(pl.multiple_of(w * count, count), count)], sum_scratch
        )
        gate_sum = SquareTerms(at, lambda s, h: gate_terms.at[s, h], gate_x, gate_y, gate_sems)
        down_sum = SquareTerms(at, lambda s, h: down_terms.at[s, h], down_x, down_y, down_sems)

        def place(index):
            step = lax.div(index, 2) + 1
            x = lax.rem(at.x + 1 + lax.rem(index, 2), 2)
            return step, x, at.beside(step) * 2 + x

        def column_load(index):
            s = place(index)[2]
            return pltpu.make_async_copy(
                normed_ref.at[:, pl.ds(pl.multiple_of(s * block, block), block)],
                columns.at[lax.rem(index, 2)],
                local.at[6 + lax.rem(index, 2)],
            )

        def leave(sum_, index):
            step, x, s = place(index)

            @pl.when(x != at.x)
            def _():
                sum_.first_x(lax.div(s, 2)).start()

            @pl.when(step < ys)
            def _():
                sum_.first_y(step, x).start()

        def down_job(index):
            s = place(index)[2]
            term = contract_first(
                actives[...], everyone[:, pl.ds(pl.multiple_of(s * block, block), block)]
            ).astype(jnp.bfloat16)
            down_terms[s, 0] = term[: units // 2]
            down_terms[s, 1] = term[units // 2 :]
            leave(down_sum, index)

        def gate_job(index):
            s = place(index)[2]
            column_load(index).wait()
            here = columns.at[lax.rem(index, 2)]
            for number, terms in enumerate((gate_terms, up_terms)):
                term = contract_first(back_all[number], here[...]).astype(jnp.bfloat16)
                terms[s, 0] = term[: units // 2]
                terms[s, 1] = term[units // 2 :]

            @pl.when(index + 2 < seq)
            def _():
                column_load(index + 2).start()

            leave(gate_sum, index)

        def fill(slot, slots):
            if slot is None:
                lax.fori_loop(0, seq, lambda index, carry: (down_job(index), carry)[1], 0)
                return

            each = -(-seq // slots)

            def step(index, carry):
                job = slot * each + index

                @pl.when(job < seq)
                def _():
                    gate_job(job)

                return carry

            lax.fori_loop(0, each, step, 0)

        def prepare():
            column_load(0).start()
            column_load(1).start()
            for load in loads:
                load.wait()

        def rows(z):
            return pl.ds(pl.multiple_of(z * 2 * count, 2 * count), 2 * count)

        def first(z):
            active_back = contract_last(everyone[rows(z), :], downs[...])
            gate_here, up_here = gate_all[rows(z), :], up_all[rows(z), :]
            share = jax.nn.sigmoid(gate_here)
            back_all[0, rows(z), :] = (
                active_back * up_here * share * (1.0 + gate_here * (1.0 - share))
            ).astype(jnp.bfloat16)
            back_all[1, rows(z), :] = (active_back * gate_here * share).astype(jnp.bfloat16)

        def second(z, piece):
            window = pl.ds(pl.multiple_of(piece * sums.width, sums.width), sums.width)
            parts[rows(z), window] = (
                jnp.dot(back_all[0, rows(z), :], gates[0, :, window], preferred_element_type=jnp.float32)
                + jnp.dot(back_all[1, rows(z), :], gates[1, :, window], preferred_element_type=jnp.float32)
            ).astype(jnp.bfloat16)

        work = Exchange(at, low, everyone, gather_sems, local.at[5], sums, first, second)
        prepare()
        work.whole(total, fill)
        stores = [
            pltpu.make_async_copy(source, target, outgoing.at[index])
            for index, (source, target) in enumerate(
                ((gate_terms, gate_out), (up_terms, up_out), (down_terms, down_out))
            )
        ]
        for copy in stores:
            copy.start()
        gain_terms[...] = jnp.zeros_like(gain_terms)

        def load_rows(window):
            return attended_ref[window, :], total[window, :], error_ref[window, :]

        def store_rows(window, value):
            grad_ref[window, :] = value
            mix_ref[window, :] = value.astype(jnp.bfloat16)

        norm_back(count, load_rows, store_rows, gain_ref[1:2, :], gain_terms)
        for copy in stores:
            copy.wait()
        gate_sum.first_wait()
        down_sum.first_wait()

    def terms_of(half):
        return jax.ShapeDtypeStruct((seq, 2) + half, jnp.bfloat16)

    def first_of(half):
        return [
            jax.ShapeDtypeStruct((ys,) + half, jnp.bfloat16),
            jax.ShapeDtypeStruct((ys, 2) + half, jnp.bfloat16),
        ]

    return remote_call(
        kernel,
        "feed_back",
        3,
        [
            jax.ShapeDtypeStruct((count, width), jnp.float32),
            jax.ShapeDtypeStruct((count, width), jnp.bfloat16),
            jax.ShapeDtypeStruct((8, width), jnp.float32),
            terms_of(half),
            terms_of(half),
            terms_of(half),
        ]
        + first_of(half)
        + first_of(half),
        [
            pltpu.VMEM((count, width), jnp.bfloat16),
            pltpu.VMEM((tokens, width), jnp.bfloat16),
            pltpu.VMEM(gate_up.shape, jnp.bfloat16),
            pltpu.VMEM((units, width), jnp.bfloat16),
            pltpu.VMEM((tokens, units), jnp.float32),
            pltpu.VMEM((tokens, units), jnp.float32),
            pltpu.VMEM((2, tokens, units), jnp.bfloat16),
            pltpu.VMEM((tokens, width), jnp.bfloat16),
            pltpu.VMEM((tokens, units), jnp.bfloat16),
            pltpu.VMEM((2, tokens, block), jnp.bfloat16),
            pltpu.VMEM((seq, 2) + half, jnp.bfloat16),
            pltpu.VMEM((seq, 2) + half, jnp.bfloat16),
            pltpu.VMEM((seq, 2) + half, jnp.bfloat16),
            pltpu.VMEM((count, width), jnp.float32),
        ]
        + LineGather.semaphores(wt, 2)
        + LinePieces.scratch(wt, (count, width), PIECES)
        + SquareTerms.semaphores(seq)
        + SquareTerms.semaphores(seq)
        + [pltpu.SemaphoreType.DMA((8,)), pltpu.SemaphoreType.DMA((3,))],
        error,
        attended,
        gain,
        gate_up,
        down,
        gate,
        up,
        active,
        normed,
        in_specs=[VMEM] * 3 + [ANY] * 6,
        out_specs=[VMEM] * 3 + [ANY] * 7,
    )


def mixer_back(
    mix_back,
    attended_grad,
    tokens,
    gain,
    out_rows,
    qkv_columns,
    hidden,
    sorted_columns,
    mixer,
    mixed_values,
    head_outputs,
    segments,
    taps,
    order,
    gain_terms,
    energy,
    gate_parts,
    up_parts,
    down_parts,
):
    seq, wt = lax.axis_size("seq"), lax.axis_size("wt")
    zs, ys = wt // 2, seq // 2
    count, width = mix_back.shape
    length = count * seq
    heads = mixed_values.shape[0]
    qkv_width = qkv_columns.shape[1]
    value_width = heads * DV
    rank = width // (seq * wt)
    gate_half, down_half = gate_parts[0].shape[2:], down_parts[0].shape[2:]
    rows_at_once = 256
    big = [out_rows, qkv_columns, hidden, sorted_columns, mixer, mixed_values, head_outputs]
    small = [mix_back, attended_grad, tokens, gain, segments, taps, order, gain_terms, energy]
    far = list(gate_parts) + list(down_parts) + list(up_parts)

    def kernel(*refs):
        big_refs, refs = refs[: len(big)], refs[len(big) :]
        small_refs, refs = refs[: len(small)], refs[len(small) :]
        (gate_t, gate_x, gate_y, down_t, down_x, down_y, up_t), refs = refs[: len(far)], refs[len(far) :]
        (grad_out, sums_out, qkv_out, w_out_out, up_x, up_y), refs = refs[:6], refs[6:]
        gate_lasts, up_lasts, down_lasts, refs = refs[:2], refs[2:4], refs[4:6], refs[6:]
        (w_out_v, w_qkv_v, hidden_v, sorted_v, mixer_v, values_v, outputs_v), refs = refs[:7], refs[7:]
        (mix_all, mixer_grad, query_acc, key_acc, value_acc, back_sorted, back_v), refs = refs[:7], refs[7:]
        (hidden_parts, qkv_parts, out_parts, hidden_total, gain_acc, spread, taps_acc), refs = refs[:7], refs[7:]
        (segment_column, tap_v), refs = refs[:2], refs[2:]
        (room_gate0, room_gate1, room_down0, room_down1, qkv_sum, first, middle, last), refs = refs[:8], refs[8:]
        hidden_scratch, refs = refs[:8], refs[8:]
        qkv_scratch, out_scratch, refs = refs[:4], refs[4:8], refs[8:]
        gate_scratch, down_scratch, up_scratch, refs = refs[:3], refs[3:6], refs[6:9], refs[9:]
        gather_sems, up_sems, refs = refs[:3], refs[3:5], refs[5:]
        local, swap, first_sems, last_sems = refs
        (
            mix_ref,
            grad_ref,
            token_ref,
            gain_ref,
            segment_ref,
            tap_ref,
            order_ref,
            gain_two,
            energy_ref,
        ) = small_refs
        at = Place(seq, wt)
        loads = [
            pltpu.make_async_copy(source, target, local.at[4 + index])
            for index, (source, target) in enumerate(
                zip(big_refs, (w_out_v, w_qkv_v, hidden_v, sorted_v, mixer_v, values_v, outputs_v))
            )
        ]
        for load in loads:
            load.start()
        at.meet(True, True)
        half = count // 2
        gather = SquareGather(
            at,
            lambda s, h: mix_all.at[pl.ds(pl.multiple_of(s * count + h * half, half), half)],
            lambda h: mix_ref.at[pl.ds(h * half, half)],
            gather_sems,
        )
        gather.start()
        own = pltpu.make_async_copy(
            mix_ref, mix_all.at[pl.ds(pl.multiple_of(at.s * count, count), count)], local.at[3]
        )
        own.start()

        def fetch(pairs):
            copies = [
                pltpu.make_async_copy(source, target, local.at[index])
                for index, (source, target) in enumerate(pairs)
            ]
            for copy in copies:
                copy.start()
            for copy in copies:
                copy.wait()

        gate_sum = SquareTerms(at, lambda s, h: gate_t.at[s, h], gate_x, gate_y, None, gate_lasts, gate_scratch)
        down_sum = SquareTerms(at, lambda s, h: down_t.at[s, h], down_x, down_y, None, down_lasts, down_scratch)
        up_sum = SquareTerms(at, lambda s, h: up_t.at[s, h], up_x, up_y, up_sems, up_lasts, up_scratch)
        gate_rooms, down_rooms = (room_gate0, room_gate1), (room_down0, room_down1)
        gate_sum.second_start(fetch, gate_rooms)
        down_sum.second_start(fetch, down_rooms)
        up_sum.second_load(fetch)
        tap_v[...] = tap_ref[...].astype(jnp.float32)
        segment_row = segment_ref[...].astype(jnp.float32)
        segment_column[...] = jnp.broadcast_to(segment_row, (128, length)).T
        own.wait()
        for load in loads:
            load.wait()
        query_acc[...] = jnp.zeros_like(query_acc)
        key_acc[...] = jnp.zeros_like(key_acc)
        value_acc[...] = jnp.zeros_like(value_acc)
        gather.relay()
        gather.finish()
        gate_sum.second_go()
        down_sum.second_go()
        up_sum.first_start()
        mixer_grad[...] = contract_last(mix_all[...], w_out_v[...]).astype(jnp.bfloat16)
        out_sum = LinePieces(at, lambda w: out_parts.at[w], out_scratch)
        out_rank = out_parts.shape[1]
        out_block = 512 if value_width % 512 == 0 else value_width

        def out_job(index, carry):
            window = pl.ds(pl.multiple_of(index * 512, 512), 512)
            term = contract_first(mixer_v[...], mix_all[:, window]).astype(jnp.bfloat16)
            for w in range(wt):
                out_parts[w, :, window] = term[w * out_rank : (w + 1) * out_rank]
            return carry

        lax.fori_loop(0, width // 512, out_job, 0)
        out_sum.begin()

        steps = length // rows_at_once
        lanes = lax.broadcasted_iota(jnp.int32, (1, 128), 1)

        def attend(index, carry):
            head, start = lax.div(index, steps), lax.rem(index, steps) * rows_at_once
            rows = pl.ds(pl.multiple_of(start, rows_at_once), rows_at_once)
            columns = pl.ds(pl.multiple_of(head * DV, DV), DV)
            mine = ((lanes >= head * FEAT) & (lanes < head * FEAT + FEAT)).astype(jnp.float32)
            queries = sorted_v[rows, value_width : value_width + 128] * mine.astype(jnp.bfloat16)
            keys = sorted_v[:, value_width + 128 :]
            scores = contract_last(queries, keys) * 0.25
            places = start + lax.broadcasted_iota(jnp.int32, scores.shape, 0)
            allowed = (segment_column[rows, :1] == segment_row) & (
                places >= lax.broadcasted_iota(jnp.int32, scores.shape, 1)
            )
            kernel_values = jnp.where(allowed, 1.0 + scores + 0.5 * scores * scores, 0.0)
            denominator = jnp.sum(kernel_values, axis=1, keepdims=True)
            incoming = mixer_grad[rows, columns].astype(jnp.float32)
            numerator_back = (incoming / denominator).astype(jnp.bfloat16)
            denominator_back = (
                -jnp.sum(incoming * outputs_v[head, rows, :], axis=1, keepdims=True) / denominator
            )
            weight_back = contract_last(numerator_back, values_v[head])
            kernel_back = jnp.where(allowed, weight_back + denominator_back, 0.0)
            dots_back = (0.25 * kernel_back * (1.0 + scores)).astype(jnp.bfloat16)
            query_acc[rows, :] += jnp.dot(dots_back, keys, preferred_element_type=jnp.float32) * mine
            key_acc[...] += contract_first(dots_back, queries)
            value_acc[:, columns] += contract_first(kernel_values.astype(jnp.bfloat16), numerator_back)
            return carry

        middle_step = heads * steps // 2
        lax.fori_loop(0, middle_step, attend, 0)
        for index in range(zs - 1, 1, -1):
            if index == zs // 2:
                lax.fori_loop(middle_step, heads * steps, attend, 0)
            out_sum.pass_on(index)
        taps_acc[...] = jnp.zeros_like(taps_acc)
        marks = tap_marks(segment_column)

        def convolve(head, carry):
            columns = pl.ds(pl.multiple_of(head * DV, DV), DV)
            mixed_back = value_acc[:, columns]
            raw = sorted_v[:, columns].astype(jnp.float32)
            raw_back = tap_v[0:1, columns] * mixed_back
            taps_acc[3:4, columns] = jnp.sum(mixed_back * raw, axis=0, keepdims=True)
            for tap in range(1, KCONV):
                masked = mixed_back * marks[tap]
                taps_acc[3 + tap : 4 + tap, columns] = jnp.sum(
                    masked * pltpu.roll(raw, tap, 0), axis=0, keepdims=True
                )
                raw_back = raw_back + tap_v[tap : tap + 1, columns] * pltpu.roll(masked, length - tap, 0)
            back_sorted[:, columns] = raw_back.astype(jnp.bfloat16)
            return carry

        lax.fori_loop(0, heads, convolve, 0)
        back_sorted[:, value_width : value_width + 128] = query_acc[...].astype(jnp.bfloat16)
        back_sorted[:, value_width + 128 :] = key_acc[...].astype(jnp.bfloat16)
        back_v[...] = contract_last(back_sorted[...], order_ref[...]).astype(jnp.bfloat16)
        hidden_sum = SquareSum(at, lambda s, h: hidden_parts.at[s, h], hidden_scratch)

        def hidden_job(index, carry):
            window = pl.ds(pl.multiple_of(index * 512, 512), 512)
            term = contract_last(back_v[...], w_qkv_v[window, :]).astype(jnp.bfloat16)
            for s in range(seq):
                for h in range(2):
                    begin = s * count + h * half
                    hidden_parts[s, h, :, window] = term[begin : begin + half]
            return carry

        lax.fori_loop(0, width // 512, hidden_job, 0)
        hidden_sum.start()
        qkv_sums = LinePieces(at, lambda w: qkv_parts.at[:, w], qkv_scratch)
        qkv_rank = qkv_parts.shape[2]

        def qkv_job(s, carry):
            block = wt * qkv_rank
            window = pl.ds(pl.multiple_of(s * block, block), block)
            term = contract_first(hidden_v[:, window], back_v[...]).astype(jnp.bfloat16)
            for w in range(wt):
                qkv_parts[s, w] = term[w * qkv_rank : (w + 1) * qkv_rank]
            return carry

        lax.fori_loop(0, seq, qkv_job, 0)
        qkv_sums.begin()
        qkv_sums.pass_on(zs - 1)
        hidden_sum.relay()
        up_sum.first_wait()
        up_sum.second_arrived()
        up_sum.second_go()
        for index in range(zs - 2, 1, -1):
            qkv_sums.pass_on(index)
        hidden_sum.finish(lambda h: hidden_total.at[h])
        gain_acc[...] = jnp.zeros_like(gain_acc)
        for h in range(2):

            def shift(window):
                return pl.ds(pl.multiple_of(h * half + window.start, 16), 16)

            def load_rows(window):
                rows = shift(window)
                return token_ref[rows, :].astype(jnp.float32), hidden_total[h, window, :], grad_ref[rows, :]

            def store_rows(window, value):
                grad_out[shift(window), :] = value

            norm_back(half, load_rows, store_rows, gain_ref[0:1, :], gain_acc)
        spread[...] = jnp.zeros_like(spread)
        spread[0:1, :] = jnp.sum(gain_acc[...], axis=0, keepdims=True)
        spread[1:2, :] = jnp.sum(gain_two[...], axis=0, keepdims=True)
        energy = jnp.sum(jnp.sum(energy_ref[...], axis=0, keepdims=True), axis=1, keepdims=True)
        spread[2:3, :] = jnp.broadcast_to(energy, (1, width))
        copies = []
        for step in range(1, seq):
            to = lax.rem(at.s + step, seq)
            window = pl.ds(pl.multiple_of(to * value_width, value_width), value_width)
            copies.append(
                send(spread.at[:, window], first.at[at.s], first_sems.at[step, 0], first_sems.at[at.s, 1], (to, at.w))
            )
        for copy in copies:
            copy.start()
        qkv_sums.finish(qkv_sum)
        for step in range(1, seq):
            to = lax.rem(at.s + step, seq)
            copy = send(qkv_sum.at[to], qkv_out.at[at.s], swap.at[step, 0], swap.at[at.s, 1], (to, at.w))
            copy.start()
            copies.append(copy)
        add_into(qkv_out.at[at.s], [qkv_sum.at[at.s]])
        out_sum.finish(w_out_out)
        terms = [spread.at[:, pl.ds(pl.multiple_of(at.s * value_width, value_width), value_width)], taps_acc]
        for step in range(1, seq):
            s = lax.rem(at.s + step, seq)
            slot = first.at[s]
            send(slot, slot, first_sems.at[step, 0], first_sems.at[s, 1], at.across()).wait_recv()
            terms.append(slot)
        add_into(middle, terms)
        for step in range(1, wt):
            to = lax.rem(at.w + step, wt)
            copy = send(middle, last.at[at.w], last_sems.at[step, 0], last_sems.at[at.w, 1], (at.s, to))
            copy.start()
            copies.append(copy)
        gate_sum.second_wait()
        down_sum.second_wait()
        terms = [middle]
        for step in range(1, wt):
            w = lax.rem(at.w + step, wt)
            slot = last.at[w]
            send(slot, slot, last_sems.at[step, 0], last_sems.at[w, 1], at.partner()).wait_recv()
            terms.append(slot)
        add_into(sums_out, terms)
        for step in range(1, seq):
            s = lax.rem(at.s + step, seq)
            slot = qkv_out.at[s]
            send(slot, slot, swap.at[step, 0], swap.at[s, 1], at.across()).wait_recv()
        up_sum.second_wait()
        for copy in copies:
            copy.wait_send()

    out_rank, qkv_rank = value_width // wt, width // (seq * wt)
    f32, low = jnp.float32, jnp.bfloat16
    tile = (8, value_width)
    results = remote_call(
        kernel,
        "mixer_back",
        4,
        [
            jax.ShapeDtypeStruct((count, width), f32),
            jax.ShapeDtypeStruct(tile, f32),
            jax.ShapeDtypeStruct((seq, qkv_rank, qkv_width), f32),
            jax.ShapeDtypeStruct((out_rank, width), f32),
            jax.ShapeDtypeStruct((ys,) + gate_half, low),
            jax.ShapeDtypeStruct((ys, 2) + gate_half, low),
        ]
        + [
            jax.ShapeDtypeStruct(shape, low)
            for shape_half in (gate_half, gate_half, down_half)
            for shape in ((ys,) + shape_half, shape_half)
        ],
        [pltpu.VMEM(array.shape, array.dtype) for array in big]
        + [
            pltpu.VMEM((length, width), low),
            pltpu.VMEM((length, value_width), low),
            pltpu.VMEM((length, 128), f32),
            pltpu.VMEM((length, 128), f32),
            pltpu.VMEM((length, value_width), f32),
            pltpu.VMEM((length, value_width + 256), low),
            pltpu.VMEM((length, qkv_width), low),
            pltpu.VMEM((seq, 2, count // 2, width), low),
            pltpu.VMEM((seq, wt, qkv_rank, qkv_width), low),
            pltpu.VMEM((wt, out_rank, width), low),
            pltpu.VMEM((2, count // 2, width), f32),
            pltpu.VMEM((8, width), f32),
            pltpu.VMEM((8, width), f32),
            pltpu.VMEM(tile, f32),
            pltpu.VMEM((length, 128), f32),
            pltpu.VMEM((KCONV, value_width), f32),
            pltpu.VMEM(gate_half, low),
            pltpu.VMEM(gate_half, low),
            pltpu.VMEM(down_half, low),
            pltpu.VMEM(down_half, low),
            pltpu.VMEM((seq, qkv_rank, qkv_width), f32),
            pltpu.VMEM((seq,) + tile, f32),
            pltpu.VMEM(tile, f32),
            pltpu.VMEM((wt,) + tile, f32),
        ]
        + SquareSum.scratch(seq, (count // 2, width))
        + LinePieces.scratch(wt, (seq, qkv_rank, qkv_width), seq)
        + LinePieces.scratch(wt, (out_rank, width), 1)
        + SquareTerms.scratch(seq, gate_half)
        + SquareTerms.scratch(seq, down_half)
        + SquareTerms.scratch(seq, gate_half)
        + SquareGather.semaphores(seq)
        + SquareTerms.semaphores(seq)
        + [
            pltpu.SemaphoreType.DMA((11,)),
            pltpu.SemaphoreType.DMA((seq, 2)),
            pltpu.SemaphoreType.DMA((seq, 2)),
            pltpu.SemaphoreType.DMA((wt, 2)),
        ],
        *big,
        *small,
        *far,
        in_specs=[ANY] * len(big) + [VMEM] * len(small) + [ANY] * len(far),
        out_specs=[VMEM] * 6 + [ANY] * 6,
    )
    grad, totals, qkv_total, out_total, up_x, up_y = results[:6]
    gate = tuple(gate_parts) + tuple(results[6:8])
    up = tuple(up_parts) + (up_x, up_y) + tuple(results[8:10])
    down = tuple(down_parts) + tuple(results[10:12])
    return grad, totals, gate, up, down, qkv_total, out_total


def last_sums(gate, up, down, qkv_total, totals, lengths, out_total, grad, final, qkv_shape):
    seq, wt = lax.axis_size("seq"), lax.axis_size("wt")
    ys = seq // 2
    f32, low = jnp.float32, jnp.bfloat16
    gate_half, down_half = gate[0].shape[2:], down[0].shape[2:]
    total_width = totals.shape[1]
    lanes_each = total_width // wt
    width = grad.shape[1]
    qkv_width = qkv_total.shape[2]
    operands = list(gate) + list(up) + list(down)
    passed = [out_total, grad, final]

    def kernel(*refs):
        groups, refs = [refs[5 * index : 5 * index + 5] for index in range(3)], refs[15:]
        (qkv_ref, totals_ref, length_ref), passed_refs, refs = refs[:3], refs[3:6], refs[6:]
        (gate_up_out, down_out, qkv_out, first_gain, second_gain, taps_out, loss_out), refs = refs[:7], refs[7:]
        passed_outs, refs = refs[:3], refs[3:]
        totals, refs = refs[:2], refs[2:]
        passed_rooms, refs = refs[:3], refs[3:]
        rooms, (loads, stores, pass_sems) = [refs[5 * index : 5 * index + 5] for index in range(3)], refs[15:]
        s = lax.axis_index("seq")
        y, x = lax.div(s, 2), lax.rem(s, 2)
        copies = []
        for number, (group, room) in enumerate(zip(groups, rooms)):
            terms, from_x, from_y, last_y, last_x = group
            sources = (terms.at[s], from_x.at[y], from_y.at[:, x], last_y, last_x)
            mine = [
                pltpu.make_async_copy(source, target, loads.at[number, index])
                for index, (source, target) in enumerate(zip(sources, room))
            ]
            for copy in mine:
                copy.start()
            copies.append(mine)
        ins = [
            pltpu.make_async_copy(source, room, pass_sems.at[index, 0])
            for index, (source, room) in enumerate(zip(passed_refs, passed_rooms))
        ]
        for copy in ins:
            copy.start()
        shift = lax.rem(total_width - lax.axis_index("wt") * lanes_each, total_width)
        mine = pltpu.roll(totals_ref[...], shift, 1)[:, :lanes_each]
        first_gain[...] = mine[0:1]
        second_gain[...] = mine[1:2]
        taps_out[...] = mine[3 : 3 + KCONV]
        counted = length_ref[0]
        for index in range(1, length_ref.shape[0]):
            counted = counted + length_ref[index]
        loss_out[...] = 2.0 * totals_ref[2:3, :1] / (jnp.full((1, 1), counted, jnp.int32).astype(f32) * width)
        for index in range(seq):
            qkv_out[:, index * qkv_width : (index + 1) * qkv_width] = qkv_ref[index]
        outs = []
        for index, (room, target) in enumerate(zip(passed_rooms, passed_outs)):
            ins[index].wait()
            copy = pltpu.make_async_copy(room, target, pass_sems.at[index, 1])
            copy.start()
            outs.append(copy)
        for number, room in enumerate(rooms):
            own, near_x, near_y, last_y, last_x = room
            total = totals[number // 2]
            base = 2 * (number % 2)
            for copy in copies[number]:
                copy.wait()
            rows = own.shape[1]
            tile = next(t for t in (64, 32, 16) if rows % t == 0)

            def step(index, carry):
                window = pl.ds(pl.multiple_of(index * tile, tile), tile)
                first = own[0, window, :].astype(f32) + near_x[window, :].astype(f32)
                second = own[1, window, :].astype(f32) + last_x[window, :].astype(f32)
                for other in range(1, ys):
                    place = lax.rem(y + other, ys)
                    first = first + last_y[place, window, :].astype(f32)
                    second = second + near_y[place, window, :].astype(f32)
                total[base, window, :] = first
                total[base + 1, window, :] = second
                return carry

            lax.fori_loop(0, rows // tile, step, 0)
            target = gate_up_out.at[pl.ds(base, 2)] if number < 2 else down_out
            copy = pltpu.make_async_copy(total.at[pl.ds(base, 2)], target, stores.at[number])
            copy.start()
            outs.append(copy)
        for copy in outs:
            copy.wait()

    def rooms(half):
        return [
            pltpu.VMEM((2,) + half, low),
            pltpu.VMEM(half, low),
            pltpu.VMEM((ys,) + half, low),
            pltpu.VMEM((ys,) + half, low),
            pltpu.VMEM(half, low),
        ]

    return pl.pallas_call(
        kernel,
        name="last_sums",
        out_shape=[
            jax.ShapeDtypeStruct((4,) + gate_half, f32),
            jax.ShapeDtypeStruct((2,) + down_half, f32),
            jax.ShapeDtypeStruct(qkv_shape, f32),
            jax.ShapeDtypeStruct((1, lanes_each), f32),
            jax.ShapeDtypeStruct((1, lanes_each), f32),
            jax.ShapeDtypeStruct((KCONV, lanes_each), f32),
            jax.ShapeDtypeStruct((1, 1), f32),
        ]
        + [jax.ShapeDtypeStruct(array.shape, array.dtype) for array in passed],
        in_specs=[ANY] * 15 + [VMEM] * 2 + [SMEM] + [ANY] * 3,
        out_specs=[ANY] * 2 + [VMEM] * 5 + [ANY] * 3,
        scratch_shapes=[pltpu.VMEM((4,) + gate_half, f32), pltpu.VMEM((2,) + down_half, f32)]
        + [pltpu.VMEM(array.shape, array.dtype) for array in passed]
        + rooms(gate_half) * 2
        + rooms(down_half)
        + [
            pltpu.SemaphoreType.DMA((3, 5)),
            pltpu.SemaphoreType.DMA((3,)),
            pltpu.SemaphoreType.DMA((3, 2)),
        ],
        compiler_params=pltpu.CompilerParams(vmem_limit_bytes=VMEM_LIMIT),
    )(*operands, qkv_total, totals, lengths, *passed)


def rows_of_tile(values, row):
    return jnp.pad(values[None, :], [(row, 7 - row), (0, 128 - values.shape[0])])


def body(
    inputs,
    segment_ids,
    valid_lengths,
    teacher,
    w_qkv,
    conv_weight,
    w_out,
    norm_gain,
    w_gate_up,
    w_down,
    mlp_gain,
):
    seq_parts = lax.axis_size("seq")
    tok_count = inputs.shape[1]
    model_width = inputs.shape[2]
    length = tok_count * seq_parts
    head_count = H // seq_parts
    qkv_width = head_count * (2 * FEAT + DV)
    rows_low = inputs[0]
    gain_lanes = norm_gain.shape[0]
    gains = rows_of_tile(norm_gain.astype(jnp.float32), 0) + rows_of_tile(mlp_gain.astype(jnp.float32), 1)
    qkv_rows = w_qkv
    if qkv_width % 128:
        qkv_rows = w_qkv.reshape(w_qkv.shape[0], seq_parts, qkv_width).transpose(1, 0, 2)
    gate_up_low = w_gate_up.swapaxes(1, 2)
    segments = segment_ids
    (
        attended,
        normed_low,
        gain_rows,
        qkv_columns,
        out_rows,
        hidden_low,
        sorted_columns,
        mixer_low,
        mixed_values,
        head_outputs,
        gate_early,
        order,
    ) = mixer_forward(rows_low, qkv_rows, w_out, gains, gate_up_low, segments, conv_weight)
    (
        final_low,
        residual_error,
        energy,
        normed_all,
        gate_all,
        up_all,
        active_all,
        down_part,
        gate_up_part,
    ) = feed_forward(normed_low, attended, teacher[0], valid_lengths, gate_early, gate_up_low, w_down)
    (
        attended_grad,
        mix_back,
        gain_two_terms,
        gate_terms,
        up_terms,
        down_terms,
        gate_from_x,
        gate_from_y,
        down_from_x,
        down_from_y,
    ) = feed_back(
        residual_error,
        attended,
        gain_rows,
        gate_up_part,
        down_part,
        gate_all,
        up_all,
        active_all,
        normed_all,
    )
    inputs_grad, totals, gate, up, down, qkv_total, out_total = mixer_back(
        mix_back,
        attended_grad,
        rows_low,
        gain_rows,
        out_rows.reshape(head_count * DV, model_width),
        qkv_columns.reshape(model_width, qkv_width),
        hidden_low,
        sorted_columns,
        mixer_low,
        mixed_values,
        head_outputs,
        segments,
        conv_weight,
        order,
        gain_two_terms,
        energy,
        (gate_terms, gate_from_x, gate_from_y),
        (up_terms,),
        (down_terms, down_from_x, down_from_y),
    )
    (
        grad_w_gate_up,
        grad_w_down,
        grad_w_qkv,
        grad_norm_gain,
        grad_mlp_gain,
        grad_conv,
        mean_loss,
        grad_w_out,
        inputs_grad,
        outputs,
    ) = last_sums(
        gate, up, down, qkv_total, totals, valid_lengths, out_total, inputs_grad, final_low, w_qkv.shape
    )
    return (
        outputs[None],
        inputs_grad[None],
        mean_loss.reshape(()),
        grad_w_qkv,
        grad_conv,
        grad_w_out,
        grad_norm_gain.reshape(norm_gain.shape),
        grad_w_gate_up.reshape(gate_up_low.shape).swapaxes(1, 2),
        grad_w_down.reshape(w_down.shape),
        grad_mlp_gain.reshape(mlp_gain.shape),
    )


def solution(mesh):
    in_specs = (
        P("wt", "seq", None),
        P("wt", None),
        P(),
        P("wt", "seq", None),
        P(("seq", "wt"), None),
        P(None, "seq"),
        P(("seq", "wt"), None),
        P(("seq", "wt")),
        P(None, "seq", "wt"),
        P("wt", "seq"),
        P(("seq", "wt")),
    )
    out_specs = (
        P("wt", "seq", None),
        P("wt", "seq", None),
        P(),
        P(("seq", "wt"), None),
        P(None, ("seq", "wt")),
        P(("seq", "wt"), None),
        P(("seq", "wt")),
        P(None, "seq", "wt"),
        P("wt", "seq"),
        P(("seq", "wt")),
    )
    return jax.shard_map(body, mesh=mesh, in_specs=in_specs, out_specs=out_specs, check_vma=False)
```

```python
from functools import partial

import jax
import jax.numpy as jnp
from jax import lax
from jax.experimental import pallas as pl
from jax.experimental.pallas import tpu as pltpu
from jax.sharding import PartitionSpec as P

H = 16
FEAT = 16
KCONV = 3
DV = 128


epsilon = 1e-05


def rms_norm(values, gain_vector):
    inverse_root = lax.rsqrt(jnp.mean(values * values, axis=-1, keepdims=True) + epsilon)
    return values * inverse_root * gain_vector


def contract_last(former, latter):
    return lax.dot_general(
        former, latter, (((1,), (1,)), ((), ())), preferred_element_type=jnp.float32
    )


def contract_first(former, latter):
    return lax.dot_general(
        former, latter, (((0,), (0,)), ((), ())), preferred_element_type=jnp.float32
    )


def shift_down(values, amount, filler):
    padding = jnp.full((amount,) + values.shape[1:], filler, values.dtype)
    return jnp.concatenate([padding, values[:-amount]], axis=0)


def gated_unit(gate_in, up_in):
    return jax.nn.silu(gate_in) * up_in


MESH = pl.DeviceIdType.MESH
VMEM = pl.BlockSpec(memory_space=pltpu.VMEM)
ANY = pl.BlockSpec(memory_space=pl.ANY)
SMEM = pl.BlockSpec(memory_space=pltpu.SMEM)
VMEM_LIMIT = 63 * 1024 * 1024


class Place:
    def __init__(self, seq, wt):
        self.seq, self.wt = seq, wt
        self.ys, self.zs = seq // 2, wt // 2
        self.s, self.w = lax.axis_index("seq"), lax.axis_index("wt")
        self.y, self.x = lax.div(self.s, 2), lax.rem(self.s, 2)
        self.z, self.c = lax.div(self.w, 2), lax.rem(self.w, 2)

    def across(self):
        return (self.y * 2 + 1 - self.x, self.w)

    def beside(self, step):
        return lax.rem(self.y + step, self.ys)

    def column(self, y):
        return (y * 2 + self.x, self.w)

    def partner(self):
        return (self.s, self.z * 2 + 1 - self.c)

    def level(self, z):
        return (self.s, z * 2 + self.c)

    def meet(self, square, line):
        barrier = pltpu.get_barrier_semaphore()
        count = 0
        if square:
            for step in range(1, self.seq):
                device = (lax.rem(self.s + step, self.seq), self.w)
                pl.semaphore_signal(barrier, inc=1, device_id=device, device_id_type=MESH)
                count += 1
        if line:
            for step in range(1, self.wt):
                device = (self.s, lax.rem(self.w + step, self.wt))
                pl.semaphore_signal(barrier, inc=1, device_id=device, device_id_type=MESH)
                count += 1
        pl.semaphore_wait(barrier, count)


def send(source, target, leaving, arriving, device):
    return pltpu.make_async_remote_copy(
        src_ref=source,
        dst_ref=target,
        send_sem=leaving,
        recv_sem=arriving,
        device_id=device,
        device_id_type=MESH,
    )


def add_into(target, sources):
    if len(target.shape) == 3:
        for index in range(target.shape[0]):
            add_into(target.at[index], [source.at[index] for source in sources])
        return
    rows = target.shape[0]
    tile = next(t for t in (64, 32, 16, 8, rows) if rows % t == 0)

    def step(index, carry):
        window = pl.ds(pl.multiple_of(index * tile, tile), tile)
        total = sources[0][window, :].astype(jnp.float32)
        for source in sources[1:]:
            total = total + source[window, :].astype(jnp.float32)
        target[window, :] = total.astype(target.dtype)
        return carry

    lax.fori_loop(0, rows // tile, step, 0)


class SquareGather:
    @staticmethod
    def semaphores(seq):
        return [
            pltpu.SemaphoreType.DMA((2 + seq // 2,)),
            pltpu.SemaphoreType.DMA((seq // 2, 3)),
            pltpu.SemaphoreType.DMA((seq, 2)),
        ]

    def __init__(self, at, view, own, sems):
        self.at, self.view, self.own = at, view, own
        self.over_x, self.over_y, self.got = sems
        self.sent = []

    def go(self, copy):
        copy().start()
        self.sent.append(copy)

    def own_x(self, half):
        at = self.at
        target = self.view(at.s, half)
        return send(self.own(half), target, self.over_x.at[half], self.got.at[at.s, half], at.across())

    def own_y(self, step, half):
        at = self.at
        target, device = self.view(at.s, half), at.column(at.beside(step))
        return send(self.own(half), target, self.over_y.at[step, half], self.got.at[at.s, half], device)

    def pass_y(self, step):
        at = self.at
        s = at.y * 2 + 1 - at.x
        slot, device = self.view(s, 0), at.column(at.beside(step))
        return send(slot, slot, self.over_y.at[step, 2], self.got.at[s, 0], device)

    def pass_x(self, step):
        s = self.at.beside(step) * 2 + self.at.x
        slot = self.view(s, 1)
        return send(slot, slot, self.over_x.at[1 + step], self.got.at[s, 1], self.at.across())

    def wait(self, s, half):
        slot = self.view(s, half)
        send(slot, slot, self.over_x.at[0], self.got.at[s, half], self.at.across()).wait_recv()

    def start(self):
        for half in range(2):
            self.go(partial(self.own_x, half))
            for step in range(1, self.at.ys):
                self.go(partial(self.own_y, step, 1 - half))

    def relay(self):
        at = self.at
        self.wait(at.y * 2 + 1 - at.x, 0)
        for step in range(1, at.ys):
            self.go(partial(self.pass_y, step))
        for step in range(1, at.ys):
            self.wait(at.beside(step) * 2 + at.x, 1)
            self.go(partial(self.pass_x, step))

    def direct(self):
        at = self.at
        self.wait(at.y * 2 + 1 - at.x, 1)
        for step in range(1, at.ys):
            self.wait(at.beside(step) * 2 + at.x, 0)

    def relayed(self):
        at = self.at
        for step in range(1, at.ys):
            y = at.beside(step)
            self.wait(y * 2 + 1 - at.x, 0)
            self.wait(y * 2 + 1 - at.x, 1)
        for copy in self.sent:
            copy().wait_send()

    def finish(self):
        self.direct()
        self.relayed()


class SquareSum:
    @staticmethod
    def scratch(seq, half_shape):
        ys = seq // 2
        return [
            pltpu.VMEM((ys,) + half_shape, jnp.bfloat16),
            pltpu.VMEM((ys, 2) + half_shape, jnp.bfloat16),
            pltpu.VMEM((ys,) + half_shape, jnp.bfloat16),
            pltpu.VMEM(half_shape, jnp.bfloat16),
            pltpu.VMEM((ys,) + half_shape, jnp.bfloat16),
            pltpu.VMEM(half_shape, jnp.bfloat16),
            pltpu.SemaphoreType.DMA((ys, 2, 2)),
            pltpu.SemaphoreType.DMA((ys, 3, 2)),
        ]

    def __init__(self, at, part, scratch):
        self.at, self.part = at, part
        self.from_x, self.from_y, self.last_y, self.last_x, self.sum_y, self.sum_x, self.xs, self.yss = scratch
        self.sent = []

    def go(self, source, target, leaving, arriving, device):
        copy = send(source, target, leaving, arriving, device)
        copy.start()
        self.sent.append(copy)

    def wait(self, slot, leaving, arriving):
        send(slot, slot, leaving, arriving, self.at.across()).wait_recv()

    def start(self):
        at = self.at
        for y in range(at.ys):
            self.go(
                self.part(y * 2 + 1 - at.x, 0),
                self.from_x.at[y],
                self.xs.at[y, 0, 0],
                self.xs.at[y, 0, 1],
                at.across(),
            )
        for step in range(1, at.ys):
            y = at.beside(step)
            for x in range(2):
                self.go(
                    self.part(y * 2 + x, 1),
                    self.from_y.at[at.y, x],
                    self.yss.at[step, x, 0],
                    self.yss.at[at.y, x, 1],
                    at.column(y),
                )

    def relay(self):
        at = self.at
        for step in range(1, at.ys):
            y = at.beside(step)
            self.wait(self.from_x.at[y], self.xs.at[y, 0, 0], self.xs.at[y, 0, 1])
            add_into(self.sum_y.at[y], [self.part(y * 2 + at.x, 0), self.from_x.at[y]])
            self.go(
                self.sum_y.at[y],
                self.last_y.at[at.y],
                self.yss.at[step, 2, 0],
                self.yss.at[at.y, 2, 1],
                at.column(y),
            )
        terms = []
        for step in range(1, at.ys):
            y = at.beside(step)
            for x in range(2):
                self.wait(self.from_y.at[y, x], self.yss.at[step, x, 0], self.yss.at[y, x, 1])
            terms.append(self.from_y.at[y, 1 - at.x])
        add_into(self.sum_x, [self.part(at.y * 2 + 1 - at.x, 1)] + terms)
        self.go(self.sum_x, self.last_x, self.xs.at[0, 1, 0], self.xs.at[0, 1, 1], at.across())

    def finish(self, total):
        at = self.at
        self.wait(self.from_x.at[at.y], self.xs.at[0, 0, 0], self.xs.at[at.y, 0, 1])
        terms = [self.part(at.s, 0), self.from_x.at[at.y]]
        for step in range(1, at.ys):
            y = at.beside(step)
            self.wait(self.last_y.at[y], self.yss.at[step, 2, 0], self.yss.at[y, 2, 1])
            terms.append(self.last_y.at[y])
        add_into(total(0), terms)
        self.wait(self.last_x, self.xs.at[0, 1, 0], self.xs.at[0, 1, 1])
        terms = [self.part(at.s, 1), self.last_x]
        for step in range(1, at.ys):
            terms.append(self.from_y.at[at.beside(step), at.x])
        add_into(total(1), terms)
        for copy in self.sent:
            copy.wait_send()


class LineGather:
    @staticmethod
    def semaphores(wt, cuts=1):
        return [pltpu.SemaphoreType.DMA((5, wt // 2, cuts))]

    def __init__(self, at, view, sems):
        self.at, self.view, self.sems = at, view, sems[0]
        self.cuts = self.sems.shape[2]

    def cut(self, ref, part):
        if self.cuts == 1:
            return ref
        rows = ref.shape[0] // self.cuts
        return ref.at[pl.ds(part * rows, rows)]

    def hop(self, z, part, kind, device, source):
        slot = self.view(z * 2 + self.at.c)
        source = slot if source is None else source
        arriving = 4 if kind == 2 else 3
        return send(
            self.cut(source, part),
            self.cut(slot, part),
            self.sems.at[kind, z, part],
            self.sems.at[arriving, z, part],
            device,
        )

    def up(self, z, part, source=None):
        return self.hop(z, part, 0, self.at.level(self.at.z + 1), source)

    def down(self, z, part, source=None):
        return self.hop(z, part, 1, self.at.level(self.at.z - 1), source)

    def over(self, z, part, source=None):
        return self.hop(z, part, 2, self.at.partner(), source)

    def start(self, source=None):
        at = self.at
        for part in range(self.cuts):

            @pl.when(at.z + 1 < at.zs)
            def _():
                self.up(at.z, part, source).start()

            @pl.when(at.z > 0)
            def _():
                self.down(at.z, part, source).start()

            self.over(at.z, part, source).start()

    def step(self, index):
        at = self.at
        below, above = at.z - 1 - index, at.z + 1 + index
        for part in range(self.cuts):

            @pl.when(below >= 0)
            def _():
                self.up(below, part).wait_recv()

                @pl.when(at.z + 1 < at.zs)
                def _():
                    self.up(below, part).start()

                self.over(below, part).start()

            @pl.when(above < at.zs)
            def _():
                self.down(above, part).wait_recv()

                @pl.when(at.z > 0)
                def _():
                    self.down(above, part).start()

                self.over(above, part).start()

    def wait_over(self, z):
        for part in range(self.cuts):
            slot = self.cut(self.view(z * 2 + 1 - self.at.c), part)
            send(slot, slot, self.sems.at[2, z, part], self.sems.at[4, z, part], self.at.partner()).wait_recv()

    def finish(self):
        for z in range(self.at.zs):
            self.wait_over(z)
        self.sent()

    def sent(self):
        at = self.at
        for z in range(at.zs):
            for part in range(self.cuts):

                @pl.when((at.z >= z) & (at.z + 1 < at.zs))
                def _():
                    self.up(z, part).wait_send()

                @pl.when((at.z <= z) & (at.z > 0))
                def _():
                    self.down(z, part).wait_send()

                self.over(z, part).wait_send()


def remote_call(kernel, name, number, outs, scratch, *operands, in_specs=None, out_specs=None):
    return pl.pallas_call(
        kernel,
        name=name,
        out_shape=outs,
        in_specs=[VMEM] * len(operands) if in_specs is None else in_specs,
        out_specs=jax.tree.map(lambda _: VMEM, outs) if out_specs is None else out_specs,
        scratch_shapes=scratch,
        compiler_params=pltpu.CompilerParams(
            collective_id=number, has_side_effects=True, vmem_limit_bytes=VMEM_LIMIT
        ),
    )(*operands)


def mixer_forward(tokens, qkv_rows, out_rows, gains, gate_up, segments, taps):
    seq, wt = lax.axis_size("seq"), lax.axis_size("wt")
    zs = wt // 2
    count, width = tokens.shape
    length = count * seq
    out_rank = out_rows.shape[0]
    heads = H // seq
    value_width = heads * DV
    qkv_width = value_width + 2 * FEAT * heads
    qkv_rank = width // (seq * wt)
    lanes_each = width // (seq * wt)
    units, block = gate_up.shape[1:]
    early = early_rows(units)
    rows_at_once = 256
    small = [
        tokens,
        qkv_rows,
        out_rows,
        gains,
        segments,
        taps,
    ]

    def kernel(*refs):
        (x_ref, qkv_ref, out_ref, gain_ref, segment_ref, tap_ref), refs = refs[:6], refs[6:]
        gate_up_ref, refs = refs[0], refs[1:]
        (attended_out, normed_out, gain_rows), refs = refs[:3], refs[3:]
        (qkv_out, w_out_out, hidden_out, sorted_out, mixer_out, values_out, outputs_out, gates_out, order_out), refs = (
            refs[:9],
            refs[9:],
        )
        (xs, qkvs, outs, gains_all, hidden_v, sorted_v, mixer_v, values_v, outputs_v, parts, total, room), refs = (
            refs[:12],
            refs[12:],
        )
        (order_v, segment_column, tap_v), refs = refs[:3], refs[3:]
        sum_scratch, x_sems, gate_sems, refs = refs[:8], refs[8:11], refs[11:14], refs[14:]
        line_sems, refs = [refs[index : index + 1] for index in range(3)], refs[3:]
        swap_q, swap_g, local, outgoing = refs
        at = Place(seq, wt)
        room_load = pltpu.make_async_copy(gate_up_ref.at[:, pl.ds(0, early)], room, local.at[4])
        room_load.start()
        at.meet(True, True)
        half = count // 2
        gather_x = SquareGather(
            at,
            lambda s, h: xs.at[pl.ds(pl.multiple_of(s * count + h * half, half), half)],
            lambda h: x_ref.at[pl.ds(h * half, half)],
            x_sems,
        )
        gather_q = LineGather(at, lambda w: qkvs.at[:, w], line_sems[0])
        gather_g = LineGather(
            at, lambda w: gains_all.at[:, pl.ds(pl.multiple_of(w * 8, 8), 8)], line_sems[1]
        )
        gather_o = LineGather(at, lambda w: outs.at[w], line_sems[2])
        gates = SquareGather(
            at,
            lambda s, h: gates_out.at[h, :, pl.ds(pl.multiple_of(s * block, block), block)],
            lambda h: gate_up_ref.at[h, pl.ds(0, early)],
            gate_sems,
        )
        gain_slot = pl.ds(pl.multiple_of(at.w * 8, 8), 8)

        def qkv_part(s):
            if len(qkv_ref.shape) == 3:
                return qkv_ref.at[s]
            return qkv_ref.at[:, pl.ds(pl.multiple_of(s * qkv_width, qkv_width), qkv_width)]

        swaps = []
        for step in range(1, seq):
            to = lax.rem(at.s + step, seq)
            swaps.append(
                send(gain_ref, gains_all.at[at.s, gain_slot], swap_g.at[step, 0], swap_g.at[at.s, 1], (to, at.w))
            )
            swaps.append(
                send(qkv_part(to), qkvs.at[at.s, at.w], swap_q.at[step, 0], swap_q.at[at.s, 1], (to, at.w))
            )
        for copy in swaps:
            copy.start()
        gather_x.start()
        own = [
            pltpu.make_async_copy(qkv_part(at.s), qkvs.at[at.s, at.w], local.at[0]),
            pltpu.make_async_copy(gain_ref, gains_all.at[at.s, gain_slot], local.at[1]),
            pltpu.make_async_copy(out_ref, outs.at[at.w], local.at[2]),
            pltpu.make_async_copy(x_ref, xs.at[pl.ds(pl.multiple_of(at.s * count, count), count)], local.at[3]),
        ]
        for copy in own:
            copy.start()
        for copy in own:
            copy.wait()
        room_load.wait()
        room_store = pltpu.make_async_copy(
            room, gates_out.at[:, :, pl.ds(pl.multiple_of(at.s * block, block), block)], local.at[4]
        )
        room_store.start()
        for step in range(1, seq):
            s = lax.rem(at.s + step, seq)
            slot = gains_all.at[s, gain_slot]
            send(slot, slot, swap_g.at[step, 0], swap_g.at[s, 1], at.across()).wait_recv()
            slot = qkvs.at[s, at.w]
            send(slot, slot, swap_q.at[step, 0], swap_q.at[s, 1], at.across()).wait_recv()
        gather_g.start()
        gather_q.start()
        tap_v[...] = tap_ref[...].astype(jnp.float32)
        segment_row = segment_ref[...].astype(jnp.float32)
        segment_column[...] = jnp.broadcast_to(segment_row, (128, length)).T
        write_order(order_v, heads)
        gather_x.relay()
        gates.start()
        for index in range(zs - 1):
            if index == zs - 2:
                gather_o.start()
            gather_g.step(index)
            gather_q.step(index)
        gather_g.finish()

        device_rows = gains_all[...].reshape(seq * wt * 8, 128).astype(jnp.bfloat16)
        gain_rows[...] = jnp.zeros_like(gain_rows)

        def spread_gains(index, carry):
            begin = pl.multiple_of(index * 256, 256)
            lane = lax.broadcasted_iota(jnp.int32, (128, 256), 0)
            column = begin + lax.broadcasted_iota(jnp.int32, (128, 256), 1)
            copied = jnp.dot(
                device_rows,
                (lane == lax.rem(column, lanes_each)).astype(jnp.float32).astype(jnp.bfloat16),
                preferred_element_type=jnp.float32,
            )
            row = lax.broadcasted_iota(jnp.int32, copied.shape, 0)
            column = begin + lax.broadcasted_iota(jnp.int32, copied.shape, 1)
            first_row = lax.div(column, lanes_each) * 8
            for number in range(2):
                gain_rows[number : number + 1, pl.ds(begin, 256)] = jnp.sum(
                    jnp.where(row == first_row + number, copied, 0.0), axis=0, keepdims=True
                )
            return carry

        lax.fori_loop(0, width // 256, spread_gains, 0)
        gather_x.finish()

        def norm_rows(index, carry):
            window = pl.ds(pl.multiple_of(index * 32, 32), 32)
            hidden_v[window, :] = rms_norm(xs[window, :].astype(jnp.float32), gain_rows[0:1, :]).astype(
                jnp.bfloat16
            )
            return carry

        lax.fori_loop(0, length // 32, norm_rows, 0)
        gather_q.finish()
        projected = jnp.dot(
            hidden_v[...], qkvs[...].reshape(width, qkv_width), preferred_element_type=jnp.float32
        ).astype(jnp.bfloat16)
        sorted_v[...] = jnp.dot(projected, order_v[...], preferred_element_type=jnp.float32).astype(
            jnp.bfloat16
        )
        stores = [
            pltpu.make_async_copy(source, target, outgoing.at[index])
            for index, (source, target) in enumerate(
                (
                    (qkvs, qkv_out),
                    (hidden_v, hidden_out),
                    (sorted_v, sorted_out),
                    (values_v, values_out),
                    (outputs_v, outputs_out),
                    (mixer_v, mixer_out),
                    (outs, w_out_out),
                    (order_v, order_out),
                )
            )
        ]
        for copy in stores[:3]:
            copy.start()
        marks = tap_marks(segment_column)

        def convolve(head, carry):
            columns = pl.ds(pl.multiple_of(head * DV, DV), DV)
            raw = sorted_v[:, columns].astype(jnp.float32)
            mixed = tap_v[0:1, columns] * raw
            for tap in range(1, KCONV):
                mixed = mixed + tap_v[tap : tap + 1, columns] * pltpu.roll(raw, tap, 0) * marks[tap]
            values_v[head] = mixed.astype(jnp.bfloat16)
            return carry

        lax.fori_loop(0, heads, convolve, 0)
        stores[3].start()
        gates.relay()
        steps = length // rows_at_once
        lanes = lax.broadcasted_iota(jnp.int32, (1, 128), 1)

        def attend(index, carry):
            head, start = lax.div(index, steps), lax.rem(index, steps) * rows_at_once
            rows = pl.ds(pl.multiple_of(start, rows_at_once), rows_at_once)
            mine = ((lanes >= head * FEAT) & (lanes < head * FEAT + FEAT)).astype(jnp.float32)
            queries = sorted_v[rows, value_width : value_width + 128] * mine.astype(jnp.bfloat16)
            scores = contract_last(queries, sorted_v[:, value_width + 128 :]) * 0.25
            places = start + lax.broadcasted_iota(jnp.int32, scores.shape, 0)
            allowed = (segment_column[rows, :1] == segment_row) & (
                places >= lax.broadcasted_iota(jnp.int32, scores.shape, 1)
            )
            kernel_values = jnp.where(allowed, 1.0 + scores + 0.5 * scores * scores, 0.0)
            denominator = jnp.sum(kernel_values, axis=1, keepdims=True)
            mixed = (
                jnp.dot(kernel_values.astype(jnp.bfloat16), values_v[head], preferred_element_type=jnp.float32)
                / denominator
            )
            outputs_v[head, rows, :] = mixed
            mixer_v[rows, pl.ds(pl.multiple_of(head * DV, DV), DV)] = mixed.astype(jnp.bfloat16)
            return carry

        turns = heads * steps
        for index in range(zs - 1):
            lax.fori_loop(turns * index // (zs - 1), turns * (index + 1) // (zs - 1), attend, 0)
            gather_o.step(index)
        gather_o.finish()
        for copy in stores[4:]:
            copy.start()

        def out_job(index, carry):
            window = pl.ds(pl.multiple_of(index * 512, 512), 512)
            term = jnp.dot(
                mixer_v[...], outs[:, :, window].reshape(value_width, 512), preferred_element_type=jnp.float32
            ).astype(jnp.bfloat16)
            for s in range(seq):
                for h in range(2):
                    begin = s * count + h * half
                    parts[s, h, :, window] = term[begin : begin + half]
            return carry

        lax.fori_loop(0, width // 512, out_job, 0)
        work = SquareSum(at, lambda s, h: parts.at[s, h], sum_scratch)
        work.start()
        work.relay()
        work.finish(lambda h: total.at[h])

        def finish_rows(index, carry):
            for h in range(2):
                window = pl.ds(pl.multiple_of(index * 16, 16), 16)
                rows = pl.ds(pl.multiple_of(h * half + index * 16, 16), 16)
                attended = x_ref[rows, :].astype(jnp.float32) + total[h, window, :]
                attended_out[rows, :] = attended
                normed_out[rows, :] = rms_norm(attended, gain_rows[1:2, :]).astype(jnp.bfloat16)
            return carry

        lax.fori_loop(0, half // 16, finish_rows, 0)
        gates.finish()
        room_store.wait()
        for copy in swaps:
            copy.wait_send()
        for copy in stores:
            copy.wait()

    low, f32 = jnp.bfloat16, jnp.float32
    sorted_width = value_width + 256
    return remote_call(
        kernel,
        "mixer_forward",
        0,
        [
            jax.ShapeDtypeStruct((count, width), f32),
            jax.ShapeDtypeStruct((count, width), low),
            jax.ShapeDtypeStruct((8, width), f32),
            jax.ShapeDtypeStruct((seq, wt, qkv_rank, qkv_width), low),
            jax.ShapeDtypeStruct((wt, out_rank, width), low),
            jax.ShapeDtypeStruct((length, width), low),
            jax.ShapeDtypeStruct((length, sorted_width), low),
            jax.ShapeDtypeStruct((length, value_width), low),
            jax.ShapeDtypeStruct((heads, length, DV), low),
            jax.ShapeDtypeStruct((heads, length, DV), f32),
            jax.ShapeDtypeStruct((2, early, width), low),
            jax.ShapeDtypeStruct((qkv_width, sorted_width), low),
        ],
        [
            pltpu.VMEM((length, width), low),
            pltpu.VMEM((seq, wt, qkv_rank, qkv_width), low),
            pltpu.VMEM((wt, out_rank, width), low),
            pltpu.VMEM((seq, wt * 8, 128), f32),
            pltpu.VMEM((length, width), low),
            pltpu.VMEM((length, sorted_width), low),
            pltpu.VMEM((length, value_width), low),
            pltpu.VMEM((heads, length, DV), low),
            pltpu.VMEM((heads, length, DV), f32),
            pltpu.VMEM((seq, 2, count // 2, width), low),
            pltpu.VMEM((2, count // 2, width), f32),
            pltpu.VMEM((2, early, block), low),
            pltpu.VMEM((qkv_width, sorted_width), low),
            pltpu.VMEM((length, 128), f32),
            pltpu.VMEM((KCONV, value_width), f32),
        ]
        + SquareSum.scratch(seq, (count // 2, width))
        + SquareGather.semaphores(seq)
        + SquareGather.semaphores(seq)
        + LineGather.semaphores(wt) * 3
        + [
            pltpu.SemaphoreType.DMA((seq, 2)),
            pltpu.SemaphoreType.DMA((seq, 2)),
            pltpu.SemaphoreType.DMA((5,)),
            pltpu.SemaphoreType.DMA((8,)),
        ],
        *small,
        gate_up,
        in_specs=[VMEM] * len(small) + [ANY],
        out_specs=[VMEM] * 3 + [ANY] * 9,
    )


def write_order(ref, heads):
    head_width, value_width = 2 * FEAT + DV, heads * DV

    def step(index, carry):
        window = pl.ds(pl.multiple_of(index * 32, 32), 32)
        shape = (32, ref.shape[1])
        column = index * 32 + lax.broadcasted_iota(jnp.int32, shape, 0)
        head = lax.div(column, head_width)
        place = lax.rem(column, head_width)
        target = jnp.where(
            place < FEAT,
            value_width + head * FEAT + place,
            jnp.where(
                place < 2 * FEAT, value_width + 128 + head * FEAT + place - FEAT, head * DV + place - 2 * FEAT
            ),
        )
        hit = target == lax.broadcasted_iota(jnp.int32, shape, 1)
        ref[window, :] = hit.astype(jnp.float32).astype(jnp.bfloat16)
        return carry

    lax.fori_loop(0, ref.shape[0] // 32, step, 0)


def tap_marks(segment_column):
    segment = segment_column[:, :1]
    place = lax.broadcasted_iota(jnp.int32, segment_column.shape, 0)[:, :1]
    marks = [None]
    for tap in range(1, KCONV):
        same = (pltpu.roll(segment_column[...], tap, 0)[:, :1] == segment) & (place >= tap)
        marks.append(same.astype(jnp.float32))
    return marks


def early_rows(units):
    return units * 3 // 4 // 16 * 16


class LinePieces:
    @staticmethod
    def scratch(wt, shape, pieces):
        zs = wt // 2
        return [pltpu.VMEM((zs,) + shape, jnp.bfloat16)] * 3 + [pltpu.SemaphoreType.DMA((6, zs, pieces))]

    def __init__(self, at, part, scratch, order=None):
        self.at, self.part, self.order = at, part, order
        self.pair, self.below, self.above, self.sems = scratch
        self.pieces = self.sems.shape[2]
        self.width = self.pair.shape[-1] // self.pieces

    def cut(self, ref, piece):
        if len(ref.shape) == 3:
            return ref.at[piece]
        return ref.at[:, self.columns(piece)]

    def columns(self, piece):
        block = piece if self.order is None else self.order(piece)
        return pl.ds(pl.multiple_of(block * self.width, self.width), self.width)

    def own(self, z, piece):
        return self.cut(self.part(z * 2 + self.at.c), piece)

    def over(self, z, piece):
        return send(
            self.cut(self.part(z * 2 + 1 - self.at.c), piece),
            self.cut(self.pair.at[z], piece),
            self.sems.at[0, z, piece],
            self.sems.at[1, z, piece],
            self.at.partner(),
        )

    def up(self, z, piece):
        return send(
            self.own(z, piece),
            self.cut(self.below.at[z], piece),
            self.sems.at[2, z, piece],
            self.sems.at[3, z, piece],
            self.at.level(self.at.z + 1),
        )

    def down(self, z, piece):
        return send(
            self.own(z, piece),
            self.cut(self.above.at[z], piece),
            self.sems.at[4, z, piece],
            self.sems.at[5, z, piece],
            self.at.level(self.at.z - 1),
        )

    def terms(self, z, piece):
        self.over(z, piece).wait_recv()
        return [self.own(z, piece), self.cut(self.pair.at[z], piece)]

    def ends(self, z, piece):
        at = self.at

        @pl.when((at.z == 0) & (z > 0))
        def _():
            add_into(self.own(z, piece), self.terms(z, piece))
            self.up(z, piece).start()

        @pl.when((at.z == at.zs - 1) & (z < at.zs - 1))
        def _():
            add_into(self.own(z, piece), self.terms(z, piece))
            self.down(z, piece).start()

    def offer(self, piece):
        zs = self.at.zs
        for index in range(zs // 2):
            self.over(index, piece).start()
            self.over(zs - 1 - index, piece).start()

    def launch(self, piece, near):
        self.ends(jnp.where(self.at.z == 0, self.at.zs - 1 - near, near), piece)

    def launch_all(self, near):
        zs = self.at.zs

        def step(index, carry):
            self.launch(lax.rem(index, self.pieces), near + lax.div(index, self.pieces))
            return carry

        lax.fori_loop(0, (zs - 1 - near) * self.pieces, step, 0)

    def pass_on(self, index, fill=None, begin=0, end=None):
        at = self.at
        upper = at.z * 2 >= at.zs
        high, low = index, at.zs - 1 - index

        def lower(piece, when):
            @pl.when((at.z > low) & (at.z < at.zs - 1) & when)
            def _():
                terms = self.terms(low, piece)
                self.down(low, piece).wait_recv()
                add_into(self.own(low, piece), terms + [self.cut(self.above.at[low], piece)])
                self.down(low, piece).start()

        def step(piece, carry):
            lower(piece, upper)

            @pl.when((at.z < high) & (at.z > 0))
            def _():
                terms = self.terms(high, piece)
                self.up(high, piece).wait_recv()
                add_into(self.own(high, piece), terms + [self.cut(self.below.at[high], piece)])
                self.up(high, piece).start()

            lower(piece, jnp.logical_not(upper))
            if fill is not None:
                fill(piece, self.pieces)
            return carry

        end = self.pieces if end is None else end
        if end - begin == 1:
            step(begin, 0)
        else:
            lax.fori_loop(begin, end, step, 0)

    def finish(self, total, done=None):
        at = self.at

        def step(piece, carry):
            terms = self.terms(at.z, piece)
            below, above = self.cut(self.below.at[at.z], piece), self.cut(self.above.at[at.z], piece)

            @pl.when(at.z == 0)
            def _():
                self.down(at.z, piece).wait_recv()
                add_into(self.cut(total, piece), terms + [above])

            @pl.when(at.z == at.zs - 1)
            def _():
                self.up(at.z, piece).wait_recv()
                add_into(self.cut(total, piece), terms + [below])

            @pl.when((at.z > 0) & (at.z < at.zs - 1))
            def _():
                self.up(at.z, piece).wait_recv()
                self.down(at.z, piece).wait_recv()
                add_into(self.cut(total, piece), terms + [below, above])

            if done is not None:
                done(piece)
            for z in range(at.zs):

                @pl.when(at.z < z)
                def _():
                    self.up(z, piece).wait_send()

                @pl.when(at.z > z)
                def _():
                    self.down(z, piece).wait_send()

                self.over(z, piece).wait_send()
            return carry

        lax.fori_loop(0, self.pieces, step, 0)


class SquareTerms:
    @staticmethod
    def semaphores(seq):
        return [pltpu.SemaphoreType.DMA((seq // 2, 2)), pltpu.SemaphoreType.DMA((seq // 2, 2, 2))]

    @staticmethod
    def scratch(seq, half_shape):
        ys = seq // 2
        return [
            pltpu.VMEM((ys,) + half_shape, jnp.bfloat16),
            pltpu.VMEM(half_shape, jnp.bfloat16),
            pltpu.SemaphoreType.DMA((ys + 1, 2)),
        ]

    def __init__(self, at, terms, from_x, from_y, sems=None, lasts=None, scratch=None):
        self.at, self.terms, self.from_x, self.from_y = at, terms, from_x, from_y
        if sems is not None:
            self.xs, self.ys = sems
        if scratch is not None:
            self.last_y, self.last_x = lasts
            self.sum_y, self.sum_x, self.last = scratch

    def first_x(self, y):
        at = self.at
        return send(
            self.terms(y * 2 + 1 - at.x, 0), self.from_x.at[y], self.xs.at[y, 0], self.xs.at[y, 1], at.across()
        )

    def first_y(self, step, x):
        at = self.at
        y = at.beside(step)
        return send(
            self.terms(y * 2 + x, 1),
            self.from_y.at[at.y, x],
            self.ys.at[step, x, 0],
            self.ys.at[at.y, x, 1],
            at.column(y),
        )

    def first_start(self):
        for y in range(self.at.ys):
            self.first_x(y).start()
        for step in range(1, self.at.ys):
            for x in range(2):
                self.first_y(step, x).start()

    def first_wait(self):
        at = self.at
        for y in range(at.ys):
            self.first_x(y).wait()
        for step in range(1, at.ys):
            y = at.beside(step)
            for x in range(2):
                self.first_y(step, x).wait_send()
                slot = self.from_y.at[y, x]
                send(slot, slot, self.ys.at[step, x, 0], self.ys.at[y, x, 1], at.across()).wait_recv()

    def second_y(self, step):
        at = self.at
        y = at.beside(step)
        return send(
            self.sum_y.at[y], self.last_y.at[at.y], self.last.at[step, 0], self.last.at[at.y, 1], at.column(y)
        )

    def second_x(self):
        at = self.at
        return send(self.sum_x, self.last_x, self.last.at[at.ys, 0], self.last.at[at.ys, 1], at.across())

    def second_start(self, fetch, rooms):
        at = self.at
        for step in range(1, at.ys):
            y = at.beside(step)
            fetch([(self.terms(y * 2 + at.x, 0), rooms[0]), (self.from_x.at[y], rooms[1])])
            add_into(self.sum_y.at[y], [rooms[0], rooms[1]])
        fetch([(self.terms(at.y * 2 + 1 - at.x, 1), self.sum_x)])
        for step in range(1, at.ys):
            y = at.beside(step)
            fetch([(self.from_y.at[y, 1 - at.x], rooms[0])])
            add_into(self.sum_x, [self.sum_x, rooms[0]])

    def second_load(self, fetch):
        at = self.at
        pairs = [(self.terms(at.y * 2 + 1 - at.x, 1), self.sum_x)]
        for step in range(1, at.ys):
            y = at.beside(step)
            pairs.append((self.terms(y * 2 + at.x, 0), self.sum_y.at[y]))
        fetch(pairs)

    def second_arrived(self):
        at = self.at
        terms = [self.sum_x]
        for step in range(1, at.ys):
            y = at.beside(step)
            add_into(self.sum_y.at[y], [self.sum_y.at[y], self.from_x.at[y]])
            terms.append(self.from_y.at[y, 1 - at.x])
        add_into(self.sum_x, terms)

    def second_go(self):
        for step in range(1, self.at.ys):
            self.second_y(step).start()
        self.second_x().start()

    def second_wait(self):
        at = self.at
        for step in range(1, at.ys):
            self.second_y(step).wait_send()
            y = at.beside(step)
            slot = self.last_y.at[y]
            send(slot, slot, self.last.at[step, 0], self.last.at[y, 1], at.across()).wait_recv()
        self.second_x().wait()


def norm_back(rows, load, store, gain, terms):
    def step(index, carry):
        window = pl.ds(pl.multiple_of(index * 16, 16), 16)
        values, incoming, base = load(window)
        root = lax.rsqrt(jnp.mean(values * values, axis=-1, keepdims=True) + epsilon)
        scaled = incoming * gain
        share = jnp.mean(values * scaled, axis=-1, keepdims=True)
        store(window, base + root * scaled - values * (root * root * root * share))
        term = incoming * values * root
        terms[...] += term[:8] + term[8:]
        return carry

    lax.fori_loop(0, rows // 16, step, 0)


class Exchange:
    def __init__(self, at, shard, everyone, gather_sems, local, sums, first, second):
        self.at, self.sums, self.first, self.second = at, sums, first, second
        count = shard.shape[0]
        slot = lambda w: everyone.at[pl.ds(pl.multiple_of(w * count, count), count)]
        self.gather = LineGather(at, slot, gather_sems)
        self.gather.start(shard)
        own = pltpu.make_async_copy(shard, slot(at.w), local)
        own.start()
        own.wait()
        self.last, self.ahead = 2 * (at.zs - 1), 0

    def step_ahead(self):
        self.gather.step(0)
        self.ahead = 1

    def level(self, index):
        at = self.at
        far, side = lax.div(index + 1, 2), lax.rem(index, 2)
        z = at.z + jnp.where(side == 1, -far, far)
        return far, side, z, (z >= 0) & (z < at.zs)

    def arrive(self, index):
        far, side, z, valid = self.level(index)

        @pl.when((side == 1) & (far > self.ahead))
        def _():
            self.gather.step(far - 1)

        @pl.when(valid)
        def _():
            self.gather.wait_over(z)
            self.first(z)

        return z, valid

    def put(self, z, begin, end):
        def step(piece, inner):
            self.second(z, piece)
            self.sums.over(z, piece).start()

            @pl.when(piece > begin)
            def _():
                self.sums.ends(z, piece - 1)

            return inner

        lax.fori_loop(begin, end, step, 0)
        self.sums.ends(z, end - 1)

    def whole(self, total, fill):
        at, sums = self.at, self.sums

        def turn(index, carry):
            z, valid = self.arrive(index)

            @pl.when(valid)
            def _():
                self.put(z, 0, sums.pieces)

            return carry

        lax.fori_loop(0, self.last + 1, turn, 0)
        fill(None, sums.pieces)
        for index in range(2, at.zs):
            sums.pass_on(index, fill if index == 2 else None)
        sums.finish(total)
        self.gather.sent()

    def by_columns(self, total, direct, relayed, near):
        at, sums = self.at, self.sums
        begin = min(3, self.last)

        def turn(index, carry):
            z, valid = self.arrive(index)

            @pl.when(index == begin)
            def _():
                direct()

            @pl.when(valid & (index >= begin))
            def _():
                self.put(z, 0, near)

            return carry

        lax.fori_loop(0, self.last + 1, turn, 0)

        def earlier(index, carry):
            _, _, z, valid = self.level(index)

            @pl.when(valid)
            def _():
                self.put(z, 0, near)

            return carry

        lax.fori_loop(1, begin, earlier, 0)
        if at.zs > 2:
            sums.pass_on(2, None, 0, near)
        relayed()

        def over(index, carry):
            _, _, z, valid = self.level(self.last - index)

            @pl.when(valid)
            def _():
                for piece in range(near, sums.pieces):
                    self.second(z, piece)
                    sums.over(z, piece).start()

            return carry

        lax.fori_loop(0, self.last, over, 0)

        def start(index, carry):
            _, _, z, valid = self.level(self.last - index)

            @pl.when(valid)
            def _():
                for piece in range(near, sums.pieces):
                    sums.ends(z, piece)

            return carry

        lax.fori_loop(0, self.last, start, 0)
        self.put(at.z, 0, sums.pieces)
        for index in range(3, at.zs):
            sums.pass_on(index, None, 0, near)
        for index in range(at.zs - 1, 1, -1):
            sums.pass_on(index, None, near, sums.pieces)
        sums.finish(total)
        self.gather.sent()


PIECES = 2


def feed_forward(normed, attended, teacher, lengths, gate_early, gate_up_shard, down_shard):
    seq, wt = lax.axis_size("seq"), lax.axis_size("wt")
    count, width = normed.shape
    units, block = gate_up_shard.shape[1:]
    early = early_rows(units)
    columns = down_shard.shape[1]
    tokens = wt * count
    zs = wt // 2
    half = units // 2

    def kernel(*refs):
        (normed_ref, attended_ref, teacher_ref, length_ref, early_ref, gate_shard_ref, shard_ref), refs = refs[:7], refs[7:]
        (final_out, error_out, energy_out), refs = refs[:3], refs[3:]
        (normed_out, gate_out, up_out, active_out, down_out, gates_out), refs = refs[:6], refs[6:]
        (everyone, gates, downs, gate_all, up_all, active_all, parts, total), refs = refs[:8], refs[8:]
        gather_sems, sum_scratch, late_sems, square_sems, (local, outgoing) = (
            refs[:1],
            refs[1:5],
            refs[5:8],
            refs[8:11],
            refs[11:],
        )
        at = Place(seq, wt)
        loads = [
            pltpu.make_async_copy(early_ref, gates.at[:, pl.ds(0, early)], local.at[4]),
            pltpu.make_async_copy(
                gate_shard_ref.at[:, pl.ds(early, units - early)],
                gates.at[:, pl.ds(early, units - early), pl.ds(pl.multiple_of(at.s * block, block), block)],
                local.at[0],
            ),
        ]
        for load in loads:
            load.start()
        at.meet(True, True)
        late = SquareGather(
            at,
            lambda s, h: gates.at[
                h, pl.ds(early, units - early), pl.ds(pl.multiple_of(s * block, block), block)
            ],
            lambda h: gate_shard_ref.at[h, pl.ds(early, units - early)],
            late_sems,
        )
        weights = SquareGather(
            at,
            lambda s, h: downs.at[
                pl.ds(h * half, half), pl.ds(pl.multiple_of(s * columns, columns), columns)
            ],
            lambda h: shard_ref.at[pl.ds(h * half, half)],
            square_sems,
        )
        ys = seq // 2

        def column_block(piece):
            if isinstance(piece, int):
                step = 0 if piece < 2 else piece - 1 if piece <= ys else piece - ys
                return at.beside(step) * 2 + (1 - at.x if piece == 1 or piece > ys else at.x)
            step = jnp.where(piece < 2, 0, jnp.where(piece <= ys, piece - 1, piece - ys))
            other = (piece == 1) | (piece > ys)
            return at.beside(step) * 2 + jnp.where(other, 1 - at.x, at.x)

        sums = LinePieces(
            at,
            lambda w: parts.at[pl.ds(pl.multiple_of(w * count, count), count)],
            sum_scratch,
            column_block,
        )
        down_store = pltpu.make_async_copy(downs, down_out, local.at[2])
        gates_store = pltpu.make_async_copy(gates, gates_out, local.at[0])

        def prepare():
            late.start()
            own = pltpu.make_async_copy(
                shard_ref, downs.at[:, pl.ds(pl.multiple_of(at.s * columns, columns), columns)], local.at[3]
            )
            own.start()
            late.relay()
            weights.start()
            work.step_ahead()
            own.wait()
            for load in loads:
                load.wait()
            late.finish()
            gates_store.start()

        def direct():
            weights.relay()
            weights.direct()

        def relayed():
            weights.relayed()
            down_store.start()

        def rows(z):
            return pl.ds(pl.multiple_of(z * 2 * count, 2 * count), 2 * count)

        def stores(z):
            return [
                pltpu.make_async_copy(source.at[rows(z)], target.at[rows(z)], outgoing.at[index, z])
                for index, (source, target) in enumerate(
                    ((everyone, normed_out), (gate_all, gate_out), (up_all, up_out), (active_all, active_out))
                )
            ]

        def first(z):
            here = everyone[rows(z), :]
            gate = contract_last(here, gates[0])
            up = contract_last(here, gates[1])
            gate_all[rows(z), :] = gate
            up_all[rows(z), :] = up
            active_all[rows(z), :] = gated_unit(gate, up).astype(jnp.bfloat16)
            for copy in stores(z):
                copy.start()

        def second(z, piece):
            window = sums.columns(piece)
            parts[rows(z), window] = jnp.dot(
                active_all[rows(z), :], downs[:, window], preferred_element_type=jnp.float32
            ).astype(jnp.bfloat16)

        work = Exchange(at, normed_ref, everyone, gather_sems, local.at[1], sums, first, second)
        prepare()
        work.by_columns(total, direct, relayed, ys + 1)
        energy_out[...] = jnp.zeros_like(energy_out)
        valid = length_ref[at.w]

        def finish_rows(index, carry):
            window = pl.ds(pl.multiple_of(index * 16, 16), 16)
            final = attended_ref[window, :] + total[window, :]
            final_out[window, :] = final.astype(jnp.bfloat16)
            place = at.s * count + index * 16 + lax.broadcasted_iota(jnp.int32, final.shape, 0)
            keep = (place < valid).astype(jnp.float32)
            error = (final - teacher_ref[window, :].astype(jnp.float32)) * keep
            error_out[window, :] = error
            squares = error * error
            energy_out[...] += 0.5 * (squares[:8] + squares[8:])
            return carry

        lax.fori_loop(0, count // 16, finish_rows, 0)
        down_store.wait()
        gates_store.wait()
        for z in range(zs):
            for copy in stores(z):
                copy.wait()

    low, f32 = jnp.bfloat16, jnp.float32
    return remote_call(
        kernel,
        "feed_forward",
        2,
        [
            jax.ShapeDtypeStruct((count, width), low),
            jax.ShapeDtypeStruct((count, width), f32),
            jax.ShapeDtypeStruct((8, width), f32),
            jax.ShapeDtypeStruct((tokens, width), low),
            jax.ShapeDtypeStruct((tokens, units), f32),
            jax.ShapeDtypeStruct((tokens, units), f32),
            jax.ShapeDtypeStruct((tokens, units), low),
            jax.ShapeDtypeStruct((units, width), low),
            jax.ShapeDtypeStruct((2, units, width), low),
        ],
        [
            pltpu.VMEM((tokens, width), low),
            pltpu.VMEM((2, units, width), low),
            pltpu.VMEM((units, width), low),
            pltpu.VMEM((tokens, units), f32),
            pltpu.VMEM((tokens, units), f32),
            pltpu.VMEM((tokens, units), low),
            pltpu.VMEM((tokens, width), low),
            pltpu.VMEM((count, width), f32),
        ]
        + LineGather.semaphores(wt, 2)
        + LinePieces.scratch(wt, (count, width), seq)
        + SquareGather.semaphores(seq)
        + SquareGather.semaphores(seq)
        + [pltpu.SemaphoreType.DMA((5,)), pltpu.SemaphoreType.DMA((4, zs))],
        normed,
        attended,
        teacher,
        lengths,
        gate_early,
        gate_up_shard,
        down_shard,
        in_specs=[VMEM] * 3 + [SMEM] + [ANY] * 2 + [VMEM],
        out_specs=[VMEM] * 3 + [ANY] * 6,
    )


def feed_back(error, attended, gain, gate_up, down, gate, up, active, normed):
    seq, wt = lax.axis_size("seq"), lax.axis_size("wt")
    count, width = error.shape
    units = gate_up.shape[1]
    tokens = wt * count
    ys = seq // 2
    block = width // seq
    half = (units // 2, block)

    def kernel(*refs):
        (error_ref, attended_ref, gain_ref, gate_up_ref, down_ref, gate_ref, up_ref, active_ref, normed_ref), refs = (
            refs[:9],
            refs[9:],
        )
        (grad_ref, mix_ref, gain_terms), refs = refs[:3], refs[3:]
        (gate_out, up_out, down_out, gate_x, gate_y, down_x, down_y), refs = refs[:7], refs[7:]
        (low, everyone, gates, downs, gate_all, up_all, back_all, parts, actives, columns), refs = refs[:10], refs[10:]
        (gate_terms, up_terms, down_terms, total), refs = refs[:4], refs[4:]
        gather_sems, sum_scratch, gate_sems, down_sems, (local, outgoing) = (
            refs[:1],
            refs[1:5],
            refs[5:7],
            refs[7:9],
            refs[9:],
        )
        at = Place(seq, wt)
        loads = [
            pltpu.make_async_copy(source, target, local.at[index])
            for index, (source, target) in enumerate(
                (
                    (down_ref, downs),
                    (gate_ref, gate_all),
                    (up_ref, up_all),
                    (gate_up_ref, gates),
                    (active_ref, actives),
                )
            )
        ]
        for load in loads:
            load.start()
        at.meet(True, True)
        low[...] = error_ref[...].astype(jnp.bfloat16)
        sums = LinePieces(
            at, lambda w: parts.at[pl.ds(pl.multiple_of(w * count, count), count)], sum_scratch
        )
        gate_sum = SquareTerms(at, lambda s, h: gate_terms.at[s, h], gate_x, gate_y, gate_sems)
        down_sum = SquareTerms(at, lambda s, h: down_terms.at[s, h], down_x, down_y, down_sems)

        def place(index):
            step = lax.div(index, 2) + 1
            x = lax.rem(at.x + 1 + lax.rem(index, 2), 2)
            return step, x, at.beside(step) * 2 + x

        def column_load(index):
            s = place(index)[2]
            return pltpu.make_async_copy(
                normed_ref.at[:, pl.ds(pl.multiple_of(s * block, block), block)],
                columns.at[lax.rem(index, 2)],
                local.at[6 + lax.rem(index, 2)],
            )

        def leave(sum_, index):
            step, x, s = place(index)

            @pl.when(x != at.x)
            def _():
                sum_.first_x(lax.div(s, 2)).start()

            @pl.when(step < ys)
            def _():
                sum_.first_y(step, x).start()

        def down_job(index):
            s = place(index)[2]
            term = contract_first(
                actives[...], everyone[:, pl.ds(pl.multiple_of(s * block, block), block)]
            ).astype(jnp.bfloat16)
            down_terms[s, 0] = term[: units // 2]
            down_terms[s, 1] = term[units // 2 :]
            leave(down_sum, index)

        def gate_job(index):
            s = place(index)[2]
            column_load(index).wait()
            here = columns.at[lax.rem(index, 2)]
            for number, terms in enumerate((gate_terms, up_terms)):
                term = contract_first(back_all[number], here[...]).astype(jnp.bfloat16)
                terms[s, 0] = term[: units // 2]
                terms[s, 1] = term[units // 2 :]

            @pl.when(index + 2 < seq)
            def _():
                column_load(index + 2).start()

            leave(gate_sum, index)

        def fill(slot, slots):
            if slot is None:
                lax.fori_loop(0, seq, lambda index, carry: (down_job(index), carry)[1], 0)
                return

            each = -(-seq // slots)

            def step(index, carry):
                job = slot * each + index

                @pl.when(job < seq)
                def _():
                    gate_job(job)

                return carry

            lax.fori_loop(0, each, step, 0)

        def prepare():
            column_load(0).start()
            column_load(1).start()
            for load in loads:
                load.wait()

        def rows(z):
            return pl.ds(pl.multiple_of(z * 2 * count, 2 * count), 2 * count)

        def first(z):
            active_back = contract_last(everyone[rows(z), :], downs[...])
            gate_here, up_here = gate_all[rows(z), :], up_all[rows(z), :]
            share = jax.nn.sigmoid(gate_here)
            back_all[0, rows(z), :] = (
                active_back * up_here * share * (1.0 + gate_here * (1.0 - share))
            ).astype(jnp.bfloat16)
            back_all[1, rows(z), :] = (active_back * gate_here * share).astype(jnp.bfloat16)

        def second(z, piece):
            window = pl.ds(pl.multiple_of(piece * sums.width, sums.width), sums.width)
            parts[rows(z), window] = (
                jnp.dot(back_all[0, rows(z), :], gates[0, :, window], preferred_element_type=jnp.float32)
                + jnp.dot(back_all[1, rows(z), :], gates[1, :, window], preferred_element_type=jnp.float32)
            ).astype(jnp.bfloat16)

        work = Exchange(at, low, everyone, gather_sems, local.at[5], sums, first, second)
        prepare()
        work.whole(total, fill)
        stores = [
            pltpu.make_async_copy(source, target, outgoing.at[index])
            for index, (source, target) in enumerate(
                ((gate_terms, gate_out), (up_terms, up_out), (down_terms, down_out))
            )
        ]
        for copy in stores:
            copy.start()
        gain_terms[...] = jnp.zeros_like(gain_terms)

        def load_rows(window):
            return attended_ref[window, :], total[window, :], error_ref[window, :]

        def store_rows(window, value):
            grad_ref[window, :] = value
            mix_ref[window, :] = value.astype(jnp.bfloat16)

        norm_back(count, load_rows, store_rows, gain_ref[1:2, :], gain_terms)
        for copy in stores:
            copy.wait()
        gate_sum.first_wait()
        down_sum.first_wait()

    def terms_of(half):
        return jax.ShapeDtypeStruct((seq, 2) + half, jnp.bfloat16)

    def first_of(half):
        return [
            jax.ShapeDtypeStruct((ys,) + half, jnp.bfloat16),
            jax.ShapeDtypeStruct((ys, 2) + half, jnp.bfloat16),
        ]

    return remote_call(
        kernel,
        "feed_back",
        3,
        [
            jax.ShapeDtypeStruct((count, width), jnp.float32),
            jax.ShapeDtypeStruct((count, width), jnp.bfloat16),
            jax.ShapeDtypeStruct((8, width), jnp.float32),
            terms_of(half),
            terms_of(half),
            terms_of(half),
        ]
        + first_of(half)
        + first_of(half),
        [
            pltpu.VMEM((count, width), jnp.bfloat16),
            pltpu.VMEM((tokens, width), jnp.bfloat16),
            pltpu.VMEM(gate_up.shape, jnp.bfloat16),
            pltpu.VMEM((units, width), jnp.bfloat16),
            pltpu.VMEM((tokens, units), jnp.float32),
            pltpu.VMEM((tokens, units), jnp.float32),
            pltpu.VMEM((2, tokens, units), jnp.bfloat16),
            pltpu.VMEM((tokens, width), jnp.bfloat16),
            pltpu.VMEM((tokens, units), jnp.bfloat16),
            pltpu.VMEM((2, tokens, block), jnp.bfloat16),
            pltpu.VMEM((seq, 2) + half, jnp.bfloat16),
            pltpu.VMEM((seq, 2) + half, jnp.bfloat16),
            pltpu.VMEM((seq, 2) + half, jnp.bfloat16),
            pltpu.VMEM((count, width), jnp.float32),
        ]
        + LineGather.semaphores(wt, 2)
        + LinePieces.scratch(wt, (count, width), PIECES)
        + SquareTerms.semaphores(seq)
        + SquareTerms.semaphores(seq)
        + [pltpu.SemaphoreType.DMA((8,)), pltpu.SemaphoreType.DMA((3,))],
        error,
        attended,
        gain,
        gate_up,
        down,
        gate,
        up,
        active,
        normed,
        in_specs=[VMEM] * 3 + [ANY] * 6,
        out_specs=[VMEM] * 3 + [ANY] * 7,
    )


def mixer_back(
    mix_back,
    attended_grad,
    tokens,
    gain,
    out_rows,
    qkv_columns,
    hidden,
    sorted_columns,
    mixer,
    mixed_values,
    head_outputs,
    segments,
    taps,
    order,
    gain_terms,
    energy,
    gate_parts,
    up_parts,
    down_parts,
):
    seq, wt = lax.axis_size("seq"), lax.axis_size("wt")
    zs, ys = wt // 2, seq // 2
    count, width = mix_back.shape
    length = count * seq
    heads = mixed_values.shape[0]
    qkv_width = qkv_columns.shape[1]
    value_width = heads * DV
    rank = width // (seq * wt)
    gate_half, down_half = gate_parts[0].shape[2:], down_parts[0].shape[2:]
    rows_at_once = 256
    big = [out_rows, qkv_columns, hidden, sorted_columns, mixer, mixed_values, head_outputs]
    small = [mix_back, attended_grad, tokens, gain, segments, taps, order, gain_terms, energy]
    far = list(gate_parts) + list(down_parts) + list(up_parts)

    def kernel(*refs):
        big_refs, refs = refs[: len(big)], refs[len(big) :]
        small_refs, refs = refs[: len(small)], refs[len(small) :]
        (gate_t, gate_x, gate_y, down_t, down_x, down_y, up_t), refs = refs[: len(far)], refs[len(far) :]
        (grad_out, sums_out, qkv_out, w_out_out, up_x, up_y), refs = refs[:6], refs[6:]
        gate_lasts, up_lasts, down_lasts, refs = refs[:2], refs[2:4], refs[4:6], refs[6:]
        (w_out_v, w_qkv_v, hidden_v, sorted_v, mixer_v, values_v, outputs_v), refs = refs[:7], refs[7:]
        (mix_all, mixer_grad, query_acc, key_acc, value_acc, back_sorted, back_v), refs = refs[:7], refs[7:]
        (hidden_parts, qkv_parts, out_parts, hidden_total, gain_acc, spread, taps_acc), refs = refs[:7], refs[7:]
        (segment_column, tap_v), refs = refs[:2], refs[2:]
        (room_gate0, room_gate1, room_down0, room_down1, qkv_sum, first, middle, last), refs = refs[:8], refs[8:]
        hidden_scratch, refs = refs[:8], refs[8:]
        qkv_scratch, out_scratch, refs = refs[:4], refs[4:8], refs[8:]
        gate_scratch, down_scratch, up_scratch, refs = refs[:3], refs[3:6], refs[6:9], refs[9:]
        gather_sems, up_sems, refs = refs[:3], refs[3:5], refs[5:]
        local, swap, first_sems, last_sems = refs
        (
            mix_ref,
            grad_ref,
            token_ref,
            gain_ref,
            segment_ref,
            tap_ref,
            order_ref,
            gain_two,
            energy_ref,
        ) = small_refs
        at = Place(seq, wt)
        loads = [
            pltpu.make_async_copy(source, target, local.at[4 + index])
            for index, (source, target) in enumerate(
                zip(big_refs, (w_out_v, w_qkv_v, hidden_v, sorted_v, mixer_v, values_v, outputs_v))
            )
        ]
        for load in loads:
            load.start()
        at.meet(True, True)
        half = count // 2
        gather = SquareGather(
            at,
            lambda s, h: mix_all.at[pl.ds(pl.multiple_of(s * count + h * half, half), half)],
            lambda h: mix_ref.at[pl.ds(h * half, half)],
            gather_sems,
        )
        gather.start()
        own = pltpu.make_async_copy(
            mix_ref, mix_all.at[pl.ds(pl.multiple_of(at.s * count, count), count)], local.at[3]
        )
        own.start()

        def fetch(pairs):
            copies = [
                pltpu.make_async_copy(source, target, local.at[index])
                for index, (source, target) in enumerate(pairs)
            ]
            for copy in copies:
                copy.start()
            for copy in copies:
                copy.wait()

        gate_sum = SquareTerms(at, lambda s, h: gate_t.at[s, h], gate_x, gate_y, None, gate_lasts, gate_scratch)
        down_sum = SquareTerms(at, lambda s, h: down_t.at[s, h], down_x, down_y, None, down_lasts, down_scratch)
        up_sum = SquareTerms(at, lambda s, h: up_t.at[s, h], up_x, up_y, up_sems, up_lasts, up_scratch)
        gate_rooms, down_rooms = (room_gate0, room_gate1), (room_down0, room_down1)
        gate_sum.second_start(fetch, gate_rooms)
        gather.relay()
        down_sum.second_start(fetch, down_rooms)
        up_sum.second_load(fetch)
        tap_v[...] = tap_ref[...].astype(jnp.float32)
        segment_row = segment_ref[...].astype(jnp.float32)
        segment_column[...] = jnp.broadcast_to(segment_row, (128, length)).T
        own.wait()
        for load in loads:
            load.wait()
        query_acc[...] = jnp.zeros_like(query_acc)
        key_acc[...] = jnp.zeros_like(key_acc)
        value_acc[...] = jnp.zeros_like(value_acc)
        gather.finish()
        gate_sum.second_go()
        down_sum.second_go()
        up_sum.first_start()
        mixer_grad[...] = contract_last(mix_all[...], w_out_v[...]).astype(jnp.bfloat16)
        out_sum = LinePieces(at, lambda w: out_parts.at[w], out_scratch)
        out_rank = out_parts.shape[1]
        out_block = 512 if value_width % 512 == 0 else value_width

        def out_job(index, carry):
            window = pl.ds(pl.multiple_of(index * 512, 512), 512)
            term = contract_first(mixer_v[...], mix_all[:, window]).astype(jnp.bfloat16)
            for w in range(wt):
                out_parts[w, :, window] = term[w * out_rank : (w + 1) * out_rank]
            return carry

        lax.fori_loop(0, width // 512, out_job, 0)
        for piece in range(out_sum.pieces):
            out_sum.offer(piece)
        out_sum.launch_all(0)

        steps = length // rows_at_once
        lanes = lax.broadcasted_iota(jnp.int32, (1, 128), 1)

        def attend(index, carry):
            head, start = lax.div(index, steps), lax.rem(index, steps) * rows_at_once
            rows = pl.ds(pl.multiple_of(start, rows_at_once), rows_at_once)
            columns = pl.ds(pl.multiple_of(head * DV, DV), DV)
            mine = ((lanes >= head * FEAT) & (lanes < head * FEAT + FEAT)).astype(jnp.float32)
            queries = sorted_v[rows, value_width : value_width + 128] * mine.astype(jnp.bfloat16)
            keys = sorted_v[:, value_width + 128 :]
            scores = contract_last(queries, keys) * 0.25
            places = start + lax.broadcasted_iota(jnp.int32, scores.shape, 0)
            allowed = (segment_column[rows, :1] == segment_row) & (
                places >= lax.broadcasted_iota(jnp.int32, scores.shape, 1)
            )
            kernel_values = jnp.where(allowed, 1.0 + scores + 0.5 * scores * scores, 0.0)
            denominator = jnp.sum(kernel_values, axis=1, keepdims=True)
            incoming = mixer_grad[rows, columns].astype(jnp.float32)
            numerator_back = (incoming / denominator).astype(jnp.bfloat16)
            denominator_back = (
                -jnp.sum(incoming * outputs_v[head, rows, :], axis=1, keepdims=True) / denominator
            )
            weight_back = contract_last(numerator_back, values_v[head])
            kernel_back = jnp.where(allowed, weight_back + denominator_back, 0.0)
            dots_back = (0.25 * kernel_back * (1.0 + scores)).astype(jnp.bfloat16)
            query_acc[rows, :] += jnp.dot(dots_back, keys, preferred_element_type=jnp.float32) * mine
            key_acc[...] += contract_first(dots_back, queries)
            value_acc[:, columns] += contract_first(kernel_values.astype(jnp.bfloat16), numerator_back)
            return carry

        middle_step = heads * steps // 2
        lax.fori_loop(0, middle_step, attend, 0)
        for index in range(zs - 1, 1, -1):
            if index == zs // 2:
                lax.fori_loop(middle_step, heads * steps, attend, 0)
            out_sum.pass_on(index)
        taps_acc[...] = jnp.zeros_like(taps_acc)
        marks = tap_marks(segment_column)

        def convolve(head, carry):
            columns = pl.ds(pl.multiple_of(head * DV, DV), DV)
            mixed_back = value_acc[:, columns]
            raw = sorted_v[:, columns].astype(jnp.float32)
            raw_back = tap_v[0:1, columns] * mixed_back
            taps_acc[3:4, columns] = jnp.sum(mixed_back * raw, axis=0, keepdims=True)
            for tap in range(1, KCONV):
                masked = mixed_back * marks[tap]
                taps_acc[3 + tap : 4 + tap, columns] = jnp.sum(
                    masked * pltpu.roll(raw, tap, 0), axis=0, keepdims=True
                )
                raw_back = raw_back + tap_v[tap : tap + 1, columns] * pltpu.roll(masked, length - tap, 0)
            back_sorted[:, columns] = raw_back.astype(jnp.bfloat16)
            return carry

        lax.fori_loop(0, heads, convolve, 0)
        back_sorted[:, value_width : value_width + 128] = query_acc[...].astype(jnp.bfloat16)
        back_sorted[:, value_width + 128 :] = key_acc[...].astype(jnp.bfloat16)
        back_v[...] = contract_last(back_sorted[...], order_ref[...]).astype(jnp.bfloat16)
        qkv_sums = LinePieces(at, lambda w: qkv_parts.at[:, w], qkv_scratch)
        qkv_rank = qkv_parts.shape[2]

        def qkv_job(s, carry):
            block = wt * qkv_rank
            window = pl.ds(pl.multiple_of(s * block, block), block)
            term = contract_first(hidden_v[:, window], back_v[...]).astype(jnp.bfloat16)
            for w in range(wt):
                qkv_parts[s, w] = term[w * qkv_rank : (w + 1) * qkv_rank]
            qkv_sums.offer(s)

            @pl.when(s > 0)
            def _():
                qkv_sums.launch(s - 1, 0)

            return carry

        lax.fori_loop(0, seq, qkv_job, 0)
        qkv_sums.launch(seq - 1, 0)
        hidden_sum = SquareSum(at, lambda s, h: hidden_parts.at[s, h], hidden_scratch)

        def hidden_job(index, carry):
            window = pl.ds(pl.multiple_of(index * 512, 512), 512)
            term = contract_last(back_v[...], w_qkv_v[window, :]).astype(jnp.bfloat16)
            for s in range(seq):
                for h in range(2):
                    begin = s * count + h * half
                    hidden_parts[s, h, :, window] = term[begin : begin + half]
            return carry

        lax.fori_loop(0, width // 512, hidden_job, 0)
        hidden_sum.start()
        qkv_sums.launch_all(1)
        qkv_sums.pass_on(zs - 1)
        hidden_sum.relay()
        up_sum.first_wait()
        up_sum.second_arrived()
        up_sum.second_go()
        for index in range(zs - 2, 1, -1):
            qkv_sums.pass_on(index)
        hidden_sum.finish(lambda h: hidden_total.at[h])
        gain_acc[...] = jnp.zeros_like(gain_acc)
        for h in range(2):

            def shift(window):
                return pl.ds(pl.multiple_of(h * half + window.start, 16), 16)

            def load_rows(window):
                rows = shift(window)
                return token_ref[rows, :].astype(jnp.float32), hidden_total[h, window, :], grad_ref[rows, :]

            def store_rows(window, value):
                grad_out[shift(window), :] = value

            norm_back(half, load_rows, store_rows, gain_ref[0:1, :], gain_acc)
        spread[...] = jnp.zeros_like(spread)
        spread[0:1, :] = jnp.sum(gain_acc[...], axis=0, keepdims=True)
        spread[1:2, :] = jnp.sum(gain_two[...], axis=0, keepdims=True)
        energy = jnp.sum(jnp.sum(energy_ref[...], axis=0, keepdims=True), axis=1, keepdims=True)
        spread[2:3, :] = jnp.broadcast_to(energy, (1, width))
        copies = []
        for step in range(1, seq):
            to = lax.rem(at.s + step, seq)
            window = pl.ds(pl.multiple_of(to * value_width, value_width), value_width)
            copies.append(
                send(spread.at[:, window], first.at[at.s], first_sems.at[step, 0], first_sems.at[at.s, 1], (to, at.w))
            )
        for copy in copies:
            copy.start()

        def give(s):
            return send(qkv_sum.at[s], qkv_out.at[at.s], swap.at[s, 0], swap.at[at.s, 1], (s, at.w))

        def done(s):
            @pl.when(s != at.s)
            def _():
                give(s).start()

        qkv_sums.finish(qkv_sum, done)
        add_into(qkv_out.at[at.s], [qkv_sum.at[at.s]])
        out_sum.finish(w_out_out)
        terms = [spread.at[:, pl.ds(pl.multiple_of(at.s * value_width, value_width), value_width)], taps_acc]
        for step in range(1, seq):
            s = lax.rem(at.s + step, seq)
            slot = first.at[s]
            send(slot, slot, first_sems.at[step, 0], first_sems.at[s, 1], at.across()).wait_recv()
            terms.append(slot)
        add_into(middle, terms)
        for step in range(1, wt):
            to = lax.rem(at.w + step, wt)
            copy = send(middle, last.at[at.w], last_sems.at[step, 0], last_sems.at[at.w, 1], (at.s, to))
            copy.start()
            copies.append(copy)
        gate_sum.second_wait()
        down_sum.second_wait()
        terms = [middle]
        for step in range(1, wt):
            w = lax.rem(at.w + step, wt)
            slot = last.at[w]
            send(slot, slot, last_sems.at[step, 0], last_sems.at[w, 1], at.partner()).wait_recv()
            terms.append(slot)
        add_into(sums_out, terms)
        for step in range(1, seq):
            s = lax.rem(at.s + step, seq)
            slot = qkv_out.at[s]
            send(slot, slot, swap.at[s, 0], swap.at[s, 1], at.across()).wait_recv()
            give(s).wait_send()
        up_sum.second_wait()
        for copy in copies:
            copy.wait_send()

    out_rank, qkv_rank = value_width // wt, width // (seq * wt)
    f32, low = jnp.float32, jnp.bfloat16
    tile = (8, value_width)
    results = remote_call(
        kernel,
        "mixer_back",
        4,
        [
            jax.ShapeDtypeStruct((count, width), f32),
            jax.ShapeDtypeStruct(tile, f32),
            jax.ShapeDtypeStruct((seq, qkv_rank, qkv_width), low),
            jax.ShapeDtypeStruct((out_rank, width), f32),
            jax.ShapeDtypeStruct((ys,) + gate_half, low),
            jax.ShapeDtypeStruct((ys, 2) + gate_half, low),
        ]
        + [
            jax.ShapeDtypeStruct(shape, low)
            for shape_half in (gate_half, gate_half, down_half)
            for shape in ((ys,) + shape_half, shape_half)
        ],
        [pltpu.VMEM(array.shape, array.dtype) for array in big]
        + [
            pltpu.VMEM((length, width), low),
            pltpu.VMEM((length, value_width), low),
            pltpu.VMEM((length, 128), f32),
            pltpu.VMEM((length, 128), f32),
            pltpu.VMEM((length, value_width), f32),
            pltpu.VMEM((length, value_width + 256), low),
            pltpu.VMEM((length, qkv_width), low),
            pltpu.VMEM((seq, 2, count // 2, width), low),
            pltpu.VMEM((seq, wt, qkv_rank, qkv_width), low),
            pltpu.VMEM((wt, out_rank, width), low),
            pltpu.VMEM((2, count // 2, width), f32),
            pltpu.VMEM((8, width), f32),
            pltpu.VMEM((8, width), f32),
            pltpu.VMEM(tile, f32),
            pltpu.VMEM((length, 128), f32),
            pltpu.VMEM((KCONV, value_width), f32),
            pltpu.VMEM(gate_half, low),
            pltpu.VMEM(gate_half, low),
            pltpu.VMEM(down_half, low),
            pltpu.VMEM(down_half, low),
            pltpu.VMEM((seq, qkv_rank, qkv_width), low),
            pltpu.VMEM((seq,) + tile, f32),
            pltpu.VMEM(tile, f32),
            pltpu.VMEM((wt,) + tile, f32),
        ]
        + SquareSum.scratch(seq, (count // 2, width))
        + LinePieces.scratch(wt, (seq, qkv_rank, qkv_width), seq)
        + LinePieces.scratch(wt, (out_rank, width), 1)
        + SquareTerms.scratch(seq, gate_half)
        + SquareTerms.scratch(seq, down_half)
        + SquareTerms.scratch(seq, gate_half)
        + SquareGather.semaphores(seq)
        + SquareTerms.semaphores(seq)
        + [
            pltpu.SemaphoreType.DMA((11,)),
            pltpu.SemaphoreType.DMA((seq, 2)),
            pltpu.SemaphoreType.DMA((seq, 2)),
            pltpu.SemaphoreType.DMA((wt, 2)),
        ],
        *big,
        *small,
        *far,
        in_specs=[ANY] * len(big) + [VMEM] * len(small) + [ANY] * len(far),
        out_specs=[VMEM] * 6 + [ANY] * 6,
    )
    grad, totals, qkv_total, out_total, up_x, up_y = results[:6]
    gate = tuple(gate_parts) + tuple(results[6:8])
    up = tuple(up_parts) + (up_x, up_y) + tuple(results[8:10])
    down = tuple(down_parts) + tuple(results[10:12])
    return grad, totals, gate, up, down, qkv_total, out_total


def last_sums(gate, up, down, qkv_total, totals, lengths, out_total, grad, final, qkv_shape):
    seq, wt = lax.axis_size("seq"), lax.axis_size("wt")
    ys = seq // 2
    f32, low = jnp.float32, jnp.bfloat16
    gate_half, down_half = gate[0].shape[2:], down[0].shape[2:]
    total_width = totals.shape[1]
    lanes_each = total_width // wt
    width = grad.shape[1]
    qkv_width = qkv_total.shape[2]
    operands = list(gate) + list(up) + list(down)
    passed = [out_total, grad, final]

    def kernel(*refs):
        groups, refs = [refs[5 * index : 5 * index + 5] for index in range(3)], refs[15:]
        (qkv_ref, totals_ref, length_ref), passed_refs, refs = refs[:3], refs[3:6], refs[6:]
        (gate_up_out, down_out, qkv_out, first_gain, second_gain, taps_out, loss_out), refs = refs[:7], refs[7:]
        passed_outs, refs = refs[:3], refs[3:]
        totals, refs = refs[:2], refs[2:]
        passed_rooms, refs = refs[:3], refs[3:]
        rooms, (loads, stores, pass_sems) = [refs[5 * index : 5 * index + 5] for index in range(3)], refs[15:]
        s = lax.axis_index("seq")
        y, x = lax.div(s, 2), lax.rem(s, 2)
        copies = []
        for number, (group, room) in enumerate(zip(groups, rooms)):
            terms, from_x, from_y, last_y, last_x = group
            pairs = [(terms.at[s], room[0]), (from_x.at[y], room[1]), (last_x, room[4])]
            for other in range(1, ys):
                place = lax.rem(y + other, ys)
                pairs.append((from_y.at[place, x], room[2].at[other - 1]))
                pairs.append((last_y.at[place], room[3].at[other - 1]))
            mine = [
                pltpu.make_async_copy(source, target, loads.at[number, index])
                for index, (source, target) in enumerate(pairs)
            ]
            for copy in mine:
                copy.start()
            copies.append(mine)
        ins = [
            pltpu.make_async_copy(source, room, pass_sems.at[index, 0])
            for index, (source, room) in enumerate(zip(passed_refs, passed_rooms))
        ]
        for copy in ins:
            copy.start()
        shift = lax.rem(total_width - lax.axis_index("wt") * lanes_each, total_width)
        mine = pltpu.roll(totals_ref[...], shift, 1)[:, :lanes_each]
        first_gain[...] = mine[0:1]
        second_gain[...] = mine[1:2]
        taps_out[...] = mine[3 : 3 + KCONV]
        counted = length_ref[0]
        for index in range(1, length_ref.shape[0]):
            counted = counted + length_ref[index]
        loss_out[...] = 2.0 * totals_ref[2:3, :1] / (jnp.full((1, 1), counted, jnp.int32).astype(f32) * width)
        for index in range(seq):
            qkv_out[:, index * qkv_width : (index + 1) * qkv_width] = qkv_ref[index].astype(f32)
        outs = []
        for index, (room, target) in enumerate(zip(passed_rooms, passed_outs)):
            ins[index].wait()
            copy = pltpu.make_async_copy(room, target, pass_sems.at[index, 1])
            copy.start()
            outs.append(copy)
        for number, room in enumerate(rooms):
            own, near_x, near_y, last_y, last_x = room
            total = totals[number // 2]
            base = 2 * (number % 2)
            for copy in copies[number]:
                copy.wait()
            rows = own.shape[1]
            tile = next(t for t in (64, 32, 16) if rows % t == 0)

            def step(index, carry):
                window = pl.ds(pl.multiple_of(index * tile, tile), tile)
                first = own[0, window, :].astype(f32) + near_x[window, :].astype(f32)
                second = own[1, window, :].astype(f32) + last_x[window, :].astype(f32)
                for other in range(ys - 1):
                    first = first + last_y[other, window, :].astype(f32)
                    second = second + near_y[other, window, :].astype(f32)
                total[base, window, :] = first
                total[base + 1, window, :] = second
                return carry

            lax.fori_loop(0, rows // tile, step, 0)
            target = gate_up_out.at[pl.ds(base, 2)] if number < 2 else down_out
            copy = pltpu.make_async_copy(total.at[pl.ds(base, 2)], target, stores.at[number])
            copy.start()
            outs.append(copy)
        for copy in outs:
            copy.wait()

    def rooms(half):
        return [
            pltpu.VMEM((2,) + half, low),
            pltpu.VMEM(half, low),
            pltpu.VMEM((ys - 1,) + half, low),
            pltpu.VMEM((ys - 1,) + half, low),
            pltpu.VMEM(half, low),
        ]

    return pl.pallas_call(
        kernel,
        name="last_sums",
        out_shape=[
            jax.ShapeDtypeStruct((4,) + gate_half, f32),
            jax.ShapeDtypeStruct((2,) + down_half, f32),
            jax.ShapeDtypeStruct(qkv_shape, f32),
            jax.ShapeDtypeStruct((1, lanes_each), f32),
            jax.ShapeDtypeStruct((1, lanes_each), f32),
            jax.ShapeDtypeStruct((KCONV, lanes_each), f32),
            jax.ShapeDtypeStruct((1, 1), f32),
        ]
        + [jax.ShapeDtypeStruct(array.shape, array.dtype) for array in passed],
        in_specs=[ANY] * 15 + [VMEM] * 2 + [SMEM] + [ANY] * 3,
        out_specs=[ANY] * 2 + [VMEM] * 5 + [ANY] * 3,
        scratch_shapes=[pltpu.VMEM((4,) + gate_half, f32), pltpu.VMEM((2,) + down_half, f32)]
        + [pltpu.VMEM(array.shape, array.dtype) for array in passed]
        + rooms(gate_half) * 2
        + rooms(down_half)
        + [
            pltpu.SemaphoreType.DMA((3, 1 + seq)),
            pltpu.SemaphoreType.DMA((3,)),
            pltpu.SemaphoreType.DMA((3, 2)),
        ],
        compiler_params=pltpu.CompilerParams(vmem_limit_bytes=VMEM_LIMIT),
    )(*operands, qkv_total, totals, lengths, *passed)


def rows_of_tile(values, row):
    return jnp.pad(values[None, :], [(row, 7 - row), (0, 128 - values.shape[0])])


def body(
    inputs,
    segment_ids,
    valid_lengths,
    teacher,
    w_qkv,
    conv_weight,
    w_out,
    norm_gain,
    w_gate_up,
    w_down,
    mlp_gain,
):
    seq_parts = lax.axis_size("seq")
    tok_count = inputs.shape[1]
    model_width = inputs.shape[2]
    length = tok_count * seq_parts
    head_count = H // seq_parts
    qkv_width = head_count * (2 * FEAT + DV)
    rows_low = inputs[0]
    gain_lanes = norm_gain.shape[0]
    gains = rows_of_tile(norm_gain.astype(jnp.float32), 0) + rows_of_tile(mlp_gain.astype(jnp.float32), 1)
    qkv_rows = w_qkv
    if qkv_width % 128:
        qkv_rows = w_qkv.reshape(w_qkv.shape[0], seq_parts, qkv_width).transpose(1, 0, 2)
    gate_up_low = w_gate_up.swapaxes(1, 2)
    segments = segment_ids
    (
        attended,
        normed_low,
        gain_rows,
        qkv_columns,
        out_rows,
        hidden_low,
        sorted_columns,
        mixer_low,
        mixed_values,
        head_outputs,
        gate_early,
        order,
    ) = mixer_forward(rows_low, qkv_rows, w_out, gains, gate_up_low, segments, conv_weight)
    (
        final_low,
        residual_error,
        energy,
        normed_all,
        gate_all,
        up_all,
        active_all,
        down_part,
        gate_up_part,
    ) = feed_forward(normed_low, attended, teacher[0], valid_lengths, gate_early, gate_up_low, w_down)
    (
        attended_grad,
        mix_back,
        gain_two_terms,
        gate_terms,
        up_terms,
        down_terms,
        gate_from_x,
        gate_from_y,
        down_from_x,
        down_from_y,
    ) = feed_back(
        residual_error,
        attended,
        gain_rows,
        gate_up_part,
        down_part,
        gate_all,
        up_all,
        active_all,
        normed_all,
    )
    inputs_grad, totals, gate, up, down, qkv_total, out_total = mixer_back(
        mix_back,
        attended_grad,
        rows_low,
        gain_rows,
        out_rows.reshape(head_count * DV, model_width),
        qkv_columns.reshape(model_width, qkv_width),
        hidden_low,
        sorted_columns,
        mixer_low,
        mixed_values,
        head_outputs,
        segments,
        conv_weight,
        order,
        gain_two_terms,
        energy,
        (gate_terms, gate_from_x, gate_from_y),
        (up_terms,),
        (down_terms, down_from_x, down_from_y),
    )
    (
        grad_w_gate_up,
        grad_w_down,
        grad_w_qkv,
        grad_norm_gain,
        grad_mlp_gain,
        grad_conv,
        mean_loss,
        grad_w_out,
        inputs_grad,
        outputs,
    ) = last_sums(
        gate, up, down, qkv_total, totals, valid_lengths, out_total, inputs_grad, final_low, w_qkv.shape
    )
    return (
        outputs[None],
        inputs_grad[None],
        mean_loss.reshape(()),
        grad_w_qkv,
        grad_conv,
        grad_w_out,
        grad_norm_gain.reshape(norm_gain.shape),
        grad_w_gate_up.reshape(gate_up_low.shape).swapaxes(1, 2),
        grad_w_down.reshape(w_down.shape),
        grad_mlp_gain.reshape(mlp_gain.shape),
    )


def solution(mesh):
    in_specs = (
        P("wt", "seq", None),
        P("wt", None),
        P(),
        P("wt", "seq", None),
        P(("seq", "wt"), None),
        P(None, "seq"),
        P(("seq", "wt"), None),
        P(("seq", "wt")),
        P(None, "seq", "wt"),
        P("wt", "seq"),
        P(("seq", "wt")),
    )
    out_specs = (
        P("wt", "seq", None),
        P("wt", "seq", None),
        P(),
        P(("seq", "wt"), None),
        P(None, ("seq", "wt")),
        P(("seq", "wt"), None),
        P(("seq", "wt")),
        P(None, "seq", "wt"),
        P("wt", "seq"),
        P(("seq", "wt")),
    )
    return jax.shard_map(body, mesh=mesh, in_specs=in_specs, out_specs=out_specs, check_vma=False)
```

```python
from functools import partial

import jax
import jax.numpy as jnp
from jax import lax
from jax.experimental import pallas as pl
from jax.experimental.pallas import tpu as pltpu
from jax.sharding import PartitionSpec as P

H = 16
FEAT = 16
KCONV = 3
DV = 128


epsilon = 1e-05


def rms_norm(values, gain_vector):
    inverse_root = lax.rsqrt(jnp.mean(values * values, axis=-1, keepdims=True) + epsilon)
    return values * inverse_root * gain_vector


def contract_last(former, latter):
    return lax.dot_general(
        former, latter, (((1,), (1,)), ((), ())), preferred_element_type=jnp.float32
    )


def contract_first(former, latter):
    return lax.dot_general(
        former, latter, (((0,), (0,)), ((), ())), preferred_element_type=jnp.float32
    )


def shift_down(values, amount, filler):
    padding = jnp.full((amount,) + values.shape[1:], filler, values.dtype)
    return jnp.concatenate([padding, values[:-amount]], axis=0)


def gated_unit(gate_in, up_in):
    return jax.nn.silu(gate_in) * up_in


MESH = pl.DeviceIdType.MESH
VMEM = pl.BlockSpec(memory_space=pltpu.VMEM)
ANY = pl.BlockSpec(memory_space=pl.ANY)
SMEM = pl.BlockSpec(memory_space=pltpu.SMEM)
VMEM_LIMIT = 67043328


class Place:
    def __init__(self, seq, wt):
        self.seq, self.wt = seq, wt
        self.ys, self.zs = seq // 2, wt // 2
        self.s, self.w = lax.axis_index("seq"), lax.axis_index("wt")
        self.y, self.x = lax.div(self.s, 2), lax.rem(self.s, 2)
        self.z, self.c = lax.div(self.w, 2), lax.rem(self.w, 2)

    def across(self):
        return (self.y * 2 + 1 - self.x, self.w)

    def beside(self, step):
        return lax.rem(self.y + step, self.ys)

    def column(self, y):
        return (y * 2 + self.x, self.w)

    def partner(self):
        return (self.s, self.z * 2 + 1 - self.c)

    def level(self, z):
        return (self.s, z * 2 + self.c)

    def meet(self, square, line):
        barrier = pltpu.get_barrier_semaphore()
        count = 0
        if square:
            for step in range(1, self.seq):
                device = (lax.rem(self.s + step, self.seq), self.w)
                pl.semaphore_signal(barrier, inc=1, device_id=device, device_id_type=MESH)
                count += 1
        if line:
            for step in range(1, self.wt):
                device = (self.s, lax.rem(self.w + step, self.wt))
                pl.semaphore_signal(barrier, inc=1, device_id=device, device_id_type=MESH)
                count += 1
        pl.semaphore_wait(barrier, count)


def send(source, target, leaving, arriving, device):
    return pltpu.make_async_remote_copy(
        src_ref=source,
        dst_ref=target,
        send_sem=leaving,
        recv_sem=arriving,
        device_id=device,
        device_id_type=MESH,
    )


def add_into(target, sources):
    if len(target.shape) == 3:
        for index in range(target.shape[0]):
            add_into(target.at[index], [source.at[index] for source in sources])
        return
    rows = target.shape[0]
    tile = next(t for t in (64, 32, 16, 8, rows) if rows % t == 0)

    def step(index, carry):
        window = pl.ds(pl.multiple_of(index * tile, tile), tile)
        total = sources[0][window, :].astype(jnp.float32)
        for source in sources[1:]:
            total = total + source[window, :].astype(jnp.float32)
        target[window, :] = total.astype(target.dtype)
        return carry

    lax.fori_loop(0, rows // tile, step, 0)


class SquareGather:
    @staticmethod
    def semaphores(seq):
        return [
            pltpu.SemaphoreType.DMA((2 + seq // 2,)),
            pltpu.SemaphoreType.DMA((seq // 2, 3)),
            pltpu.SemaphoreType.DMA((seq, 2)),
        ]

    def __init__(self, at, view, own, sems):
        self.at, self.view, self.own = at, view, own
        self.over_x, self.over_y, self.got = sems
        self.sent = []

    def go(self, copy):
        copy().start()
        self.sent.append(copy)

    def own_x(self, half):
        at = self.at
        target = self.view(at.s, half)
        return send(self.own(half), target, self.over_x.at[half], self.got.at[at.s, half], at.across())

    def own_y(self, step, half):
        at = self.at
        target, device = self.view(at.s, half), at.column(at.beside(step))
        return send(self.own(half), target, self.over_y.at[step, half], self.got.at[at.s, half], device)

    def pass_y(self, step):
        at = self.at
        s = at.y * 2 + 1 - at.x
        slot, device = self.view(s, 0), at.column(at.beside(step))
        return send(slot, slot, self.over_y.at[step, 2], self.got.at[s, 0], device)

    def pass_x(self, step):
        s = self.at.beside(step) * 2 + self.at.x
        slot = self.view(s, 1)
        return send(slot, slot, self.over_x.at[1 + step], self.got.at[s, 1], self.at.across())

    def wait(self, s, half):
        slot = self.view(s, half)
        send(slot, slot, self.over_x.at[0], self.got.at[s, half], self.at.across()).wait_recv()

    def start(self):
        for half in range(2):
            self.go(partial(self.own_x, half))
            for step in range(1, self.at.ys):
                self.go(partial(self.own_y, step, 1 - half))

    def relay(self):
        at = self.at
        self.wait(at.y * 2 + 1 - at.x, 0)
        for step in range(1, at.ys):
            self.go(partial(self.pass_y, step))
        for step in range(1, at.ys):
            self.wait(at.beside(step) * 2 + at.x, 1)
            self.go(partial(self.pass_x, step))

    def direct(self):
        at = self.at
        self.wait(at.y * 2 + 1 - at.x, 1)
        for step in range(1, at.ys):
            self.wait(at.beside(step) * 2 + at.x, 0)

    def relayed(self):
        at = self.at
        for step in range(1, at.ys):
            y = at.beside(step)
            self.wait(y * 2 + 1 - at.x, 0)
            self.wait(y * 2 + 1 - at.x, 1)
        for copy in self.sent:
            copy().wait_send()

    def finish(self):
        self.direct()
        self.relayed()


class SquareSum:
    @staticmethod
    def scratch(seq, half_shape):
        ys = seq // 2
        return [
            pltpu.VMEM((ys,) + half_shape, jnp.bfloat16),
            pltpu.VMEM((ys, 2) + half_shape, jnp.bfloat16),
            pltpu.VMEM((ys,) + half_shape, jnp.bfloat16),
            pltpu.VMEM(half_shape, jnp.bfloat16),
            pltpu.VMEM((ys,) + half_shape, jnp.bfloat16),
            pltpu.VMEM(half_shape, jnp.bfloat16),
            pltpu.SemaphoreType.DMA((ys, 2, 2)),
            pltpu.SemaphoreType.DMA((ys, 3, 2)),
        ]

    def __init__(self, at, part, scratch):
        self.at, self.part = at, part
        self.from_x, self.from_y, self.last_y, self.last_x, self.sum_y, self.sum_x, self.xs, self.yss = scratch
        self.sent = []

    def go(self, source, target, leaving, arriving, device):
        copy = send(source, target, leaving, arriving, device)
        copy.start()
        self.sent.append(copy)

    def wait(self, slot, leaving, arriving):
        send(slot, slot, leaving, arriving, self.at.across()).wait_recv()

    def start(self):
        at = self.at
        for y in range(at.ys):
            self.go(
                self.part(y * 2 + 1 - at.x, 0),
                self.from_x.at[y],
                self.xs.at[y, 0, 0],
                self.xs.at[y, 0, 1],
                at.across(),
            )
        for step in range(1, at.ys):
            y = at.beside(step)
            for x in range(2):
                self.go(
                    self.part(y * 2 + x, 1),
                    self.from_y.at[at.y, x],
                    self.yss.at[step, x, 0],
                    self.yss.at[at.y, x, 1],
                    at.column(y),
                )

    def relay(self):
        at = self.at
        for step in range(1, at.ys):
            y = at.beside(step)
            self.wait(self.from_x.at[y], self.xs.at[y, 0, 0], self.xs.at[y, 0, 1])
            add_into(self.sum_y.at[y], [self.part(y * 2 + at.x, 0), self.from_x.at[y]])
            self.go(
                self.sum_y.at[y],
                self.last_y.at[at.y],
                self.yss.at[step, 2, 0],
                self.yss.at[at.y, 2, 1],
                at.column(y),
            )
        terms = []
        for step in range(1, at.ys):
            y = at.beside(step)
            for x in range(2):
                self.wait(self.from_y.at[y, x], self.yss.at[step, x, 0], self.yss.at[y, x, 1])
            terms.append(self.from_y.at[y, 1 - at.x])
        add_into(self.sum_x, [self.part(at.y * 2 + 1 - at.x, 1)] + terms)
        self.go(self.sum_x, self.last_x, self.xs.at[0, 1, 0], self.xs.at[0, 1, 1], at.across())

    def finish(self, total):
        at = self.at
        self.wait(self.from_x.at[at.y], self.xs.at[0, 0, 0], self.xs.at[at.y, 0, 1])
        terms = [self.part(at.s, 0), self.from_x.at[at.y]]
        for step in range(1, at.ys):
            y = at.beside(step)
            self.wait(self.last_y.at[y], self.yss.at[step, 2, 0], self.yss.at[y, 2, 1])
            terms.append(self.last_y.at[y])
        add_into(total(0), terms)
        self.wait(self.last_x, self.xs.at[0, 1, 0], self.xs.at[0, 1, 1])
        terms = [self.part(at.s, 1), self.last_x]
        for step in range(1, at.ys):
            terms.append(self.from_y.at[at.beside(step), at.x])
        add_into(total(1), terms)
        for copy in self.sent:
            copy.wait_send()


class LineGather:
    @staticmethod
    def semaphores(wt, cuts=1):
        return [pltpu.SemaphoreType.DMA((5, wt // 2, cuts))]

    def __init__(self, at, view, sems):
        self.at, self.view, self.sems = at, view, sems[0]
        self.cuts = self.sems.shape[2]

    def cut(self, ref, part):
        if self.cuts == 1:
            return ref
        rows = ref.shape[0] // self.cuts
        return ref.at[pl.ds(part * rows, rows)]

    def hop(self, z, part, kind, device, source):
        slot = self.view(z * 2 + self.at.c)
        source = slot if source is None else source
        arriving = 4 if kind == 2 else 3
        return send(
            self.cut(source, part),
            self.cut(slot, part),
            self.sems.at[kind, z, part],
            self.sems.at[arriving, z, part],
            device,
        )

    def up(self, z, part, source=None):
        return self.hop(z, part, 0, self.at.level(self.at.z + 1), source)

    def down(self, z, part, source=None):
        return self.hop(z, part, 1, self.at.level(self.at.z - 1), source)

    def over(self, z, part, source=None):
        return self.hop(z, part, 2, self.at.partner(), source)

    def start(self, source=None):
        at = self.at
        for part in range(self.cuts):

            @pl.when(at.z + 1 < at.zs)
            def _():
                self.up(at.z, part, source).start()

            @pl.when(at.z > 0)
            def _():
                self.down(at.z, part, source).start()

            self.over(at.z, part, source).start()

    def step(self, index):
        at = self.at
        below, above = at.z - 1 - index, at.z + 1 + index
        for part in range(self.cuts):

            @pl.when(below >= 0)
            def _():
                self.up(below, part).wait_recv()

                @pl.when(at.z + 1 < at.zs)
                def _():
                    self.up(below, part).start()

                self.over(below, part).start()

            @pl.when(above < at.zs)
            def _():
                self.down(above, part).wait_recv()

                @pl.when(at.z > 0)
                def _():
                    self.down(above, part).start()

                self.over(above, part).start()

    def wait_over(self, z):
        for part in range(self.cuts):
            slot = self.cut(self.view(z * 2 + 1 - self.at.c), part)
            send(slot, slot, self.sems.at[2, z, part], self.sems.at[4, z, part], self.at.partner()).wait_recv()

    def finish(self):
        for z in range(self.at.zs):
            self.wait_over(z)
        self.sent()

    def sent(self):
        at = self.at
        for z in range(at.zs):
            for part in range(self.cuts):

                @pl.when((at.z >= z) & (at.z + 1 < at.zs))
                def _():
                    self.up(z, part).wait_send()

                @pl.when((at.z <= z) & (at.z > 0))
                def _():
                    self.down(z, part).wait_send()

                self.over(z, part).wait_send()


def remote_call(kernel, name, number, outs, scratch, *operands, in_specs=None, out_specs=None):
    return pl.pallas_call(
        kernel,
        name=name,
        out_shape=outs,
        in_specs=[VMEM] * len(operands) if in_specs is None else in_specs,
        out_specs=jax.tree.map(lambda _: VMEM, outs) if out_specs is None else out_specs,
        scratch_shapes=scratch,
        compiler_params=pltpu.CompilerParams(
            collective_id=number, has_side_effects=True, vmem_limit_bytes=VMEM_LIMIT
        ),
    )(*operands)


def write_order(ref, heads):
    head_width, value_width = 2 * FEAT + DV, heads * DV

    def step(index, carry):
        window = pl.ds(pl.multiple_of(index * 32, 32), 32)
        shape = (32, ref.shape[1])
        column = index * 32 + lax.broadcasted_iota(jnp.int32, shape, 0)
        head = lax.div(column, head_width)
        place = lax.rem(column, head_width)
        target = jnp.where(
            place < FEAT,
            value_width + head * FEAT + place,
            jnp.where(
                place < 2 * FEAT, value_width + 128 + head * FEAT + place - FEAT, head * DV + place - 2 * FEAT
            ),
        )
        hit = target == lax.broadcasted_iota(jnp.int32, shape, 1)
        ref[window, :] = hit.astype(jnp.float32).astype(jnp.bfloat16)
        return carry

    lax.fori_loop(0, ref.shape[0] // 32, step, 0)


def tap_marks(segment_column):
    segment = segment_column[:, :1]
    place = lax.broadcasted_iota(jnp.int32, segment_column.shape, 0)[:, :1]
    marks = [None]
    for tap in range(1, KCONV):
        same = (pltpu.roll(segment_column[...], tap, 0)[:, :1] == segment) & (place >= tap)
        marks.append(same.astype(jnp.float32))
    return marks


def early_rows(units):
    return units * 3 // 4 // 16 * 16


class LinePieces:
    @staticmethod
    def scratch(wt, shape, pieces):
        zs = wt // 2
        return [pltpu.VMEM((zs,) + shape, jnp.bfloat16)] * 3 + [pltpu.SemaphoreType.DMA((6, zs, pieces))]

    def __init__(self, at, part, scratch, order=None):
        self.at, self.part, self.order = at, part, order
        self.pair, self.below, self.above, self.sems = scratch
        self.pieces = self.sems.shape[2]
        self.width = self.pair.shape[-1] // self.pieces

    def cut(self, ref, piece):
        if len(ref.shape) == 3:
            return ref.at[piece]
        return ref.at[:, self.columns(piece)]

    def columns(self, piece):
        block = piece if self.order is None else self.order(piece)
        return pl.ds(pl.multiple_of(block * self.width, self.width), self.width)

    def own(self, z, piece):
        return self.cut(self.part(z * 2 + self.at.c), piece)

    def over(self, z, piece):
        return send(
            self.cut(self.part(z * 2 + 1 - self.at.c), piece),
            self.cut(self.pair.at[z], piece),
            self.sems.at[0, z, piece],
            self.sems.at[1, z, piece],
            self.at.partner(),
        )

    def up(self, z, piece):
        return send(
            self.own(z, piece),
            self.cut(self.below.at[z], piece),
            self.sems.at[2, z, piece],
            self.sems.at[3, z, piece],
            self.at.level(self.at.z + 1),
        )

    def down(self, z, piece):
        return send(
            self.own(z, piece),
            self.cut(self.above.at[z], piece),
            self.sems.at[4, z, piece],
            self.sems.at[5, z, piece],
            self.at.level(self.at.z - 1),
        )

    def terms(self, z, piece):
        self.over(z, piece).wait_recv()
        return [self.own(z, piece), self.cut(self.pair.at[z], piece)]

    def ends(self, z, piece):
        at = self.at

        @pl.when((at.z == 0) & (z > 0))
        def _():
            add_into(self.own(z, piece), self.terms(z, piece))
            self.up(z, piece).start()

        @pl.when((at.z == at.zs - 1) & (z < at.zs - 1))
        def _():
            add_into(self.own(z, piece), self.terms(z, piece))
            self.down(z, piece).start()

    def offer(self, piece):
        zs = self.at.zs
        for index in range(zs // 2):
            self.over(index, piece).start()
            self.over(zs - 1 - index, piece).start()

    def launch(self, piece, near):
        self.ends(jnp.where(self.at.z == 0, self.at.zs - 1 - near, near), piece)

    def launch_all(self, near):
        zs = self.at.zs

        def step(index, carry):
            self.launch(lax.rem(index, self.pieces), near + lax.div(index, self.pieces))
            return carry

        lax.fori_loop(0, (zs - 1 - near) * self.pieces, step, 0)

    def pass_on(self, index, fill=None, begin=0, end=None):
        at = self.at
        upper = at.z * 2 >= at.zs
        high, low = index, at.zs - 1 - index

        def lower(piece, when):
            @pl.when((at.z > low) & (at.z < at.zs - 1) & when)
            def _():
                terms = self.terms(low, piece)
                self.down(low, piece).wait_recv()
                add_into(self.own(low, piece), terms + [self.cut(self.above.at[low], piece)])
                self.down(low, piece).start()

        def step(piece, carry):
            lower(piece, upper)

            @pl.when((at.z < high) & (at.z > 0))
            def _():
                terms = self.terms(high, piece)
                self.up(high, piece).wait_recv()
                add_into(self.own(high, piece), terms + [self.cut(self.below.at[high], piece)])
                self.up(high, piece).start()

            lower(piece, jnp.logical_not(upper))
            if fill is not None:
                fill(piece, self.pieces)
            return carry

        end = self.pieces if end is None else end
        if end - begin == 1:
            step(begin, 0)
        else:
            lax.fori_loop(begin, end, step, 0)

    def finish(self, total, done=None):
        at = self.at

        def step(piece, carry):
            terms = self.terms(at.z, piece)
            below, above = self.cut(self.below.at[at.z], piece), self.cut(self.above.at[at.z], piece)

            @pl.when(at.z == 0)
            def _():
                self.down(at.z, piece).wait_recv()
                add_into(self.cut(total, piece), terms + [above])

            @pl.when(at.z == at.zs - 1)
            def _():
                self.up(at.z, piece).wait_recv()
                add_into(self.cut(total, piece), terms + [below])

            @pl.when((at.z > 0) & (at.z < at.zs - 1))
            def _():
                self.up(at.z, piece).wait_recv()
                self.down(at.z, piece).wait_recv()
                add_into(self.cut(total, piece), terms + [below, above])

            if done is not None:
                done(piece)
            for z in range(at.zs):

                @pl.when(at.z < z)
                def _():
                    self.up(z, piece).wait_send()

                @pl.when(at.z > z)
                def _():
                    self.down(z, piece).wait_send()

                self.over(z, piece).wait_send()
            return carry

        lax.fori_loop(0, self.pieces, step, 0)


class SquareTerms:
    @staticmethod
    def semaphores(seq):
        return [pltpu.SemaphoreType.DMA((seq // 2, 2)), pltpu.SemaphoreType.DMA((seq // 2, 2, 2))]

    @staticmethod
    def scratch(seq, half_shape):
        ys = seq // 2
        return [
            pltpu.VMEM((ys,) + half_shape, jnp.bfloat16),
            pltpu.VMEM(half_shape, jnp.bfloat16),
            pltpu.SemaphoreType.DMA((ys + 1, 2)),
        ]

    def __init__(self, at, terms, from_x, from_y, sems=None, lasts=None, scratch=None):
        self.at, self.terms, self.from_x, self.from_y = at, terms, from_x, from_y
        if sems is not None:
            self.xs, self.ys = sems
        if scratch is not None:
            self.last_y, self.last_x = lasts
            self.sum_y, self.sum_x, self.last = scratch

    def first_x(self, y):
        at = self.at
        return send(
            self.terms(y * 2 + 1 - at.x, 0), self.from_x.at[y], self.xs.at[y, 0], self.xs.at[y, 1], at.across()
        )

    def first_y(self, step, x):
        at = self.at
        y = at.beside(step)
        return send(
            self.terms(y * 2 + x, 1),
            self.from_y.at[at.y, x],
            self.ys.at[step, x, 0],
            self.ys.at[at.y, x, 1],
            at.column(y),
        )

    def first_start(self):
        for y in range(self.at.ys):
            self.first_x(y).start()
        for step in range(1, self.at.ys):
            for x in range(2):
                self.first_y(step, x).start()

    def first_wait(self):
        at = self.at
        for y in range(at.ys):
            self.first_x(y).wait()
        for step in range(1, at.ys):
            y = at.beside(step)
            for x in range(2):
                self.first_y(step, x).wait_send()
                slot = self.from_y.at[y, x]
                send(slot, slot, self.ys.at[step, x, 0], self.ys.at[y, x, 1], at.across()).wait_recv()

    def second_y(self, step):
        at = self.at
        y = at.beside(step)
        return send(
            self.sum_y.at[y], self.last_y.at[at.y], self.last.at[step, 0], self.last.at[at.y, 1], at.column(y)
        )

    def second_x(self):
        at = self.at
        return send(self.sum_x, self.last_x, self.last.at[at.ys, 0], self.last.at[at.ys, 1], at.across())

    def second_start(self, fetch, rooms):
        at = self.at
        for step in range(1, at.ys):
            y = at.beside(step)
            fetch([(self.terms(y * 2 + at.x, 0), rooms[0]), (self.from_x.at[y], rooms[1])])
            add_into(self.sum_y.at[y], [rooms[0], rooms[1]])
        fetch([(self.terms(at.y * 2 + 1 - at.x, 1), self.sum_x)])
        for step in range(1, at.ys):
            y = at.beside(step)
            fetch([(self.from_y.at[y, 1 - at.x], rooms[0])])
            add_into(self.sum_x, [self.sum_x, rooms[0]])

    def second_load(self, fetch):
        at = self.at
        pairs = [(self.terms(at.y * 2 + 1 - at.x, 1), self.sum_x)]
        for step in range(1, at.ys):
            y = at.beside(step)
            pairs.append((self.terms(y * 2 + at.x, 0), self.sum_y.at[y]))
        fetch(pairs)

    def second_arrived(self):
        at = self.at
        terms = [self.sum_x]
        for step in range(1, at.ys):
            y = at.beside(step)
            add_into(self.sum_y.at[y], [self.sum_y.at[y], self.from_x.at[y]])
            terms.append(self.from_y.at[y, 1 - at.x])
        add_into(self.sum_x, terms)

    def second_go(self):
        for step in range(1, self.at.ys):
            self.second_y(step).start()
        self.second_x().start()

    def second_wait(self):
        at = self.at
        for step in range(1, at.ys):
            self.second_y(step).wait_send()
            y = at.beside(step)
            slot = self.last_y.at[y]
            send(slot, slot, self.last.at[step, 0], self.last.at[y, 1], at.across()).wait_recv()
        self.second_x().wait()


def norm_back(rows, load, store, gain, terms):
    def step(index, carry):
        window = pl.ds(pl.multiple_of(index * 16, 16), 16)
        values, incoming, base = load(window)
        root = lax.rsqrt(jnp.mean(values * values, axis=-1, keepdims=True) + epsilon)
        scaled = incoming * gain
        share = jnp.mean(values * scaled, axis=-1, keepdims=True)
        store(window, base + root * scaled - values * (root * root * root * share))
        term = incoming * values * root
        terms[...] += term[:8] + term[8:]
        return carry

    lax.fori_loop(0, rows // 16, step, 0)


class Exchange:
    def __init__(self, at, shard, everyone, gather_sems, local, sums, first, second):
        self.at, self.sums, self.first, self.second = at, sums, first, second
        count = shard.shape[0]
        slot = lambda w: everyone.at[pl.ds(pl.multiple_of(w * count, count), count)]
        self.gather = LineGather(at, slot, gather_sems)
        self.gather.start(shard)
        own = pltpu.make_async_copy(shard, slot(at.w), local)
        own.start()
        own.wait()
        self.last, self.ahead = 2 * (at.zs - 1), 0

    def step_ahead(self):
        self.gather.step(0)
        self.ahead = 1

    def level(self, index):
        at = self.at
        far, side = lax.div(index + 1, 2), lax.rem(index, 2)
        z = at.z + jnp.where(side == 1, -far, far)
        return far, side, z, (z >= 0) & (z < at.zs)

    def arrive(self, index):
        far, side, z, valid = self.level(index)

        @pl.when((side == 1) & (far > self.ahead))
        def _():
            self.gather.step(far - 1)

        @pl.when(valid)
        def _():
            self.gather.wait_over(z)
            self.first(z)

        return z, valid

    def put(self, z, begin, end):
        def step(piece, inner):
            self.second(z, piece)
            self.sums.over(z, piece).start()

            @pl.when(piece > begin)
            def _():
                self.sums.ends(z, piece - 1)

            return inner

        lax.fori_loop(begin, end, step, 0)
        self.sums.ends(z, end - 1)

    def whole(self, total, fill):
        at, sums = self.at, self.sums

        def turn(index, carry):
            z, valid = self.arrive(index)

            @pl.when(valid)
            def _():
                self.put(z, 0, sums.pieces)

            return carry

        lax.fori_loop(0, self.last + 1, turn, 0)
        fill(None, sums.pieces)
        for index in range(2, at.zs):
            sums.pass_on(index, fill if index == 2 else None)
        sums.finish(total)
        self.gather.sent()

    def by_columns(self, total, direct, relayed, near):
        at, sums = self.at, self.sums
        begin = min(3, self.last)

        def turn(index, carry):
            z, valid = self.arrive(index)

            @pl.when(index == begin)
            def _():
                direct()

            @pl.when(valid & (index >= begin))
            def _():
                self.put(z, 0, near)

            return carry

        lax.fori_loop(0, self.last + 1, turn, 0)

        def earlier(index, carry):
            _, _, z, valid = self.level(index)

            @pl.when(valid)
            def _():
                self.put(z, 0, near)

            return carry

        lax.fori_loop(1, begin, earlier, 0)
        if at.zs > 2:
            sums.pass_on(2, None, 0, near)
        relayed()

        def over(index, carry):
            _, _, z, valid = self.level(self.last - index)

            @pl.when(valid)
            def _():
                for piece in range(near, sums.pieces):
                    self.second(z, piece)
                    sums.over(z, piece).start()

            return carry

        lax.fori_loop(0, self.last, over, 0)

        def start(index, carry):
            _, _, z, valid = self.level(self.last - index)

            @pl.when(valid)
            def _():
                for piece in range(near, sums.pieces):
                    sums.ends(z, piece)

            return carry

        lax.fori_loop(0, self.last, start, 0)
        self.put(at.z, 0, sums.pieces)
        for index in range(3, at.zs):
            sums.pass_on(index, None, 0, near)
        for index in range(at.zs - 1, 1, -1):
            sums.pass_on(index, None, near, sums.pieces)
        sums.finish(total)
        self.gather.sent()


PIECES = 2


def feed_forward(at, sizes, inputs, outputs, scratch):
    count, width, units, block, columns = sizes
    early, half, zs, seq = early_rows(units), units // 2, at.zs, at.seq
    normed_ref, attended_ref, teacher_ref, length_ref, gate_shard_ref, shard_ref = inputs
    (final_out, error_out, energy_out), outputs = outputs[:3], outputs[3:]
    normed_out, gate_out, up_out, active_out, down_out, gates_out = outputs
    everyone, gates, downs, gate_all, up_all, active_all, parts, total = scratch[:8]
    gather_sems, sum_scratch, late_sems, square_sems, (local, outgoing) = (
        scratch[8:9],
        scratch[9:13],
        scratch[13:16],
        scratch[16:19],
        scratch[19:],
    )
    late = SquareGather(
        at,
        lambda s, h: gates.at[
            h, pl.ds(early, units - early), pl.ds(pl.multiple_of(s * block, block), block)
        ],
        lambda h: gate_shard_ref.at[h, pl.ds(early, units - early)],
        late_sems,
    )
    weights = SquareGather(
        at,
        lambda s, h: downs.at[
            pl.ds(h * half, half), pl.ds(pl.multiple_of(s * columns, columns), columns)
        ],
        lambda h: shard_ref.at[pl.ds(h * half, half)],
        square_sems,
    )
    ys = seq // 2

    def column_block(piece):
        if isinstance(piece, int):
            step = 0 if piece < 2 else piece - 1 if piece <= ys else piece - ys
            return at.beside(step) * 2 + (1 - at.x if piece == 1 or piece > ys else at.x)
        step = jnp.where(piece < 2, 0, jnp.where(piece <= ys, piece - 1, piece - ys))
        other = (piece == 1) | (piece > ys)
        return at.beside(step) * 2 + jnp.where(other, 1 - at.x, at.x)

    sums = LinePieces(
        at,
        lambda w: parts.at[pl.ds(pl.multiple_of(w * count, count), count)],
        sum_scratch,
        column_block,
    )
    down_store = pltpu.make_async_copy(downs, down_out, local.at[2])
    gates_store = pltpu.make_async_copy(gates, gates_out, local.at[0])

    def direct():
        weights.relay()
        weights.direct()

    def relayed():
        weights.relayed()
        down_store.start()

    def rows(z):
        return pl.ds(pl.multiple_of(z * 2 * count, 2 * count), 2 * count)

    def stores(z):
        return [
            pltpu.make_async_copy(source.at[rows(z)], target.at[rows(z)], outgoing.at[index, z])
            for index, (source, target) in enumerate(
                ((everyone, normed_out), (gate_all, gate_out), (up_all, up_out), (active_all, active_out))
            )
        ]

    def first(z):
        here = everyone[rows(z), :]
        gate = contract_last(here, gates[0])
        up = contract_last(here, gates[1])
        gate_all[rows(z), :] = gate
        up_all[rows(z), :] = up
        active_all[rows(z), :] = gated_unit(gate, up).astype(jnp.bfloat16)
        for copy in stores(z):
            copy.start()

    def second(z, piece):
        window = sums.columns(piece)
        parts[rows(z), window] = jnp.dot(
            active_all[rows(z), :], downs[:, window], preferred_element_type=jnp.float32
        ).astype(jnp.bfloat16)

    def run():
        work = Exchange(at, normed_ref, everyone, gather_sems, local.at[1], sums, first, second)
        late.relay()
        weights.start()
        own = pltpu.make_async_copy(
            shard_ref, downs.at[:, pl.ds(pl.multiple_of(at.s * columns, columns), columns)], local.at[3]
        )
        own.start()
        work.step_ahead()
        own.wait()
        late.finish()
        gates_store.start()
        work.by_columns(total, direct, relayed, ys + 1)
        energy_out[...] = jnp.zeros_like(energy_out)
        valid = length_ref[at.w]

        def finish_rows(index, carry):
            window = pl.ds(pl.multiple_of(index * 16, 16), 16)
            final = attended_ref[window, :] + total[window, :]
            final_out[window, :] = final.astype(jnp.bfloat16)
            place = at.s * count + index * 16 + lax.broadcasted_iota(jnp.int32, final.shape, 0)
            keep = (place < valid).astype(jnp.float32)
            error = (final - teacher_ref[window, :].astype(jnp.float32)) * keep
            error_out[window, :] = error
            squares = error * error
            energy_out[...] += 0.5 * (squares[:8] + squares[8:])
            return carry

        lax.fori_loop(0, count // 16, finish_rows, 0)
        down_store.wait()
        gates_store.wait()
        for z in range(zs):
            for copy in stores(z):
                copy.wait()

    return late.start, run


def forward_pass(tokens, qkv_rows, out_rows, gains, segments, taps, teacher, down, lengths, gate_up):
    seq, wt = lax.axis_size("seq"), lax.axis_size("wt")
    zs = wt // 2
    count, width = tokens.shape
    length = count * seq
    out_rank = out_rows.shape[0]
    heads = H // seq
    value_width = heads * DV
    qkv_width = value_width + 2 * FEAT * heads
    qkv_rank = width // (seq * wt)
    lanes_each = width // (seq * wt)
    units, block = gate_up.shape[1:]
    early = early_rows(units)
    rows_at_once = 256
    small = [
        tokens,
        qkv_rows,
        out_rows,
        gains,
        segments,
        taps,
        teacher,
        down,
    ]
    token_count = wt * count

    def kernel(*refs):
        (x_ref, qkv_ref, out_ref, gain_ref, segment_ref, tap_ref, teacher_ref, down_ref), refs = refs[:8], refs[8:]
        (length_ref, gate_up_ref), refs = refs[:2], refs[2:]
        (attended_out, normed_out, gain_rows), refs = refs[:3], refs[3:]
        (qkv_out, w_out_out, hidden_out, sorted_out, mixer_out, values_out, outputs_out, order_out), refs = (
            refs[:8],
            refs[8:],
        )
        feed_outputs, refs = refs[:9], refs[9:]
        (xs, qkvs, outs, gains_all, sorted_v, values_v, outputs_v), refs = refs[:7], refs[7:]
        (order_v, segment_column, tap_v), refs = refs[:3], refs[3:]
        sum_scratch, x_sems, gate_sems, refs = refs[:8], refs[8:11], refs[11:14], refs[14:]
        line_sems, refs = [refs[index : index + 1] for index in range(3)], refs[3:]
        (swap_q, swap_g, local, outgoing), feed_scratch = refs[:4], refs[4:]
        at = Place(seq, wt)
        gates_ref, parts, total = feed_scratch[1], feed_scratch[6], feed_scratch[7]
        hidden_v = parts.at[pl.ds(length, length)]
        mixer_v = feed_scratch[5].at[pl.ds(0, length), pl.ds(0, value_width)]
        gates_own = pltpu.make_async_copy(
            gate_up_ref, gates_ref.at[:, :, pl.ds(pl.multiple_of(at.s * block, block), block)], local.at[4]
        )
        gates_own.start()
        late_start, feed = feed_forward(
            at,
            (count, width, units, block, down.shape[1]),
            (normed_out, attended_out, teacher_ref, length_ref, gate_up_ref, down_ref),
            feed_outputs,
            feed_scratch,
        )
        at.meet(True, True)
        half = count // 2
        gather_x = SquareGather(
            at,
            lambda s, h: xs.at[pl.ds(pl.multiple_of(s * count + h * half, half), half)],
            lambda h: x_ref.at[pl.ds(h * half, half)],
            x_sems,
        )
        gather_q = LineGather(at, lambda w: qkvs.at[:, w], line_sems[0])
        gather_g = LineGather(
            at, lambda w: gains_all.at[:, pl.ds(pl.multiple_of(w * 8, 8), 8)], line_sems[1]
        )
        gather_o = LineGather(at, lambda w: outs.at[w], line_sems[2])
        gates = SquareGather(
            at,
            lambda s, h: gates_ref.at[h, pl.ds(0, early), pl.ds(pl.multiple_of(s * block, block), block)],
            lambda h: gate_up_ref.at[h, pl.ds(0, early)],
            gate_sems,
        )
        gain_slot = pl.ds(pl.multiple_of(at.w * 8, 8), 8)

        def qkv_part(s):
            if len(qkv_ref.shape) == 3:
                return qkv_ref.at[s]
            return qkv_ref.at[:, pl.ds(pl.multiple_of(s * qkv_width, qkv_width), qkv_width)]

        swaps = []
        for step in range(1, seq):
            to = lax.rem(at.s + step, seq)
            swaps.append(
                send(gain_ref, gains_all.at[at.s, gain_slot], swap_g.at[step, 0], swap_g.at[at.s, 1], (to, at.w))
            )
            swaps.append(
                send(qkv_part(to), qkvs.at[at.s, at.w], swap_q.at[step, 0], swap_q.at[at.s, 1], (to, at.w))
            )
        for copy in swaps:
            copy.start()
        gather_x.start()
        own = [
            pltpu.make_async_copy(qkv_part(at.s), qkvs.at[at.s, at.w], local.at[0]),
            pltpu.make_async_copy(gain_ref, gains_all.at[at.s, gain_slot], local.at[1]),
            pltpu.make_async_copy(out_ref, outs.at[at.w], local.at[2]),
            pltpu.make_async_copy(x_ref, xs.at[pl.ds(pl.multiple_of(at.s * count, count), count)], local.at[3]),
        ]
        for copy in own:
            copy.start()
        for copy in own:
            copy.wait()
        for step in range(1, seq):
            s = lax.rem(at.s + step, seq)
            slot = gains_all.at[s, gain_slot]
            send(slot, slot, swap_g.at[step, 0], swap_g.at[s, 1], at.across()).wait_recv()
            slot = qkvs.at[s, at.w]
            send(slot, slot, swap_q.at[step, 0], swap_q.at[s, 1], at.across()).wait_recv()
        gather_g.start()
        gather_q.start()
        tap_v[...] = tap_ref[...].astype(jnp.float32)
        segment_row = segment_ref[...].astype(jnp.float32)
        segment_column[...] = jnp.broadcast_to(segment_row, (128, length)).T
        write_order(order_v, heads)
        gather_x.relay()
        gates.start()
        for index in range(zs - 1):
            if index == zs - 2:
                gather_o.start()
            gather_g.step(index)
            gather_q.step(index)
        gather_g.finish()

        device_rows = gains_all[...].reshape(seq * wt * 8, 128).astype(jnp.bfloat16)
        gain_rows[...] = jnp.zeros_like(gain_rows)

        def spread_gains(index, carry):
            begin = pl.multiple_of(index * 256, 256)
            lane = lax.broadcasted_iota(jnp.int32, (128, 256), 0)
            column = begin + lax.broadcasted_iota(jnp.int32, (128, 256), 1)
            copied = jnp.dot(
                device_rows,
                (lane == lax.rem(column, lanes_each)).astype(jnp.float32).astype(jnp.bfloat16),
                preferred_element_type=jnp.float32,
            )
            row = lax.broadcasted_iota(jnp.int32, copied.shape, 0)
            column = begin + lax.broadcasted_iota(jnp.int32, copied.shape, 1)
            first_row = lax.div(column, lanes_each) * 8
            for number in range(2):
                gain_rows[number : number + 1, pl.ds(begin, 256)] = jnp.sum(
                    jnp.where(row == first_row + number, copied, 0.0), axis=0, keepdims=True
                )
            return carry

        lax.fori_loop(0, width // 256, spread_gains, 0)
        gather_x.finish()

        def norm_rows(index, carry):
            window = pl.ds(pl.multiple_of(index * 32, 32), 32)
            hidden_v[window, :] = rms_norm(xs[window, :].astype(jnp.float32), gain_rows[0:1, :]).astype(
                jnp.bfloat16
            )
            return carry

        lax.fori_loop(0, length // 32, norm_rows, 0)
        gather_q.finish()
        projected = jnp.dot(
            hidden_v[...], qkvs[...].reshape(width, qkv_width), preferred_element_type=jnp.float32
        ).astype(jnp.bfloat16)
        sorted_v[...] = jnp.dot(projected, order_v[...], preferred_element_type=jnp.float32).astype(
            jnp.bfloat16
        )
        stores = [
            pltpu.make_async_copy(source, target, outgoing.at[index])
            for index, (source, target) in enumerate(
                (
                    (qkvs, qkv_out),
                    (hidden_v, hidden_out),
                    (sorted_v, sorted_out),
                    (values_v, values_out),
                    (outputs_v, outputs_out),
                    (mixer_v, mixer_out),
                    (outs, w_out_out),
                    (order_v, order_out),
                )
            )
        ]
        for copy in stores[:3]:
            copy.start()
        marks = tap_marks(segment_column)

        def convolve(head, carry):
            columns = pl.ds(pl.multiple_of(head * DV, DV), DV)
            raw = sorted_v[:, columns].astype(jnp.float32)
            mixed = tap_v[0:1, columns] * raw
            for tap in range(1, KCONV):
                mixed = mixed + tap_v[tap : tap + 1, columns] * pltpu.roll(raw, tap, 0) * marks[tap]
            values_v[head] = mixed.astype(jnp.bfloat16)
            return carry

        lax.fori_loop(0, heads, convolve, 0)
        stores[3].start()
        gates.relay()
        steps = length // rows_at_once
        lanes = lax.broadcasted_iota(jnp.int32, (1, 128), 1)

        def attend(index, carry):
            head, start = lax.div(index, steps), lax.rem(index, steps) * rows_at_once
            rows = pl.ds(pl.multiple_of(start, rows_at_once), rows_at_once)
            mine = ((lanes >= head * FEAT) & (lanes < head * FEAT + FEAT)).astype(jnp.float32)
            queries = sorted_v[rows, value_width : value_width + 128] * mine.astype(jnp.bfloat16)
            scores = contract_last(queries, sorted_v[:, value_width + 128 :]) * 0.25
            places = start + lax.broadcasted_iota(jnp.int32, scores.shape, 0)
            allowed = (segment_column[rows, :1] == segment_row) & (
                places >= lax.broadcasted_iota(jnp.int32, scores.shape, 1)
            )
            kernel_values = jnp.where(allowed, 1.0 + scores + 0.5 * scores * scores, 0.0)
            denominator = jnp.sum(kernel_values, axis=1, keepdims=True)
            mixed = (
                jnp.dot(kernel_values.astype(jnp.bfloat16), values_v[head], preferred_element_type=jnp.float32)
                / denominator
            )
            outputs_v[head, rows, :] = mixed
            mixer_v[rows, pl.ds(pl.multiple_of(head * DV, DV), DV)] = mixed.astype(jnp.bfloat16)
            return carry

        turns = heads * steps
        for index in range(zs - 1):
            lax.fori_loop(turns * index // (zs - 1), turns * (index + 1) // (zs - 1), attend, 0)
            gather_o.step(index)
        gather_o.finish()
        for copy in stores[4:]:
            copy.start()

        def out_job(index, carry):
            window = pl.ds(pl.multiple_of(index * 512, 512), 512)
            term = jnp.dot(
                mixer_v[...], outs[:, :, window].reshape(value_width, 512), preferred_element_type=jnp.float32
            ).astype(jnp.bfloat16)
            for s in range(seq):
                for h in range(2):
                    begin = s * count + h * half
                    parts[begin : begin + half, window] = term[begin : begin + half]
            return carry

        lax.fori_loop(0, width // 512, out_job, 0)
        work = SquareSum(
            at, lambda s, h: parts.at[pl.ds(pl.multiple_of(s * count + h * half, half), half)], sum_scratch
        )
        work.start()
        work.relay()
        late_start()
        work.finish(lambda h: total.at[pl.ds(h * half, half)])

        def finish_rows(index, carry):
            for h in range(2):
                rows = pl.ds(pl.multiple_of(h * half + index * 16, 16), 16)
                attended = x_ref[rows, :].astype(jnp.float32) + total[rows, :]
                attended_out[rows, :] = attended
                normed_out[rows, :] = rms_norm(attended, gain_rows[1:2, :]).astype(jnp.bfloat16)
            return carry

        lax.fori_loop(0, half // 16, finish_rows, 0)
        gates.finish()
        gates_own.wait()
        stores[1].wait()
        stores[5].wait()
        feed()
        for copy in swaps:
            copy.wait_send()
        for index, copy in enumerate(stores):
            if index not in (1, 5):
                copy.wait()

    low, f32 = jnp.bfloat16, jnp.float32
    sorted_width = value_width + 256
    return remote_call(
        kernel,
        "forward_pass",
        0,
        [
            jax.ShapeDtypeStruct((count, width), f32),
            jax.ShapeDtypeStruct((count, width), low),
            jax.ShapeDtypeStruct((8, width), f32),
            jax.ShapeDtypeStruct((seq, wt, qkv_rank, qkv_width), low),
            jax.ShapeDtypeStruct((wt, out_rank, width), low),
            jax.ShapeDtypeStruct((length, width), low),
            jax.ShapeDtypeStruct((length, sorted_width), low),
            jax.ShapeDtypeStruct((length, value_width), low),
            jax.ShapeDtypeStruct((heads, length, DV), low),
            jax.ShapeDtypeStruct((heads, length, DV), f32),
            jax.ShapeDtypeStruct((qkv_width, sorted_width), low),
            jax.ShapeDtypeStruct((count, width), low),
            jax.ShapeDtypeStruct((count, width), f32),
            jax.ShapeDtypeStruct((8, width), f32),
            jax.ShapeDtypeStruct((token_count, width), low),
            jax.ShapeDtypeStruct((token_count, units), f32),
            jax.ShapeDtypeStruct((token_count, units), f32),
            jax.ShapeDtypeStruct((token_count, units), low),
            jax.ShapeDtypeStruct((units, width), low),
            jax.ShapeDtypeStruct((2, units, width), low),
        ],
        [
            pltpu.VMEM((length, width), low),
            pltpu.VMEM((seq, wt, qkv_rank, qkv_width), low),
            pltpu.VMEM((wt, out_rank, width), low),
            pltpu.VMEM((seq, wt * 8, 128), f32),
            pltpu.VMEM((length, sorted_width), low),
            pltpu.VMEM((heads, length, DV), low),
            pltpu.VMEM((heads, length, DV), f32),
            pltpu.VMEM((qkv_width, sorted_width), low),
            pltpu.VMEM((length, 128), f32),
            pltpu.VMEM((KCONV, value_width), f32),
        ]
        + SquareSum.scratch(seq, (count // 2, width))
        + SquareGather.semaphores(seq)
        + SquareGather.semaphores(seq)
        + LineGather.semaphores(wt) * 3
        + [
            pltpu.SemaphoreType.DMA((seq, 2)),
            pltpu.SemaphoreType.DMA((seq, 2)),
            pltpu.SemaphoreType.DMA((5,)),
            pltpu.SemaphoreType.DMA((8,)),
            pltpu.VMEM((token_count, width), low),
            pltpu.VMEM((2, units, width), low),
            pltpu.VMEM((units, width), low),
            pltpu.VMEM((token_count, units), f32),
            pltpu.VMEM((token_count, units), f32),
            pltpu.VMEM((token_count, units), low),
            pltpu.VMEM((token_count, width), low),
            pltpu.VMEM((count, width), f32),
        ]
        + LineGather.semaphores(wt, 2)
        + LinePieces.scratch(wt, (count, width), seq)
        + SquareGather.semaphores(seq)
        + SquareGather.semaphores(seq)
        + [pltpu.SemaphoreType.DMA((5,)), pltpu.SemaphoreType.DMA((4, zs))],
        *small,
        lengths,
        gate_up,
        in_specs=[VMEM] * len(small) + [SMEM, ANY],
        out_specs=[VMEM] * 3 + [ANY] * 8 + [VMEM] * 3 + [ANY] * 6,
    )


def feed_back(error, attended, gain, gate_up, down, gate, up, active, normed):
    seq, wt = lax.axis_size("seq"), lax.axis_size("wt")
    count, width = error.shape
    units = gate_up.shape[1]
    tokens = wt * count
    ys = seq // 2
    block = width // seq
    half = (units // 2, block)

    def kernel(*refs):
        (error_ref, attended_ref, gain_ref, gate_up_ref, down_ref, gate_ref, up_ref, active_ref, normed_ref), refs = (
            refs[:9],
            refs[9:],
        )
        (grad_ref, mix_ref, gain_terms), refs = refs[:3], refs[3:]
        (gate_out, up_out, down_out, gate_x, gate_y, down_x, down_y), refs = refs[:7], refs[7:]
        (low, everyone, gates, downs, gate_all, up_all, back_all, parts, actives, columns), refs = refs[:10], refs[10:]
        (gate_terms, up_terms, down_terms, total), refs = refs[:4], refs[4:]
        gather_sems, sum_scratch, gate_sems, down_sems, (local, outgoing) = (
            refs[:1],
            refs[1:5],
            refs[5:7],
            refs[7:9],
            refs[9:],
        )
        at = Place(seq, wt)
        loads = [
            pltpu.make_async_copy(source, target, local.at[index])
            for index, (source, target) in enumerate(
                (
                    (down_ref, downs),
                    (gate_ref, gate_all),
                    (up_ref, up_all),
                    (gate_up_ref, gates),
                    (active_ref, actives),
                )
            )
        ]
        for load in loads:
            load.start()
        at.meet(True, True)
        low[...] = error_ref[...].astype(jnp.bfloat16)
        sums = LinePieces(
            at, lambda w: parts.at[pl.ds(pl.multiple_of(w * count, count), count)], sum_scratch
        )
        gate_sum = SquareTerms(at, lambda s, h: gate_terms.at[s, h], gate_x, gate_y, gate_sems)
        down_sum = SquareTerms(at, lambda s, h: down_terms.at[s, h], down_x, down_y, down_sems)

        def place(index):
            step = lax.div(index, 2) + 1
            x = lax.rem(at.x + 1 + lax.rem(index, 2), 2)
            return step, x, at.beside(step) * 2 + x

        def column_load(index):
            s = place(index)[2]
            return pltpu.make_async_copy(
                normed_ref.at[:, pl.ds(pl.multiple_of(s * block, block), block)],
                columns.at[lax.rem(index, 2)],
                local.at[6 + lax.rem(index, 2)],
            )

        def leave(sum_, index):
            step, x, s = place(index)

            @pl.when(x != at.x)
            def _():
                sum_.first_x(lax.div(s, 2)).start()

            @pl.when(step < ys)
            def _():
                sum_.first_y(step, x).start()

        def down_job(index):
            s = place(index)[2]
            term = contract_first(
                actives[...], everyone[:, pl.ds(pl.multiple_of(s * block, block), block)]
            ).astype(jnp.bfloat16)
            down_terms[s, 0] = term[: units // 2]
            down_terms[s, 1] = term[units // 2 :]
            leave(down_sum, index)

        def gate_job(index):
            s = place(index)[2]
            column_load(index).wait()
            here = columns.at[lax.rem(index, 2)]
            for number, terms in enumerate((gate_terms, up_terms)):
                term = contract_first(back_all[number], here[...]).astype(jnp.bfloat16)
                terms[s, 0] = term[: units // 2]
                terms[s, 1] = term[units // 2 :]

            @pl.when(index + 2 < seq)
            def _():
                column_load(index + 2).start()

            leave(gate_sum, index)

        def fill(slot, slots):
            if slot is None:
                lax.fori_loop(0, seq, lambda index, carry: (down_job(index), carry)[1], 0)
                return

            each = -(-seq // slots)

            def step(index, carry):
                job = slot * each + index

                @pl.when(job < seq)
                def _():
                    gate_job(job)

                return carry

            lax.fori_loop(0, each, step, 0)

        def prepare():
            column_load(0).start()
            column_load(1).start()
            for load in loads:
                load.wait()

        def rows(z):
            return pl.ds(pl.multiple_of(z * 2 * count, 2 * count), 2 * count)

        def first(z):
            active_back = contract_last(everyone[rows(z), :], downs[...])
            gate_here, up_here = gate_all[rows(z), :], up_all[rows(z), :]
            share = jax.nn.sigmoid(gate_here)
            back_all[0, rows(z), :] = (
                active_back * up_here * share * (1.0 + gate_here * (1.0 - share))
            ).astype(jnp.bfloat16)
            back_all[1, rows(z), :] = (active_back * gate_here * share).astype(jnp.bfloat16)

        def second(z, piece):
            window = pl.ds(pl.multiple_of(piece * sums.width, sums.width), sums.width)
            parts[rows(z), window] = (
                jnp.dot(back_all[0, rows(z), :], gates[0, :, window], preferred_element_type=jnp.float32)
                + jnp.dot(back_all[1, rows(z), :], gates[1, :, window], preferred_element_type=jnp.float32)
            ).astype(jnp.bfloat16)

        work = Exchange(at, low, everyone, gather_sems, local.at[5], sums, first, second)
        prepare()
        work.whole(total, fill)
        stores = [
            pltpu.make_async_copy(source, target, outgoing.at[index])
            for index, (source, target) in enumerate(
                ((gate_terms, gate_out), (up_terms, up_out), (down_terms, down_out))
            )
        ]
        for copy in stores:
            copy.start()
        gain_terms[...] = jnp.zeros_like(gain_terms)

        def load_rows(window):
            return attended_ref[window, :], total[window, :], error_ref[window, :]

        def store_rows(window, value):
            grad_ref[window, :] = value
            mix_ref[window, :] = value.astype(jnp.bfloat16)

        norm_back(count, load_rows, store_rows, gain_ref[1:2, :], gain_terms)
        for copy in stores:
            copy.wait()
        gate_sum.first_wait()
        down_sum.first_wait()

    def terms_of(half):
        return jax.ShapeDtypeStruct((seq, 2) + half, jnp.bfloat16)

    def first_of(half):
        return [
            jax.ShapeDtypeStruct((ys,) + half, jnp.bfloat16),
            jax.ShapeDtypeStruct((ys, 2) + half, jnp.bfloat16),
        ]

    return remote_call(
        kernel,
        "feed_back",
        3,
        [
            jax.ShapeDtypeStruct((count, width), jnp.float32),
            jax.ShapeDtypeStruct((count, width), jnp.bfloat16),
            jax.ShapeDtypeStruct((8, width), jnp.float32),
            terms_of(half),
            terms_of(half),
            terms_of(half),
        ]
        + first_of(half)
        + first_of(half),
        [
            pltpu.VMEM((count, width), jnp.bfloat16),
            pltpu.VMEM((tokens, width), jnp.bfloat16),
            pltpu.VMEM(gate_up.shape, jnp.bfloat16),
            pltpu.VMEM((units, width), jnp.bfloat16),
            pltpu.VMEM((tokens, units), jnp.float32),
            pltpu.VMEM((tokens, units), jnp.float32),
            pltpu.VMEM((2, tokens, units), jnp.bfloat16),
            pltpu.VMEM((tokens, width), jnp.bfloat16),
            pltpu.VMEM((tokens, units), jnp.bfloat16),
            pltpu.VMEM((2, tokens, block), jnp.bfloat16),
            pltpu.VMEM((seq, 2) + half, jnp.bfloat16),
            pltpu.VMEM((seq, 2) + half, jnp.bfloat16),
            pltpu.VMEM((seq, 2) + half, jnp.bfloat16),
            pltpu.VMEM((count, width), jnp.float32),
        ]
        + LineGather.semaphores(wt, 2)
        + LinePieces.scratch(wt, (count, width), PIECES)
        + SquareTerms.semaphores(seq)
        + SquareTerms.semaphores(seq)
        + [pltpu.SemaphoreType.DMA((8,)), pltpu.SemaphoreType.DMA((3,))],
        error,
        attended,
        gain,
        gate_up,
        down,
        gate,
        up,
        active,
        normed,
        in_specs=[VMEM] * 3 + [ANY] * 6,
        out_specs=[VMEM] * 3 + [ANY] * 7,
    )


def mixer_back(
    mix_back,
    attended_grad,
    tokens,
    gain,
    out_rows,
    qkv_columns,
    hidden,
    sorted_columns,
    mixer,
    mixed_values,
    head_outputs,
    segments,
    taps,
    order,
    gain_terms,
    energy,
    gate_parts,
    up_parts,
    down_parts,
):
    seq, wt = lax.axis_size("seq"), lax.axis_size("wt")
    zs, ys = wt // 2, seq // 2
    count, width = mix_back.shape
    length = count * seq
    heads = mixed_values.shape[0]
    qkv_width = qkv_columns.shape[1]
    value_width = heads * DV
    rank = width // (seq * wt)
    gate_half, down_half = gate_parts[0].shape[2:], down_parts[0].shape[2:]
    rows_at_once = 256
    big = [out_rows, qkv_columns, hidden, sorted_columns, mixer, mixed_values, head_outputs]
    small = [mix_back, attended_grad, tokens, gain, segments, taps, order, gain_terms, energy]
    far = list(gate_parts) + list(down_parts) + list(up_parts)

    def kernel(*refs):
        big_refs, refs = refs[: len(big)], refs[len(big) :]
        small_refs, refs = refs[: len(small)], refs[len(small) :]
        (gate_t, gate_x, gate_y, down_t, down_x, down_y, up_t), refs = refs[: len(far)], refs[len(far) :]
        (grad_out, sums_out, qkv_out, w_out_out, up_x, up_y), refs = refs[:6], refs[6:]
        gate_lasts, up_lasts, down_lasts, refs = refs[:2], refs[2:4], refs[4:6], refs[6:]
        (w_out_v, w_qkv_v, hidden_v, sorted_v, mixer_v, values_v, outputs_v), refs = refs[:7], refs[7:]
        (mix_all, mixer_grad, query_acc, key_acc, value_acc, back_sorted, back_v), refs = refs[:7], refs[7:]
        (hidden_parts, qkv_parts, out_parts, hidden_total, gain_acc, spread, taps_acc), refs = refs[:7], refs[7:]
        (segment_column, tap_v), refs = refs[:2], refs[2:]
        (room_gate0, room_gate1, room_down0, room_down1, qkv_sum, first, middle, last), refs = refs[:8], refs[8:]
        hidden_scratch, refs = refs[:8], refs[8:]
        qkv_scratch, out_scratch, refs = refs[:4], refs[4:8], refs[8:]
        gate_scratch, down_scratch, up_scratch, refs = refs[:3], refs[3:6], refs[6:9], refs[9:]
        gather_sems, up_sems, refs = refs[:3], refs[3:5], refs[5:]
        local, swap, first_sems, last_sems = refs
        (
            mix_ref,
            grad_ref,
            token_ref,
            gain_ref,
            segment_ref,
            tap_ref,
            order_ref,
            gain_two,
            energy_ref,
        ) = small_refs
        at = Place(seq, wt)
        loads = [
            pltpu.make_async_copy(source, target, local.at[4 + index])
            for index, (source, target) in enumerate(
                zip(big_refs, (w_out_v, w_qkv_v, hidden_v, sorted_v, mixer_v, values_v, outputs_v))
            )
        ]
        for load in loads:
            load.start()
        at.meet(True, True)
        half = count // 2
        gather = SquareGather(
            at,
            lambda s, h: mix_all.at[pl.ds(pl.multiple_of(s * count + h * half, half), half)],
            lambda h: mix_ref.at[pl.ds(h * half, half)],
            gather_sems,
        )
        gather.start()
        own = pltpu.make_async_copy(
            mix_ref, mix_all.at[pl.ds(pl.multiple_of(at.s * count, count), count)], local.at[3]
        )
        own.start()

        def fetch(pairs):
            copies = [
                pltpu.make_async_copy(source, target, local.at[index])
                for index, (source, target) in enumerate(pairs)
            ]
            for copy in copies:
                copy.start()
            for copy in copies:
                copy.wait()

        gate_sum = SquareTerms(at, lambda s, h: gate_t.at[s, h], gate_x, gate_y, None, gate_lasts, gate_scratch)
        down_sum = SquareTerms(at, lambda s, h: down_t.at[s, h], down_x, down_y, None, down_lasts, down_scratch)
        up_sum = SquareTerms(at, lambda s, h: up_t.at[s, h], up_x, up_y, up_sems, up_lasts, up_scratch)
        gate_rooms, down_rooms = (room_gate0, room_gate1), (room_down0, room_down1)
        gate_sum.second_start(fetch, gate_rooms)
        gather.relay()
        down_sum.second_start(fetch, down_rooms)
        up_sum.second_load(fetch)
        tap_v[...] = tap_ref[...].astype(jnp.float32)
        segment_row = segment_ref[...].astype(jnp.float32)
        segment_column[...] = jnp.broadcast_to(segment_row, (128, length)).T
        own.wait()
        for load in loads:
            load.wait()
        query_acc[...] = jnp.zeros_like(query_acc)
        key_acc[...] = jnp.zeros_like(key_acc)
        value_acc[...] = jnp.zeros_like(value_acc)
        gather.finish()
        gate_sum.second_go()
        down_sum.second_go()
        up_sum.first_start()
        mixer_grad[...] = contract_last(mix_all[...], w_out_v[...]).astype(jnp.bfloat16)
        out_sum = LinePieces(at, lambda w: out_parts.at[w], out_scratch)
        out_rank = out_parts.shape[1]
        out_block = 512 if value_width % 512 == 0 else value_width

        def out_job(index, carry):
            window = pl.ds(pl.multiple_of(index * 512, 512), 512)
            term = contract_first(mixer_v[...], mix_all[:, window]).astype(jnp.bfloat16)
            for w in range(wt):
                out_parts[w, :, window] = term[w * out_rank : (w + 1) * out_rank]
            return carry

        lax.fori_loop(0, width // 512, out_job, 0)
        for piece in range(out_sum.pieces):
            out_sum.offer(piece)
        out_sum.launch_all(0)

        steps = length // rows_at_once
        lanes = lax.broadcasted_iota(jnp.int32, (1, 128), 1)

        def attend(index, carry):
            head, start = lax.div(index, steps), lax.rem(index, steps) * rows_at_once
            rows = pl.ds(pl.multiple_of(start, rows_at_once), rows_at_once)
            columns = pl.ds(pl.multiple_of(head * DV, DV), DV)
            mine = ((lanes >= head * FEAT) & (lanes < head * FEAT + FEAT)).astype(jnp.float32)
            queries = sorted_v[rows, value_width : value_width + 128] * mine.astype(jnp.bfloat16)
            keys = sorted_v[:, value_width + 128 :]
            scores = contract_last(queries, keys) * 0.25
            places = start + lax.broadcasted_iota(jnp.int32, scores.shape, 0)
            allowed = (segment_column[rows, :1] == segment_row) & (
                places >= lax.broadcasted_iota(jnp.int32, scores.shape, 1)
            )
            kernel_values = jnp.where(allowed, 1.0 + scores + 0.5 * scores * scores, 0.0)
            denominator = jnp.sum(kernel_values, axis=1, keepdims=True)
            incoming = mixer_grad[rows, columns].astype(jnp.float32)
            numerator_back = (incoming / denominator).astype(jnp.bfloat16)
            denominator_back = (
                -jnp.sum(incoming * outputs_v[head, rows, :], axis=1, keepdims=True) / denominator
            )
            weight_back = contract_last(numerator_back, values_v[head])
            kernel_back = jnp.where(allowed, weight_back + denominator_back, 0.0)
            dots_back = (0.25 * kernel_back * (1.0 + scores)).astype(jnp.bfloat16)
            query_acc[rows, :] += jnp.dot(dots_back, keys, preferred_element_type=jnp.float32) * mine
            key_acc[...] += contract_first(dots_back, queries)
            value_acc[:, columns] += contract_first(kernel_values.astype(jnp.bfloat16), numerator_back)
            return carry

        middle_step = heads * steps // 2
        lax.fori_loop(0, middle_step, attend, 0)
        for index in range(zs - 1, 1, -1):
            if index == zs // 2:
                lax.fori_loop(middle_step, heads * steps, attend, 0)
            out_sum.pass_on(index)
        taps_acc[...] = jnp.zeros_like(taps_acc)
        marks = tap_marks(segment_column)

        def convolve(head, carry):
            columns = pl.ds(pl.multiple_of(head * DV, DV), DV)
            mixed_back = value_acc[:, columns]
            raw = sorted_v[:, columns].astype(jnp.float32)
            raw_back = tap_v[0:1, columns] * mixed_back
            taps_acc[3:4, columns] = jnp.sum(mixed_back * raw, axis=0, keepdims=True)
            for tap in range(1, KCONV):
                masked = mixed_back * marks[tap]
                taps_acc[3 + tap : 4 + tap, columns] = jnp.sum(
                    masked * pltpu.roll(raw, tap, 0), axis=0, keepdims=True
                )
                raw_back = raw_back + tap_v[tap : tap + 1, columns] * pltpu.roll(masked, length - tap, 0)
            back_sorted[:, columns] = raw_back.astype(jnp.bfloat16)
            return carry

        lax.fori_loop(0, heads, convolve, 0)
        back_sorted[:, value_width : value_width + 128] = query_acc[...].astype(jnp.bfloat16)
        back_sorted[:, value_width + 128 :] = key_acc[...].astype(jnp.bfloat16)
        back_v[...] = contract_last(back_sorted[...], order_ref[...]).astype(jnp.bfloat16)
        qkv_sums = LinePieces(at, lambda w: qkv_parts.at[:, w], qkv_scratch)
        qkv_rank = qkv_parts.shape[2]

        def qkv_job(s, carry):
            block = wt * qkv_rank
            window = pl.ds(pl.multiple_of(s * block, block), block)
            term = contract_first(hidden_v[:, window], back_v[...]).astype(jnp.bfloat16)
            for w in range(wt):
                qkv_parts[s, w] = term[w * qkv_rank : (w + 1) * qkv_rank]
            qkv_sums.offer(s)

            @pl.when(s > 0)
            def _():
                qkv_sums.launch(s - 1, 0)

            return carry

        lax.fori_loop(0, seq, qkv_job, 0)
        qkv_sums.launch(seq - 1, 0)
        hidden_sum = SquareSum(at, lambda s, h: hidden_parts.at[s, h], hidden_scratch)

        def hidden_job(index, carry):
            window = pl.ds(pl.multiple_of(index * 512, 512), 512)
            term = contract_last(back_v[...], w_qkv_v[window, :]).astype(jnp.bfloat16)
            for s in range(seq):
                for h in range(2):
                    begin = s * count + h * half
                    hidden_parts[s, h, :, window] = term[begin : begin + half]
            return carry

        lax.fori_loop(0, width // 512, hidden_job, 0)
        hidden_sum.start()
        qkv_sums.launch_all(1)
        qkv_sums.pass_on(zs - 1)
        hidden_sum.relay()
        up_sum.first_wait()
        up_sum.second_arrived()
        up_sum.second_go()
        for index in range(zs - 2, 1, -1):
            qkv_sums.pass_on(index)
        hidden_sum.finish(lambda h: hidden_total.at[h])
        gain_acc[...] = jnp.zeros_like(gain_acc)
        for h in range(2):

            def shift(window):
                return pl.ds(pl.multiple_of(h * half + window.start, 16), 16)

            def load_rows(window):
                rows = shift(window)
                return token_ref[rows, :].astype(jnp.float32), hidden_total[h, window, :], grad_ref[rows, :]

            def store_rows(window, value):
                grad_out[shift(window), :] = value

            norm_back(half, load_rows, store_rows, gain_ref[0:1, :], gain_acc)
        spread[...] = jnp.zeros_like(spread)
        spread[0:1, :] = jnp.sum(gain_acc[...], axis=0, keepdims=True)
        spread[1:2, :] = jnp.sum(gain_two[...], axis=0, keepdims=True)
        energy = jnp.sum(jnp.sum(energy_ref[...], axis=0, keepdims=True), axis=1, keepdims=True)
        spread[2:3, :] = jnp.broadcast_to(energy, (1, width))
        copies = []
        for step in range(1, seq):
            to = lax.rem(at.s + step, seq)
            window = pl.ds(pl.multiple_of(to * value_width, value_width), value_width)
            copies.append(
                send(spread.at[:, window], first.at[at.s], first_sems.at[step, 0], first_sems.at[at.s, 1], (to, at.w))
            )
        for copy in copies:
            copy.start()

        def give(s):
            return send(qkv_sum.at[s], qkv_out.at[at.s], swap.at[s, 0], swap.at[at.s, 1], (s, at.w))

        def done(s):
            @pl.when(s != at.s)
            def _():
                give(s).start()

        qkv_sums.finish(qkv_sum, done)
        add_into(qkv_out.at[at.s], [qkv_sum.at[at.s]])
        out_sum.finish(w_out_out)
        terms = [spread.at[:, pl.ds(pl.multiple_of(at.s * value_width, value_width), value_width)], taps_acc]
        for step in range(1, seq):
            s = lax.rem(at.s + step, seq)
            slot = first.at[s]
            send(slot, slot, first_sems.at[step, 0], first_sems.at[s, 1], at.across()).wait_recv()
            terms.append(slot)
        add_into(middle, terms)
        for step in range(1, wt):
            to = lax.rem(at.w + step, wt)
            copy = send(middle, last.at[at.w], last_sems.at[step, 0], last_sems.at[at.w, 1], (at.s, to))
            copy.start()
            copies.append(copy)
        gate_sum.second_wait()
        down_sum.second_wait()
        terms = [middle]
        for step in range(1, wt):
            w = lax.rem(at.w + step, wt)
            slot = last.at[w]
            send(slot, slot, last_sems.at[step, 0], last_sems.at[w, 1], at.partner()).wait_recv()
            terms.append(slot)
        add_into(sums_out, terms)
        for step in range(1, seq):
            s = lax.rem(at.s + step, seq)
            slot = qkv_out.at[s]
            send(slot, slot, swap.at[s, 0], swap.at[s, 1], at.across()).wait_recv()
            give(s).wait_send()
        up_sum.second_wait()
        for copy in copies:
            copy.wait_send()

    out_rank, qkv_rank = value_width // wt, width // (seq * wt)
    f32, low = jnp.float32, jnp.bfloat16
    tile = (8, value_width)
    results = remote_call(
        kernel,
        "mixer_back",
        4,
        [
            jax.ShapeDtypeStruct((count, width), f32),
            jax.ShapeDtypeStruct(tile, f32),
            jax.ShapeDtypeStruct((seq, qkv_rank, qkv_width), low),
            jax.ShapeDtypeStruct((out_rank, width), f32),
            jax.ShapeDtypeStruct((ys,) + gate_half, low),
            jax.ShapeDtypeStruct((ys, 2) + gate_half, low),
        ]
        + [
            jax.ShapeDtypeStruct(shape, low)
            for shape_half in (gate_half, gate_half, down_half)
            for shape in ((ys,) + shape_half, shape_half)
        ],
        [pltpu.VMEM(array.shape, array.dtype) for array in big]
        + [
            pltpu.VMEM((length, width), low),
            pltpu.VMEM((length, value_width), low),
            pltpu.VMEM((length, 128), f32),
            pltpu.VMEM((length, 128), f32),
            pltpu.VMEM((length, value_width), f32),
            pltpu.VMEM((length, value_width + 256), low),
            pltpu.VMEM((length, qkv_width), low),
            pltpu.VMEM((seq, 2, count // 2, width), low),
            pltpu.VMEM((seq, wt, qkv_rank, qkv_width), low),
            pltpu.VMEM((wt, out_rank, width), low),
            pltpu.VMEM((2, count // 2, width), f32),
            pltpu.VMEM((8, width), f32),
            pltpu.VMEM((8, width), f32),
            pltpu.VMEM(tile, f32),
            pltpu.VMEM((length, 128), f32),
            pltpu.VMEM((KCONV, value_width), f32),
            pltpu.VMEM(gate_half, low),
            pltpu.VMEM(gate_half, low),
            pltpu.VMEM(down_half, low),
            pltpu.VMEM(down_half, low),
            pltpu.VMEM((seq, qkv_rank, qkv_width), low),
            pltpu.VMEM((seq,) + tile, f32),
            pltpu.VMEM(tile, f32),
            pltpu.VMEM((wt,) + tile, f32),
        ]
        + SquareSum.scratch(seq, (count // 2, width))
        + LinePieces.scratch(wt, (seq, qkv_rank, qkv_width), seq)
        + LinePieces.scratch(wt, (out_rank, width), 1)
        + SquareTerms.scratch(seq, gate_half)
        + SquareTerms.scratch(seq, down_half)
        + SquareTerms.scratch(seq, gate_half)
        + SquareGather.semaphores(seq)
        + SquareTerms.semaphores(seq)
        + [
            pltpu.SemaphoreType.DMA((11,)),
            pltpu.SemaphoreType.DMA((seq, 2)),
            pltpu.SemaphoreType.DMA((seq, 2)),
            pltpu.SemaphoreType.DMA((wt, 2)),
        ],
        *big,
        *small,
        *far,
        in_specs=[ANY] * len(big) + [VMEM] * len(small) + [ANY] * len(far),
        out_specs=[VMEM] * 6 + [ANY] * 6,
    )
    grad, totals, qkv_total, out_total, up_x, up_y = results[:6]
    gate = tuple(gate_parts) + tuple(results[6:8])
    up = tuple(up_parts) + (up_x, up_y) + tuple(results[8:10])
    down = tuple(down_parts) + tuple(results[10:12])
    return grad, totals, gate, up, down, qkv_total, out_total


def last_sums(gate, up, down, qkv_total, totals, lengths, out_total, grad, final, qkv_shape):
    seq, wt = lax.axis_size("seq"), lax.axis_size("wt")
    ys = seq // 2
    f32, low = jnp.float32, jnp.bfloat16
    gate_half, down_half = gate[0].shape[2:], down[0].shape[2:]
    total_width = totals.shape[1]
    lanes_each = total_width // wt
    width = grad.shape[1]
    qkv_width = qkv_total.shape[2]
    operands = list(gate) + list(up) + list(down)
    passed = [out_total, grad, final]

    def kernel(*refs):
        groups, refs = [refs[5 * index : 5 * index + 5] for index in range(3)], refs[15:]
        (qkv_ref, totals_ref, length_ref), passed_refs, refs = refs[:3], refs[3:6], refs[6:]
        (gate_up_out, down_out, qkv_out, first_gain, second_gain, taps_out, loss_out), refs = refs[:7], refs[7:]
        passed_outs, refs = refs[:3], refs[3:]
        totals, refs = refs[:2], refs[2:]
        passed_rooms, refs = refs[:3], refs[3:]
        rooms, (loads, stores, pass_sems) = [refs[5 * index : 5 * index + 5] for index in range(3)], refs[15:]
        s = lax.axis_index("seq")
        y, x = lax.div(s, 2), lax.rem(s, 2)
        copies = []
        for number, (group, room) in enumerate(zip(groups, rooms)):
            terms, from_x, from_y, last_y, last_x = group
            pairs = [(terms.at[s], room[0]), (from_x.at[y], room[1]), (last_x, room[4])]
            for other in range(1, ys):
                place = lax.rem(y + other, ys)
                pairs.append((from_y.at[place, x], room[2].at[other - 1]))
                pairs.append((last_y.at[place], room[3].at[other - 1]))
            mine = [
                pltpu.make_async_copy(source, target, loads.at[number, index])
                for index, (source, target) in enumerate(pairs)
            ]
            for copy in mine:
                copy.start()
            copies.append(mine)
        ins = [
            pltpu.make_async_copy(source, room, pass_sems.at[index, 0])
            for index, (source, room) in enumerate(zip(passed_refs, passed_rooms))
        ]
        for copy in ins:
            copy.start()
        shift = lax.rem(total_width - lax.axis_index("wt") * lanes_each, total_width)
        mine = pltpu.roll(totals_ref[...], shift, 1)[:, :lanes_each]
        first_gain[...] = mine[0:1]
        second_gain[...] = mine[1:2]
        taps_out[...] = mine[3 : 3 + KCONV]
        counted = length_ref[0]
        for index in range(1, length_ref.shape[0]):
            counted = counted + length_ref[index]
        loss_out[...] = 2.0 * totals_ref[2:3, :1] / (jnp.full((1, 1), counted, jnp.int32).astype(f32) * width)
        for index in range(seq):
            qkv_out[:, index * qkv_width : (index + 1) * qkv_width] = qkv_ref[index].astype(f32)
        outs = []
        for index, (room, target) in enumerate(zip(passed_rooms, passed_outs)):
            ins[index].wait()
            copy = pltpu.make_async_copy(room, target, pass_sems.at[index, 1])
            copy.start()
            outs.append(copy)
        for number, room in enumerate(rooms):
            own, near_x, near_y, last_y, last_x = room
            total = totals[number // 2]
            base = 2 * (number % 2)
            for copy in copies[number]:
                copy.wait()
            rows = own.shape[1]
            tile = next(t for t in (64, 32, 16) if rows % t == 0)

            def step(index, carry):
                window = pl.ds(pl.multiple_of(index * tile, tile), tile)
                first = own[0, window, :].astype(f32) + near_x[window, :].astype(f32)
                second = own[1, window, :].astype(f32) + last_x[window, :].astype(f32)
                for other in range(ys - 1):
                    first = first + last_y[other, window, :].astype(f32)
                    second = second + near_y[other, window, :].astype(f32)
                total[base, window, :] = first
                total[base + 1, window, :] = second
                return carry

            lax.fori_loop(0, rows // tile, step, 0)
            target = gate_up_out.at[pl.ds(base, 2)] if number < 2 else down_out
            copy = pltpu.make_async_copy(total.at[pl.ds(base, 2)], target, stores.at[number])
            copy.start()
            outs.append(copy)
        for copy in outs:
            copy.wait()

    def rooms(half):
        return [
            pltpu.VMEM((2,) + half, low),
            pltpu.VMEM(half, low),
            pltpu.VMEM((ys - 1,) + half, low),
            pltpu.VMEM((ys - 1,) + half, low),
            pltpu.VMEM(half, low),
        ]

    return pl.pallas_call(
        kernel,
        name="last_sums",
        out_shape=[
            jax.ShapeDtypeStruct((4,) + gate_half, f32),
            jax.ShapeDtypeStruct((2,) + down_half, f32),
            jax.ShapeDtypeStruct(qkv_shape, f32),
            jax.ShapeDtypeStruct((1, lanes_each), f32),
            jax.ShapeDtypeStruct((1, lanes_each), f32),
            jax.ShapeDtypeStruct((KCONV, lanes_each), f32),
            jax.ShapeDtypeStruct((1, 1), f32),
        ]
        + [jax.ShapeDtypeStruct(array.shape, array.dtype) for array in passed],
        in_specs=[ANY] * 15 + [VMEM] * 2 + [SMEM] + [ANY] * 3,
        out_specs=[ANY] * 2 + [VMEM] * 5 + [ANY] * 3,
        scratch_shapes=[pltpu.VMEM((4,) + gate_half, f32), pltpu.VMEM((2,) + down_half, f32)]
        + [pltpu.VMEM(array.shape, array.dtype) for array in passed]
        + rooms(gate_half) * 2
        + rooms(down_half)
        + [
            pltpu.SemaphoreType.DMA((3, 1 + seq)),
            pltpu.SemaphoreType.DMA((3,)),
            pltpu.SemaphoreType.DMA((3, 2)),
        ],
        compiler_params=pltpu.CompilerParams(vmem_limit_bytes=VMEM_LIMIT),
    )(*operands, qkv_total, totals, lengths, *passed)


def rows_of_tile(values, row):
    return jnp.pad(values[None, :], [(row, 7 - row), (0, 128 - values.shape[0])])


def body(
    inputs,
    segment_ids,
    valid_lengths,
    teacher,
    w_qkv,
    conv_weight,
    w_out,
    norm_gain,
    w_gate_up,
    w_down,
    mlp_gain,
):
    seq_parts = lax.axis_size("seq")
    tok_count = inputs.shape[1]
    model_width = inputs.shape[2]
    length = tok_count * seq_parts
    head_count = H // seq_parts
    qkv_width = head_count * (2 * FEAT + DV)
    rows_low = inputs[0]
    gain_lanes = norm_gain.shape[0]
    gains = rows_of_tile(norm_gain.astype(jnp.float32), 0) + rows_of_tile(mlp_gain.astype(jnp.float32), 1)
    qkv_rows = w_qkv
    if qkv_width % 128:
        qkv_rows = w_qkv.reshape(w_qkv.shape[0], seq_parts, qkv_width).transpose(1, 0, 2)
    gate_up_low = w_gate_up.swapaxes(1, 2)
    segments = segment_ids
    (
        attended,
        _,
        gain_rows,
        qkv_columns,
        out_rows,
        hidden_low,
        sorted_columns,
        mixer_low,
        mixed_values,
        head_outputs,
        order,
        final_low,
        residual_error,
        energy,
        normed_all,
        gate_all,
        up_all,
        active_all,
        down_part,
        gate_up_part,
    ) = forward_pass(
        rows_low,
        qkv_rows,
        w_out,
        gains,
        segments,
        conv_weight,
        teacher[0],
        w_down,
        valid_lengths,
        gate_up_low,
    )
    (
        attended_grad,
        mix_back,
        gain_two_terms,
        gate_terms,
        up_terms,
        down_terms,
        gate_from_x,
        gate_from_y,
        down_from_x,
        down_from_y,
    ) = feed_back(
        residual_error,
        attended,
        gain_rows,
        gate_up_part,
        down_part,
        gate_all,
        up_all,
        active_all,
        normed_all,
    )
    inputs_grad, totals, gate, up, down, qkv_total, out_total = mixer_back(
        mix_back,
        attended_grad,
        rows_low,
        gain_rows,
        out_rows.reshape(head_count * DV, model_width),
        qkv_columns.reshape(model_width, qkv_width),
        hidden_low,
        sorted_columns,
        mixer_low,
        mixed_values,
        head_outputs,
        segments,
        conv_weight,
        order,
        gain_two_terms,
        energy,
        (gate_terms, gate_from_x, gate_from_y),
        (up_terms,),
        (down_terms, down_from_x, down_from_y),
    )
    (
        grad_w_gate_up,
        grad_w_down,
        grad_w_qkv,
        grad_norm_gain,
        grad_mlp_gain,
        grad_conv,
        mean_loss,
        grad_w_out,
        inputs_grad,
        outputs,
    ) = last_sums(
        gate, up, down, qkv_total, totals, valid_lengths, out_total, inputs_grad, final_low, w_qkv.shape
    )
    return (
        outputs[None],
        inputs_grad[None],
        mean_loss.reshape(()),
        grad_w_qkv,
        grad_conv,
        grad_w_out,
        grad_norm_gain.reshape(norm_gain.shape),
        grad_w_gate_up.reshape(gate_up_low.shape).swapaxes(1, 2),
        grad_w_down.reshape(w_down.shape),
        grad_mlp_gain.reshape(mlp_gain.shape),
    )


def solution(mesh):
    in_specs = (
        P("wt", "seq", None),
        P("wt", None),
        P(),
        P("wt", "seq", None),
        P(("seq", "wt"), None),
        P(None, "seq"),
        P(("seq", "wt"), None),
        P(("seq", "wt")),
        P(None, "seq", "wt"),
        P("wt", "seq"),
        P(("seq", "wt")),
    )
    out_specs = (
        P("wt", "seq", None),
        P("wt", "seq", None),
        P(),
        P(("seq", "wt"), None),
        P(None, ("seq", "wt")),
        P(("seq", "wt"), None),
        P(("seq", "wt")),
        P(None, "seq", "wt"),
        P("wt", "seq"),
        P(("seq", "wt")),
    )
    return jax.shard_map(body, mesh=mesh, in_specs=in_specs, out_specs=out_specs, check_vma=False)
```

```python
from functools import partial

import jax
import jax.numpy as jnp
from jax import lax
from jax.experimental import pallas as pl
from jax.experimental.pallas import tpu as pltpu
from jax.sharding import PartitionSpec as P

H = 16
FEAT = 16
KCONV = 3
DV = 128


epsilon = 1e-05


def rms_norm(values, gain_vector):
    inverse_root = lax.rsqrt(jnp.mean(values * values, axis=-1, keepdims=True) + epsilon)
    return values * inverse_root * gain_vector


def contract_last(former, latter):
    return lax.dot_general(
        former, latter, (((1,), (1,)), ((), ())), preferred_element_type=jnp.float32
    )


def contract_first(former, latter):
    return lax.dot_general(
        former, latter, (((0,), (0,)), ((), ())), preferred_element_type=jnp.float32
    )


def gated_unit(gate_in, up_in):
    return jax.nn.silu(gate_in) * up_in


MESH = pl.DeviceIdType.MESH
VMEM = pl.BlockSpec(memory_space=pltpu.VMEM)
ANY = pl.BlockSpec(memory_space=pl.ANY)
SMEM = pl.BlockSpec(memory_space=pltpu.SMEM)
VMEM_LIMIT = 67043328


class Place:
    def __init__(self, seq, wt):
        self.seq, self.wt = seq, wt
        self.ys, self.zs = seq // 2, wt // 2
        self.s, self.w = lax.axis_index("seq"), lax.axis_index("wt")
        self.y, self.x = lax.div(self.s, 2), lax.rem(self.s, 2)
        self.z, self.c = lax.div(self.w, 2), lax.rem(self.w, 2)

    def across(self):
        return (self.y * 2 + 1 - self.x, self.w)

    def beside(self, step):
        return lax.rem(self.y + step, self.ys)

    def column(self, y):
        return (y * 2 + self.x, self.w)

    def partner(self):
        return (self.s, self.z * 2 + 1 - self.c)

    def level(self, z):
        return (self.s, z * 2 + self.c)

    def meet(self, square, line):
        barrier = pltpu.get_barrier_semaphore()
        count = 0
        if square:
            for step in range(1, self.seq):
                device = (lax.rem(self.s + step, self.seq), self.w)
                pl.semaphore_signal(barrier, inc=1, device_id=device, device_id_type=MESH)
                count += 1
        if line:
            for step in range(1, self.wt):
                device = (self.s, lax.rem(self.w + step, self.wt))
                pl.semaphore_signal(barrier, inc=1, device_id=device, device_id_type=MESH)
                count += 1
        pl.semaphore_wait(barrier, count)


def send(source, target, leaving, arriving, device):
    return pltpu.make_async_remote_copy(
        src_ref=source,
        dst_ref=target,
        send_sem=leaving,
        recv_sem=arriving,
        device_id=device,
        device_id_type=MESH,
    )


def add_into(target, sources):
    if len(target.shape) == 3:
        for index in range(target.shape[0]):
            add_into(target.at[index], [source.at[index] for source in sources])
        return
    rows = target.shape[0]
    tile = next(t for t in (64, 32, 16, 8, rows) if rows % t == 0)

    def step(index, carry):
        window = pl.ds(pl.multiple_of(index * tile, tile), tile)
        total = sources[0][window, :].astype(jnp.float32)
        for source in sources[1:]:
            total = total + source[window, :].astype(jnp.float32)
        target[window, :] = total.astype(target.dtype)
        return carry

    lax.fori_loop(0, rows // tile, step, 0)


class SquareGather:
    @staticmethod
    def semaphores(seq):
        return [
            pltpu.SemaphoreType.DMA((2 + seq // 2,)),
            pltpu.SemaphoreType.DMA((seq // 2, 3)),
            pltpu.SemaphoreType.DMA((seq, 2)),
        ]

    def __init__(self, at, view, own, sems):
        self.at, self.view, self.own = at, view, own
        self.over_x, self.over_y, self.got = sems
        self.sent = []

    def go(self, copy):
        copy().start()
        self.sent.append(copy)

    def own_x(self, half):
        at = self.at
        target = self.view(at.s, half)
        return send(self.own(half), target, self.over_x.at[half], self.got.at[at.s, half], at.across())

    def own_y(self, step, half):
        at = self.at
        target, device = self.view(at.s, half), at.column(at.beside(step))
        return send(self.own(half), target, self.over_y.at[step, half], self.got.at[at.s, half], device)

    def pass_y(self, step):
        at = self.at
        s = at.y * 2 + 1 - at.x
        slot, device = self.view(s, 0), at.column(at.beside(step))
        return send(slot, slot, self.over_y.at[step, 2], self.got.at[s, 0], device)

    def pass_x(self, step):
        s = self.at.beside(step) * 2 + self.at.x
        slot = self.view(s, 1)
        return send(slot, slot, self.over_x.at[1 + step], self.got.at[s, 1], self.at.across())

    def wait(self, s, half):
        slot = self.view(s, half)
        send(slot, slot, self.over_x.at[0], self.got.at[s, half], self.at.across()).wait_recv()

    def start(self):
        for half in range(2):
            self.go(partial(self.own_x, half))
            for step in range(1, self.at.ys):
                self.go(partial(self.own_y, step, 1 - half))

    def relay(self):
        at = self.at
        self.wait(at.y * 2 + 1 - at.x, 0)
        for step in range(1, at.ys):
            self.go(partial(self.pass_y, step))
        for step in range(1, at.ys):
            self.wait(at.beside(step) * 2 + at.x, 1)
            self.go(partial(self.pass_x, step))

    def direct(self):
        at = self.at
        self.wait(at.y * 2 + 1 - at.x, 1)
        for step in range(1, at.ys):
            self.wait(at.beside(step) * 2 + at.x, 0)

    def relayed(self):
        at = self.at
        for step in range(1, at.ys):
            y = at.beside(step)
            self.wait(y * 2 + 1 - at.x, 0)
            self.wait(y * 2 + 1 - at.x, 1)
        for copy in self.sent:
            copy().wait_send()

    def finish(self):
        self.direct()
        self.relayed()


class SquareSum:
    @staticmethod
    def scratch(seq, half_shape):
        ys = seq // 2
        return [
            pltpu.VMEM((ys,) + half_shape, jnp.bfloat16),
            pltpu.VMEM((ys, 2) + half_shape, jnp.bfloat16),
            pltpu.VMEM((ys,) + half_shape, jnp.bfloat16),
            pltpu.VMEM(half_shape, jnp.bfloat16),
            pltpu.VMEM((ys,) + half_shape, jnp.bfloat16),
            pltpu.VMEM(half_shape, jnp.bfloat16),
            pltpu.SemaphoreType.DMA((ys, 2, 2)),
            pltpu.SemaphoreType.DMA((ys, 3, 2)),
        ]

    def __init__(self, at, part, scratch):
        self.at, self.part = at, part
        self.from_x, self.from_y, self.last_y, self.last_x, self.sum_y, self.sum_x, self.xs, self.yss = scratch
        self.sent = []

    def go(self, source, target, leaving, arriving, device):
        copy = send(source, target, leaving, arriving, device)
        copy.start()
        self.sent.append(copy)

    def wait(self, slot, leaving, arriving):
        send(slot, slot, leaving, arriving, self.at.across()).wait_recv()

    def start(self):
        at = self.at
        for y in range(at.ys):
            self.go(
                self.part(y * 2 + 1 - at.x, 0),
                self.from_x.at[y],
                self.xs.at[y, 0, 0],
                self.xs.at[y, 0, 1],
                at.across(),
            )
        for step in range(1, at.ys):
            y = at.beside(step)
            for x in range(2):
                self.go(
                    self.part(y * 2 + x, 1),
                    self.from_y.at[at.y, x],
                    self.yss.at[step, x, 0],
                    self.yss.at[at.y, x, 1],
                    at.column(y),
                )

    def relay(self):
        at = self.at
        for step in range(1, at.ys):
            y = at.beside(step)
            self.wait(self.from_x.at[y], self.xs.at[y, 0, 0], self.xs.at[y, 0, 1])
            add_into(self.sum_y.at[y], [self.part(y * 2 + at.x, 0), self.from_x.at[y]])
            self.go(
                self.sum_y.at[y],
                self.last_y.at[at.y],
                self.yss.at[step, 2, 0],
                self.yss.at[at.y, 2, 1],
                at.column(y),
            )
        terms = []
        for step in range(1, at.ys):
            y = at.beside(step)
            for x in range(2):
                self.wait(self.from_y.at[y, x], self.yss.at[step, x, 0], self.yss.at[y, x, 1])
            terms.append(self.from_y.at[y, 1 - at.x])
        add_into(self.sum_x, [self.part(at.y * 2 + 1 - at.x, 1)] + terms)
        self.go(self.sum_x, self.last_x, self.xs.at[0, 1, 0], self.xs.at[0, 1, 1], at.across())

    def finish(self, total):
        at = self.at
        self.wait(self.from_x.at[at.y], self.xs.at[0, 0, 0], self.xs.at[at.y, 0, 1])
        terms = [self.part(at.s, 0), self.from_x.at[at.y]]
        for step in range(1, at.ys):
            y = at.beside(step)
            self.wait(self.last_y.at[y], self.yss.at[step, 2, 0], self.yss.at[y, 2, 1])
            terms.append(self.last_y.at[y])
        add_into(total(0), terms)
        self.wait(self.last_x, self.xs.at[0, 1, 0], self.xs.at[0, 1, 1])
        terms = [self.part(at.s, 1), self.last_x]
        for step in range(1, at.ys):
            terms.append(self.from_y.at[at.beside(step), at.x])
        add_into(total(1), terms)
        for copy in self.sent:
            copy.wait_send()


class LineGather:
    @staticmethod
    def semaphores(wt, cuts=1):
        return [pltpu.SemaphoreType.DMA((5, wt // 2, cuts))]

    def __init__(self, at, view, sems):
        self.at, self.view, self.sems = at, view, sems[0]
        self.cuts = self.sems.shape[2]

    def cut(self, ref, part):
        if self.cuts == 1:
            return ref
        rows = ref.shape[0] // self.cuts
        return ref.at[pl.ds(part * rows, rows)]

    def hop(self, z, part, kind, device, source):
        slot = self.view(z * 2 + self.at.c)
        source = slot if source is None else source
        arriving = 4 if kind == 2 else 3
        return send(
            self.cut(source, part),
            self.cut(slot, part),
            self.sems.at[kind, z, part],
            self.sems.at[arriving, z, part],
            device,
        )

    def up(self, z, part, source=None):
        return self.hop(z, part, 0, self.at.level(self.at.z + 1), source)

    def down(self, z, part, source=None):
        return self.hop(z, part, 1, self.at.level(self.at.z - 1), source)

    def over(self, z, part, source=None):
        return self.hop(z, part, 2, self.at.partner(), source)

    def start(self, source=None):
        at = self.at
        for part in range(self.cuts):

            @pl.when(at.z + 1 < at.zs)
            def _():
                self.up(at.z, part, source).start()

            @pl.when(at.z > 0)
            def _():
                self.down(at.z, part, source).start()

            self.over(at.z, part, source).start()

    def step(self, index):
        at = self.at
        below, above = at.z - 1 - index, at.z + 1 + index
        for part in range(self.cuts):

            @pl.when(below >= 0)
            def _():
                self.up(below, part).wait_recv()

                @pl.when(at.z + 1 < at.zs)
                def _():
                    self.up(below, part).start()

                self.over(below, part).start()

            @pl.when(above < at.zs)
            def _():
                self.down(above, part).wait_recv()

                @pl.when(at.z > 0)
                def _():
                    self.down(above, part).start()

                self.over(above, part).start()

    def wait_over(self, z):
        for part in range(self.cuts):
            slot = self.cut(self.view(z * 2 + 1 - self.at.c), part)
            send(slot, slot, self.sems.at[2, z, part], self.sems.at[4, z, part], self.at.partner()).wait_recv()

    def finish(self):
        for z in range(self.at.zs):
            self.wait_over(z)
        self.sent()

    def sent(self):
        at = self.at
        for z in range(at.zs):
            for part in range(self.cuts):

                @pl.when((at.z >= z) & (at.z + 1 < at.zs))
                def _():
                    self.up(z, part).wait_send()

                @pl.when((at.z <= z) & (at.z > 0))
                def _():
                    self.down(z, part).wait_send()

                self.over(z, part).wait_send()


def remote_call(kernel, name, number, outs, scratch, *operands, in_specs=None, out_specs=None):
    return pl.pallas_call(
        kernel,
        name=name,
        out_shape=outs,
        in_specs=[VMEM] * len(operands) if in_specs is None else in_specs,
        out_specs=jax.tree.map(lambda _: VMEM, outs) if out_specs is None else out_specs,
        scratch_shapes=scratch,
        compiler_params=pltpu.CompilerParams(
            collective_id=number, has_side_effects=True, vmem_limit_bytes=VMEM_LIMIT
        ),
    )(*operands)


def write_order(ref, heads):
    head_width, value_width = 2 * FEAT + DV, heads * DV

    def step(index, carry):
        window = pl.ds(pl.multiple_of(index * 32, 32), 32)
        shape = (32, ref.shape[1])
        column = index * 32 + lax.broadcasted_iota(jnp.int32, shape, 0)
        head = lax.div(column, head_width)
        place = lax.rem(column, head_width)
        target = jnp.where(
            place < FEAT,
            value_width + head * FEAT + place,
            jnp.where(
                place < 2 * FEAT, value_width + 128 + head * FEAT + place - FEAT, head * DV + place - 2 * FEAT
            ),
        )
        hit = target == lax.broadcasted_iota(jnp.int32, shape, 1)
        ref[window, :] = hit.astype(jnp.float32).astype(jnp.bfloat16)
        return carry

    lax.fori_loop(0, ref.shape[0] // 32, step, 0)


def tap_marks(segment_column):
    segment = segment_column[:, :1]
    place = lax.broadcasted_iota(jnp.int32, segment_column.shape, 0)[:, :1]
    marks = [None]
    for tap in range(1, KCONV):
        same = (pltpu.roll(segment_column[...], tap, 0)[:, :1] == segment) & (place >= tap)
        marks.append(same.astype(jnp.float32))
    return marks


def early_rows(units):
    return units * 3 // 4 // 16 * 16


class LinePieces:
    @staticmethod
    def scratch(wt, shape, pieces):
        zs = wt // 2
        return [pltpu.VMEM((zs,) + shape, jnp.bfloat16)] * 3 + [pltpu.SemaphoreType.DMA((6, zs, pieces))]

    def __init__(self, at, part, scratch, order=None):
        self.at, self.part, self.order = at, part, order
        self.pair, self.below, self.above, self.sems = scratch
        self.pieces = self.sems.shape[2]
        self.width = self.pair.shape[-1] // self.pieces

    def cut(self, ref, piece):
        if len(ref.shape) == 3:
            return ref.at[piece]
        return ref.at[:, self.columns(piece)]

    def columns(self, piece):
        block = piece if self.order is None else self.order(piece)
        return pl.ds(pl.multiple_of(block * self.width, self.width), self.width)

    def own(self, z, piece):
        return self.cut(self.part(z * 2 + self.at.c), piece)

    def over(self, z, piece):
        return send(
            self.cut(self.part(z * 2 + 1 - self.at.c), piece),
            self.cut(self.pair.at[z], piece),
            self.sems.at[0, z, piece],
            self.sems.at[1, z, piece],
            self.at.partner(),
        )

    def up(self, z, piece):
        return send(
            self.own(z, piece),
            self.cut(self.below.at[z], piece),
            self.sems.at[2, z, piece],
            self.sems.at[3, z, piece],
            self.at.level(self.at.z + 1),
        )

    def down(self, z, piece):
        return send(
            self.own(z, piece),
            self.cut(self.above.at[z], piece),
            self.sems.at[4, z, piece],
            self.sems.at[5, z, piece],
            self.at.level(self.at.z - 1),
        )

    def terms(self, z, piece):
        self.over(z, piece).wait_recv()
        return [self.own(z, piece), self.cut(self.pair.at[z], piece)]

    def ends(self, z, piece):
        at = self.at

        @pl.when((at.z == 0) & (z > 0))
        def _():
            add_into(self.own(z, piece), self.terms(z, piece))
            self.up(z, piece).start()

        @pl.when((at.z == at.zs - 1) & (z < at.zs - 1))
        def _():
            add_into(self.own(z, piece), self.terms(z, piece))
            self.down(z, piece).start()

    def offer(self, piece):
        zs = self.at.zs
        for index in range(zs // 2):
            self.over(index, piece).start()
            self.over(zs - 1 - index, piece).start()

    def launch(self, piece, near):
        self.ends(jnp.where(self.at.z == 0, self.at.zs - 1 - near, near), piece)

    def launch_all(self, near):
        zs = self.at.zs

        def step(index, carry):
            self.launch(lax.rem(index, self.pieces), near + lax.div(index, self.pieces))
            return carry

        lax.fori_loop(0, (zs - 1 - near) * self.pieces, step, 0)

    def pass_on(self, index, fill=None, begin=0, end=None):
        at = self.at
        upper = at.z * 2 >= at.zs
        high, low = index, at.zs - 1 - index

        def lower(piece, when):
            @pl.when((at.z > low) & (at.z < at.zs - 1) & when)
            def _():
                terms = self.terms(low, piece)
                self.down(low, piece).wait_recv()
                add_into(self.own(low, piece), terms + [self.cut(self.above.at[low], piece)])
                self.down(low, piece).start()

        def step(piece, carry):
            lower(piece, upper)

            @pl.when((at.z < high) & (at.z > 0))
            def _():
                terms = self.terms(high, piece)
                self.up(high, piece).wait_recv()
                add_into(self.own(high, piece), terms + [self.cut(self.below.at[high], piece)])
                self.up(high, piece).start()

            lower(piece, jnp.logical_not(upper))
            if fill is not None:
                fill(piece, self.pieces)
            return carry

        end = self.pieces if end is None else end
        if end - begin == 1:
            step(begin, 0)
        else:
            lax.fori_loop(begin, end, step, 0)

    def finish(self, total, done=None):
        at = self.at

        def step(piece, carry):
            terms = self.terms(at.z, piece)
            below, above = self.cut(self.below.at[at.z], piece), self.cut(self.above.at[at.z], piece)

            @pl.when(at.z == 0)
            def _():
                self.down(at.z, piece).wait_recv()
                add_into(self.cut(total, piece), terms + [above])

            @pl.when(at.z == at.zs - 1)
            def _():
                self.up(at.z, piece).wait_recv()
                add_into(self.cut(total, piece), terms + [below])

            @pl.when((at.z > 0) & (at.z < at.zs - 1))
            def _():
                self.up(at.z, piece).wait_recv()
                self.down(at.z, piece).wait_recv()
                add_into(self.cut(total, piece), terms + [below, above])

            if done is not None:
                done(piece)
            for z in range(at.zs):

                @pl.when(at.z < z)
                def _():
                    self.up(z, piece).wait_send()

                @pl.when(at.z > z)
                def _():
                    self.down(z, piece).wait_send()

                self.over(z, piece).wait_send()
            return carry

        lax.fori_loop(0, self.pieces, step, 0)


class SquareTerms:
    @staticmethod
    def semaphores(seq):
        return [pltpu.SemaphoreType.DMA((seq // 2, 2)), pltpu.SemaphoreType.DMA((seq // 2, 2, 2))]

    @staticmethod
    def scratch(seq, half_shape):
        ys = seq // 2
        return [
            pltpu.VMEM((ys,) + half_shape, jnp.bfloat16),
            pltpu.VMEM(half_shape, jnp.bfloat16),
            pltpu.SemaphoreType.DMA((ys + 1, 2)),
        ]

    def __init__(self, at, terms, from_x, from_y, sems=None, lasts=None, scratch=None):
        self.at, self.terms, self.from_x, self.from_y = at, terms, from_x, from_y
        if sems is not None:
            self.xs, self.ys = sems
        if scratch is not None:
            self.last_y, self.last_x = lasts
            self.sum_y, self.sum_x, self.last = scratch

    def first_x(self, y):
        at = self.at
        return send(
            self.terms(y * 2 + 1 - at.x, 0), self.from_x.at[y], self.xs.at[y, 0], self.xs.at[y, 1], at.across()
        )

    def first_y(self, step, x):
        at = self.at
        y = at.beside(step)
        return send(
            self.terms(y * 2 + x, 1),
            self.from_y.at[at.y, x],
            self.ys.at[step, x, 0],
            self.ys.at[at.y, x, 1],
            at.column(y),
        )

    def first_start(self):
        for y in range(self.at.ys):
            self.first_x(y).start()
        for step in range(1, self.at.ys):
            for x in range(2):
                self.first_y(step, x).start()

    def first_wait(self):
        at = self.at
        for y in range(at.ys):
            self.first_x(y).wait()
        for step in range(1, at.ys):
            y = at.beside(step)
            for x in range(2):
                self.first_y(step, x).wait_send()
                slot = self.from_y.at[y, x]
                send(slot, slot, self.ys.at[step, x, 0], self.ys.at[y, x, 1], at.across()).wait_recv()

    def second_y(self, step):
        at = self.at
        y = at.beside(step)
        return send(
            self.sum_y.at[y], self.last_y.at[at.y], self.last.at[step, 0], self.last.at[at.y, 1], at.column(y)
        )

    def second_x(self):
        at = self.at
        return send(self.sum_x, self.last_x, self.last.at[at.ys, 0], self.last.at[at.ys, 1], at.across())

    def second_pairs(self, rooms=None):
        at = self.at
        pairs = [(self.terms(at.y * 2 + 1 - at.x, 1), self.sum_x)]
        for step in range(1, at.ys):
            y = at.beside(step)
            pairs.append((self.terms(y * 2 + at.x, 0), self.sum_y.at[y]))
            if rooms is not None:
                pairs.append((self.from_x.at[y], rooms[0].at[step - 1]))
                pairs.append((self.from_y.at[y, 1 - at.x], rooms[1].at[step - 1]))
        return pairs

    def second_add(self, rooms=None):
        at = self.at
        terms = [self.sum_x]
        for step in range(1, at.ys):
            y = at.beside(step)
            near = self.from_x.at[y] if rooms is None else rooms[0].at[step - 1]
            add_into(self.sum_y.at[y], [self.sum_y.at[y], near])
            terms.append(self.from_y.at[y, 1 - at.x] if rooms is None else rooms[1].at[step - 1])
        add_into(self.sum_x, terms)

    def second_go(self):
        for step in range(1, self.at.ys):
            self.second_y(step).start()
        self.second_x().start()

    def second_wait(self):
        at = self.at
        for step in range(1, at.ys):
            self.second_y(step).wait_send()
            y = at.beside(step)
            slot = self.last_y.at[y]
            send(slot, slot, self.last.at[step, 0], self.last.at[y, 1], at.across()).wait_recv()
        self.second_x().wait()


def norm_back(rows, load, store, gain, terms):
    def step(index, carry):
        window = pl.ds(pl.multiple_of(index * 16, 16), 16)
        values, incoming, base = load(window)
        root = lax.rsqrt(jnp.mean(values * values, axis=-1, keepdims=True) + epsilon)
        scaled = incoming * gain
        share = jnp.mean(values * scaled, axis=-1, keepdims=True)
        store(window, base + root * scaled - values * (root * root * root * share))
        term = incoming * values * root
        terms[...] += term[:8] + term[8:]
        return carry

    lax.fori_loop(0, rows // 16, step, 0)


class Exchange:
    def __init__(self, at, shard, everyone, gather_sems, local, sums, first, second):
        self.at, self.sums, self.first, self.second = at, sums, first, second
        count = shard.shape[0]
        slot = lambda w: everyone.at[pl.ds(pl.multiple_of(w * count, count), count)]
        self.gather = LineGather(at, slot, gather_sems)
        self.gather.start(shard)
        own = pltpu.make_async_copy(shard, slot(at.w), local)
        own.start()
        own.wait()
        self.last, self.ahead = 2 * (at.zs - 1), 0

    def step_ahead(self):
        self.gather.step(0)
        self.ahead = 1

    def level(self, index):
        at = self.at
        far, side = lax.div(index + 1, 2), lax.rem(index, 2)
        z = at.z + jnp.where(side == 1, -far, far)
        return far, side, z, (z >= 0) & (z < at.zs)

    def arrive(self, index):
        far, side, z, valid = self.level(index)

        @pl.when((side == 1) & (far > self.ahead))
        def _():
            self.gather.step(far - 1)

        @pl.when(valid)
        def _():
            self.gather.wait_over(z)
            self.first(z)

        return z, valid

    def put(self, z, begin, end):
        def step(piece, inner):
            self.second(z, piece)
            self.sums.over(z, piece).start()

            @pl.when(piece > begin)
            def _():
                self.sums.ends(z, piece - 1)

            return inner

        lax.fori_loop(begin, end, step, 0)
        self.sums.ends(z, end - 1)

    def whole(self, total, fill):
        at, sums = self.at, self.sums

        def turn(index, carry):
            z, valid = self.arrive(index)

            @pl.when(valid)
            def _():
                self.put(z, 0, sums.pieces)

            return carry

        lax.fori_loop(0, self.last + 1, turn, 0)
        fill(None, sums.pieces)
        for index in range(2, at.zs):
            sums.pass_on(index, fill if index == 2 else None)
        sums.finish(total)
        self.gather.sent()

    def by_columns(self, total, direct, relayed, near):
        at, sums = self.at, self.sums
        begin = min(3, self.last)

        def turn(index, carry):
            z, valid = self.arrive(index)

            @pl.when(index == begin)
            def _():
                direct()

            @pl.when(valid & (index >= begin))
            def _():
                self.put(z, 0, near)

            return carry

        lax.fori_loop(0, self.last + 1, turn, 0)

        def earlier(index, carry):
            _, _, z, valid = self.level(index)

            @pl.when(valid)
            def _():
                self.put(z, 0, near)

            return carry

        lax.fori_loop(1, begin, earlier, 0)
        if at.zs > 2:
            sums.pass_on(2, None, 0, near)
        relayed()

        def over(index, carry):
            _, _, z, valid = self.level(self.last - index)

            @pl.when(valid)
            def _():
                for piece in range(near, sums.pieces):
                    self.second(z, piece)
                    sums.over(z, piece).start()

            return carry

        lax.fori_loop(0, self.last, over, 0)

        def start(index, carry):
            _, _, z, valid = self.level(self.last - index)

            @pl.when(valid)
            def _():
                for piece in range(near, sums.pieces):
                    sums.ends(z, piece)

            return carry

        lax.fori_loop(0, self.last, start, 0)
        self.put(at.z, 0, sums.pieces)
        for index in range(3, at.zs):
            sums.pass_on(index, None, 0, near)
        for index in range(at.zs - 1, 1, -1):
            sums.pass_on(index, None, near, sums.pieces)
        sums.finish(total)
        self.gather.sent()


PIECES = 2


def feed_forward(at, sizes, inputs, outputs, scratch):
    count, width, units, block, columns = sizes
    early, half, zs, seq = early_rows(units), units // 2, at.zs, at.seq
    normed_ref, attended_ref, teacher_ref, length_ref, gate_shard_ref, shard_ref = inputs
    (final_out, error_out, energy_out), outputs = outputs[:3], outputs[3:]
    normed_out, gate_out, up_out, active_out, down_out, gates_out = outputs
    everyone, gates, downs, gate_all, up_all, active_all, parts, total = scratch[:8]
    gather_sems, sum_scratch, late_sems, square_sems, (local, outgoing) = (
        scratch[8:9],
        scratch[9:13],
        scratch[13:16],
        scratch[16:19],
        scratch[19:],
    )
    late = SquareGather(
        at,
        lambda s, h: gates.at[
            h, pl.ds(early, units - early), pl.ds(pl.multiple_of(s * block, block), block)
        ],
        lambda h: gate_shard_ref.at[h, pl.ds(early, units - early)],
        late_sems,
    )
    weights = SquareGather(
        at,
        lambda s, h: downs.at[
            pl.ds(h * half, half), pl.ds(pl.multiple_of(s * columns, columns), columns)
        ],
        lambda h: shard_ref.at[pl.ds(h * half, half)],
        square_sems,
    )
    ys = seq // 2

    def column_block(piece):
        if isinstance(piece, int):
            step = 0 if piece < 2 else piece - 1 if piece <= ys else piece - ys
            return at.beside(step) * 2 + (1 - at.x if piece == 1 or piece > ys else at.x)
        step = jnp.where(piece < 2, 0, jnp.where(piece <= ys, piece - 1, piece - ys))
        other = (piece == 1) | (piece > ys)
        return at.beside(step) * 2 + jnp.where(other, 1 - at.x, at.x)

    sums = LinePieces(
        at,
        lambda w: parts.at[pl.ds(pl.multiple_of(w * count, count), count)],
        sum_scratch,
        column_block,
    )
    down_store = pltpu.make_async_copy(downs, down_out, local.at[2])
    gates_store = pltpu.make_async_copy(gates, gates_out, local.at[0])

    def direct():
        weights.relay()
        weights.direct()

    def relayed():
        weights.relayed()
        down_store.start()

    def rows(z):
        return pl.ds(pl.multiple_of(z * 2 * count, 2 * count), 2 * count)

    def stores(z):
        return [
            pltpu.make_async_copy(source.at[rows(z)], target.at[rows(z)], outgoing.at[index, z])
            for index, (source, target) in enumerate(
                ((everyone, normed_out), (gate_all, gate_out), (up_all, up_out), (active_all, active_out))
            )
        ]

    def first(z):
        here = everyone[rows(z), :]
        gate = contract_last(here, gates[0])
        up = contract_last(here, gates[1])
        gate_all[rows(z), :] = gate
        up_all[rows(z), :] = up
        active_all[rows(z), :] = gated_unit(gate, up).astype(jnp.bfloat16)
        for copy in stores(z):
            copy.start()

    def second(z, piece):
        window = sums.columns(piece)
        parts[rows(z), window] = jnp.dot(
            active_all[rows(z), :], downs[:, window], preferred_element_type=jnp.float32
        ).astype(jnp.bfloat16)

    def run():
        work = Exchange(at, normed_ref, everyone, gather_sems, local.at[1], sums, first, second)
        late.relay()
        weights.start()
        own = pltpu.make_async_copy(
            shard_ref, downs.at[:, pl.ds(pl.multiple_of(at.s * columns, columns), columns)], local.at[3]
        )
        own.start()
        work.step_ahead()
        own.wait()
        late.finish()
        gates_store.start()
        work.by_columns(total, direct, relayed, ys + 1)
        energy_out[...] = jnp.zeros_like(energy_out)
        valid = length_ref[at.w]

        def finish_rows(index, carry):
            window = pl.ds(pl.multiple_of(index * 16, 16), 16)
            final = attended_ref[window, :] + total[window, :]
            final_out[window, :] = final.astype(jnp.bfloat16)
            place = at.s * count + index * 16 + lax.broadcasted_iota(jnp.int32, final.shape, 0)
            keep = (place < valid).astype(jnp.float32)
            error = (final - teacher_ref[window, :].astype(jnp.float32)) * keep
            error_out[window, :] = error
            squares = error * error
            energy_out[...] += 0.5 * (squares[:8] + squares[8:])
            return carry

        lax.fori_loop(0, count // 16, finish_rows, 0)
        down_store.wait()
        gates_store.wait()
        for z in range(zs):
            for copy in stores(z):
                copy.wait()

    return late.start, run


def forward_pass(tokens, qkv_rows, out_rows, norm_gain, mlp_gain, segments, taps, teacher, down, lengths, gate_up):
    seq, wt = lax.axis_size("seq"), lax.axis_size("wt")
    zs = wt // 2
    count, width = tokens.shape
    length = count * seq
    out_rank = out_rows.shape[0]
    heads = H // seq
    value_width = heads * DV
    qkv_width = value_width + 2 * FEAT * heads
    qkv_rank = width // (seq * wt)
    lanes_each = width // (seq * wt)
    units, block = gate_up.shape[1:]
    early = early_rows(units)
    rows_at_once = 256
    small = [
        tokens,
        qkv_rows,
        out_rows,
        norm_gain[None],
        mlp_gain[None],
        segments,
        taps,
        teacher,
        down,
    ]
    token_count = wt * count

    def kernel(*refs):
        (x_ref, qkv_ref, out_ref, first_gain, second_gain, segment_ref, tap_ref), refs = refs[:7], refs[7:]
        (teacher_ref, down_ref), refs = refs[:2], refs[2:]
        (length_ref, gate_up_ref), refs = refs[:2], refs[2:]
        (attended_out, normed_out, gain_rows), refs = refs[:3], refs[3:]
        (qkv_out, w_out_out, hidden_out, sorted_out, mixer_out, values_out, outputs_out, order_out), refs = (
            refs[:8],
            refs[8:],
        )
        feed_outputs, refs = refs[:9], refs[9:]
        (xs, qkvs, outs, gains_all, sorted_v, values_v, outputs_v), refs = refs[:7], refs[7:]
        (order_v, segment_column, tap_v, gain_ref), refs = refs[:4], refs[4:]
        sum_scratch, x_sems, gate_sems, refs = refs[:8], refs[8:11], refs[11:14], refs[14:]
        line_sems, refs = [refs[index : index + 1] for index in range(3)], refs[3:]
        (swap_q, swap_g, local, outgoing), feed_scratch = refs[:4], refs[4:]
        at = Place(seq, wt)
        gates_ref, parts, total = feed_scratch[1], feed_scratch[6], feed_scratch[7]
        hidden_v = parts.at[pl.ds(length, length)]
        mixer_v = feed_scratch[5].at[pl.ds(0, length), pl.ds(0, value_width)]
        gates_own = pltpu.make_async_copy(
            gate_up_ref, gates_ref.at[:, :, pl.ds(pl.multiple_of(at.s * block, block), block)], local.at[4]
        )
        gates_own.start()
        gain_ref[...] = jnp.zeros_like(gain_ref)
        gain_ref[0:1, :lanes_each] = first_gain[...].astype(jnp.float32)
        gain_ref[1:2, :lanes_each] = second_gain[...].astype(jnp.float32)
        late_start, feed = feed_forward(
            at,
            (count, width, units, block, down.shape[1]),
            (normed_out, attended_out, teacher_ref, length_ref, gate_up_ref, down_ref),
            feed_outputs,
            feed_scratch,
        )
        at.meet(True, True)
        half = count // 2
        gather_x = SquareGather(
            at,
            lambda s, h: xs.at[pl.ds(pl.multiple_of(s * count + h * half, half), half)],
            lambda h: x_ref.at[pl.ds(h * half, half)],
            x_sems,
        )
        gather_q = LineGather(at, lambda w: qkvs.at[:, w], line_sems[0])
        gather_g = LineGather(
            at, lambda w: gains_all.at[:, pl.ds(pl.multiple_of(w * 8, 8), 8)], line_sems[1]
        )
        gather_o = LineGather(at, lambda w: outs.at[w], line_sems[2])
        gates = SquareGather(
            at,
            lambda s, h: gates_ref.at[h, pl.ds(0, early), pl.ds(pl.multiple_of(s * block, block), block)],
            lambda h: gate_up_ref.at[h, pl.ds(0, early)],
            gate_sems,
        )
        gain_slot = pl.ds(pl.multiple_of(at.w * 8, 8), 8)

        def qkv_part(s):
            if len(qkv_ref.shape) == 3:
                return qkv_ref.at[s]
            return qkv_ref.at[:, pl.ds(pl.multiple_of(s * qkv_width, qkv_width), qkv_width)]

        swaps = []
        for step in range(1, seq):
            to = lax.rem(at.s + step, seq)
            swaps.append(
                send(gain_ref, gains_all.at[at.s, gain_slot], swap_g.at[step, 0], swap_g.at[at.s, 1], (to, at.w))
            )
            swaps.append(
                send(qkv_part(to), qkvs.at[at.s, at.w], swap_q.at[step, 0], swap_q.at[at.s, 1], (to, at.w))
            )
        for copy in swaps:
            copy.start()
        gather_x.start()
        own = [
            pltpu.make_async_copy(qkv_part(at.s), qkvs.at[at.s, at.w], local.at[0]),
            pltpu.make_async_copy(gain_ref, gains_all.at[at.s, gain_slot], local.at[1]),
            pltpu.make_async_copy(out_ref, outs.at[at.w], local.at[2]),
            pltpu.make_async_copy(x_ref, xs.at[pl.ds(pl.multiple_of(at.s * count, count), count)], local.at[3]),
        ]
        for copy in own:
            copy.start()
        for copy in own:
            copy.wait()
        gather_o.start()
        for step in range(1, seq):
            s = lax.rem(at.s + step, seq)
            slot = gains_all.at[s, gain_slot]
            send(slot, slot, swap_g.at[step, 0], swap_g.at[s, 1], at.across()).wait_recv()
            slot = qkvs.at[s, at.w]
            send(slot, slot, swap_q.at[step, 0], swap_q.at[s, 1], at.across()).wait_recv()
        gather_g.start()
        gather_q.start()
        tap_v[...] = tap_ref[...].astype(jnp.float32)
        segment_row = segment_ref[...].astype(jnp.float32)
        segment_column[...] = jnp.broadcast_to(segment_row, (128, length)).T
        write_order(order_v, heads)
        gather_x.relay()
        gates.start()
        for index in range(zs - 1):
            gather_g.step(index)
            gather_q.step(index)
        gather_o.step(0)
        gather_g.finish()

        device_rows = gains_all[...].reshape(seq * wt * 8, 128).astype(jnp.bfloat16)
        gain_rows[...] = jnp.zeros_like(gain_rows)

        def spread_gains(index, carry):
            begin = pl.multiple_of(index * 256, 256)
            lane = lax.broadcasted_iota(jnp.int32, (128, 256), 0)
            column = begin + lax.broadcasted_iota(jnp.int32, (128, 256), 1)
            copied = jnp.dot(
                device_rows,
                (lane == lax.rem(column, lanes_each)).astype(jnp.float32).astype(jnp.bfloat16),
                preferred_element_type=jnp.float32,
            )
            row = lax.broadcasted_iota(jnp.int32, copied.shape, 0)
            column = begin + lax.broadcasted_iota(jnp.int32, copied.shape, 1)
            first_row = lax.div(column, lanes_each) * 8
            for number in range(2):
                gain_rows[number : number + 1, pl.ds(begin, 256)] = jnp.sum(
                    jnp.where(row == first_row + number, copied, 0.0), axis=0, keepdims=True
                )
            return carry

        lax.fori_loop(0, width // 256, spread_gains, 0)
        gather_x.finish()

        def norm_rows(index, carry):
            window = pl.ds(pl.multiple_of(index * 32, 32), 32)
            hidden_v[window, :] = rms_norm(xs[window, :].astype(jnp.float32), gain_rows[0:1, :]).astype(
                jnp.bfloat16
            )
            return carry

        lax.fori_loop(0, length // 32, norm_rows, 0)
        gather_q.finish()
        projected = jnp.dot(
            hidden_v[...], qkvs[...].reshape(width, qkv_width), preferred_element_type=jnp.float32
        ).astype(jnp.bfloat16)
        sorted_v[...] = jnp.dot(projected, order_v[...], preferred_element_type=jnp.float32).astype(
            jnp.bfloat16
        )
        stores = [
            pltpu.make_async_copy(source, target, outgoing.at[index])
            for index, (source, target) in enumerate(
                (
                    (qkvs, qkv_out),
                    (hidden_v, hidden_out),
                    (sorted_v, sorted_out),
                    (values_v, values_out),
                    (outputs_v, outputs_out),
                    (mixer_v, mixer_out),
                    (outs, w_out_out),
                    (order_v, order_out),
                )
            )
        ]
        for copy in stores[:3]:
            copy.start()
        marks = tap_marks(segment_column)

        def convolve(head, carry):
            columns = pl.ds(pl.multiple_of(head * DV, DV), DV)
            raw = sorted_v[:, columns].astype(jnp.float32)
            mixed = tap_v[0:1, columns] * raw
            for tap in range(1, KCONV):
                mixed = mixed + tap_v[tap : tap + 1, columns] * pltpu.roll(raw, tap, 0) * marks[tap]
            values_v[head] = mixed.astype(jnp.bfloat16)
            return carry

        lax.fori_loop(0, heads, convolve, 0)
        stores[3].start()
        gates.relay()
        steps = length // rows_at_once
        lanes = lax.broadcasted_iota(jnp.int32, (1, 128), 1)

        def attend(index, carry):
            head, start = lax.div(index, steps), lax.rem(index, steps) * rows_at_once
            rows = pl.ds(pl.multiple_of(start, rows_at_once), rows_at_once)
            mine = ((lanes >= head * FEAT) & (lanes < head * FEAT + FEAT)).astype(jnp.float32)
            queries = sorted_v[rows, value_width : value_width + 128] * mine.astype(jnp.bfloat16)
            scores = contract_last(queries, sorted_v[:, value_width + 128 :]) * 0.25
            places = start + lax.broadcasted_iota(jnp.int32, scores.shape, 0)
            allowed = (segment_column[rows, :1] == segment_row) & (
                places >= lax.broadcasted_iota(jnp.int32, scores.shape, 1)
            )
            kernel_values = jnp.where(allowed, 1.0 + scores + 0.5 * scores * scores, 0.0)
            denominator = jnp.sum(kernel_values, axis=1, keepdims=True)
            mixed = (
                jnp.dot(kernel_values.astype(jnp.bfloat16), values_v[head], preferred_element_type=jnp.float32)
                / denominator
            )
            outputs_v[head, rows, :] = mixed
            mixer_v[rows, pl.ds(pl.multiple_of(head * DV, DV), DV)] = mixed.astype(jnp.bfloat16)
            return carry

        turns = heads * steps
        for index in range(zs - 1):
            lax.fori_loop(turns * index // (zs - 1), turns * (index + 1) // (zs - 1), attend, 0)
            if index > 0:
                gather_o.step(index)
        gather_o.finish()
        for copy in stores[4:]:
            copy.start()

        def out_job(index, carry):
            window = pl.ds(pl.multiple_of(index * 512, 512), 512)
            term = jnp.dot(
                mixer_v[...], outs[:, :, window].reshape(value_width, 512), preferred_element_type=jnp.float32
            ).astype(jnp.bfloat16)
            for s in range(seq):
                for h in range(2):
                    begin = s * count + h * half
                    parts[begin : begin + half, window] = term[begin : begin + half]
            return carry

        lax.fori_loop(0, width // 512, out_job, 0)
        work = SquareSum(
            at, lambda s, h: parts.at[pl.ds(pl.multiple_of(s * count + h * half, half), half)], sum_scratch
        )
        work.start()
        work.relay()
        late_start()
        work.finish(lambda h: total.at[pl.ds(h * half, half)])

        def finish_rows(index, carry):
            for h in range(2):
                rows = pl.ds(pl.multiple_of(h * half + index * 16, 16), 16)
                attended = x_ref[rows, :].astype(jnp.float32) + total[rows, :]
                attended_out[rows, :] = attended
                normed_out[rows, :] = rms_norm(attended, gain_rows[1:2, :]).astype(jnp.bfloat16)
            return carry

        lax.fori_loop(0, half // 16, finish_rows, 0)
        gates.finish()
        gates_own.wait()
        stores[1].wait()
        stores[5].wait()
        feed()
        for copy in swaps:
            copy.wait_send()
        for index, copy in enumerate(stores):
            if index not in (1, 5):
                copy.wait()

    low, f32 = jnp.bfloat16, jnp.float32
    sorted_width = value_width + 256
    return remote_call(
        kernel,
        "forward_pass",
        0,
        [
            jax.ShapeDtypeStruct((count, width), f32),
            jax.ShapeDtypeStruct((count, width), low),
            jax.ShapeDtypeStruct((8, width), f32),
            jax.ShapeDtypeStruct((seq, wt, qkv_rank, qkv_width), low),
            jax.ShapeDtypeStruct((wt, out_rank, width), low),
            jax.ShapeDtypeStruct((length, width), low),
            jax.ShapeDtypeStruct((length, sorted_width), low),
            jax.ShapeDtypeStruct((length, value_width), low),
            jax.ShapeDtypeStruct((heads, length, DV), low),
            jax.ShapeDtypeStruct((heads, length, DV), f32),
            jax.ShapeDtypeStruct((qkv_width, sorted_width), low),
            jax.ShapeDtypeStruct((count, width), low),
            jax.ShapeDtypeStruct((count, width), f32),
            jax.ShapeDtypeStruct((8, width), f32),
            jax.ShapeDtypeStruct((token_count, width), low),
            jax.ShapeDtypeStruct((token_count, units), f32),
            jax.ShapeDtypeStruct((token_count, units), f32),
            jax.ShapeDtypeStruct((token_count, units), low),
            jax.ShapeDtypeStruct((units, width), low),
            jax.ShapeDtypeStruct((2, units, width), low),
        ],
        [
            pltpu.VMEM((length, width), low),
            pltpu.VMEM((seq, wt, qkv_rank, qkv_width), low),
            pltpu.VMEM((wt, out_rank, width), low),
            pltpu.VMEM((seq, wt * 8, 128), f32),
            pltpu.VMEM((length, sorted_width), low),
            pltpu.VMEM((heads, length, DV), low),
            pltpu.VMEM((heads, length, DV), f32),
            pltpu.VMEM((qkv_width, sorted_width), low),
            pltpu.VMEM((length, 128), f32),
            pltpu.VMEM((KCONV, value_width), f32),
            pltpu.VMEM((8, 128), f32),
        ]
        + SquareSum.scratch(seq, (count // 2, width))
        + SquareGather.semaphores(seq)
        + SquareGather.semaphores(seq)
        + LineGather.semaphores(wt, 2)
        + LineGather.semaphores(wt)
        + LineGather.semaphores(wt, 2)
        + [
            pltpu.SemaphoreType.DMA((seq, 2)),
            pltpu.SemaphoreType.DMA((seq, 2)),
            pltpu.SemaphoreType.DMA((5,)),
            pltpu.SemaphoreType.DMA((8,)),
            pltpu.VMEM((token_count, width), low),
            pltpu.VMEM((2, units, width), low),
            pltpu.VMEM((units, width), low),
            pltpu.VMEM((token_count, units), f32),
            pltpu.VMEM((token_count, units), f32),
            pltpu.VMEM((token_count, units), low),
            pltpu.VMEM((token_count, width), low),
            pltpu.VMEM((count, width), f32),
        ]
        + LineGather.semaphores(wt, 2)
        + LinePieces.scratch(wt, (count, width), seq)
        + SquareGather.semaphores(seq)
        + SquareGather.semaphores(seq)
        + [pltpu.SemaphoreType.DMA((5,)), pltpu.SemaphoreType.DMA((4, zs))],
        *small,
        lengths,
        gate_up,
        in_specs=[VMEM] * len(small) + [SMEM, ANY],
        out_specs=[VMEM] * 3 + [ANY] * 8 + [VMEM] * 3 + [ANY] * 6,
    )


def feed_back(error, attended, gain, gate_up, down, gate, up, active, normed):
    seq, wt = lax.axis_size("seq"), lax.axis_size("wt")
    count, width = error.shape
    units = gate_up.shape[1]
    tokens = wt * count
    ys = seq // 2
    block = width // seq
    half = (units // 2, block)

    def kernel(*refs):
        (error_ref, attended_ref, gain_ref, gate_up_ref, down_ref, gate_ref, up_ref, active_ref, normed_ref), refs = (
            refs[:9],
            refs[9:],
        )
        (grad_ref, mix_ref, gain_terms), refs = refs[:3], refs[3:]
        (gate_out, up_out, down_out, gate_x, gate_y, down_x, down_y), refs = refs[:7], refs[7:]
        (low, everyone, gates, downs, gate_all, up_all, back_all, parts, actives, columns), refs = refs[:10], refs[10:]
        (gate_terms, up_terms, down_terms, total), refs = refs[:4], refs[4:]
        gather_sems, sum_scratch, gate_sems, down_sems, (local, outgoing) = (
            refs[:1],
            refs[1:5],
            refs[5:7],
            refs[7:9],
            refs[9:],
        )
        at = Place(seq, wt)
        loads = [
            pltpu.make_async_copy(source, target, local.at[index])
            for index, (source, target) in enumerate(
                (
                    (down_ref, downs),
                    (gate_ref, gate_all),
                    (up_ref, up_all),
                    (gate_up_ref, gates),
                    (active_ref, actives),
                )
            )
        ]
        for load in loads:
            load.start()
        at.meet(True, True)
        low[...] = error_ref[...].astype(jnp.bfloat16)
        sums = LinePieces(
            at, lambda w: parts.at[pl.ds(pl.multiple_of(w * count, count), count)], sum_scratch
        )
        gate_sum = SquareTerms(at, lambda s, h: gate_terms.at[s, h], gate_x, gate_y, gate_sems)
        down_sum = SquareTerms(at, lambda s, h: down_terms.at[s, h], down_x, down_y, down_sems)

        def place(index):
            step = lax.div(index, 2) + 1
            x = lax.rem(at.x + 1 + lax.rem(index, 2), 2)
            return step, x, at.beside(step) * 2 + x

        def column_load(index):
            s = place(index)[2]
            return pltpu.make_async_copy(
                normed_ref.at[:, pl.ds(pl.multiple_of(s * block, block), block)],
                columns.at[lax.rem(index, 2)],
                local.at[6 + lax.rem(index, 2)],
            )

        def leave(sum_, index):
            step, x, s = place(index)

            @pl.when(x != at.x)
            def _():
                sum_.first_x(lax.div(s, 2)).start()

            @pl.when(step < ys)
            def _():
                sum_.first_y(step, x).start()

        def down_job(index):
            s = place(index)[2]
            term = contract_first(
                actives[...], everyone[:, pl.ds(pl.multiple_of(s * block, block), block)]
            ).astype(jnp.bfloat16)
            down_terms[s, 0] = term[: units // 2]
            down_terms[s, 1] = term[units // 2 :]
            leave(down_sum, index)

        def gate_job(index):
            s = place(index)[2]
            column_load(index).wait()
            here = columns.at[lax.rem(index, 2)]
            for number, terms in enumerate((gate_terms, up_terms)):
                term = contract_first(back_all[number], here[...]).astype(jnp.bfloat16)
                terms[s, 0] = term[: units // 2]
                terms[s, 1] = term[units // 2 :]

            @pl.when(index + 2 < seq)
            def _():
                column_load(index + 2).start()

            leave(gate_sum, index)

        def fill(slot, slots):
            if slot is None:
                lax.fori_loop(0, seq, lambda index, carry: (down_job(index), carry)[1], 0)
                return

            each = -(-seq // slots)

            def step(index, carry):
                job = slot * each + index

                @pl.when(job < seq)
                def _():
                    gate_job(job)

                return carry

            lax.fori_loop(0, each, step, 0)

        def prepare():
            column_load(0).start()
            column_load(1).start()
            for load in loads:
                load.wait()

        def rows(z):
            return pl.ds(pl.multiple_of(z * 2 * count, 2 * count), 2 * count)

        def first(z):
            active_back = contract_last(everyone[rows(z), :], downs[...])
            gate_here, up_here = gate_all[rows(z), :], up_all[rows(z), :]
            share = jax.nn.sigmoid(gate_here)
            back_all[0, rows(z), :] = (
                active_back * up_here * share * (1.0 + gate_here * (1.0 - share))
            ).astype(jnp.bfloat16)
            back_all[1, rows(z), :] = (active_back * gate_here * share).astype(jnp.bfloat16)

        def second(z, piece):
            window = pl.ds(pl.multiple_of(piece * sums.width, sums.width), sums.width)
            parts[rows(z), window] = (
                jnp.dot(back_all[0, rows(z), :], gates[0, :, window], preferred_element_type=jnp.float32)
                + jnp.dot(back_all[1, rows(z), :], gates[1, :, window], preferred_element_type=jnp.float32)
            ).astype(jnp.bfloat16)

        work = Exchange(at, low, everyone, gather_sems, local.at[5], sums, first, second)
        prepare()
        work.whole(total, fill)
        stores = [
            pltpu.make_async_copy(source, target, outgoing.at[index])
            for index, (source, target) in enumerate(
                ((gate_terms, gate_out), (up_terms, up_out), (down_terms, down_out))
            )
        ]
        for copy in stores:
            copy.start()
        gain_terms[...] = jnp.zeros_like(gain_terms)

        def load_rows(window):
            return attended_ref[window, :], total[window, :], error_ref[window, :]

        def store_rows(window, value):
            grad_ref[window, :] = value
            mix_ref[window, :] = value.astype(jnp.bfloat16)

        norm_back(count, load_rows, store_rows, gain_ref[1:2, :], gain_terms)
        for copy in stores:
            copy.wait()
        gate_sum.first_wait()
        down_sum.first_wait()

    def terms_of(half):
        return jax.ShapeDtypeStruct((seq, 2) + half, jnp.bfloat16)

    def first_of(half):
        return [
            jax.ShapeDtypeStruct((ys,) + half, jnp.bfloat16),
            jax.ShapeDtypeStruct((ys, 2) + half, jnp.bfloat16),
        ]

    return remote_call(
        kernel,
        "feed_back",
        3,
        [
            jax.ShapeDtypeStruct((count, width), jnp.float32),
            jax.ShapeDtypeStruct((count, width), jnp.bfloat16),
            jax.ShapeDtypeStruct((8, width), jnp.float32),
            terms_of(half),
            terms_of(half),
            terms_of(half),
        ]
        + first_of(half)
        + first_of(half),
        [
            pltpu.VMEM((count, width), jnp.bfloat16),
            pltpu.VMEM((tokens, width), jnp.bfloat16),
            pltpu.VMEM(gate_up.shape, jnp.bfloat16),
            pltpu.VMEM((units, width), jnp.bfloat16),
            pltpu.VMEM((tokens, units), jnp.float32),
            pltpu.VMEM((tokens, units), jnp.float32),
            pltpu.VMEM((2, tokens, units), jnp.bfloat16),
            pltpu.VMEM((tokens, width), jnp.bfloat16),
            pltpu.VMEM((tokens, units), jnp.bfloat16),
            pltpu.VMEM((2, tokens, block), jnp.bfloat16),
            pltpu.VMEM((seq, 2) + half, jnp.bfloat16),
            pltpu.VMEM((seq, 2) + half, jnp.bfloat16),
            pltpu.VMEM((seq, 2) + half, jnp.bfloat16),
            pltpu.VMEM((count, width), jnp.float32),
        ]
        + LineGather.semaphores(wt, 2)
        + LinePieces.scratch(wt, (count, width), PIECES)
        + SquareTerms.semaphores(seq)
        + SquareTerms.semaphores(seq)
        + [pltpu.SemaphoreType.DMA((8,)), pltpu.SemaphoreType.DMA((3,))],
        error,
        attended,
        gain,
        gate_up,
        down,
        gate,
        up,
        active,
        normed,
        in_specs=[VMEM] * 3 + [ANY] * 6,
        out_specs=[VMEM] * 3 + [ANY] * 7,
    )


def mixer_back(
    mix_back,
    attended_grad,
    tokens,
    gain,
    out_rows,
    qkv_columns,
    hidden,
    sorted_columns,
    mixer,
    mixed_values,
    head_outputs,
    segments,
    taps,
    order,
    gain_terms,
    energy,
    gate_parts,
    up_parts,
    down_parts,
):
    seq, wt = lax.axis_size("seq"), lax.axis_size("wt")
    zs, ys = wt // 2, seq // 2
    count, width = mix_back.shape
    length = count * seq
    heads = mixed_values.shape[0]
    qkv_width = qkv_columns.shape[1]
    value_width = heads * DV
    rank = width // (seq * wt)
    gate_half, down_half = gate_parts[0].shape[2:], down_parts[0].shape[2:]
    rows_at_once = 256
    turns = heads * length // rows_at_once
    big = [out_rows, qkv_columns, hidden, sorted_columns, mixer, mixed_values, head_outputs]
    small = [mix_back, attended_grad, tokens, gain, segments, taps, order, gain_terms, energy]
    far = list(gate_parts) + list(down_parts) + list(up_parts)

    def kernel(*refs):
        big_refs, refs = refs[: len(big)], refs[len(big) :]
        small_refs, refs = refs[: len(small)], refs[len(small) :]
        (gate_t, gate_x, gate_y, down_t, down_x, down_y, up_t), refs = refs[: len(far)], refs[len(far) :]
        (grad_out, sums_out, qkv_out, w_out_out, up_x, up_y), refs = refs[:6], refs[6:]
        gate_lasts, up_lasts, down_lasts, refs = refs[:2], refs[2:4], refs[4:6], refs[6:]
        (w_out_v, w_qkv_v, hidden_v, sorted_v, mixer_v, values_v, outputs_v), refs = refs[:7], refs[7:]
        (mix_all, mixer_grad, query_acc, key_acc, value_acc, back_sorted, back_v), refs = refs[:7], refs[7:]
        (hidden_parts, qkv_parts, out_parts, hidden_total, gain_acc, spread, taps_acc), refs = refs[:7], refs[7:]
        (segment_column, tap_v, slopes_v, weights_v, denominators_v), refs = refs[:5], refs[5:]
        (room_gate0, room_gate1, room_down0, room_down1, qkv_sum, first, middle, last), refs = refs[:8], refs[8:]
        hidden_scratch, refs = refs[:8], refs[8:]
        qkv_scratch, out_scratch, refs = refs[:4], refs[4:8], refs[8:]
        gate_scratch, down_scratch, up_scratch, refs = refs[:3], refs[3:6], refs[6:9], refs[9:]
        gather_sems, up_sems, refs = refs[:3], refs[3:5], refs[5:]
        local, swap, first_sems, last_sems, fetch_sems = refs
        (
            mix_ref,
            grad_ref,
            token_ref,
            gain_ref,
            segment_ref,
            tap_ref,
            order_ref,
            gain_two,
            energy_ref,
        ) = small_refs
        at = Place(seq, wt)
        loads = [
            pltpu.make_async_copy(source, target, local.at[4 + index])
            for index, (source, target) in enumerate(
                zip(big_refs, (w_out_v, w_qkv_v, hidden_v, sorted_v, mixer_v, values_v, outputs_v))
            )
        ]
        for load in loads:
            load.start()
        gate_sum = SquareTerms(at, lambda s, h: gate_t.at[s, h], gate_x, gate_y, None, gate_lasts, gate_scratch)
        down_sum = SquareTerms(at, lambda s, h: down_t.at[s, h], down_x, down_y, None, down_lasts, down_scratch)
        up_sum = SquareTerms(at, lambda s, h: up_t.at[s, h], up_x, up_y, up_sems, up_lasts, up_scratch)
        gate_rooms, down_rooms = (room_gate0, room_gate1), (room_down0, room_down1)
        fetches = [
            pltpu.make_async_copy(source, target, fetch_sems.at[number, index])
            for number, pairs in enumerate(
                (gate_sum.second_pairs(gate_rooms), down_sum.second_pairs(down_rooms), up_sum.second_pairs())
            )
            for index, (source, target) in enumerate(pairs)
        ]
        for copy in fetches:
            copy.start()
        at.meet(True, True)
        half = count // 2
        gather = SquareGather(
            at,
            lambda s, h: mix_all.at[pl.ds(pl.multiple_of(s * count + h * half, half), half)],
            lambda h: mix_ref.at[pl.ds(h * half, half)],
            gather_sems,
        )
        gather.start()
        own = pltpu.make_async_copy(
            mix_ref, mix_all.at[pl.ds(pl.multiple_of(at.s * count, count), count)], local.at[3]
        )
        own.start()

        tap_v[...] = tap_ref[...].astype(jnp.float32)
        segment_row = segment_ref[...].astype(jnp.float32)
        segment_column[...] = jnp.broadcast_to(segment_row, (128, length)).T
        for load in loads:
            load.wait()
        query_acc[...] = jnp.zeros_like(query_acc)
        key_acc[...] = jnp.zeros_like(key_acc)
        value_acc[...] = jnp.zeros_like(value_acc)
        steps = length // rows_at_once
        lanes = lax.broadcasted_iota(jnp.int32, (1, 128), 1)

        def turn_of(index):
            head, start = lax.div(index, steps), lax.rem(index, steps) * rows_at_once
            rows = pl.ds(pl.multiple_of(start, rows_at_once), rows_at_once)
            mine = ((lanes >= head * FEAT) & (lanes < head * FEAT + FEAT)).astype(jnp.float32)
            queries = sorted_v[rows, value_width : value_width + 128] * mine.astype(jnp.bfloat16)
            return head, start, rows, mine, queries

        def prepare(index, carry):
            head, start, rows, mine, queries = turn_of(index)
            scores = contract_last(queries, sorted_v[:, value_width + 128 :]) * 0.25
            places = start + lax.broadcasted_iota(jnp.int32, scores.shape, 0)
            allowed = (segment_column[rows, :1] == segment_row) & (
                places >= lax.broadcasted_iota(jnp.int32, scores.shape, 1)
            )
            kernel_values = jnp.where(allowed, 1.0 + scores + 0.5 * scores * scores, 0.0)
            slopes_v[index] = jnp.where(allowed, 0.25 * (1.0 + scores), 0.0)
            weights_v[index] = kernel_values.astype(jnp.bfloat16)
            denominators_v[index] = jnp.broadcast_to(
                jnp.sum(kernel_values, axis=1, keepdims=True), (rows_at_once, 128)
            )
            return carry

        middle_step = heads * steps // 2
        lax.fori_loop(0, middle_step, prepare, 0)
        gather.relay()
        lax.fori_loop(middle_step, heads * steps, prepare, 0)
        for copy in fetches:
            copy.wait()
        gate_sum.second_add(gate_rooms)
        down_sum.second_add(down_rooms)
        own.wait()
        gather.finish()
        up_sum.first_start()
        gate_sum.second_go()
        down_sum.second_go()
        mixer_grad[...] = contract_last(mix_all[...], w_out_v[...]).astype(jnp.bfloat16)
        out_sum = LinePieces(at, lambda w: out_parts.at[w], out_scratch)
        out_rank = out_parts.shape[1]
        out_block = 512 if value_width % 512 == 0 else value_width

        def out_job(index, carry):
            window = pl.ds(pl.multiple_of(index * 512, 512), 512)
            term = contract_first(mixer_v[...], mix_all[:, window]).astype(jnp.bfloat16)
            for w in range(wt):
                out_parts[w, :, window] = term[w * out_rank : (w + 1) * out_rank]
            return carry

        lax.fori_loop(0, width // 512, out_job, 0)
        for piece in range(out_sum.pieces):
            out_sum.offer(piece)
        for piece in range(out_sum.pieces):
            out_sum.launch(piece, 0)

        def attend(index, carry):
            head, start, rows, mine, queries = turn_of(index)
            columns = pl.ds(pl.multiple_of(head * DV, DV), DV)
            denominator = denominators_v[index][:, :1]
            incoming = mixer_grad[rows, columns].astype(jnp.float32)
            numerator_back = (incoming / denominator).astype(jnp.bfloat16)
            denominator_back = (
                -jnp.sum(incoming * outputs_v[head, rows, :], axis=1, keepdims=True) / denominator
            )
            weight_back = contract_last(numerator_back, values_v[head])
            dots_back = ((weight_back + denominator_back) * slopes_v[index]).astype(jnp.bfloat16)
            query_acc[rows, :] += (
                jnp.dot(dots_back, sorted_v[:, value_width + 128 :], preferred_element_type=jnp.float32) * mine
            )
            key_acc[...] += contract_first(dots_back, queries)
            value_acc[:, columns] += contract_first(weights_v[index], numerator_back)
            return carry

        lax.fori_loop(0, heads * steps, attend, 0)
        taps_acc[...] = jnp.zeros_like(taps_acc)
        marks = tap_marks(segment_column)

        def convolve(head, carry):
            columns = pl.ds(pl.multiple_of(head * DV, DV), DV)
            mixed_back = value_acc[:, columns]
            raw = sorted_v[:, columns].astype(jnp.float32)
            raw_back = tap_v[0:1, columns] * mixed_back
            taps_acc[3:4, columns] = jnp.sum(mixed_back * raw, axis=0, keepdims=True)
            for tap in range(1, KCONV):
                masked = mixed_back * marks[tap]
                taps_acc[3 + tap : 4 + tap, columns] = jnp.sum(
                    masked * pltpu.roll(raw, tap, 0), axis=0, keepdims=True
                )
                raw_back = raw_back + tap_v[tap : tap + 1, columns] * pltpu.roll(masked, length - tap, 0)
            back_sorted[:, columns] = raw_back.astype(jnp.bfloat16)
            return carry

        lax.fori_loop(0, heads, convolve, 0)
        back_sorted[:, value_width : value_width + 128] = query_acc[...].astype(jnp.bfloat16)
        back_sorted[:, value_width + 128 :] = key_acc[...].astype(jnp.bfloat16)
        back_v[...] = contract_last(back_sorted[...], order_ref[...]).astype(jnp.bfloat16)
        out_sum.launch_all(1)
        qkv_sums = LinePieces(at, lambda w: qkv_parts.at[:, w], qkv_scratch)
        qkv_rank = qkv_parts.shape[2]

        def qkv_job(s, carry):
            block = wt * qkv_rank
            window = pl.ds(pl.multiple_of(s * block, block), block)
            term = contract_first(hidden_v[:, window], back_v[...]).astype(jnp.bfloat16)
            for w in range(wt):
                qkv_parts[s, w] = term[w * qkv_rank : (w + 1) * qkv_rank]
            qkv_sums.offer(s)

            @pl.when(s > 0)
            def _():
                qkv_sums.launch(s - 1, 0)

            return carry

        lax.fori_loop(0, seq, qkv_job, 0)
        qkv_sums.launch(seq - 1, 0)
        hidden_sum = SquareSum(at, lambda s, h: hidden_parts.at[s, h], hidden_scratch)

        def hidden_job(index, carry):
            window = pl.ds(pl.multiple_of(index * 512, 512), 512)
            term = contract_last(back_v[...], w_qkv_v[window, :]).astype(jnp.bfloat16)
            for s in range(seq):
                for h in range(2):
                    begin = s * count + h * half
                    hidden_parts[s, h, :, window] = term[begin : begin + half]
            return carry

        lax.fori_loop(0, width // 512, hidden_job, 0)
        hidden_sum.start()
        for index in range(zs - 1, 1, -1):
            out_sum.pass_on(index)
        qkv_sums.launch_all(1)
        qkv_sums.pass_on(zs - 1)
        hidden_sum.relay()
        up_sum.first_wait()
        up_sum.second_add()
        up_sum.second_go()
        for index in range(zs - 2, 1, -1):
            qkv_sums.pass_on(index)
        hidden_sum.finish(lambda h: hidden_total.at[h])
        gain_acc[...] = jnp.zeros_like(gain_acc)
        for h in range(2):

            def shift(window):
                return pl.ds(pl.multiple_of(h * half + window.start, 16), 16)

            def load_rows(window):
                rows = shift(window)
                return token_ref[rows, :].astype(jnp.float32), hidden_total[h, window, :], grad_ref[rows, :]

            def store_rows(window, value):
                grad_out[shift(window), :] = value

            norm_back(half, load_rows, store_rows, gain_ref[0:1, :], gain_acc)
        spread[...] = jnp.zeros_like(spread)
        spread[0:1, :] = jnp.sum(gain_acc[...], axis=0, keepdims=True)
        spread[1:2, :] = jnp.sum(gain_two[...], axis=0, keepdims=True)
        energy = jnp.sum(jnp.sum(energy_ref[...], axis=0, keepdims=True), axis=1, keepdims=True)
        spread[2:3, :] = jnp.broadcast_to(energy, (1, width))
        copies = []
        for step in range(1, seq):
            to = lax.rem(at.s + step, seq)
            window = pl.ds(pl.multiple_of(to * value_width, value_width), value_width)
            copies.append(
                send(spread.at[:, window], first.at[at.s], first_sems.at[step, 0], first_sems.at[at.s, 1], (to, at.w))
            )
        for copy in copies:
            copy.start()

        def give(s):
            return send(qkv_sum.at[s], qkv_out.at[at.s], swap.at[s, 0], swap.at[at.s, 1], (s, at.w))

        def done(s):
            @pl.when(s != at.s)
            def _():
                give(s).start()

        qkv_sums.finish(qkv_sum, done)
        add_into(qkv_out.at[at.s], [qkv_sum.at[at.s]])
        out_sum.finish(w_out_out)
        terms = [spread.at[:, pl.ds(pl.multiple_of(at.s * value_width, value_width), value_width)], taps_acc]
        for step in range(1, seq):
            s = lax.rem(at.s + step, seq)
            slot = first.at[s]
            send(slot, slot, first_sems.at[step, 0], first_sems.at[s, 1], at.across()).wait_recv()
            terms.append(slot)
        add_into(middle, terms)
        for step in range(1, wt):
            to = lax.rem(at.w + step, wt)
            copy = send(middle, last.at[at.w], last_sems.at[step, 0], last_sems.at[at.w, 1], (at.s, to))
            copy.start()
            copies.append(copy)
        gate_sum.second_wait()
        down_sum.second_wait()
        terms = [middle]
        for step in range(1, wt):
            w = lax.rem(at.w + step, wt)
            slot = last.at[w]
            send(slot, slot, last_sems.at[step, 0], last_sems.at[w, 1], at.partner()).wait_recv()
            terms.append(slot)
        add_into(sums_out, terms)
        for step in range(1, seq):
            s = lax.rem(at.s + step, seq)
            slot = qkv_out.at[s]
            send(slot, slot, swap.at[s, 0], swap.at[s, 1], at.across()).wait_recv()
            give(s).wait_send()
        up_sum.second_wait()
        for copy in copies:
            copy.wait_send()

    out_rank, qkv_rank = value_width // wt, width // (seq * wt)
    f32, low = jnp.float32, jnp.bfloat16
    tile = (8, value_width)
    results = remote_call(
        kernel,
        "mixer_back",
        4,
        [
            jax.ShapeDtypeStruct((count, width), f32),
            jax.ShapeDtypeStruct(tile, f32),
            jax.ShapeDtypeStruct((seq, qkv_rank, qkv_width), low),
            jax.ShapeDtypeStruct((out_rank, width), f32),
            jax.ShapeDtypeStruct((ys,) + gate_half, low),
            jax.ShapeDtypeStruct((ys, 2) + gate_half, low),
        ]
        + [
            jax.ShapeDtypeStruct(shape, low)
            for shape_half in (gate_half, gate_half, down_half)
            for shape in ((ys,) + shape_half, shape_half)
        ],
        [pltpu.VMEM(array.shape, array.dtype) for array in big]
        + [
            pltpu.VMEM((length, width), low),
            pltpu.VMEM((length, value_width), low),
            pltpu.VMEM((length, 128), f32),
            pltpu.VMEM((length, 128), f32),
            pltpu.VMEM((length, value_width), f32),
            pltpu.VMEM((length, value_width + 256), low),
            pltpu.VMEM((length, qkv_width), low),
            pltpu.VMEM((seq, 2, count // 2, width), low),
            pltpu.VMEM((seq, wt, qkv_rank, qkv_width), low),
            pltpu.VMEM((wt, out_rank, width), low),
            pltpu.VMEM((2, count // 2, width), f32),
            pltpu.VMEM((8, width), f32),
            pltpu.VMEM((8, width), f32),
            pltpu.VMEM(tile, f32),
            pltpu.VMEM((length, 128), f32),
            pltpu.VMEM((KCONV, value_width), f32),
            pltpu.VMEM((turns, rows_at_once, length), f32),
            pltpu.VMEM((turns, rows_at_once, length), low),
            pltpu.VMEM((turns, rows_at_once, 128), f32),
            pltpu.VMEM((ys - 1,) + gate_half, low),
            pltpu.VMEM((ys - 1,) + gate_half, low),
            pltpu.VMEM((ys - 1,) + down_half, low),
            pltpu.VMEM((ys - 1,) + down_half, low),
            pltpu.VMEM((seq, qkv_rank, qkv_width), low),
            pltpu.VMEM((seq,) + tile, f32),
            pltpu.VMEM(tile, f32),
            pltpu.VMEM((wt,) + tile, f32),
        ]
        + SquareSum.scratch(seq, (count // 2, width))
        + LinePieces.scratch(wt, (seq, qkv_rank, qkv_width), seq)
        + LinePieces.scratch(wt, (out_rank, width), 1)
        + SquareTerms.scratch(seq, gate_half)
        + SquareTerms.scratch(seq, down_half)
        + SquareTerms.scratch(seq, gate_half)
        + SquareGather.semaphores(seq)
        + SquareTerms.semaphores(seq)
        + [
            pltpu.SemaphoreType.DMA((11,)),
            pltpu.SemaphoreType.DMA((seq, 2)),
            pltpu.SemaphoreType.DMA((seq, 2)),
            pltpu.SemaphoreType.DMA((wt, 2)),
            pltpu.SemaphoreType.DMA((3, 3 * (ys - 1) + 1)),
        ],
        *big,
        *small,
        *far,
        in_specs=[ANY] * len(big) + [VMEM] * len(small) + [ANY] * len(far),
        out_specs=[VMEM] * 6 + [ANY] * 6,
    )
    grad, totals, qkv_total, out_total, up_x, up_y = results[:6]
    gate = tuple(gate_parts) + tuple(results[6:8])
    up = tuple(up_parts) + (up_x, up_y) + tuple(results[8:10])
    down = tuple(down_parts) + tuple(results[10:12])
    return grad, totals, gate, up, down, qkv_total, out_total


def last_sums(gate, up, down, qkv_total, totals, lengths, out_total, grad, final, qkv_shape):
    seq, wt = lax.axis_size("seq"), lax.axis_size("wt")
    ys = seq // 2
    f32, low = jnp.float32, jnp.bfloat16
    gate_half, down_half = gate[0].shape[2:], down[0].shape[2:]
    total_width = totals.shape[1]
    lanes_each = total_width // wt
    width = grad.shape[1]
    qkv_width = qkv_total.shape[2]
    operands = list(gate) + list(up) + list(down)
    passed = [out_total, grad, final]

    def kernel(*refs):
        groups, refs = [refs[5 * index : 5 * index + 5] for index in range(3)], refs[15:]
        (qkv_ref, totals_ref, length_ref), passed_refs, refs = refs[:3], refs[3:6], refs[6:]
        (gate_up_out, down_out, qkv_out, first_gain, second_gain, taps_out, loss_out), refs = refs[:7], refs[7:]
        passed_outs, refs = refs[:3], refs[3:]
        totals, refs = refs[:2], refs[2:]
        passed_rooms, refs = refs[:3], refs[3:]
        rooms, (loads, stores, pass_sems) = [refs[5 * index : 5 * index + 5] for index in range(3)], refs[15:]
        s = lax.axis_index("seq")
        y, x = lax.div(s, 2), lax.rem(s, 2)
        copies = []
        for number, (group, room) in enumerate(zip(groups, rooms)):
            terms, from_x, from_y, last_y, last_x = group
            pairs = [(terms.at[s], room[0]), (from_x.at[y], room[1]), (last_x, room[4])]
            for other in range(1, ys):
                place = lax.rem(y + other, ys)
                pairs.append((from_y.at[place, x], room[2].at[other - 1]))
                pairs.append((last_y.at[place], room[3].at[other - 1]))
            mine = [
                pltpu.make_async_copy(source, target, loads.at[number, index])
                for index, (source, target) in enumerate(pairs)
            ]
            for copy in mine:
                copy.start()
            copies.append(mine)
        ins = [
            pltpu.make_async_copy(source, room, pass_sems.at[index, 0])
            for index, (source, room) in enumerate(zip(passed_refs, passed_rooms))
        ]
        for copy in ins:
            copy.start()
        shift = lax.rem(total_width - lax.axis_index("wt") * lanes_each, total_width)
        mine = pltpu.roll(totals_ref[...], shift, 1)[:, :lanes_each]
        first_gain[...] = mine[0:1]
        second_gain[...] = mine[1:2]
        taps_out[...] = mine[3 : 3 + KCONV]
        counted = length_ref[0]
        for index in range(1, length_ref.shape[0]):
            counted = counted + length_ref[index]
        loss_out[...] = 2.0 * totals_ref[2:3, :1] / (jnp.full((1, 1), counted, jnp.int32).astype(f32) * width)
        for index in range(seq):
            qkv_out[:, index * qkv_width : (index + 1) * qkv_width] = qkv_ref[index].astype(f32)
        outs = []
        for index, (room, target) in enumerate(zip(passed_rooms, passed_outs)):
            ins[index].wait()
            copy = pltpu.make_async_copy(room, target, pass_sems.at[index, 1])
            copy.start()
            outs.append(copy)
        for number, room in enumerate(rooms):
            own, near_x, near_y, last_y, last_x = room
            total = totals[number // 2]
            base = 2 * (number % 2)
            for copy in copies[number]:
                copy.wait()
            rows = own.shape[1]
            tile = next(t for t in (64, 32, 16) if rows % t == 0)

            def step(index, carry):
                window = pl.ds(pl.multiple_of(index * tile, tile), tile)
                first = own[0, window, :].astype(f32) + near_x[window, :].astype(f32)
                second = own[1, window, :].astype(f32) + last_x[window, :].astype(f32)
                for other in range(ys - 1):
                    first = first + last_y[other, window, :].astype(f32)
                    second = second + near_y[other, window, :].astype(f32)
                total[base, window, :] = first
                total[base + 1, window, :] = second
                return carry

            lax.fori_loop(0, rows // tile, step, 0)
            target = gate_up_out.at[pl.ds(base, 2)] if number < 2 else down_out
            copy = pltpu.make_async_copy(total.at[pl.ds(base, 2)], target, stores.at[number])
            copy.start()
            outs.append(copy)
        for copy in outs:
            copy.wait()

    def rooms(half):
        return [
            pltpu.VMEM((2,) + half, low),
            pltpu.VMEM(half, low),
            pltpu.VMEM((ys - 1,) + half, low),
            pltpu.VMEM((ys - 1,) + half, low),
            pltpu.VMEM(half, low),
        ]

    return pl.pallas_call(
        kernel,
        name="last_sums",
        out_shape=[
            jax.ShapeDtypeStruct((4,) + gate_half, f32),
            jax.ShapeDtypeStruct((2,) + down_half, f32),
            jax.ShapeDtypeStruct(qkv_shape, f32),
            jax.ShapeDtypeStruct((1, lanes_each), f32),
            jax.ShapeDtypeStruct((1, lanes_each), f32),
            jax.ShapeDtypeStruct((KCONV, lanes_each), f32),
            jax.ShapeDtypeStruct((1, 1), f32),
        ]
        + [jax.ShapeDtypeStruct(array.shape, array.dtype) for array in passed],
        in_specs=[ANY] * 15 + [VMEM] * 2 + [SMEM] + [ANY] * 3,
        out_specs=[ANY] * 2 + [VMEM] * 5 + [ANY] * 3,
        scratch_shapes=[pltpu.VMEM((4,) + gate_half, f32), pltpu.VMEM((2,) + down_half, f32)]
        + [pltpu.VMEM(array.shape, array.dtype) for array in passed]
        + rooms(gate_half) * 2
        + rooms(down_half)
        + [
            pltpu.SemaphoreType.DMA((3, 1 + seq)),
            pltpu.SemaphoreType.DMA((3,)),
            pltpu.SemaphoreType.DMA((3, 2)),
        ],
        compiler_params=pltpu.CompilerParams(vmem_limit_bytes=VMEM_LIMIT),
    )(*operands, qkv_total, totals, lengths, *passed)


def body(
    inputs,
    segment_ids,
    valid_lengths,
    teacher,
    w_qkv,
    conv_weight,
    w_out,
    norm_gain,
    w_gate_up,
    w_down,
    mlp_gain,
):
    seq_parts = lax.axis_size("seq")
    tok_count = inputs.shape[1]
    model_width = inputs.shape[2]
    length = tok_count * seq_parts
    head_count = H // seq_parts
    qkv_width = head_count * (2 * FEAT + DV)
    rows_low = inputs[0]
    gain_lanes = norm_gain.shape[0]
    qkv_rows = w_qkv
    if qkv_width % 128:
        qkv_rows = w_qkv.reshape(w_qkv.shape[0], seq_parts, qkv_width).transpose(1, 0, 2)
    gate_up_low = w_gate_up.swapaxes(1, 2)
    segments = segment_ids
    (
        attended,
        _,
        gain_rows,
        qkv_columns,
        out_rows,
        hidden_low,
        sorted_columns,
        mixer_low,
        mixed_values,
        head_outputs,
        order,
        final_low,
        residual_error,
        energy,
        normed_all,
        gate_all,
        up_all,
        active_all,
        down_part,
        gate_up_part,
    ) = forward_pass(
        rows_low,
        qkv_rows,
        w_out,
        norm_gain,
        mlp_gain,
        segments,
        conv_weight,
        teacher[0],
        w_down,
        valid_lengths,
        gate_up_low,
    )
    (
        attended_grad,
        mix_back,
        gain_two_terms,
        gate_terms,
        up_terms,
        down_terms,
        gate_from_x,
        gate_from_y,
        down_from_x,
        down_from_y,
    ) = feed_back(
        residual_error,
        attended,
        gain_rows,
        gate_up_part,
        down_part,
        gate_all,
        up_all,
        active_all,
        normed_all,
    )
    inputs_grad, totals, gate, up, down, qkv_total, out_total = mixer_back(
        mix_back,
        attended_grad,
        rows_low,
        gain_rows,
        out_rows.reshape(head_count * DV, model_width),
        qkv_columns.reshape(model_width, qkv_width),
        hidden_low,
        sorted_columns,
        mixer_low,
        mixed_values,
        head_outputs,
        segments,
        conv_weight,
        order,
        gain_two_terms,
        energy,
        (gate_terms, gate_from_x, gate_from_y),
        (up_terms,),
        (down_terms, down_from_x, down_from_y),
    )
    (
        grad_w_gate_up,
        grad_w_down,
        grad_w_qkv,
        grad_norm_gain,
        grad_mlp_gain,
        grad_conv,
        mean_loss,
        grad_w_out,
        inputs_grad,
        outputs,
    ) = last_sums(
        gate, up, down, qkv_total, totals, valid_lengths, out_total, inputs_grad, final_low, w_qkv.shape
    )
    return (
        outputs[None],
        inputs_grad[None],
        mean_loss.reshape(()),
        grad_w_qkv,
        grad_conv,
        grad_w_out,
        grad_norm_gain.reshape(norm_gain.shape),
        grad_w_gate_up.reshape(gate_up_low.shape).swapaxes(1, 2),
        grad_w_down.reshape(w_down.shape),
        grad_mlp_gain.reshape(mlp_gain.shape),
    )


def solution(mesh):
    in_specs = (
        P("wt", "seq", None),
        P("wt", None),
        P(),
        P("wt", "seq", None),
        P(("seq", "wt"), None),
        P(None, "seq"),
        P(("seq", "wt"), None),
        P(("seq", "wt")),
        P(None, "seq", "wt"),
        P("wt", "seq"),
        P(("seq", "wt")),
    )
    out_specs = (
        P("wt", "seq", None),
        P("wt", "seq", None),
        P(),
        P(("seq", "wt"), None),
        P(None, ("seq", "wt")),
        P(("seq", "wt"), None),
        P(("seq", "wt")),
        P(None, "seq", "wt"),
        P("wt", "seq"),
        P(("seq", "wt")),
    )
    return jax.shard_map(body, mesh=mesh, in_specs=in_specs, out_specs=out_specs, check_vma=False)
```

```python
from functools import partial

import jax
import jax.numpy as jnp
from jax import lax
from jax.experimental import pallas as pl
from jax.experimental.pallas import tpu as pltpu
from jax.sharding import PartitionSpec as P

H = 16
FEAT = 16
KCONV = 3
DV = 128


epsilon = 1e-05


def rms_norm(values, gain_vector):
    inverse_root = lax.rsqrt(jnp.mean(values * values, axis=-1, keepdims=True) + epsilon)
    return values * inverse_root * gain_vector


def contract_last(former, latter):
    return lax.dot_general(
        former, latter, (((1,), (1,)), ((), ())), preferred_element_type=jnp.float32
    )


def contract_first(former, latter):
    return lax.dot_general(
        former, latter, (((0,), (0,)), ((), ())), preferred_element_type=jnp.float32
    )


def gated_unit(gate_in, up_in):
    return jax.nn.silu(gate_in) * up_in


MESH = pl.DeviceIdType.MESH
VMEM = pl.BlockSpec(memory_space=pltpu.VMEM)
ANY = pl.BlockSpec(memory_space=pl.ANY)
SMEM = pl.BlockSpec(memory_space=pltpu.SMEM)
VMEM_LIMIT = 67043328


class Place:
    def __init__(self, seq, wt):
        self.seq, self.wt = seq, wt
        self.ys, self.zs = seq // 2, wt // 2
        self.s, self.w = lax.axis_index("seq"), lax.axis_index("wt")
        self.y, self.x = lax.div(self.s, 2), lax.rem(self.s, 2)
        self.z, self.c = lax.div(self.w, 2), lax.rem(self.w, 2)

    def across(self):
        return (self.y * 2 + 1 - self.x, self.w)

    def beside(self, step):
        return lax.rem(self.y + step, self.ys)

    def column(self, y):
        return (y * 2 + self.x, self.w)

    def partner(self):
        return (self.s, self.z * 2 + 1 - self.c)

    def level(self, z):
        return (self.s, z * 2 + self.c)

    def meet(self, square, line):
        barrier = pltpu.get_barrier_semaphore()
        count = 0
        if square:
            for step in range(1, self.seq):
                device = (lax.rem(self.s + step, self.seq), self.w)
                pl.semaphore_signal(barrier, inc=1, device_id=device, device_id_type=MESH)
                count += 1
        if line:
            for step in range(1, self.wt):
                device = (self.s, lax.rem(self.w + step, self.wt))
                pl.semaphore_signal(barrier, inc=1, device_id=device, device_id_type=MESH)
                count += 1
        pl.semaphore_wait(barrier, count)


def send(source, target, leaving, arriving, device):
    return pltpu.make_async_remote_copy(
        src_ref=source,
        dst_ref=target,
        send_sem=leaving,
        recv_sem=arriving,
        device_id=device,
        device_id_type=MESH,
    )


def add_into(target, sources):
    if len(target.shape) == 3:
        for index in range(target.shape[0]):
            add_into(target.at[index], [source.at[index] for source in sources])
        return
    rows = target.shape[0]
    tile = next(t for t in (64, 32, 16, 8, rows) if rows % t == 0)

    def step(index, carry):
        window = pl.ds(pl.multiple_of(index * tile, tile), tile)
        total = sources[0][window, :].astype(jnp.float32)
        for source in sources[1:]:
            total = total + source[window, :].astype(jnp.float32)
        target[window, :] = total.astype(target.dtype)
        return carry

    lax.fori_loop(0, rows // tile, step, 0)


class SquareGather:
    @staticmethod
    def semaphores(seq):
        return [
            pltpu.SemaphoreType.DMA((2 + seq // 2,)),
            pltpu.SemaphoreType.DMA((seq // 2, 3)),
            pltpu.SemaphoreType.DMA((seq, 2)),
        ]

    def __init__(self, at, view, own, sems):
        self.at, self.view, self.own = at, view, own
        self.over_x, self.over_y, self.got = sems
        self.sent = []

    def go(self, copy):
        copy().start()
        self.sent.append(copy)

    def own_x(self, half):
        at = self.at
        target = self.view(at.s, half)
        return send(self.own(half), target, self.over_x.at[half], self.got.at[at.s, half], at.across())

    def own_y(self, step, half):
        at = self.at
        target, device = self.view(at.s, half), at.column(at.beside(step))
        return send(self.own(half), target, self.over_y.at[step, half], self.got.at[at.s, half], device)

    def pass_y(self, step):
        at = self.at
        s = at.y * 2 + 1 - at.x
        slot, device = self.view(s, 0), at.column(at.beside(step))
        return send(slot, slot, self.over_y.at[step, 2], self.got.at[s, 0], device)

    def pass_x(self, step):
        s = self.at.beside(step) * 2 + self.at.x
        slot = self.view(s, 1)
        return send(slot, slot, self.over_x.at[1 + step], self.got.at[s, 1], self.at.across())

    def wait(self, s, half):
        slot = self.view(s, half)
        send(slot, slot, self.over_x.at[0], self.got.at[s, half], self.at.across()).wait_recv()

    def start(self):
        for half in range(2):
            self.go(partial(self.own_x, half))
            for step in range(1, self.at.ys):
                self.go(partial(self.own_y, step, 1 - half))

    def relay(self):
        at = self.at
        self.wait(at.y * 2 + 1 - at.x, 0)
        for step in range(1, at.ys):
            self.go(partial(self.pass_y, step))
        for step in range(1, at.ys):
            self.wait(at.beside(step) * 2 + at.x, 1)
            self.go(partial(self.pass_x, step))

    def direct(self):
        at = self.at
        self.wait(at.y * 2 + 1 - at.x, 1)
        for step in range(1, at.ys):
            self.wait(at.beside(step) * 2 + at.x, 0)

    def relayed(self):
        at = self.at
        for step in range(1, at.ys):
            y = at.beside(step)
            self.wait(y * 2 + 1 - at.x, 0)
            self.wait(y * 2 + 1 - at.x, 1)
        for copy in self.sent:
            copy().wait_send()

    def finish(self):
        self.direct()
        self.relayed()


class SquareSum:
    @staticmethod
    def scratch(seq, half_shape):
        ys = seq // 2
        return [
            pltpu.VMEM((ys,) + half_shape, jnp.bfloat16),
            pltpu.VMEM((ys, 2) + half_shape, jnp.bfloat16),
            pltpu.VMEM((ys,) + half_shape, jnp.bfloat16),
            pltpu.VMEM(half_shape, jnp.bfloat16),
            pltpu.VMEM((ys,) + half_shape, jnp.bfloat16),
            pltpu.VMEM(half_shape, jnp.bfloat16),
            pltpu.SemaphoreType.DMA((ys, 2, 2)),
            pltpu.SemaphoreType.DMA((ys, 3, 2)),
        ]

    def __init__(self, at, part, scratch):
        self.at, self.part = at, part
        self.from_x, self.from_y, self.last_y, self.last_x, self.sum_y, self.sum_x, self.xs, self.yss = scratch
        self.sent = []

    def go(self, source, target, leaving, arriving, device):
        copy = send(source, target, leaving, arriving, device)
        copy.start()
        self.sent.append(copy)

    def wait(self, slot, leaving, arriving):
        send(slot, slot, leaving, arriving, self.at.across()).wait_recv()

    def start(self):
        at = self.at
        for y in range(at.ys):
            self.go(
                self.part(y * 2 + 1 - at.x, 0),
                self.from_x.at[y],
                self.xs.at[y, 0, 0],
                self.xs.at[y, 0, 1],
                at.across(),
            )
        for step in range(1, at.ys):
            y = at.beside(step)
            for x in range(2):
                self.go(
                    self.part(y * 2 + x, 1),
                    self.from_y.at[at.y, x],
                    self.yss.at[step, x, 0],
                    self.yss.at[at.y, x, 1],
                    at.column(y),
                )

    def relay(self):
        at = self.at
        for step in range(1, at.ys):
            y = at.beside(step)
            self.wait(self.from_x.at[y], self.xs.at[y, 0, 0], self.xs.at[y, 0, 1])
            add_into(self.sum_y.at[y], [self.part(y * 2 + at.x, 0), self.from_x.at[y]])
            self.go(
                self.sum_y.at[y],
                self.last_y.at[at.y],
                self.yss.at[step, 2, 0],
                self.yss.at[at.y, 2, 1],
                at.column(y),
            )
        terms = []
        for step in range(1, at.ys):
            y = at.beside(step)
            for x in range(2):
                self.wait(self.from_y.at[y, x], self.yss.at[step, x, 0], self.yss.at[y, x, 1])
            terms.append(self.from_y.at[y, 1 - at.x])
        add_into(self.sum_x, [self.part(at.y * 2 + 1 - at.x, 1)] + terms)
        self.go(self.sum_x, self.last_x, self.xs.at[0, 1, 0], self.xs.at[0, 1, 1], at.across())

    def finish(self, total):
        at = self.at
        self.wait(self.from_x.at[at.y], self.xs.at[0, 0, 0], self.xs.at[at.y, 0, 1])
        terms = [self.part(at.s, 0), self.from_x.at[at.y]]
        for step in range(1, at.ys):
            y = at.beside(step)
            self.wait(self.last_y.at[y], self.yss.at[step, 2, 0], self.yss.at[y, 2, 1])
            terms.append(self.last_y.at[y])
        add_into(total(0), terms)
        self.wait(self.last_x, self.xs.at[0, 1, 0], self.xs.at[0, 1, 1])
        terms = [self.part(at.s, 1), self.last_x]
        for step in range(1, at.ys):
            terms.append(self.from_y.at[at.beside(step), at.x])
        add_into(total(1), terms)
        for copy in self.sent:
            copy.wait_send()


class LineGather:
    @staticmethod
    def semaphores(wt, cuts=1):
        return [pltpu.SemaphoreType.DMA((5, wt // 2, cuts))]

    def __init__(self, at, view, sems):
        self.at, self.view, self.sems = at, view, sems[0]
        self.cuts = self.sems.shape[2]

    def cut(self, ref, part):
        if self.cuts == 1:
            return ref
        rows = ref.shape[0] // self.cuts
        return ref.at[pl.ds(part * rows, rows)]

    def hop(self, z, part, kind, device, source):
        slot = self.view(z * 2 + self.at.c)
        source = slot if source is None else source
        arriving = 4 if kind == 2 else 3
        return send(
            self.cut(source, part),
            self.cut(slot, part),
            self.sems.at[kind, z, part],
            self.sems.at[arriving, z, part],
            device,
        )

    def up(self, z, part, source=None):
        return self.hop(z, part, 0, self.at.level(self.at.z + 1), source)

    def down(self, z, part, source=None):
        return self.hop(z, part, 1, self.at.level(self.at.z - 1), source)

    def over(self, z, part, source=None):
        return self.hop(z, part, 2, self.at.partner(), source)

    def start(self, source=None):
        at = self.at
        for part in range(self.cuts):

            @pl.when(at.z + 1 < at.zs)
            def _():
                self.up(at.z, part, source).start()

            @pl.when(at.z > 0)
            def _():
                self.down(at.z, part, source).start()

            self.over(at.z, part, source).start()

    def step(self, index):
        at = self.at
        below, above = at.z - 1 - index, at.z + 1 + index
        for part in range(self.cuts):

            @pl.when(below >= 0)
            def _():
                self.up(below, part).wait_recv()

                @pl.when(at.z + 1 < at.zs)
                def _():
                    self.up(below, part).start()

                self.over(below, part).start()

            @pl.when(above < at.zs)
            def _():
                self.down(above, part).wait_recv()

                @pl.when(at.z > 0)
                def _():
                    self.down(above, part).start()

                self.over(above, part).start()

    def wait_over(self, z):
        for part in range(self.cuts):
            slot = self.cut(self.view(z * 2 + 1 - self.at.c), part)
            send(slot, slot, self.sems.at[2, z, part], self.sems.at[4, z, part], self.at.partner()).wait_recv()

    def finish(self):
        for z in range(self.at.zs):
            self.wait_over(z)
        self.sent()

    def sent(self):
        at = self.at
        for z in range(at.zs):
            for part in range(self.cuts):

                @pl.when((at.z >= z) & (at.z + 1 < at.zs))
                def _():
                    self.up(z, part).wait_send()

                @pl.when((at.z <= z) & (at.z > 0))
                def _():
                    self.down(z, part).wait_send()

                self.over(z, part).wait_send()


def remote_call(kernel, name, number, outs, scratch, *operands, in_specs=None, out_specs=None):
    return pl.pallas_call(
        kernel,
        name=name,
        out_shape=outs,
        in_specs=[VMEM] * len(operands) if in_specs is None else in_specs,
        out_specs=jax.tree.map(lambda _: VMEM, outs) if out_specs is None else out_specs,
        scratch_shapes=scratch,
        compiler_params=pltpu.CompilerParams(
            collective_id=number, has_side_effects=True, vmem_limit_bytes=VMEM_LIMIT
        ),
    )(*operands)


def write_order(ref, heads):
    head_width, value_width = 2 * FEAT + DV, heads * DV

    def step(index, carry):
        window = pl.ds(pl.multiple_of(index * 32, 32), 32)
        shape = (32, ref.shape[1])
        column = index * 32 + lax.broadcasted_iota(jnp.int32, shape, 0)
        head = lax.div(column, head_width)
        place = lax.rem(column, head_width)
        target = jnp.where(
            place < FEAT,
            value_width + head * FEAT + place,
            jnp.where(
                place < 2 * FEAT, value_width + 128 + head * FEAT + place - FEAT, head * DV + place - 2 * FEAT
            ),
        )
        hit = target == lax.broadcasted_iota(jnp.int32, shape, 1)
        ref[window, :] = hit.astype(jnp.float32).astype(jnp.bfloat16)
        return carry

    lax.fori_loop(0, ref.shape[0] // 32, step, 0)


def tap_marks(segment_column):
    segment = segment_column[:, :1]
    place = lax.broadcasted_iota(jnp.int32, segment_column.shape, 0)[:, :1]
    marks = [None]
    for tap in range(1, KCONV):
        same = (pltpu.roll(segment_column[...], tap, 0)[:, :1] == segment) & (place >= tap)
        marks.append(same.astype(jnp.float32))
    return marks


def early_rows(units):
    return units * 3 // 4 // 16 * 16


class LinePieces:
    @staticmethod
    def scratch(wt, shape, pieces):
        zs = wt // 2
        return [pltpu.VMEM((zs,) + shape, jnp.bfloat16)] * 3 + [pltpu.SemaphoreType.DMA((6, zs, pieces))]

    def __init__(self, at, part, scratch, order=None):
        self.at, self.part, self.order = at, part, order
        self.pair, self.below, self.above, self.sems = scratch
        self.pieces = self.sems.shape[2]
        self.width = self.pair.shape[-1] // self.pieces

    def cut(self, ref, piece):
        if len(ref.shape) == 3:
            return ref.at[piece]
        return ref.at[:, self.columns(piece)]

    def columns(self, piece):
        block = piece if self.order is None else self.order(piece)
        return pl.ds(pl.multiple_of(block * self.width, self.width), self.width)

    def own(self, z, piece):
        return self.cut(self.part(z * 2 + self.at.c), piece)

    def over(self, z, piece):
        return send(
            self.cut(self.part(z * 2 + 1 - self.at.c), piece),
            self.cut(self.pair.at[z], piece),
            self.sems.at[0, z, piece],
            self.sems.at[1, z, piece],
            self.at.partner(),
        )

    def up(self, z, piece):
        return send(
            self.own(z, piece),
            self.cut(self.below.at[z], piece),
            self.sems.at[2, z, piece],
            self.sems.at[3, z, piece],
            self.at.level(self.at.z + 1),
        )

    def down(self, z, piece):
        return send(
            self.own(z, piece),
            self.cut(self.above.at[z], piece),
            self.sems.at[4, z, piece],
            self.sems.at[5, z, piece],
            self.at.level(self.at.z - 1),
        )

    def terms(self, z, piece):
        self.over(z, piece).wait_recv()
        return [self.own(z, piece), self.cut(self.pair.at[z], piece)]

    def ends(self, z, piece):
        at = self.at

        @pl.when((at.z == 0) & (z > 0))
        def _():
            add_into(self.own(z, piece), self.terms(z, piece))
            self.up(z, piece).start()

        @pl.when((at.z == at.zs - 1) & (z < at.zs - 1))
        def _():
            add_into(self.own(z, piece), self.terms(z, piece))
            self.down(z, piece).start()

    def offer(self, piece):
        zs = self.at.zs
        for index in range(zs // 2):
            self.over(index, piece).start()
            self.over(zs - 1 - index, piece).start()

    def launch(self, piece, near):
        self.ends(jnp.where(self.at.z == 0, self.at.zs - 1 - near, near), piece)

    def launch_all(self, near):
        zs = self.at.zs

        def step(index, carry):
            self.launch(lax.rem(index, self.pieces), near + lax.div(index, self.pieces))
            return carry

        lax.fori_loop(0, (zs - 1 - near) * self.pieces, step, 0)

    def pass_on(self, index, fill=None, begin=0, end=None):
        at = self.at
        upper = at.z * 2 >= at.zs
        high, low = index, at.zs - 1 - index

        def lower(piece, when):
            @pl.when((at.z > low) & (at.z < at.zs - 1) & when)
            def _():
                terms = self.terms(low, piece)
                self.down(low, piece).wait_recv()
                add_into(self.own(low, piece), terms + [self.cut(self.above.at[low], piece)])
                self.down(low, piece).start()

        def step(piece, carry):
            lower(piece, upper)

            @pl.when((at.z < high) & (at.z > 0))
            def _():
                terms = self.terms(high, piece)
                self.up(high, piece).wait_recv()
                add_into(self.own(high, piece), terms + [self.cut(self.below.at[high], piece)])
                self.up(high, piece).start()

            lower(piece, jnp.logical_not(upper))
            if fill is not None:
                fill(piece, self.pieces)
            return carry

        end = self.pieces if end is None else end
        if end - begin == 1:
            step(begin, 0)
        else:
            lax.fori_loop(begin, end, step, 0)

    def finish(self, total, done=None):
        at = self.at

        def step(piece, carry):
            terms = self.terms(at.z, piece)
            below, above = self.cut(self.below.at[at.z], piece), self.cut(self.above.at[at.z], piece)

            @pl.when(at.z == 0)
            def _():
                self.down(at.z, piece).wait_recv()
                add_into(self.cut(total, piece), terms + [above])

            @pl.when(at.z == at.zs - 1)
            def _():
                self.up(at.z, piece).wait_recv()
                add_into(self.cut(total, piece), terms + [below])

            @pl.when((at.z > 0) & (at.z < at.zs - 1))
            def _():
                self.up(at.z, piece).wait_recv()
                self.down(at.z, piece).wait_recv()
                add_into(self.cut(total, piece), terms + [below, above])

            if done is not None:
                done(piece)
            for z in range(at.zs):

                @pl.when(at.z < z)
                def _():
                    self.up(z, piece).wait_send()

                @pl.when(at.z > z)
                def _():
                    self.down(z, piece).wait_send()

                self.over(z, piece).wait_send()
            return carry

        lax.fori_loop(0, self.pieces, step, 0)


class SquareTerms:
    @staticmethod
    def semaphores(seq):
        return [pltpu.SemaphoreType.DMA((seq // 2, 2)), pltpu.SemaphoreType.DMA((seq // 2, 2, 2))]

    @staticmethod
    def scratch(seq, half_shape):
        ys = seq // 2
        return [
            pltpu.VMEM((ys,) + half_shape, jnp.bfloat16),
            pltpu.VMEM(half_shape, jnp.bfloat16),
            pltpu.SemaphoreType.DMA((ys + 1, 2)),
        ]

    def __init__(self, at, terms, from_x, from_y, sems=None, lasts=None, scratch=None):
        self.at, self.terms, self.from_x, self.from_y = at, terms, from_x, from_y
        if sems is not None:
            self.xs, self.ys = sems
        if scratch is not None:
            self.last_y, self.last_x = lasts
            self.sum_y, self.sum_x, self.last = scratch

    def first_x(self, y):
        at = self.at
        return send(
            self.terms(y * 2 + 1 - at.x, 0), self.from_x.at[y], self.xs.at[y, 0], self.xs.at[y, 1], at.across()
        )

    def first_y(self, step, x):
        at = self.at
        y = at.beside(step)
        return send(
            self.terms(y * 2 + x, 1),
            self.from_y.at[at.y, x],
            self.ys.at[step, x, 0],
            self.ys.at[at.y, x, 1],
            at.column(y),
        )

    def first_start(self):
        for y in range(self.at.ys):
            self.first_x(y).start()
        for step in range(1, self.at.ys):
            for x in range(2):
                self.first_y(step, x).start()

    def first_wait(self):
        at = self.at
        for y in range(at.ys):
            self.first_x(y).wait()
        for step in range(1, at.ys):
            y = at.beside(step)
            for x in range(2):
                self.first_y(step, x).wait_send()
                slot = self.from_y.at[y, x]
                send(slot, slot, self.ys.at[step, x, 0], self.ys.at[y, x, 1], at.across()).wait_recv()

    def second_y(self, step):
        at = self.at
        y = at.beside(step)
        return send(
            self.sum_y.at[y], self.last_y.at[at.y], self.last.at[step, 0], self.last.at[at.y, 1], at.column(y)
        )

    def second_x(self):
        at = self.at
        return send(self.sum_x, self.last_x, self.last.at[at.ys, 0], self.last.at[at.ys, 1], at.across())

    def second_pairs(self, rooms=None):
        at = self.at
        pairs = [(self.terms(at.y * 2 + 1 - at.x, 1), self.sum_x)]
        for step in range(1, at.ys):
            y = at.beside(step)
            pairs.append((self.terms(y * 2 + at.x, 0), self.sum_y.at[y]))
            if rooms is not None:
                pairs.append((self.from_x.at[y], rooms[0].at[step - 1]))
                pairs.append((self.from_y.at[y, 1 - at.x], rooms[1].at[step - 1]))
        return pairs

    def second_add(self, rooms=None):
        at = self.at
        terms = [self.sum_x]
        for step in range(1, at.ys):
            y = at.beside(step)
            near = self.from_x.at[y] if rooms is None else rooms[0].at[step - 1]
            add_into(self.sum_y.at[y], [self.sum_y.at[y], near])
            terms.append(self.from_y.at[y, 1 - at.x] if rooms is None else rooms[1].at[step - 1])
        add_into(self.sum_x, terms)

    def second_go(self):
        for step in range(1, self.at.ys):
            self.second_y(step).start()
        self.second_x().start()

    def second_wait(self):
        at = self.at
        for step in range(1, at.ys):
            self.second_y(step).wait_send()
            y = at.beside(step)
            slot = self.last_y.at[y]
            send(slot, slot, self.last.at[step, 0], self.last.at[y, 1], at.across()).wait_recv()
        self.second_x().wait()


def norm_back(rows, load, store, gain, terms):
    def step(index, carry):
        window = pl.ds(pl.multiple_of(index * 16, 16), 16)
        values, incoming, base = load(window)
        root = lax.rsqrt(jnp.mean(values * values, axis=-1, keepdims=True) + epsilon)
        scaled = incoming * gain
        share = jnp.mean(values * scaled, axis=-1, keepdims=True)
        store(window, base + root * scaled - values * (root * root * root * share))
        term = incoming * values * root
        terms[...] += term[:8] + term[8:]
        return carry

    lax.fori_loop(0, rows // 16, step, 0)


class Exchange:
    def __init__(self, at, shard, everyone, gather_sems, local, sums, first, second):
        self.at, self.sums, self.first, self.second = at, sums, first, second
        count = shard.shape[0]
        slot = lambda w: everyone.at[pl.ds(pl.multiple_of(w * count, count), count)]
        self.gather = LineGather(at, slot, gather_sems)
        self.gather.start(shard)
        own = pltpu.make_async_copy(shard, slot(at.w), local)
        own.start()
        own.wait()
        self.last, self.ahead = 2 * (at.zs - 1), 0

    def step_ahead(self):
        self.gather.step(0)
        self.ahead = 1

    def level(self, index):
        at = self.at
        far, side = lax.div(index + 1, 2), lax.rem(index, 2)
        z = at.z + jnp.where(side == 1, -far, far)
        return far, side, z, (z >= 0) & (z < at.zs)

    def arrive(self, index):
        far, side, z, valid = self.level(index)

        @pl.when((side == 1) & (far > self.ahead))
        def _():
            self.gather.step(far - 1)

        @pl.when(valid)
        def _():
            self.gather.wait_over(z)
            self.first(z)

        return z, valid

    def put(self, z, begin, end):
        def step(piece, inner):
            self.second(z, piece)
            self.sums.over(z, piece).start()

            @pl.when(piece > begin)
            def _():
                self.sums.ends(z, piece - 1)

            return inner

        lax.fori_loop(begin, end, step, 0)
        self.sums.ends(z, end - 1)

    def whole(self, total, fill):
        at, sums = self.at, self.sums

        def turn(index, carry):
            z, valid = self.arrive(index)

            @pl.when(valid)
            def _():
                self.put(z, 0, sums.pieces)

            return carry

        lax.fori_loop(0, self.last + 1, turn, 0)
        fill(None, sums.pieces)
        for index in range(2, at.zs):
            sums.pass_on(index, fill if index == 2 else None)
        sums.finish(total)
        self.gather.sent()

    def by_columns(self, total, direct, relayed, near):
        at, sums = self.at, self.sums
        begin = min(3, self.last)

        def turn(index, carry):
            z, valid = self.arrive(index)

            @pl.when(index == begin)
            def _():
                direct()

            @pl.when(valid & (index >= begin))
            def _():
                self.put(z, 0, near)

            return carry

        lax.fori_loop(0, self.last + 1, turn, 0)

        def earlier(index, carry):
            _, _, z, valid = self.level(index)

            @pl.when(valid)
            def _():
                self.put(z, 0, near)

            return carry

        lax.fori_loop(1, begin, earlier, 0)
        if at.zs > 2:
            sums.pass_on(2, None, 0, near)
        relayed()

        def over(index, carry):
            _, _, z, valid = self.level(self.last - index)

            @pl.when(valid)
            def _():
                for piece in range(near, sums.pieces):
                    self.second(z, piece)
                    sums.over(z, piece).start()

            return carry

        lax.fori_loop(0, self.last, over, 0)

        def start(index, carry):
            _, _, z, valid = self.level(self.last - index)

            @pl.when(valid)
            def _():
                for piece in range(near, sums.pieces):
                    sums.ends(z, piece)

            return carry

        lax.fori_loop(0, self.last, start, 0)
        self.put(at.z, 0, sums.pieces)
        for index in range(3, at.zs):
            sums.pass_on(index, None, 0, near)
        for index in range(at.zs - 1, 1, -1):
            sums.pass_on(index, None, near, sums.pieces)
        sums.finish(total)
        self.gather.sent()


PIECES = 2


def feed_forward(at, sizes, inputs, outputs, scratch):
    count, width, units, block, columns = sizes
    early, half, zs, seq = early_rows(units), units // 2, at.zs, at.seq
    normed_ref, attended_ref, teacher_ref, length_ref, gate_shard_ref, shard_ref = inputs
    (final_out, error_out, energy_out), outputs = outputs[:3], outputs[3:]
    normed_out, gate_out, up_out, active_out, down_out, gates_out = outputs
    everyone, gates, downs, gate_all, up_all, active_all, parts, total = scratch[:8]
    gather_sems, sum_scratch, late_sems, square_sems, (local, outgoing) = (
        scratch[8:9],
        scratch[9:13],
        scratch[13:16],
        scratch[16:19],
        scratch[19:],
    )
    late = SquareGather(
        at,
        lambda s, h: gates.at[
            h, pl.ds(early, units - early), pl.ds(pl.multiple_of(s * block, block), block)
        ],
        lambda h: gate_shard_ref.at[h, pl.ds(early, units - early)],
        late_sems,
    )
    weights = SquareGather(
        at,
        lambda s, h: downs.at[
            pl.ds(h * half, half), pl.ds(pl.multiple_of(s * columns, columns), columns)
        ],
        lambda h: shard_ref.at[pl.ds(h * half, half)],
        square_sems,
    )
    ys = seq // 2

    def column_block(piece):
        if isinstance(piece, int):
            step = 0 if piece < 2 else piece - 1 if piece <= ys else piece - ys
            return at.beside(step) * 2 + (1 - at.x if piece == 1 or piece > ys else at.x)
        step = jnp.where(piece < 2, 0, jnp.where(piece <= ys, piece - 1, piece - ys))
        other = (piece == 1) | (piece > ys)
        return at.beside(step) * 2 + jnp.where(other, 1 - at.x, at.x)

    sums = LinePieces(
        at,
        lambda w: parts.at[pl.ds(pl.multiple_of(w * count, count), count)],
        sum_scratch,
        column_block,
    )
    down_store = pltpu.make_async_copy(downs, down_out, local.at[2])
    gates_store = pltpu.make_async_copy(gates, gates_out, local.at[0])

    def direct():
        weights.relay()
        weights.direct()

    def relayed():
        weights.relayed()
        down_store.start()

    def rows(z):
        return pl.ds(pl.multiple_of(z * 2 * count, 2 * count), 2 * count)

    def stores(z):
        return [
            pltpu.make_async_copy(source.at[rows(z)], target.at[rows(z)], outgoing.at[index, z])
            for index, (source, target) in enumerate(
                ((everyone, normed_out), (gate_all, gate_out), (up_all, up_out), (active_all, active_out))
            )
        ]

    def first(z):
        here = everyone[rows(z), :]
        gate = contract_last(here, gates[0])
        up = contract_last(here, gates[1])
        gate_all[rows(z), :] = gate
        up_all[rows(z), :] = up
        active_all[rows(z), :] = gated_unit(gate, up).astype(jnp.bfloat16)
        for copy in stores(z):
            copy.start()

    def second(z, piece):
        window = sums.columns(piece)
        parts[rows(z), window] = jnp.dot(
            active_all[rows(z), :], downs[:, window], preferred_element_type=jnp.float32
        ).astype(jnp.bfloat16)

    def run():
        work = Exchange(at, normed_ref, everyone, gather_sems, local.at[1], sums, first, second)
        late.relay()
        weights.start()
        own = pltpu.make_async_copy(
            shard_ref, downs.at[:, pl.ds(pl.multiple_of(at.s * columns, columns), columns)], local.at[3]
        )
        own.start()
        work.step_ahead()
        own.wait()
        late.finish()
        gates_store.start()
        work.by_columns(total, direct, relayed, ys + 1)
        energy_out[...] = jnp.zeros_like(energy_out)
        valid = length_ref[at.w]

        def finish_rows(index, carry):
            window = pl.ds(pl.multiple_of(index * 16, 16), 16)
            final = attended_ref[window, :] + total[window, :]
            final_out[window, :] = final.astype(jnp.bfloat16)
            place = at.s * count + index * 16 + lax.broadcasted_iota(jnp.int32, final.shape, 0)
            keep = (place < valid).astype(jnp.float32)
            error = (final - teacher_ref[window, :].astype(jnp.float32)) * keep
            error_out[window, :] = error
            squares = error * error
            energy_out[...] += 0.5 * (squares[:8] + squares[8:])
            return carry

        lax.fori_loop(0, count // 16, finish_rows, 0)
        down_store.wait()
        gates_store.wait()
        for z in range(zs):
            for copy in stores(z):
                copy.wait()

    return late.start, run


def forward_pass(tokens, qkv_rows, out_rows, norm_gain, mlp_gain, segments, taps, teacher, down, lengths, gate_up):
    seq, wt = lax.axis_size("seq"), lax.axis_size("wt")
    zs = wt // 2
    count, width = tokens.shape
    length = count * seq
    out_rank = out_rows.shape[0]
    heads = H // seq
    value_width = heads * DV
    qkv_width = value_width + 2 * FEAT * heads
    qkv_rank = width // (seq * wt)
    lanes_each = width // (seq * wt)
    units, block = gate_up.shape[1:]
    early = early_rows(units)
    rows_at_once = 256
    small = [
        tokens,
        qkv_rows,
        out_rows,
        norm_gain[None],
        mlp_gain[None],
        segments,
        taps,
        teacher,
    ]
    token_count = wt * count

    def kernel(*refs):
        (x_ref, qkv_ref, out_ref, first_gain, second_gain, segment_ref, tap_ref), refs = refs[:7], refs[7:]
        (teacher_ref, length_ref, gate_up_ref, down_ref), refs = refs[:4], refs[4:]
        (attended_out, normed_out, gain_rows), refs = refs[:3], refs[3:]
        (qkv_out, w_out_out, hidden_out, sorted_out, mixer_out, values_out, outputs_out, order_out), refs = (
            refs[:8],
            refs[8:],
        )
        feed_outputs, refs = refs[:9], refs[9:]
        (xs, qkvs, outs, gains_all, sorted_v, values_v, outputs_v), refs = refs[:7], refs[7:]
        (order_v, segment_column, tap_v, gain_ref), refs = refs[:4], refs[4:]
        sum_scratch, x_sems, gate_sems, refs = refs[:8], refs[8:11], refs[11:14], refs[14:]
        line_sems, refs = [refs[index : index + 1] for index in range(3)], refs[3:]
        (swap_q, swap_g, local, outgoing), feed_scratch = refs[:4], refs[4:]
        at = Place(seq, wt)
        gates_ref, parts, total = feed_scratch[1], feed_scratch[6], feed_scratch[7]
        hidden_v = parts.at[pl.ds(length, length)]
        mixer_v = feed_scratch[5].at[pl.ds(0, length), pl.ds(0, value_width)]
        gates_own = pltpu.make_async_copy(
            gate_up_ref, gates_ref.at[:, :, pl.ds(pl.multiple_of(at.s * block, block), block)], local.at[4]
        )
        gates_own.start()
        gain_ref[...] = jnp.zeros_like(gain_ref)
        gain_ref[0:1, :lanes_each] = first_gain[...].astype(jnp.float32)
        gain_ref[1:2, :lanes_each] = second_gain[...].astype(jnp.float32)
        late_start, feed = feed_forward(
            at,
            (count, width, units, block, down.shape[1]),
            (normed_out, attended_out, teacher_ref, length_ref, gate_up_ref, down_ref),
            feed_outputs,
            feed_scratch,
        )
        at.meet(True, True)
        half = count // 2
        gather_x = SquareGather(
            at,
            lambda s, h: xs.at[pl.ds(pl.multiple_of(s * count + h * half, half), half)],
            lambda h: x_ref.at[pl.ds(h * half, half)],
            x_sems,
        )
        gather_q = LineGather(at, lambda w: qkvs.at[:, w], line_sems[0])
        gather_g = LineGather(
            at, lambda w: gains_all.at[:, pl.ds(pl.multiple_of(w * 8, 8), 8)], line_sems[1]
        )
        gather_o = LineGather(at, lambda w: outs.at[w], line_sems[2])
        gates = SquareGather(
            at,
            lambda s, h: gates_ref.at[h, pl.ds(0, early), pl.ds(pl.multiple_of(s * block, block), block)],
            lambda h: gate_up_ref.at[h, pl.ds(0, early)],
            gate_sems,
        )
        gain_slot = pl.ds(pl.multiple_of(at.w * 8, 8), 8)

        def qkv_part(s):
            if len(qkv_ref.shape) == 3:
                return qkv_ref.at[s]
            return qkv_ref.at[:, pl.ds(pl.multiple_of(s * qkv_width, qkv_width), qkv_width)]

        swaps = []
        for step in range(1, seq):
            to = lax.rem(at.s + step, seq)
            swaps.append(
                send(gain_ref, gains_all.at[at.s, gain_slot], swap_g.at[step, 0], swap_g.at[at.s, 1], (to, at.w))
            )
            swaps.append(
                send(qkv_part(to), qkvs.at[at.s, at.w], swap_q.at[step, 0], swap_q.at[at.s, 1], (to, at.w))
            )
        for copy in swaps:
            copy.start()
        gather_x.start()
        own = [
            pltpu.make_async_copy(qkv_part(at.s), qkvs.at[at.s, at.w], local.at[0]),
            pltpu.make_async_copy(gain_ref, gains_all.at[at.s, gain_slot], local.at[1]),
            pltpu.make_async_copy(out_ref, outs.at[at.w], local.at[2]),
            pltpu.make_async_copy(x_ref, xs.at[pl.ds(pl.multiple_of(at.s * count, count), count)], local.at[3]),
        ]
        for copy in own:
            copy.start()
        for copy in own:
            copy.wait()
        gather_o.start()
        for step in range(1, seq):
            s = lax.rem(at.s + step, seq)
            slot = gains_all.at[s, gain_slot]
            send(slot, slot, swap_g.at[step, 0], swap_g.at[s, 1], at.across()).wait_recv()
            slot = qkvs.at[s, at.w]
            send(slot, slot, swap_q.at[step, 0], swap_q.at[s, 1], at.across()).wait_recv()
        gather_g.start()
        gather_q.start()
        tap_v[...] = tap_ref[...].astype(jnp.float32)
        segment_row = segment_ref[...].astype(jnp.float32)
        segment_column[...] = jnp.broadcast_to(segment_row, (128, length)).T
        write_order(order_v, heads)
        gather_x.relay()
        gates.start()
        for index in range(zs - 1):
            gather_g.step(index)
            gather_q.step(index)
        gather_o.step(0)
        gather_g.finish()

        device_rows = gains_all[...].reshape(seq * wt * 8, 128).astype(jnp.bfloat16)
        gain_rows[...] = jnp.zeros_like(gain_rows)

        def spread_gains(index, carry):
            begin = pl.multiple_of(index * 256, 256)
            lane = lax.broadcasted_iota(jnp.int32, (128, 256), 0)
            column = begin + lax.broadcasted_iota(jnp.int32, (128, 256), 1)
            copied = jnp.dot(
                device_rows,
                (lane == lax.rem(column, lanes_each)).astype(jnp.float32).astype(jnp.bfloat16),
                preferred_element_type=jnp.float32,
            )
            row = lax.broadcasted_iota(jnp.int32, copied.shape, 0)
            column = begin + lax.broadcasted_iota(jnp.int32, copied.shape, 1)
            first_row = lax.div(column, lanes_each) * 8
            for number in range(2):
                gain_rows[number : number + 1, pl.ds(begin, 256)] = jnp.sum(
                    jnp.where(row == first_row + number, copied, 0.0), axis=0, keepdims=True
                )
            return carry

        lax.fori_loop(0, width // 256, spread_gains, 0)
        gather_x.finish()

        def norm_rows(index, carry):
            window = pl.ds(pl.multiple_of(index * 32, 32), 32)
            hidden_v[window, :] = rms_norm(xs[window, :].astype(jnp.float32), gain_rows[0:1, :]).astype(
                jnp.bfloat16
            )
            return carry

        lax.fori_loop(0, length // 32, norm_rows, 0)
        gather_q.finish()
        projected = jnp.dot(
            hidden_v[...], qkvs[...].reshape(width, qkv_width), preferred_element_type=jnp.float32
        ).astype(jnp.bfloat16)
        sorted_v[...] = jnp.dot(projected, order_v[...], preferred_element_type=jnp.float32).astype(
            jnp.bfloat16
        )
        stores = [
            pltpu.make_async_copy(source, target, outgoing.at[index])
            for index, (source, target) in enumerate(
                (
                    (qkvs, qkv_out),
                    (hidden_v, hidden_out),
                    (sorted_v, sorted_out),
                    (values_v, values_out),
                    (outputs_v, outputs_out),
                    (mixer_v, mixer_out),
                    (outs, w_out_out),
                    (order_v, order_out),
                )
            )
        ]
        for copy in stores[:3]:
            copy.start()
        marks = tap_marks(segment_column)

        def convolve(head, carry):
            columns = pl.ds(pl.multiple_of(head * DV, DV), DV)
            raw = sorted_v[:, columns].astype(jnp.float32)
            mixed = tap_v[0:1, columns] * raw
            for tap in range(1, KCONV):
                mixed = mixed + tap_v[tap : tap + 1, columns] * pltpu.roll(raw, tap, 0) * marks[tap]
            values_v[head] = mixed.astype(jnp.bfloat16)
            return carry

        lax.fori_loop(0, heads, convolve, 0)
        stores[3].start()
        gates.relay()
        steps = length // rows_at_once
        lanes = lax.broadcasted_iota(jnp.int32, (1, 128), 1)

        def attend(index, carry):
            head, start = lax.div(index, steps), lax.rem(index, steps) * rows_at_once
            rows = pl.ds(pl.multiple_of(start, rows_at_once), rows_at_once)
            mine = ((lanes >= head * FEAT) & (lanes < head * FEAT + FEAT)).astype(jnp.float32)
            queries = sorted_v[rows, value_width : value_width + 128] * mine.astype(jnp.bfloat16)
            scores = contract_last(queries, sorted_v[:, value_width + 128 :]) * 0.25
            places = start + lax.broadcasted_iota(jnp.int32, scores.shape, 0)
            allowed = (segment_column[rows, :1] == segment_row) & (
                places >= lax.broadcasted_iota(jnp.int32, scores.shape, 1)
            )
            kernel_values = jnp.where(allowed, 1.0 + scores + 0.5 * scores * scores, 0.0)
            denominator = jnp.sum(kernel_values, axis=1, keepdims=True)
            mixed = (
                jnp.dot(kernel_values.astype(jnp.bfloat16), values_v[head], preferred_element_type=jnp.float32)
                / denominator
            )
            outputs_v[head, rows, :] = mixed
            mixer_v[rows, pl.ds(pl.multiple_of(head * DV, DV), DV)] = mixed.astype(jnp.bfloat16)
            return carry

        turns = heads * steps
        for index in range(zs - 1):
            lax.fori_loop(turns * index // (zs - 1), turns * (index + 1) // (zs - 1), attend, 0)
            if index > 0:
                gather_o.step(index)
        gather_o.finish()
        for copy in stores[4:]:
            copy.start()

        def out_job(index, carry):
            window = pl.ds(pl.multiple_of(index * 512, 512), 512)
            term = jnp.dot(
                mixer_v[...], outs[:, :, window].reshape(value_width, 512), preferred_element_type=jnp.float32
            ).astype(jnp.bfloat16)
            for s in range(seq):
                for h in range(2):
                    begin = s * count + h * half
                    parts[begin : begin + half, window] = term[begin : begin + half]
            return carry

        lax.fori_loop(0, width // 512, out_job, 0)
        work = SquareSum(
            at, lambda s, h: parts.at[pl.ds(pl.multiple_of(s * count + h * half, half), half)], sum_scratch
        )
        work.start()
        work.relay()
        late_start()
        work.finish(lambda h: total.at[pl.ds(h * half, half)])

        def finish_rows(index, carry):
            for h in range(2):
                rows = pl.ds(pl.multiple_of(h * half + index * 16, 16), 16)
                attended = x_ref[rows, :].astype(jnp.float32) + total[rows, :]
                attended_out[rows, :] = attended
                normed_out[rows, :] = rms_norm(attended, gain_rows[1:2, :]).astype(jnp.bfloat16)
            return carry

        lax.fori_loop(0, half // 16, finish_rows, 0)
        gates.finish()
        gates_own.wait()
        stores[1].wait()
        stores[5].wait()
        feed()
        for copy in swaps:
            copy.wait_send()
        for index, copy in enumerate(stores):
            if index not in (1, 5):
                copy.wait()

    low, f32 = jnp.bfloat16, jnp.float32
    sorted_width = value_width + 256
    return remote_call(
        kernel,
        "forward_pass",
        0,
        [
            jax.ShapeDtypeStruct((count, width), f32),
            jax.ShapeDtypeStruct((count, width), low),
            jax.ShapeDtypeStruct((8, width), f32),
            jax.ShapeDtypeStruct((seq, wt, qkv_rank, qkv_width), low),
            jax.ShapeDtypeStruct((wt, out_rank, width), low),
            jax.ShapeDtypeStruct((length, width), low),
            jax.ShapeDtypeStruct((length, sorted_width), low),
            jax.ShapeDtypeStruct((length, value_width), low),
            jax.ShapeDtypeStruct((heads, length, DV), low),
            jax.ShapeDtypeStruct((heads, length, DV), f32),
            jax.ShapeDtypeStruct((qkv_width, sorted_width), low),
            jax.ShapeDtypeStruct((count, width), low),
            jax.ShapeDtypeStruct((count, width), f32),
            jax.ShapeDtypeStruct((8, width), f32),
            jax.ShapeDtypeStruct((token_count, width), low),
            jax.ShapeDtypeStruct((token_count, units), f32),
            jax.ShapeDtypeStruct((token_count, units), f32),
            jax.ShapeDtypeStruct((token_count, units), low),
            jax.ShapeDtypeStruct((units, width), low),
            jax.ShapeDtypeStruct((2, units, width), low),
        ],
        [
            pltpu.VMEM((length, width), low),
            pltpu.VMEM((seq, wt, qkv_rank, qkv_width), low),
            pltpu.VMEM((wt, out_rank, width), low),
            pltpu.VMEM((seq, wt * 8, 128), f32),
            pltpu.VMEM((length, sorted_width), low),
            pltpu.VMEM((heads, length, DV), low),
            pltpu.VMEM((heads, length, DV), f32),
            pltpu.VMEM((qkv_width, sorted_width), low),
            pltpu.VMEM((length, 128), f32),
            pltpu.VMEM((KCONV, value_width), f32),
            pltpu.VMEM((8, 128), f32),
        ]
        + SquareSum.scratch(seq, (count // 2, width))
        + SquareGather.semaphores(seq)
        + SquareGather.semaphores(seq)
        + LineGather.semaphores(wt, 2)
        + LineGather.semaphores(wt)
        + LineGather.semaphores(wt, 2)
        + [
            pltpu.SemaphoreType.DMA((seq, 2)),
            pltpu.SemaphoreType.DMA((seq, 2)),
            pltpu.SemaphoreType.DMA((5,)),
            pltpu.SemaphoreType.DMA((8,)),
            pltpu.VMEM((token_count, width), low),
            pltpu.VMEM((2, units, width), low),
            pltpu.VMEM((units, width), low),
            pltpu.VMEM((token_count, units), f32),
            pltpu.VMEM((token_count, units), f32),
            pltpu.VMEM((token_count, units), low),
            pltpu.VMEM((token_count, width), low),
            pltpu.VMEM((count, width), f32),
        ]
        + LineGather.semaphores(wt, 2)
        + LinePieces.scratch(wt, (count, width), seq)
        + SquareGather.semaphores(seq)
        + SquareGather.semaphores(seq)
        + [pltpu.SemaphoreType.DMA((5,)), pltpu.SemaphoreType.DMA((4, zs))],
        *small,
        lengths,
        gate_up,
        down,
        in_specs=[VMEM] * len(small) + [SMEM, ANY, ANY],
        out_specs=[VMEM] * 3 + [ANY] * 8 + [VMEM] * 3 + [ANY] * 6,
    )


def feed_back(error, attended, gain, gate_up, down, gate, up, active, normed):
    seq, wt = lax.axis_size("seq"), lax.axis_size("wt")
    count, width = error.shape
    units = gate_up.shape[1]
    tokens = wt * count
    ys = seq // 2
    block = width // seq
    half = (units // 2, block)

    def kernel(*refs):
        (error_ref, attended_ref, gain_ref, gate_up_ref, down_ref, gate_ref, up_ref, active_ref, normed_ref), refs = (
            refs[:9],
            refs[9:],
        )
        (grad_ref, mix_ref, gain_terms), refs = refs[:3], refs[3:]
        (gate_out, up_out, down_out, gate_x, gate_y, down_x, down_y), refs = refs[:7], refs[7:]
        (low, everyone, gates, downs, gate_all, up_all, back_all, parts, actives, columns), refs = refs[:10], refs[10:]
        (gate_terms, up_terms, down_terms, total), refs = refs[:4], refs[4:]
        gather_sems, sum_scratch, gate_sems, down_sems, (local, outgoing) = (
            refs[:1],
            refs[1:5],
            refs[5:7],
            refs[7:9],
            refs[9:],
        )
        at = Place(seq, wt)
        loads = [
            pltpu.make_async_copy(source, target, local.at[index])
            for index, (source, target) in enumerate(
                (
                    (down_ref, downs),
                    (gate_ref, gate_all),
                    (up_ref, up_all),
                    (gate_up_ref, gates),
                    (active_ref, actives),
                )
            )
        ]
        for load in loads:
            load.start()
        at.meet(True, True)
        low[...] = error_ref[...].astype(jnp.bfloat16)
        sums = LinePieces(
            at, lambda w: parts.at[pl.ds(pl.multiple_of(w * count, count), count)], sum_scratch
        )
        gate_sum = SquareTerms(at, lambda s, h: gate_terms.at[s, h], gate_x, gate_y, gate_sems)
        down_sum = SquareTerms(at, lambda s, h: down_terms.at[s, h], down_x, down_y, down_sems)

        def place(index):
            step = lax.div(index, 2) + 1
            x = lax.rem(at.x + 1 + lax.rem(index, 2), 2)
            return step, x, at.beside(step) * 2 + x

        def column_load(index):
            s = place(index)[2]
            return pltpu.make_async_copy(
                normed_ref.at[:, pl.ds(pl.multiple_of(s * block, block), block)],
                columns.at[lax.rem(index, 2)],
                local.at[6 + lax.rem(index, 2)],
            )

        def leave(sum_, index):
            step, x, s = place(index)

            @pl.when(x != at.x)
            def _():
                sum_.first_x(lax.div(s, 2)).start()

            @pl.when(step < ys)
            def _():
                sum_.first_y(step, x).start()

        def down_job(index):
            s = place(index)[2]
            term = contract_first(
                actives[...], everyone[:, pl.ds(pl.multiple_of(s * block, block), block)]
            ).astype(jnp.bfloat16)
            down_terms[s, 0] = term[: units // 2]
            down_terms[s, 1] = term[units // 2 :]
            leave(down_sum, index)

        def gate_job(index):
            s = place(index)[2]
            column_load(index).wait()
            here = columns.at[lax.rem(index, 2)]
            for number, terms in enumerate((gate_terms, up_terms)):
                term = contract_first(back_all[number], here[...]).astype(jnp.bfloat16)
                terms[s, 0] = term[: units // 2]
                terms[s, 1] = term[units // 2 :]

            @pl.when(index + 2 < seq)
            def _():
                column_load(index + 2).start()

            leave(gate_sum, index)

        def fill(slot, slots):
            if slot is None:
                lax.fori_loop(0, seq, lambda index, carry: (down_job(index), carry)[1], 0)
                return

            each = -(-seq // slots)

            def step(index, carry):
                job = slot * each + index

                @pl.when(job < seq)
                def _():
                    gate_job(job)

                return carry

            lax.fori_loop(0, each, step, 0)

        def prepare():
            column_load(0).start()
            column_load(1).start()
            for load in loads:
                load.wait()

        def rows(z):
            return pl.ds(pl.multiple_of(z * 2 * count, 2 * count), 2 * count)

        def first(z):
            active_back = contract_last(everyone[rows(z), :], downs[...])
            gate_here, up_here = gate_all[rows(z), :], up_all[rows(z), :]
            share = jax.nn.sigmoid(gate_here)
            back_all[0, rows(z), :] = (
                active_back * up_here * share * (1.0 + gate_here * (1.0 - share))
            ).astype(jnp.bfloat16)
            back_all[1, rows(z), :] = (active_back * gate_here * share).astype(jnp.bfloat16)

        def second(z, piece):
            window = pl.ds(pl.multiple_of(piece * sums.width, sums.width), sums.width)
            parts[rows(z), window] = (
                jnp.dot(back_all[0, rows(z), :], gates[0, :, window], preferred_element_type=jnp.float32)
                + jnp.dot(back_all[1, rows(z), :], gates[1, :, window], preferred_element_type=jnp.float32)
            ).astype(jnp.bfloat16)

        work = Exchange(at, low, everyone, gather_sems, local.at[5], sums, first, second)
        prepare()
        work.whole(total, fill)
        stores = [
            pltpu.make_async_copy(source, target, outgoing.at[index])
            for index, (source, target) in enumerate(
                ((gate_terms, gate_out), (up_terms, up_out), (down_terms, down_out))
            )
        ]
        for copy in stores:
            copy.start()
        gain_terms[...] = jnp.zeros_like(gain_terms)

        def load_rows(window):
            return attended_ref[window, :], total[window, :], error_ref[window, :]

        def store_rows(window, value):
            grad_ref[window, :] = value
            mix_ref[window, :] = value.astype(jnp.bfloat16)

        norm_back(count, load_rows, store_rows, gain_ref[1:2, :], gain_terms)
        for copy in stores:
            copy.wait()
        gate_sum.first_wait()
        down_sum.first_wait()

    def terms_of(half):
        return jax.ShapeDtypeStruct((seq, 2) + half, jnp.bfloat16)

    def first_of(half):
        return [
            jax.ShapeDtypeStruct((ys,) + half, jnp.bfloat16),
            jax.ShapeDtypeStruct((ys, 2) + half, jnp.bfloat16),
        ]

    return remote_call(
        kernel,
        "feed_back",
        3,
        [
            jax.ShapeDtypeStruct((count, width), jnp.float32),
            jax.ShapeDtypeStruct((count, width), jnp.bfloat16),
            jax.ShapeDtypeStruct((8, width), jnp.float32),
            terms_of(half),
            terms_of(half),
            terms_of(half),
        ]
        + first_of(half)
        + first_of(half),
        [
            pltpu.VMEM((count, width), jnp.bfloat16),
            pltpu.VMEM((tokens, width), jnp.bfloat16),
            pltpu.VMEM(gate_up.shape, jnp.bfloat16),
            pltpu.VMEM((units, width), jnp.bfloat16),
            pltpu.VMEM((tokens, units), jnp.float32),
            pltpu.VMEM((tokens, units), jnp.float32),
            pltpu.VMEM((2, tokens, units), jnp.bfloat16),
            pltpu.VMEM((tokens, width), jnp.bfloat16),
            pltpu.VMEM((tokens, units), jnp.bfloat16),
            pltpu.VMEM((2, tokens, block), jnp.bfloat16),
            pltpu.VMEM((seq, 2) + half, jnp.bfloat16),
            pltpu.VMEM((seq, 2) + half, jnp.bfloat16),
            pltpu.VMEM((seq, 2) + half, jnp.bfloat16),
            pltpu.VMEM((count, width), jnp.float32),
        ]
        + LineGather.semaphores(wt, 2)
        + LinePieces.scratch(wt, (count, width), PIECES)
        + SquareTerms.semaphores(seq)
        + SquareTerms.semaphores(seq)
        + [pltpu.SemaphoreType.DMA((8,)), pltpu.SemaphoreType.DMA((3,))],
        error,
        attended,
        gain,
        gate_up,
        down,
        gate,
        up,
        active,
        normed,
        in_specs=[VMEM] * 3 + [ANY] * 6,
        out_specs=[VMEM] * 3 + [ANY] * 7,
    )


def mixer_back(
    mix_back,
    attended_grad,
    tokens,
    gain,
    out_rows,
    qkv_columns,
    hidden,
    sorted_columns,
    mixer,
    mixed_values,
    head_outputs,
    segments,
    taps,
    order,
    gain_terms,
    energy,
    gate_parts,
    up_parts,
    down_parts,
):
    seq, wt = lax.axis_size("seq"), lax.axis_size("wt")
    zs, ys = wt // 2, seq // 2
    count, width = mix_back.shape
    length = count * seq
    heads = mixed_values.shape[0]
    qkv_width = qkv_columns.shape[1]
    value_width = heads * DV
    rank = width // (seq * wt)
    gate_half, down_half = gate_parts[0].shape[2:], down_parts[0].shape[2:]
    rows_at_once = 256
    turns = heads * length // rows_at_once
    soon = [out_rows, qkv_columns, hidden, sorted_columns, mixer, mixed_values, head_outputs]
    big = soon + [attended_grad, tokens, order, gain_terms, energy]
    small = [mix_back, gain, segments, taps]
    far = list(gate_parts) + list(down_parts) + list(up_parts)

    def kernel(*refs):
        big_refs, refs = refs[: len(big)], refs[len(big) :]
        small_refs, refs = refs[: len(small)], refs[len(small) :]
        (gate_t, gate_x, gate_y, down_t, down_x, down_y, up_t), refs = refs[: len(far)], refs[len(far) :]
        (grad_out, sums_out, qkv_out, w_out_out, up_x, up_y), refs = refs[:6], refs[6:]
        gate_lasts, up_lasts, down_lasts, refs = refs[:2], refs[2:4], refs[4:6], refs[6:]
        big_rooms, refs = refs[: len(big)], refs[len(big) :]
        w_out_v, w_qkv_v, hidden_v, sorted_v, mixer_v, values_v, outputs_v = big_rooms[: len(soon)]
        grad_ref, token_ref, order_ref, gain_two, energy_ref = big_rooms[len(soon) :]
        (mix_all, mixer_grad, query_acc, key_acc, value_acc, back_sorted, back_v), refs = refs[:7], refs[7:]
        (hidden_parts, qkv_parts, out_parts, hidden_total, gain_acc, spread, taps_acc), refs = refs[:7], refs[7:]
        (segment_column, tap_v, slopes_v, weights_v, denominators_v), refs = refs[:5], refs[5:]
        (room_gate0, room_gate1, room_down0, room_down1, qkv_sum, first, middle, last), refs = refs[:8], refs[8:]
        hidden_scratch, refs = refs[:8], refs[8:]
        qkv_scratch, out_scratch, refs = refs[:4], refs[4:8], refs[8:]
        gate_scratch, down_scratch, up_scratch, refs = refs[:3], refs[3:6], refs[6:9], refs[9:]
        gather_sems, up_sems, refs = refs[:3], refs[3:5], refs[5:]
        local, swap, first_sems, last_sems, fetch_sems = refs
        mix_ref, gain_ref, segment_ref, tap_ref = small_refs
        at = Place(seq, wt)
        loads = [
            pltpu.make_async_copy(source, target, local.at[4 + index])
            for index, (source, target) in enumerate(zip(big_refs, big_rooms))
        ]
        for load in loads:
            load.start()
        gate_sum = SquareTerms(at, lambda s, h: gate_t.at[s, h], gate_x, gate_y, None, gate_lasts, gate_scratch)
        down_sum = SquareTerms(at, lambda s, h: down_t.at[s, h], down_x, down_y, None, down_lasts, down_scratch)
        up_sum = SquareTerms(at, lambda s, h: up_t.at[s, h], up_x, up_y, up_sems, up_lasts, up_scratch)
        gate_rooms, down_rooms = (room_gate0, room_gate1), (room_down0, room_down1)
        fetches = [
            pltpu.make_async_copy(source, target, fetch_sems.at[number, index])
            for number, pairs in enumerate(
                (gate_sum.second_pairs(gate_rooms), down_sum.second_pairs(down_rooms), up_sum.second_pairs())
            )
            for index, (source, target) in enumerate(pairs)
        ]
        for copy in fetches:
            copy.start()
        at.meet(True, True)
        half = count // 2
        gather = SquareGather(
            at,
            lambda s, h: mix_all.at[pl.ds(pl.multiple_of(s * count + h * half, half), half)],
            lambda h: mix_ref.at[pl.ds(h * half, half)],
            gather_sems,
        )
        gather.start()
        own = pltpu.make_async_copy(
            mix_ref, mix_all.at[pl.ds(pl.multiple_of(at.s * count, count), count)], local.at[3]
        )
        own.start()

        tap_v[...] = tap_ref[...].astype(jnp.float32)
        segment_row = segment_ref[...].astype(jnp.float32)
        segment_column[...] = jnp.broadcast_to(segment_row, (128, length)).T
        for load in loads[: len(soon)]:
            load.wait()
        query_acc[...] = jnp.zeros_like(query_acc)
        key_acc[...] = jnp.zeros_like(key_acc)
        value_acc[...] = jnp.zeros_like(value_acc)
        steps = length // rows_at_once
        lanes = lax.broadcasted_iota(jnp.int32, (1, 128), 1)

        def turn_of(index):
            head, start = lax.div(index, steps), lax.rem(index, steps) * rows_at_once
            rows = pl.ds(pl.multiple_of(start, rows_at_once), rows_at_once)
            mine = ((lanes >= head * FEAT) & (lanes < head * FEAT + FEAT)).astype(jnp.float32)
            queries = sorted_v[rows, value_width : value_width + 128] * mine.astype(jnp.bfloat16)
            return head, start, rows, mine, queries

        def prepare(index, carry):
            head, start, rows, mine, queries = turn_of(index)
            scores = contract_last(queries, sorted_v[:, value_width + 128 :]) * 0.25
            places = start + lax.broadcasted_iota(jnp.int32, scores.shape, 0)
            allowed = (segment_column[rows, :1] == segment_row) & (
                places >= lax.broadcasted_iota(jnp.int32, scores.shape, 1)
            )
            kernel_values = jnp.where(allowed, 1.0 + scores + 0.5 * scores * scores, 0.0)
            slopes_v[index] = jnp.where(allowed, 0.25 * (1.0 + scores), 0.0)
            weights_v[index] = kernel_values.astype(jnp.bfloat16)
            denominators_v[index] = jnp.broadcast_to(
                jnp.sum(kernel_values, axis=1, keepdims=True), (rows_at_once, 128)
            )
            return carry

        middle_step = heads * steps // 2
        lax.fori_loop(0, middle_step, prepare, 0)
        gather.relay()
        lax.fori_loop(middle_step, heads * steps, prepare, 0)
        for copy in fetches:
            copy.wait()
        gate_sum.second_add(gate_rooms)
        down_sum.second_add(down_rooms)
        own.wait()
        for load in loads[len(soon) :]:
            load.wait()
        gather.finish()
        up_sum.first_start()
        gate_sum.second_go()
        down_sum.second_go()
        mixer_grad[...] = contract_last(mix_all[...], w_out_v[...]).astype(jnp.bfloat16)
        out_sum = LinePieces(at, lambda w: out_parts.at[w], out_scratch)
        out_rank = out_parts.shape[1]
        out_block = 512 if value_width % 512 == 0 else value_width

        def out_job(index, carry):
            window = pl.ds(pl.multiple_of(index * 512, 512), 512)
            term = contract_first(mixer_v[...], mix_all[:, window]).astype(jnp.bfloat16)
            for w in range(wt):
                out_parts[w, :, window] = term[w * out_rank : (w + 1) * out_rank]
            return carry

        lax.fori_loop(0, width // 512, out_job, 0)
        for piece in range(out_sum.pieces):
            out_sum.offer(piece)
        for piece in range(out_sum.pieces):
            out_sum.launch(piece, 0)

        def attend(index, carry):
            head, start, rows, mine, queries = turn_of(index)
            columns = pl.ds(pl.multiple_of(head * DV, DV), DV)
            denominator = denominators_v[index][:, :1]
            incoming = mixer_grad[rows, columns].astype(jnp.float32)
            numerator_back = (incoming / denominator).astype(jnp.bfloat16)
            denominator_back = (
                -jnp.sum(incoming * outputs_v[head, rows, :], axis=1, keepdims=True) / denominator
            )
            weight_back = contract_last(numerator_back, values_v[head])
            dots_back = ((weight_back + denominator_back) * slopes_v[index]).astype(jnp.bfloat16)
            query_acc[rows, :] += (
                jnp.dot(dots_back, sorted_v[:, value_width + 128 :], preferred_element_type=jnp.float32) * mine
            )
            key_acc[...] += contract_first(dots_back, queries)
            value_acc[:, columns] += contract_first(weights_v[index], numerator_back)
            return carry

        lax.fori_loop(0, heads * steps, attend, 0)
        taps_acc[...] = jnp.zeros_like(taps_acc)
        marks = tap_marks(segment_column)

        def convolve(head, carry):
            columns = pl.ds(pl.multiple_of(head * DV, DV), DV)
            mixed_back = value_acc[:, columns]
            raw = sorted_v[:, columns].astype(jnp.float32)
            raw_back = tap_v[0:1, columns] * mixed_back
            taps_acc[3:4, columns] = jnp.sum(mixed_back * raw, axis=0, keepdims=True)
            for tap in range(1, KCONV):
                masked = mixed_back * marks[tap]
                taps_acc[3 + tap : 4 + tap, columns] = jnp.sum(
                    masked * pltpu.roll(raw, tap, 0), axis=0, keepdims=True
                )
                raw_back = raw_back + tap_v[tap : tap + 1, columns] * pltpu.roll(masked, length - tap, 0)
            back_sorted[:, columns] = raw_back.astype(jnp.bfloat16)
            return carry

        lax.fori_loop(0, heads, convolve, 0)
        back_sorted[:, value_width : value_width + 128] = query_acc[...].astype(jnp.bfloat16)
        back_sorted[:, value_width + 128 :] = key_acc[...].astype(jnp.bfloat16)
        back_v[...] = contract_last(back_sorted[...], order_ref[...]).astype(jnp.bfloat16)
        out_sum.launch_all(1)
        qkv_sums = LinePieces(at, lambda w: qkv_parts.at[:, w], qkv_scratch)
        qkv_rank = qkv_parts.shape[2]

        def qkv_job(s, carry):
            block = wt * qkv_rank
            window = pl.ds(pl.multiple_of(s * block, block), block)
            term = contract_first(hidden_v[:, window], back_v[...]).astype(jnp.bfloat16)
            for w in range(wt):
                qkv_parts[s, w] = term[w * qkv_rank : (w + 1) * qkv_rank]
            qkv_sums.offer(s)

            @pl.when(s > 0)
            def _():
                qkv_sums.launch(s - 1, 0)

            return carry

        lax.fori_loop(0, seq, qkv_job, 0)
        qkv_sums.launch(seq - 1, 0)
        hidden_sum = SquareSum(at, lambda s, h: hidden_parts.at[s, h], hidden_scratch)

        def hidden_job(index, carry):
            window = pl.ds(pl.multiple_of(index * 512, 512), 512)
            term = contract_last(back_v[...], w_qkv_v[window, :]).astype(jnp.bfloat16)
            for s in range(seq):
                for h in range(2):
                    begin = s * count + h * half
                    hidden_parts[s, h, :, window] = term[begin : begin + half]
            return carry

        lax.fori_loop(0, width // 512, hidden_job, 0)
        hidden_sum.start()
        for index in range(zs - 1, 1, -1):
            out_sum.pass_on(index)
        qkv_sums.launch_all(1)
        qkv_sums.pass_on(zs - 1)
        hidden_sum.relay()
        up_sum.first_wait()
        up_sum.second_add()
        up_sum.second_go()
        for index in range(zs - 2, 1, -1):
            qkv_sums.pass_on(index)
        hidden_sum.finish(lambda h: hidden_total.at[h])
        gain_acc[...] = jnp.zeros_like(gain_acc)
        for h in range(2):

            def shift(window):
                return pl.ds(pl.multiple_of(h * half + window.start, 16), 16)

            def load_rows(window):
                rows = shift(window)
                return token_ref[rows, :].astype(jnp.float32), hidden_total[h, window, :], grad_ref[rows, :]

            def store_rows(window, value):
                grad_out[shift(window), :] = value

            norm_back(half, load_rows, store_rows, gain_ref[0:1, :], gain_acc)
        spread[...] = jnp.zeros_like(spread)
        spread[0:1, :] = jnp.sum(gain_acc[...], axis=0, keepdims=True)
        spread[1:2, :] = jnp.sum(gain_two[...], axis=0, keepdims=True)
        energy = jnp.sum(jnp.sum(energy_ref[...], axis=0, keepdims=True), axis=1, keepdims=True)
        spread[2:3, :] = jnp.broadcast_to(energy, (1, width))
        copies = []
        for step in range(1, seq):
            to = lax.rem(at.s + step, seq)
            window = pl.ds(pl.multiple_of(to * value_width, value_width), value_width)
            copies.append(
                send(spread.at[:, window], first.at[at.s], first_sems.at[step, 0], first_sems.at[at.s, 1], (to, at.w))
            )
        for copy in copies:
            copy.start()

        def give(s):
            return send(qkv_sum.at[s], qkv_out.at[at.s], swap.at[s, 0], swap.at[at.s, 1], (s, at.w))

        def done(s):
            @pl.when(s != at.s)
            def _():
                give(s).start()

        qkv_sums.finish(qkv_sum, done)
        add_into(qkv_out.at[at.s], [qkv_sum.at[at.s]])
        out_sum.finish(w_out_out)
        terms = [spread.at[:, pl.ds(pl.multiple_of(at.s * value_width, value_width), value_width)], taps_acc]
        for step in range(1, seq):
            s = lax.rem(at.s + step, seq)
            slot = first.at[s]
            send(slot, slot, first_sems.at[step, 0], first_sems.at[s, 1], at.across()).wait_recv()
            terms.append(slot)
        add_into(middle, terms)
        for step in range(1, wt):
            to = lax.rem(at.w + step, wt)
            copy = send(middle, last.at[at.w], last_sems.at[step, 0], last_sems.at[at.w, 1], (at.s, to))
            copy.start()
            copies.append(copy)
        gate_sum.second_wait()
        down_sum.second_wait()
        terms = [middle]
        for step in range(1, wt):
            w = lax.rem(at.w + step, wt)
            slot = last.at[w]
            send(slot, slot, last_sems.at[step, 0], last_sems.at[w, 1], at.partner()).wait_recv()
            terms.append(slot)
        add_into(sums_out, terms)
        for step in range(1, seq):
            s = lax.rem(at.s + step, seq)
            slot = qkv_out.at[s]
            send(slot, slot, swap.at[s, 0], swap.at[s, 1], at.across()).wait_recv()
            give(s).wait_send()
        up_sum.second_wait()
        for copy in copies:
            copy.wait_send()

    out_rank, qkv_rank = value_width // wt, width // (seq * wt)
    f32, low = jnp.float32, jnp.bfloat16
    tile = (8, value_width)
    results = remote_call(
        kernel,
        "mixer_back",
        4,
        [
            jax.ShapeDtypeStruct((count, width), f32),
            jax.ShapeDtypeStruct(tile, f32),
            jax.ShapeDtypeStruct((seq, qkv_rank, qkv_width), low),
            jax.ShapeDtypeStruct((out_rank, width), f32),
            jax.ShapeDtypeStruct((ys,) + gate_half, low),
            jax.ShapeDtypeStruct((ys, 2) + gate_half, low),
        ]
        + [
            jax.ShapeDtypeStruct(shape, low)
            for shape_half in (gate_half, gate_half, down_half)
            for shape in ((ys,) + shape_half, shape_half)
        ],
        [pltpu.VMEM(array.shape, array.dtype) for array in big]
        + [
            pltpu.VMEM((length, width), low),
            pltpu.VMEM((length, value_width), low),
            pltpu.VMEM((length, 128), f32),
            pltpu.VMEM((length, 128), f32),
            pltpu.VMEM((length, value_width), f32),
            pltpu.VMEM((length, value_width + 256), low),
            pltpu.VMEM((length, qkv_width), low),
            pltpu.VMEM((seq, 2, count // 2, width), low),
            pltpu.VMEM((seq, wt, qkv_rank, qkv_width), low),
            pltpu.VMEM((wt, out_rank, width), low),
            pltpu.VMEM((2, count // 2, width), f32),
            pltpu.VMEM((8, width), f32),
            pltpu.VMEM((8, width), f32),
            pltpu.VMEM(tile, f32),
            pltpu.VMEM((length, 128), f32),
            pltpu.VMEM((KCONV, value_width), f32),
            pltpu.VMEM((turns, rows_at_once, length), f32),
            pltpu.VMEM((turns, rows_at_once, length), low),
            pltpu.VMEM((turns, rows_at_once, 128), f32),
            pltpu.VMEM((ys - 1,) + gate_half, low),
            pltpu.VMEM((ys - 1,) + gate_half, low),
            pltpu.VMEM((ys - 1,) + down_half, low),
            pltpu.VMEM((ys - 1,) + down_half, low),
            pltpu.VMEM((seq, qkv_rank, qkv_width), low),
            pltpu.VMEM((seq,) + tile, f32),
            pltpu.VMEM(tile, f32),
            pltpu.VMEM((wt,) + tile, f32),
        ]
        + SquareSum.scratch(seq, (count // 2, width))
        + LinePieces.scratch(wt, (seq, qkv_rank, qkv_width), seq)
        + LinePieces.scratch(wt, (out_rank, width), 1)
        + SquareTerms.scratch(seq, gate_half)
        + SquareTerms.scratch(seq, down_half)
        + SquareTerms.scratch(seq, gate_half)
        + SquareGather.semaphores(seq)
        + SquareTerms.semaphores(seq)
        + [
            pltpu.SemaphoreType.DMA((4 + len(big),)),
            pltpu.SemaphoreType.DMA((seq, 2)),
            pltpu.SemaphoreType.DMA((seq, 2)),
            pltpu.SemaphoreType.DMA((wt, 2)),
            pltpu.SemaphoreType.DMA((3, 3 * (ys - 1) + 1)),
        ],
        *big,
        *small,
        *far,
        in_specs=[ANY] * len(big) + [VMEM] * len(small) + [ANY] * len(far),
        out_specs=[VMEM] * 6 + [ANY] * 6,
    )
    grad, totals, qkv_total, out_total, up_x, up_y = results[:6]
    gate = tuple(gate_parts) + tuple(results[6:8])
    up = tuple(up_parts) + (up_x, up_y) + tuple(results[8:10])
    down = tuple(down_parts) + tuple(results[10:12])
    return grad, totals, gate, up, down, qkv_total, out_total


def last_sums(gate, up, down, qkv_total, totals, lengths, out_total, grad, final, qkv_shape):
    seq, wt = lax.axis_size("seq"), lax.axis_size("wt")
    ys = seq // 2
    f32, low = jnp.float32, jnp.bfloat16
    gate_half, down_half = gate[0].shape[2:], down[0].shape[2:]
    total_width = totals.shape[1]
    lanes_each = total_width // wt
    width = grad.shape[1]
    qkv_width = qkv_total.shape[2]
    operands = list(gate) + list(up) + list(down)
    passed = [out_total, grad, final]

    def kernel(*refs):
        groups, refs = [refs[5 * index : 5 * index + 5] for index in range(3)], refs[15:]
        (qkv_ref, totals_ref, length_ref), passed_refs, refs = refs[:3], refs[3:6], refs[6:]
        (gate_up_out, down_out, qkv_out, first_gain, second_gain, taps_out, loss_out), refs = refs[:7], refs[7:]
        passed_outs, refs = refs[:3], refs[3:]
        totals, refs = refs[:2], refs[2:]
        passed_rooms, refs = refs[:3], refs[3:]
        rooms, (loads, stores, pass_sems) = [refs[5 * index : 5 * index + 5] for index in range(3)], refs[15:]
        s = lax.axis_index("seq")
        y, x = lax.div(s, 2), lax.rem(s, 2)
        copies = []
        for number, (group, room) in enumerate(zip(groups, rooms)):
            terms, from_x, from_y, last_y, last_x = group
            pairs = [(terms.at[s], room[0]), (from_x.at[y], room[1]), (last_x, room[4])]
            for other in range(1, ys):
                place = lax.rem(y + other, ys)
                pairs.append((from_y.at[place, x], room[2].at[other - 1]))
                pairs.append((last_y.at[place], room[3].at[other - 1]))
            mine = [
                pltpu.make_async_copy(source, target, loads.at[number, index])
                for index, (source, target) in enumerate(pairs)
            ]
            for copy in mine:
                copy.start()
            copies.append(mine)
        ins = [
            pltpu.make_async_copy(source, room, pass_sems.at[index, 0])
            for index, (source, room) in enumerate(zip(passed_refs, passed_rooms))
        ]
        for copy in ins:
            copy.start()
        shift = lax.rem(total_width - lax.axis_index("wt") * lanes_each, total_width)
        mine = pltpu.roll(totals_ref[...], shift, 1)[:, :lanes_each]
        first_gain[...] = mine[0:1]
        second_gain[...] = mine[1:2]
        taps_out[...] = mine[3 : 3 + KCONV]
        counted = length_ref[0]
        for index in range(1, length_ref.shape[0]):
            counted = counted + length_ref[index]
        loss_out[...] = 2.0 * totals_ref[2:3, :1] / (jnp.full((1, 1), counted, jnp.int32).astype(f32) * width)
        for index in range(seq):
            qkv_out[:, index * qkv_width : (index + 1) * qkv_width] = qkv_ref[index].astype(f32)
        outs = []
        for index, (room, target) in enumerate(zip(passed_rooms, passed_outs)):
            ins[index].wait()
            copy = pltpu.make_async_copy(room, target, pass_sems.at[index, 1])
            copy.start()
            outs.append(copy)
        for number, room in enumerate(rooms):
            own, near_x, near_y, last_y, last_x = room
            total = totals[number // 2]
            base = 2 * (number % 2)
            for copy in copies[number]:
                copy.wait()
            rows = own.shape[1]
            tile = next(t for t in (176, 64, 32, 16) if rows % t == 0)

            def step(index, carry):
                window = pl.ds(pl.multiple_of(index * tile, tile), tile)
                first = own[0, window, :].astype(f32) + near_x[window, :].astype(f32)
                second = own[1, window, :].astype(f32) + last_x[window, :].astype(f32)
                for other in range(ys - 1):
                    first = first + last_y[other, window, :].astype(f32)
                    second = second + near_y[other, window, :].astype(f32)
                total[base, window, :] = first
                total[base + 1, window, :] = second
                return carry

            lax.fori_loop(0, rows // tile, step, 0)
            target = gate_up_out.at[pl.ds(base, 2)] if number < 2 else down_out
            copy = pltpu.make_async_copy(total.at[pl.ds(base, 2)], target, stores.at[number])
            copy.start()
            outs.append(copy)
        for copy in outs:
            copy.wait()

    def rooms(half):
        return [
            pltpu.VMEM((2,) + half, low),
            pltpu.VMEM(half, low),
            pltpu.VMEM((ys - 1,) + half, low),
            pltpu.VMEM((ys - 1,) + half, low),
            pltpu.VMEM(half, low),
        ]

    return pl.pallas_call(
        kernel,
        name="last_sums",
        out_shape=[
            jax.ShapeDtypeStruct((4,) + gate_half, f32),
            jax.ShapeDtypeStruct((2,) + down_half, f32),
            jax.ShapeDtypeStruct(qkv_shape, f32),
            jax.ShapeDtypeStruct((1, lanes_each), f32),
            jax.ShapeDtypeStruct((1, lanes_each), f32),
            jax.ShapeDtypeStruct((KCONV, lanes_each), f32),
            jax.ShapeDtypeStruct((1, 1), f32),
        ]
        + [jax.ShapeDtypeStruct(array.shape, array.dtype) for array in passed],
        in_specs=[ANY] * 15 + [VMEM] * 2 + [SMEM] + [ANY] * 3,
        out_specs=[ANY] * 2 + [VMEM] * 5 + [ANY] * 3,
        scratch_shapes=[pltpu.VMEM((4,) + gate_half, f32), pltpu.VMEM((2,) + down_half, f32)]
        + [pltpu.VMEM(array.shape, array.dtype) for array in passed]
        + rooms(gate_half) * 2
        + rooms(down_half)
        + [
            pltpu.SemaphoreType.DMA((3, 1 + seq)),
            pltpu.SemaphoreType.DMA((3,)),
            pltpu.SemaphoreType.DMA((3, 2)),
        ],
        compiler_params=pltpu.CompilerParams(vmem_limit_bytes=VMEM_LIMIT),
    )(*operands, qkv_total, totals, lengths, *passed)


def body(
    inputs,
    segment_ids,
    valid_lengths,
    teacher,
    w_qkv,
    conv_weight,
    w_out,
    norm_gain,
    w_gate_up,
    w_down,
    mlp_gain,
):
    seq_parts = lax.axis_size("seq")
    tok_count = inputs.shape[1]
    model_width = inputs.shape[2]
    length = tok_count * seq_parts
    head_count = H // seq_parts
    qkv_width = head_count * (2 * FEAT + DV)
    rows_low = inputs[0]
    gain_lanes = norm_gain.shape[0]
    qkv_rows = w_qkv
    if qkv_width % 128:
        qkv_rows = w_qkv.reshape(w_qkv.shape[0], seq_parts, qkv_width).transpose(1, 0, 2)
    gate_up_low = w_gate_up.swapaxes(1, 2)
    segments = segment_ids
    (
        attended,
        _,
        gain_rows,
        qkv_columns,
        out_rows,
        hidden_low,
        sorted_columns,
        mixer_low,
        mixed_values,
        head_outputs,
        order,
        final_low,
        residual_error,
        energy,
        normed_all,
        gate_all,
        up_all,
        active_all,
        down_part,
        gate_up_part,
    ) = forward_pass(
        rows_low,
        qkv_rows,
        w_out,
        norm_gain,
        mlp_gain,
        segments,
        conv_weight,
        teacher[0],
        w_down,
        valid_lengths,
        gate_up_low,
    )
    (
        attended_grad,
        mix_back,
        gain_two_terms,
        gate_terms,
        up_terms,
        down_terms,
        gate_from_x,
        gate_from_y,
        down_from_x,
        down_from_y,
    ) = feed_back(
        residual_error,
        attended,
        gain_rows,
        gate_up_part,
        down_part,
        gate_all,
        up_all,
        active_all,
        normed_all,
    )
    inputs_grad, totals, gate, up, down, qkv_total, out_total = mixer_back(
        mix_back,
        attended_grad,
        rows_low,
        gain_rows,
        out_rows.reshape(head_count * DV, model_width),
        qkv_columns.reshape(model_width, qkv_width),
        hidden_low,
        sorted_columns,
        mixer_low,
        mixed_values,
        head_outputs,
        segments,
        conv_weight,
        order,
        gain_two_terms,
        energy,
        (gate_terms, gate_from_x, gate_from_y),
        (up_terms,),
        (down_terms, down_from_x, down_from_y),
    )
    (
        grad_w_gate_up,
        grad_w_down,
        grad_w_qkv,
        grad_norm_gain,
        grad_mlp_gain,
        grad_conv,
        mean_loss,
        grad_w_out,
        inputs_grad,
        outputs,
    ) = last_sums(
        gate, up, down, qkv_total, totals, valid_lengths, out_total, inputs_grad, final_low, w_qkv.shape
    )
    return (
        outputs[None],
        inputs_grad[None],
        mean_loss.reshape(()),
        grad_w_qkv,
        grad_conv,
        grad_w_out,
        grad_norm_gain.reshape(norm_gain.shape),
        grad_w_gate_up.reshape(gate_up_low.shape).swapaxes(1, 2),
        grad_w_down.reshape(w_down.shape),
        grad_mlp_gain.reshape(mlp_gain.shape),
    )


def solution(mesh):
    in_specs = (
        P("wt", "seq", None),
        P("wt", None),
        P(),
        P("wt", "seq", None),
        P(("seq", "wt"), None),
        P(None, "seq"),
        P(("seq", "wt"), None),
        P(("seq", "wt")),
        P(None, "seq", "wt"),
        P("wt", "seq"),
        P(("seq", "wt")),
    )
    out_specs = (
        P("wt", "seq", None),
        P("wt", "seq", None),
        P(),
        P(("seq", "wt"), None),
        P(None, ("seq", "wt")),
        P(("seq", "wt"), None),
        P(("seq", "wt")),
        P(None, "seq", "wt"),
        P("wt", "seq"),
        P(("seq", "wt")),
    )
    return jax.shard_map(body, mesh=mesh, in_specs=in_specs, out_specs=out_specs, check_vma=False)
```
